32 devices in a mesh: slides: 1, row: 2 (over core), col: 16 (over z, y, x).
Axes of the slice: x: 2, y: 2, z: 4, core: 2. Of those that a mesh axis runs over, the one named last changes fastest.
Arguments:
- slide: bfloat16 [56, 112, 1024], P(('slides', 'row'), 'col'), may hold values from -6 to 6
- tissue: int32 [56, 112], P(('slides', 'row'), 'col'), may hold values from 0 to 1, as said below
- w_in: bfloat16 [1024, 2048], replicated, may hold values from -0.1875 to 0.1875
- w_bcd: bfloat16 [1024, 48], replicated, may hold values from -0.1875 to 0.1875
- dt_bias: float32 [16], replicated, may hold values from -2 to 1
- rate_x: float32 [16], replicated, as said below
- rate_y: float32 [16], replicated, as said below
- d_skip: float32 [16], replicated, may hold values from 0.5 to 2
- norm_gain: float32 [1024], replicated, may hold values from 0.1 to 1.9
- w_out: bfloat16 [1024, 1024], replicated, may hold values from -0.1875 to 0.1875
Outputs:
- mixed: bfloat16 [56, 112, 1024], P(('slides', 'row'), 'col')
The draws below stay inside these ranges and needn't reach their ends.
Inputs may be any that keep to these rules, and one draw needn't show every extreme that they name: 1 marks a tissue patch, 0 background. `rate_x`: positive decay rates per head. `rate_y`: positive decay rates per head.
All inputs are finite; a program needn't handle non-finite values.
Results may differ from the reference program's by a relative error of at most 0.013.
Values may be sent and summed in bfloat16 or wider, within the bound.
No kernel may reach another device: no remote copies, remote signals or barrier semaphores. Data moves between devices by JAX's collectives and lax.ppermute only.
A program may use at most 320 MiB of HBM per device.

```python
import math
import jax
import jax.numpy as jnp
from jax import lax

D = 1024
HEADS = 16
HEAD_DIM = 64
STATE = 16
TILE_COLS = 7
INNER = 1024
ROWS = 56
COLS = 112


def draw_tissue(key, part):
    first_key, second_key = jax.random.split(key)
    tile_level = jax.random.randint(first_key, (COLS // TILE_COLS,), 0, 5)
    cell_draw = jax.random.randint(second_key, (ROWS, COLS), 0, 4)
    return (cell_draw < jnp.repeat(tile_level, TILE_COLS)[None, :]).astype(jnp.int32)


def draw_rate_x(key, part):
    picked = jax.random.uniform(jax.random.fold_in(key, 11), (HEADS,), jnp.float32)
    lower_end = jnp.log(0.2 / COLS)
    upper_end = jnp.log(1.0 / 24.0)
    return jnp.exp(lower_end + picked * (upper_end - lower_end)).astype(jnp.float32)


def draw_rate_y(key, part):
    picked = jax.random.uniform(jax.random.fold_in(key, 23), (HEADS,), jnp.float32)
    lower_end = jnp.log(0.2 / ROWS)
    upper_end = jnp.log(max(1.0 / 24.0, 4.0 / ROWS))
    return jnp.exp(lower_end + picked * (upper_end - lower_end)).astype(jnp.float32)


def block_levels(stream_key, shape, pieces, least, largest):
    loudness = 1.0
    for axis_at, blocks in pieces:
        heights = jax.random.uniform(jax.random.fold_in(jax.random.fold_in(stream_key, 6), axis_at), (blocks,), jnp.float32, least / len(pieces), largest / len(pieces))
        loudness = loudness * jnp.repeat(jnp.exp(heights), shape[axis_at] // blocks).reshape((-1,) + (1,) * (len(shape) - 1 - axis_at))
    return loudness


def centred(own_key, extent, width, reach, cuts=(), held_as=jnp.bfloat16):
    values = width * jax.random.normal(own_key, extent, jnp.float32)
    if cuts:
        values = values * block_levels(own_key, extent, cuts, -0.22, 0.18)
    return jnp.clip(values, -reach, reach).astype(held_as)


def setup_inputs(seed: int = 0, part: int = 0) -> dict:
    splits = jax.random.split(jax.random.key(seed), 11)
    own_keys = jax.random.split(jax.random.fold_in(splits[10], part), 11)
    slide = centred(own_keys[0], (ROWS, COLS, D), 1.0, 6.0, ((0, 2), (1, 16)))
    tissue = draw_tissue(jax.random.fold_in(jax.random.fold_in(splits[10], part), 71), part)
    w_in = centred(splits[2], (D, 2 * INNER), D ** -0.5, 0.1875)
    w_bcd = centred(splits[3], (D, 2 * STATE + HEADS), D ** -0.5, 0.1875)
    dt_bias = jnp.clip(jax.random.uniform(splits[4], (HEADS,), jnp.float32, -2.0, 1.0), -2.0, 1.0)
    rate_x = draw_rate_x(jax.random.fold_in(splits[10], 71), part)
    rate_y = draw_rate_y(jax.random.fold_in(splits[10], 71), part)
    d_skip = jnp.clip(jnp.exp(jax.random.uniform(splits[7], (HEADS,), jnp.float32, math.log(0.5), math.log(2.0))), 0.5, 2.0)
    norm_gain = jnp.clip(1.0 + 0.18 * jax.random.normal(splits[8], (INNER,), jnp.float32), 0.1, 1.9)
    w_out = centred(splits[9], (INNER, D), INNER ** -0.5, 0.1875)
    return dict(slide=slide, tissue=tissue, w_in=w_in, w_bcd=w_bcd, dt_bias=dt_bias, rate_x=rate_x, rate_y=rate_y, d_skip=d_skip, norm_gain=norm_gain, w_out=w_out)


def pair_chain(earlier, later):
    return (earlier[0] * later[0], later[0] * earlier[1] + later[1])

def reference(slide, tissue, w_in, w_bcd, dt_bias, rate_x, rate_y, d_skip, norm_gain, w_out):
    cell_mask = tissue.astype(jnp.float32).reshape(ROWS * COLS, 1)
    flat_cells = slide.reshape(ROWS * COLS, D)
    projected = jnp.dot(flat_cells, w_in, preferred_element_type=jnp.float32)
    values = projected[:, :INNER].astype(jnp.bfloat16) * cell_mask.astype(jnp.bfloat16)
    gate_z = projected[:, INNER:].astype(jnp.bfloat16)
    terms = jnp.dot(flat_cells, w_bcd, preferred_element_type=jnp.float32)
    b_map = terms[:, :STATE].astype(jnp.bfloat16).astype(jnp.float32).reshape(ROWS, COLS, STATE)
    c_map = terms[:, STATE:2 * STATE].astype(jnp.bfloat16).astype(jnp.float32).reshape(ROWS, COLS, STATE)
    step_sizes = (cell_mask * jax.nn.softplus(terms[:, 2 * STATE:] + dt_bias)).astype(jnp.bfloat16)
    step_sizes = step_sizes.astype(jnp.float32).reshape(ROWS, COLS, HEADS)
    channel_vals = values.astype(jnp.float32).reshape(ROWS, COLS, HEADS, HEAD_DIM)
    log_x = -step_sizes * rate_x
    log_y = -step_sizes * rate_y

    def row_step(carried, row_data):
        x_row, dt_row, b_row, c_row, lx_row, ly_row = row_data
        source = b_row[:, :, None, None] * (dt_row[..., None] * x_row)[:, None]
        decay = jnp.exp(lx_row)[:, None, :, None]
        scanned = lax.associative_scan(pair_chain, (decay, source), axis=0)
        state_row = jnp.exp(ly_row)[:, None, :, None] * carried + scanned[1]
        out_row = jnp.einsum('jn,jnhp->jhp', c_row, state_row, precision=lax.Precision.HIGHEST)
        out_row = out_row + d_skip[:, None] * x_row
        return (state_row, out_row)
    initial = jnp.zeros((COLS, STATE, HEADS, HEAD_DIM), jnp.float32)
    _, outputs = lax.scan(row_step, initial, (channel_vals, step_sizes, b_map, c_map, log_x, log_y))
    y_cells = outputs.reshape(ROWS * COLS, INNER).astype(jnp.bfloat16)
    gated = y_cells.astype(jnp.float32) * jax.nn.silu(gate_z.astype(jnp.float32))
    scaled = gated * lax.rsqrt(lax.optimization_barrier(jnp.mean(gated * gated, axis=-1, keepdims=True)) + 1e-05) * norm_gain
    result = jnp.dot(scaled.astype(jnp.bfloat16), w_out, preferred_element_type=jnp.float32) * cell_mask
    return result.astype(jnp.bfloat16).reshape(ROWS, COLS, D)
```

```python
import functools

import jax
import jax.numpy as jnp
import numpy as np
from jax import lax
from jax.experimental import pallas as pl
from jax.experimental.pallas import tpu as pltpu
from jax.sharding import PartitionSpec as P

norm_eps = 1e-05
LANES = 128
F32 = jnp.float32
BF16 = jnp.bfloat16


def round_up(value, step):
    return -(-value // step) * step


def mm(a, b):
    return jnp.dot(a, b, preferred_element_type=F32)


def nt_dot(a, b):
    return lax.dot_general(a, b, (((1,), (1,)), ((), ())), preferred_element_type=F32)


class Plan:
    def __init__(self, rows, cols, states, heads, width, devices):
        self.rows, self.cols, self.states, self.heads = rows, cols, states, heads
        self.cells = rows * cols
        self.padded = round_up(self.cells, 8)
        self.group = width // devices
        self.devices = devices
        self.head_width = width // heads
        self.width = width
        assert self.head_width % self.group == 0
        assert self.group + 2 * states + heads <= LANES and LANES % self.group == 0
        self.row_pad = LANES // (LANES // round_up(rows, 8))
        while LANES % self.row_pad:
            self.row_pad += 8
        self.copies = LANES // self.row_pad
        assert states % self.copies == 0
        self.col_pad = round_up(cols, 8)
        self.edge = states * self.row_pad
        self.top = states * self.col_pad
        self.blocks = LANES // self.group
        self.block = round_up(-(-self.cells // self.blocks), 8)

    def constants(self):
        rows, cols, cells, padded = self.rows, self.cols, self.cells, self.padded
        i = np.arange(padded) // cols
        j = np.arange(padded) % cols
        real = np.arange(padded) < cells
        io = np.concatenate([i, np.full(self.col_pad, rows - 1)])
        jo = np.concatenate([j, np.arange(self.col_pad)])
        ro = np.concatenate([real, np.arange(self.col_pad) < cols])
        le = np.arange(self.row_pad)
        both = real[:, None] & real[None, :]
        out = {}
        a1 = (j[None] <= jo[:, None]) & ro[:, None] & real[None]
        a2 = (j[None] == jo[:, None]) & (i[None] <= io[:, None]) & ro[:, None] & real[None]
        out["a1"], out["a2"] = a1, a2
        out["b1"] = (i[:, None] == i[None]) & (j[:, None] > j[None]) & both
        out["b2"] = (i[:, None] > i[None]) & both
        edge = np.tile(le, self.copies)
        out["e1"] = (i[:, None] == edge[None]) & real[:, None]
        out["e2"] = (i[:, None] > edge[None]) & real[:, None]
        out["mask"] = (io[:, None] >= i[None]) & (jo[:, None] >= j[None]) & ro[:, None] & real[None]
        out["emask"] = (io[:, None] >= edge[None]) & (edge < rows)[None] & ro[:, None]
        out["rowsel"] = (le[:, None] == i[None]) & real[None]
        n = np.arange(self.states)
        out["rep"] = n[:, None] == np.repeat(n, self.row_pad)[None]
        out["rep8"] = n[:, None] == np.repeat(n, self.col_pad)[None]
        out["diag"] = np.repeat(n, self.col_pad)[:, None] == np.repeat(n, self.row_pad)[None]
        out["colsel"] = (
            np.tile(np.arange(self.col_pad), self.states)[None] == j[:, None]
        ) & real[:, None]
        return {k: jnp.asarray(x.astype(np.float32), BF16) for k, x in out.items()}


def full(shape):
    return pl.BlockSpec(shape, lambda *_: (0,) * len(shape))


def project_kernel(plan, tile, x_ref, w_ref, wt_ref, mask_ref, bias_ref, v_ref, pay_ref, terms):
    step = pl.program_id(0)
    group, states, cells = plan.group, plan.states, plan.cells
    x = x_ref[...]
    m = mask_ref[...]
    lane = lax.broadcasted_iota(jnp.int32, (cells, LANES), 1)

    @pl.when(step == 0)
    def _():
        t = mm(x, wt_ref[...])
        z = t + bias_ref[...]
        soft = jnp.maximum(z, 0.0) + jnp.log1p(jnp.exp(-jnp.abs(z)))
        t = jnp.where(lane < group + 2 * states, t, m * soft)
        terms[...] = jnp.where(lane < group + 2 * states + plan.heads, t, 0.0)

    v = mm(x, w_ref[...]).astype(BF16).astype(F32) * m
    v_ref[...] = v.astype(BF16)
    rest = terms[...]
    for k in range(tile // group):
        lo = k * group
        base = lo // LANES * LANES
        part = v[:, base : base + LANES]
        if lo % LANES:
            part = pltpu.roll(part, LANES - lo % LANES, 1)
        pay_ref[k, 0:cells, :] = jnp.where(lane < group, part, rest).astype(BF16)
        if plan.padded > cells:
            pay_ref[k, cells : plan.padded, :] = jnp.zeros((plan.padded - cells, LANES), BF16)


def project(plan, x, w_in, w_bcd, cell_mask, dt_bias):
    group, states, heads = plan.group, plan.states, plan.heads
    tile = max(2 * LANES, group)
    before = group
    after = LANES - group - 2 * states - heads
    wt = jnp.pad(w_bcd, ((0, 0), (before, after)))
    bias = jnp.pad(dt_bias, (group + 2 * states, after)).reshape(1, LANES)
    depth = x.shape[1]
    return pl.pallas_call(
        functools.partial(project_kernel, plan, tile),
        grid=(plan.width // tile,),
        in_specs=[
            full(x.shape),
            pl.BlockSpec((depth, tile), lambda s: (0, s)),
            full(wt.shape),
            full(cell_mask.shape),
            full(bias.shape),
        ],
        out_specs=[
            pl.BlockSpec((plan.cells, tile), lambda s: (0, s)),
            pl.BlockSpec((tile // group, plan.padded, LANES), lambda s: (s, 0, 0)),
        ],
        out_shape=[
            jax.ShapeDtypeStruct((plan.cells, plan.width), BF16),
            jax.ShapeDtypeStruct((plan.devices, plan.padded, LANES), BF16),
        ],
        scratch_shapes=[pltpu.VMEM((plan.cells, LANES), F32)],
        name="project",
    )(x, w_in, wt, cell_mask, bias)


def my_head(plan, axis):
    return lax.axis_index(axis) * plan.group // plan.head_width


def rows_of(plan, head, pay):
    shape = (plan.states + 16, LANES)
    at = lax.broadcasted_iota(jnp.int32, shape, 0)
    lane = lax.broadcasted_iota(jnp.int32, shape, 1)
    first = plan.group + 2 * plan.states
    wanted = jnp.where(at < plan.states, plan.group + at, first + head)
    select = (lane == wanted).astype(F32).astype(BF16)
    return nt_dot(select, pay)


def edges_kernel(
    plan, axis, rates, pay_ref, a1_ref, a2_ref, b1_ref, b2_ref, e1_ref, e2_ref, mask_ref, emask_ref,
    rowsel_ref, diag_ref, edge_ref, top_ref, carry,
):
    states, group, padded = plan.states, plan.group, plan.padded
    head = my_head(plan, axis)
    rate_x, rate_y = rates[0, head], rates[1, head]

    @pl.when(pl.program_id(0) == 0)
    def _():
        carry[...] = jnp.zeros_like(carry)

    pay = pay_ref[0]
    v = pay[:, :group]
    table = rows_of(plan, head, pay)
    dt_row = table[states : states + 1]
    dt_low = table[states : states + 16].astype(BF16)
    bdt = table[:states] * dt_row
    before = carry[...]
    before_low = before.astype(BF16)
    edge_ref[0] = before_low

    right = jnp.exp(-rate_x * mm(dt_low, b1_ref[...])[0:1])
    bd = (bdt * right).astype(BF16)
    rowsel = rowsel_ref[...]
    left_map = jnp.concatenate(
        [rowsel * jnp.broadcast_to(bd[n : n + 1], rowsel.shape) for n in range(states)], axis=0
    )
    total = jnp.sum(rowsel.astype(F32) * dt_row, axis=1, keepdims=True)
    decay = jnp.broadcast_to(jnp.exp(-rate_x * total), (plan.row_pad, group))
    decay = jnp.concatenate([decay] * states, axis=0)
    carry[...] = decay * before + mm(left_map, v)

    dt_cells = dt_low[0:1]
    a1 = a1_ref[...] * dt_cells
    a2 = a2_ref[...] * dt_cells
    down = jnp.exp(-(rate_x * mm(a1, b1_ref[...]) + rate_y * mm(a2, b2_ref[...])))
    down = down * mask_ref[...].astype(F32)
    side = jnp.exp(-(rate_x * mm(a1, e1_ref[...]) + rate_y * mm(a2, e2_ref[...])))
    side = side * emask_ref[...].astype(F32)
    top_map = jnp.concatenate(
        [down * jnp.broadcast_to(bdt[n : n + 1], down.shape) for n in range(states)], axis=0
    ).astype(BF16)
    side = jnp.concatenate([side] * (states // plan.copies), axis=1)
    side_map = jnp.concatenate([side] * states, axis=0).astype(BF16) * diag_ref[...]
    top_ref[0] = (mm(top_map, v) + mm(side_map, before_low)).astype(BF16)


def cells_kernel(
    plan, axis, rates, pay_ref, edge_ref, top_ref, a1_ref, a2_ref, b1_ref, b2_ref, e1_ref, e2_ref,
    mask_ref, emask_ref, rep_ref, rep8_ref, colsel_ref, out_ref,
):
    states, group, padded = plan.states, plan.group, plan.padded
    head = my_head(plan, axis)
    rate_x, rate_y = rates[0, head], rates[1, head]
    pay = pay_ref[0]
    v = pay[:, :group]
    table = rows_of(plan, head, pay)
    dt_row = table[states : states + 1]
    dt_cells = dt_row.astype(BF16)
    bdt = (table[:states] * dt_row).astype(BF16)
    c = pay[:, group + states : group + 2 * states]

    a1 = a1_ref[...] * dt_cells
    a2 = a2_ref[...] * dt_cells
    inner = jnp.exp(-(rate_x * mm(a1, b1_ref[...]) + rate_y * mm(a2, b2_ref[...])))
    scores = mm(c, bdt) * inner * mask_ref[...].astype(F32)
    y = mm(scores.astype(BF16), v)

    side = jnp.exp(-(rate_x * mm(a1, e1_ref[...]) + rate_y * mm(a2, e2_ref[...])))
    side = side * emask_ref[...].astype(F32)
    side = jnp.concatenate([side] * (states // plan.copies), axis=1)
    y = y + mm((mm(c, rep_ref[...]) * side).astype(BF16), edge_ref[0])

    above = jnp.exp(-rate_y * jnp.sum(a2.astype(F32), axis=1, keepdims=True))
    down = mm(c, rep8_ref[...]) * colsel_ref[...].astype(F32) * above
    y = y + mm(down.astype(BF16), top_ref[0])

    y = y.astype(BF16).astype(F32)
    for k in range(plan.blocks):
        lo, hi = k * plan.block, min((k + 1) * plan.block, padded)
        if lo < hi:
            out_ref[0, 0 : hi - lo, k * group : (k + 1) * group] = y[lo:hi].astype(BF16)


def scan_calls(plan, row_axis, col_axis, pay, rates):
    consts = plan.constants()
    tiles = plan.devices
    cut = plan.padded
    tile_spec = pl.BlockSpec((1, plan.padded, LANES), lambda t: (t, 0, 0))
    edge_spec = pl.BlockSpec((1, plan.edge, plan.group), lambda t: (t, 0, 0))
    top_spec = pl.BlockSpec((1, plan.top, plan.group), lambda t: (t, 0, 0))
    smem = pl.BlockSpec(memory_space=pltpu.SMEM)
    shared = [consts[k] for k in ("b1", "b2", "e1", "e2")]
    low = [consts[k][cut:] for k in ("a1", "a2")]
    low += shared + [consts["mask"][cut:], consts["emask"][cut:], consts["rowsel"], consts["diag"]]
    edges, tops = pl.pallas_call(
        functools.partial(edges_kernel, plan, col_axis),
        grid=(tiles,),
        in_specs=[smem, tile_spec] + [full(x.shape) for x in low],
        out_specs=[edge_spec, top_spec],
        out_shape=[
            jax.ShapeDtypeStruct((tiles, plan.edge, plan.group), BF16),
            jax.ShapeDtypeStruct((tiles, plan.top, plan.group), BF16),
        ],
        scratch_shapes=[pltpu.VMEM((plan.edge, plan.group), F32)],
        name="edges",
    )(rates, pay, *low)

    count = lax.axis_size(row_axis)
    down = [(r, r + 1) for r in range(count - 1)]
    entry = lax.ppermute(tops, row_axis, down)
    if count > 2:
        head = my_head(plan, col_axis)
        at = plan.group + 2 * plan.states + head
        dt = lax.dynamic_slice_in_dim(pay[:, : plan.cells].astype(F32), at, 1, 2)
        total = jnp.sum(dt.reshape(tiles, plan.rows, plan.cols), axis=1)
        total = jnp.pad(total, ((0, 0), (0, plan.col_pad - plan.cols)))
        keep = jnp.tile(jnp.exp(-rates[1, head] * total), (1, plan.states))[..., None]
        for _ in range(count - 2):
            entry = lax.ppermute(
                (tops.astype(F32) + keep * entry.astype(F32)).astype(BF16), row_axis, down
            )

    high = [consts[k][:cut] for k in ("a1", "a2")]
    high += shared + [consts["mask"][:cut], consts["emask"][:cut]]
    high += [consts[k] for k in ("rep", "rep8", "colsel")]
    return pl.pallas_call(
        functools.partial(cells_kernel, plan, col_axis),
        grid=(tiles,),
        in_specs=[smem, tile_spec, edge_spec, top_spec] + [full(x.shape) for x in high],
        out_specs=pl.BlockSpec((1, plan.block, LANES), lambda t: (t, 0, 0)),
        out_shape=jax.ShapeDtypeStruct((tiles, plan.block, LANES), BF16),
        name="cells",
    )(rates, pay, edges, entry, *high)


def finish_kernel(plan, y_ref, v_ref, z_ref, skip_ref, gain_ref, mask_ref, w_ref, out_ref, full_ref):
    group, blocks, block, cells = plan.group, plan.blocks, plan.block, plan.cells
    lane = lax.broadcasted_iota(jnp.int32, (block, LANES), 1)
    for tile in range(plan.width // LANES):
        for k in range(blocks):
            lo, hi = k * block, min((k + 1) * block, cells)
            if lo >= hi:
                continue
            joined = None
            for d in range(blocks):
                part = y_ref[tile * blocks + d].astype(F32)
                shift = (d - k) * group % LANES
                if shift:
                    part = pltpu.roll(part, shift, 1)
                joined = part if joined is None else jnp.where(lane < d * group, joined, part)
            full_ref[lo:hi, tile * LANES : (tile + 1) * LANES] = joined[: hi - lo]
    y = full_ref[...] + skip_ref[...] * v_ref[...].astype(F32)
    y = y.astype(BF16).astype(F32)
    z = z_ref[...].astype(F32)
    gated = y * (z * (1.0 / (1.0 + jnp.exp(-z))))
    scale = lax.rsqrt(jnp.mean(gated * gated, axis=-1, keepdims=True) + norm_eps)
    normed = (gated * scale * gain_ref[...]).astype(BF16)
    out_ref[...] = (mm(normed, w_ref[...]) * mask_ref[...]).astype(BF16)


def finish(plan, y, v, z, skip, gain, cell_mask, w_out):
    args = (y, v, z, skip, gain, cell_mask, w_out)
    return pl.pallas_call(
        functools.partial(finish_kernel, plan),
        in_specs=[full(a.shape) for a in args],
        out_specs=full((plan.cells, w_out.shape[1])),
        out_shape=jax.ShapeDtypeStruct((plan.cells, w_out.shape[1]), BF16),
        scratch_shapes=[pltpu.VMEM((plan.cells, plan.width), F32)],
        grid=(1,),
        name="finish",
    )(*args)


def per_device(slide, tissue, w_in, w_bcd, dt_bias, rate_x, rate_y, d_skip, norm_gain, w_out):
    rows, cols, model_width = slide.shape
    width = w_out.shape[0]
    heads = dt_bias.shape[0]
    states = (w_bcd.shape[1] - heads) // 2
    plan = Plan(rows, cols, states, heads, width, lax.axis_size("col"))
    cell_mask = tissue.astype(F32).reshape(plan.cells, 1)
    x = slide.reshape(plan.cells, model_width)
    v, pay = project(plan, x, w_in, w_bcd, cell_mask, dt_bias)
    pay = lax.all_to_all(pay, "col", 0, 0, tiled=True)
    z = jnp.dot(x, w_in[:, width:], preferred_element_type=F32).astype(BF16)
    rates = jnp.stack([rate_x, rate_y])
    y = scan_calls(plan, "row", "col", pay, rates)
    y = lax.all_to_all(y, "col", 0, 0, tiled=True)
    skip = jnp.repeat(d_skip, width // heads).reshape(1, width)
    out = finish(plan, y, v, z, skip, norm_gain.reshape(1, width), cell_mask, w_out)
    return out.reshape(rows, cols, model_width)


def solution(mesh):
    placed = (
        P(("slides", "row"), "col", None),
        P(("slides", "row"), "col"),
        P(),
        P(),
        P(),
        P(),
        P(),
        P(),
        P(),
        P(),
    )
    return jax.shard_map(
        per_device,
        mesh=mesh,
        in_specs=placed,
        out_specs=P(("slides", "row"), "col", None),
        check_vma=False,
    )
```

```python
import functools

import jax
import jax.numpy as jnp
import numpy as np
from jax import lax
from jax.experimental import pallas as pl
from jax.experimental.pallas import tpu as pltpu
from jax.sharding import PartitionSpec as P

norm_eps = 1e-05
LANES = 128
HALF = LANES // 2
F32 = jnp.float32
BF16 = jnp.bfloat16


def round_up(value, step):
    return -(-value // step) * step


def mm(a, b):
    return jnp.dot(a, b, preferred_element_type=F32)


def nt_dot(a, b):
    return lax.dot_general(a, b, (((1,), (1,)), ((), ())), preferred_element_type=F32)


def tn_dot(a, b):
    return lax.dot_general(a, b, (((0,), (0,)), ((), ())), preferred_element_type=F32)


class Plan:
    def __init__(self, rows, cols, states, heads, width, devices):
        self.rows, self.cols, self.states, self.heads = rows, cols, states, heads
        self.width, self.devices = width, devices
        self.group = width // devices
        self.head_width = width // heads
        self.col_pad = round_up(cols, 8)
        self.upper = -(-rows // 2)
        self.half = round_up(self.upper * self.col_pad, 8)
        self.cells = rows * self.col_pad
        self.row_pad = 32
        self.edge = states * self.row_pad
        self.top = states * self.col_pad
        self.bc = 2 * states
        self.at_bc = self.half
        self.at_dt = self.at_bc + 2 * self.bc
        self.message = round_up(self.at_dt + 2, 8)
        assert self.head_width % self.group == 0 and self.group <= HALF
        assert LANES % self.head_width == 0 and self.half <= LANES
        assert rows <= self.row_pad and self.cells - self.half <= self.half
        assert states % 16 == 0 and self.edge % LANES == 0 and heads % 8 == 0

    def lanes(self):
        at = np.arange(2 * LANES)
        cell = np.where(at < LANES, at, at - LANES + self.half)
        live = np.where(at < LANES, at < self.half, cell < self.cells)
        i, j = cell // self.col_pad, cell % self.col_pad
        return i, j, live & (j < self.cols)

    def constants(self):
        i, j, real = self.lanes()
        both = real[:, None] & real[None]
        cell = np.arange(self.cells)
        ci, cj = cell // self.col_pad, cell % self.col_pad
        creal = cj < self.cols
        le = np.arange(self.row_pad)
        lj = np.arange(self.col_pad)
        n = np.arange(self.states)
        edge = np.tile(le, LANES // self.row_pad)
        out = {}
        out["to1"] = (j[:, None] <= j[None]) & both
        out["to2"] = (j[:, None] == j[None]) & (i[:, None] <= i[None]) & both
        out["from1"] = (i[:, None] == i[None]) & (j[:, None] > j[None]) & both
        out["from2"] = (i[:, None] > i[None]) & both
        out["side1"] = (i[None] == le[:, None]) & real[None]
        out["side2"] = (i[None] > le[:, None]) & real[None]
        out["sidemask"] = (i[None] >= le[:, None]) & (le < self.rows)[:, None] & real[None]
        out["down1"] = (j[None] <= lj[:, None]) & real[None]
        out["down2"] = (j[None] == lj[:, None]) & real[None]
        out["downmask"] = (j[None] <= lj[:, None]) & (lj < self.cols)[:, None] & real[None]
        out["keep"] = (i[:, None] == edge[None]) & real[:, None]
        out["pick"] = (
            (i == self.rows - 1)[:, None] & real[:, None] & (j[:, None] == np.tile(lj, self.states)[None])
        )
        out["diag"] = np.repeat(n, self.row_pad)[:, None] == np.repeat(n, self.col_pad)[None]
        cboth = creal[:, None] & real[None]
        out["own1"] = (j[None] <= cj[:, None]) & cboth
        out["own2"] = (j[None] == cj[:, None]) & (i[None] <= ci[:, None]) & cboth
        out["ownmask"] = (i[None] <= ci[:, None]) & (j[None] <= cj[:, None]) & cboth
        out["rowj"] = cj[:, None] == np.arange(self.cols)[None]
        out["rowi"] = ci[:, None] == np.arange(self.rows)[None]
        out["lanei"] = (np.arange(self.rows)[:, None] == i[None]) & real[None]
        out["lanej"] = (np.arange(self.cols)[:, None] == j[None]) & real[None]
        return {k: jnp.asarray(x.astype(np.float32), BF16) for k, x in out.items()}


def full(shape):
    return pl.BlockSpec(shape, lambda *_: (0,) * len(shape))


SMEM = pl.BlockSpec(memory_space=pltpu.SMEM)


def cell_mask_of(t_ref, rowj_ref, rowi_ref):
    t = t_ref[...].astype(F32).astype(BF16)
    return jnp.sum(mm(rowj_ref[...], t) * rowi_ref[...].astype(F32), axis=1, keepdims=True)


def project_kernel(
    plan, tile, bias_ref, x_ref, w_ref, wt_ref, t_ref, rowj_ref, rowi_ref, lanei_ref, lanej_ref,
    v_ref, pay_ref, rows_ref, flat_ref, wide, keep,
):
    step = pl.program_id(0)
    group, states, cells, heads = plan.group, plan.states, plan.cells, plan.heads
    half, rest = plan.half, plan.cells - plan.half

    @pl.when(step == 0)
    def _():
        wide[...] = jnp.zeros_like(wide)
        for i in range(plan.rows):
            wide[i * plan.col_pad : i * plan.col_pad + plan.cols, :] = x_ref[i].astype(F32)
        flat_ref[...] = wide[...].astype(BF16)
        keep[...] = jnp.broadcast_to(cell_mask_of(t_ref, rowj_ref, rowi_ref), keep.shape)
        t = t_ref[...].astype(F32).astype(BF16)
        m = jnp.sum(mm(t, lanei_ref[...]) * lanej_ref[...].astype(F32), axis=0, keepdims=True)
        x = flat_ref[...]
        table = nt_dot(wt_ref[...], x)
        ext = jnp.concatenate([table, jnp.zeros((table.shape[0], 2 * LANES - cells), F32)], axis=1)
        lane = lax.broadcasted_iota(jnp.int32, (table.shape[0], LANES), 1)
        lo, hi = ext[:, :LANES], ext[:, LANES:]
        shift = half % LANES
        if shift:
            moved = jnp.where(
                lane < LANES - shift, pltpu.roll(lo, LANES - shift, 1), pltpu.roll(hi, LANES - shift, 1)
            )
        else:
            moved = hi
        table = jnp.concatenate([jnp.where(lane < half, lo, 0.0), jnp.where(lane < rest, moved, 0.0)], axis=1)
        z = table[2 * states :]
        at = lax.broadcasted_iota(jnp.int32, z.shape, 0)
        for h in range(heads):
            z = jnp.where(at == h, z + bias_ref[h], z)
        soft = m * (jnp.maximum(z, 0.0) + jnp.log1p(jnp.exp(-jnp.abs(z))))
        rows_ref[...] = jnp.concatenate([table[: 2 * states], soft], axis=0).astype(BF16).astype(F32)
        v_ref[...] = jnp.zeros_like(v_ref)

    v = mm(flat_ref[...], w_ref[...]).astype(BF16).astype(F32) * keep[:, :1]
    low = v.astype(BF16)
    v_ref[0:half, :] = low[:half]
    v_ref[LANES : LANES + rest, :] = low[half:]
    lane = lax.broadcasted_iota(jnp.int32, (half, LANES), 1)
    for k in range(tile // group):
        base = k * group // LANES * LANES
        at = k * group % LANES
        first = v[:half, base : base + LANES]
        last = v[half:, base : base + LANES]
        if rest < half:
            last = jnp.concatenate([last, jnp.zeros((half - rest, LANES), F32)], axis=0)
        if at:
            first = pltpu.roll(first, LANES - at, 1)
        if at != HALF:
            last = pltpu.roll(last, (HALF - at) % LANES, 1)
        both = jnp.where(lane < HALF, first, last)
        if group < HALF:
            both = jnp.where(lane % HALF < group, both, 0.0)
        pay_ref[k, 0:half, :] = both.astype(BF16)
        bc = rows_ref[0 : 2 * states, :].astype(BF16)
        pay_ref[k, plan.at_bc : plan.at_bc + plan.bc, :] = bc[:, :LANES]
        pay_ref[k, plan.at_bc + plan.bc : plan.at_dt, :] = bc[:, LANES:]
        head = (step * tile + k * group) // plan.head_width
        dt = rows_ref[pl.ds(2 * states + head, 1), :]
        dt = jnp.concatenate(
            [dt[:, :LANES], dt[:, LANES:], jnp.zeros((plan.message - plan.at_dt - 2, LANES), F32)], axis=0
        )
        pay_ref[k, plan.at_dt : plan.message, :] = dt.astype(BF16)


def project(plan, consts, slide, w_in, w_bcd, tissue, dt_bias):
    tile = plan.width // 2
    picks = [consts[k] for k in ("rowj", "rowi", "lanei", "lanej")]
    wt, t = w_bcd.T, tissue.T
    depth = slide.shape[2]
    count = 2 * plan.states + plan.heads
    return pl.pallas_call(
        functools.partial(project_kernel, plan, tile),
        grid=(plan.width // tile,),
        in_specs=[
            SMEM,
            full(slide.shape),
            pl.BlockSpec((depth, tile), lambda s: (0, s)),
            full(wt.shape),
            full(t.shape),
        ]
        + [full(x.shape) for x in picks],
        out_specs=[
            pl.BlockSpec((2 * LANES, tile), lambda s: (0, s)),
            pl.BlockSpec((tile // plan.group, plan.message, LANES), lambda s: (s, 0, 0)),
            full((count, 2 * LANES)),
            full((plan.cells, depth)),
        ],
        out_shape=[
            jax.ShapeDtypeStruct((2 * LANES, plan.width), BF16),
            jax.ShapeDtypeStruct((plan.devices, plan.message, LANES), BF16),
            jax.ShapeDtypeStruct((count, 2 * LANES), F32),
            jax.ShapeDtypeStruct((plan.cells, depth), BF16),
        ],
        scratch_shapes=[pltpu.VMEM((plan.cells, depth), F32), pltpu.VMEM((plan.cells, LANES), F32)],
        name="project",
    )(dt_bias, slide, w_in, wt, t, *picks)


def own_kernel(
    plan, rx_ref, ry_ref, skip_ref, v_ref, rows_ref, own1_ref, own2_ref, from1_ref, from2_ref,
    mask_ref, out_ref, pair,
):
    states, cells, half = plan.states, plan.cells, plan.half
    b = rows_ref[0:states, :].astype(BF16)
    c = rows_ref[states : 2 * states, :].astype(BF16)
    pairs = tn_dot(c, b)
    pairs = jnp.concatenate([pairs[:half], pairs[LANES : LANES + cells - half]], axis=0)
    pair[...] = pairs * mask_ref[...].astype(F32)
    lane = lax.broadcasted_iota(jnp.int32, (cells, LANES), 1)
    per = LANES // plan.head_width
    for block in range(plan.width // LANES):
        v = v_ref[:, block * LANES : (block + 1) * LANES]
        vc = jnp.concatenate([v[:half], v[LANES : LANES + cells - half]], axis=0).astype(F32)
        total = None
        for k in range(per):
            h = block * per + k
            dt = rows_ref[2 * states + h : 2 * states + h + 1, :]
            low = dt.astype(BF16)
            x = mm(own1_ref[...] * low, from1_ref[...])
            y = mm(own2_ref[...] * low, from2_ref[...])
            weight = jnp.exp(-(rx_ref[h] * x + ry_ref[h] * y)) * pair[...] * dt
            part = mm(weight.astype(BF16), v) + skip_ref[h] * vc
            total = part if total is None else jnp.where(lane < k * plan.head_width, total, part)
        out_ref[:, block * LANES : (block + 1) * LANES] = total.astype(BF16)


def own_tile(plan, consts, v, rows, rate_x, rate_y, d_skip):
    maps = [consts[k] for k in ("own1", "own2", "from1", "from2", "ownmask")]
    args = [v, rows] + maps
    return pl.pallas_call(
        functools.partial(own_kernel, plan),
        grid=(1,),
        in_specs=[SMEM, SMEM, SMEM] + [full(x.shape) for x in args],
        out_specs=full((plan.cells, plan.width)),
        out_shape=jax.ShapeDtypeStruct((plan.cells, plan.width), BF16),
        scratch_shapes=[pltpu.VMEM((plan.cells, 2 * LANES), F32)],
        name="own",
    )(rate_x, rate_y, d_skip, *args)


def my_head(plan, axis):
    return lax.axis_index(axis) * plan.group // plan.head_width


def wide_rows(pay_ref, t, at, count, gap):
    return jnp.concatenate([pay_ref[t, at : at + count, :], pay_ref[t, at + gap : at + gap + count, :]], axis=1)


def unroll_of(plan):
    return plan.devices if plan.devices <= 16 else 1


def edges_kernel(
    plan, axis, rx_ref, ry_ref, pay_ref, to1_ref, to2_ref, from1_ref, from2_ref, side1_ref, side2_ref,
    sidemask_ref, down1_ref, down2_ref, downmask_ref, keep_ref, pick_ref, diag_ref,
    edge_ref, top_ref, side_ref, above_ref, dts, inner, kept, s1, s2, d1, d2, down, bottom, carry,
):
    states, tiles, rp, cp = plan.states, plan.devices, plan.row_pad, plan.col_pad
    head = my_head(plan, axis)
    rate_x, rate_y = rx_ref[head], ry_ref[head]
    for t in range(tiles):
        both = pay_ref[t, plan.at_dt : plan.message, :].astype(F32)
        dts[t : t + 1, :LANES] = both[0:1]
        dts[t : t + 1, LANES:] = both[1:2]
    dt = dts[...]
    low = dt.astype(BF16)
    inner[...] = jnp.exp(-rate_x * mm(low, from1_ref[...])) * dt
    kept[...] = jnp.exp(-rate_x * mm(low, keep_ref[...]))
    above_ref[...] = jnp.exp(-rate_y * mm(low, to2_ref[...]))
    for t in range(tiles):
        row = low[t : t + 1]
        s1[t * rp : (t + 1) * rp, :] = side1_ref[...] * row
        s2[t * rp : (t + 1) * rp, :] = side2_ref[...] * row
        rf = dts[t : t + 1, :]
        d1[t * cp : (t + 1) * cp, :] = down1_ref[...].astype(F32) * rf
        d2[t * cp : (t + 1) * cp, :] = down2_ref[...].astype(F32) * rf
    sides = jnp.exp(-(rate_x * mm(s1[...], to1_ref[...]) + rate_y * mm(s2[...], to2_ref[...])))
    mask = sidemask_ref[...].astype(F32)
    for t in range(tiles):
        side_ref[t] = (sides[t * rp : (t + 1) * rp] * mask).astype(BF16)
    falls = jnp.exp(
        -(rate_x * mm(d1[...].astype(BF16), from1_ref[...]) + rate_y * mm(d2[...].astype(BF16), from2_ref[...]))
    )
    mask = downmask_ref[...].astype(F32)
    for t in range(tiles):
        down[t * cp : (t + 1) * cp, :] = falls[t * cp : (t + 1) * cp] * mask
        bottom[t] = mm(side_ref[t], pick_ref[...]).astype(BF16)
    carry[...] = jnp.zeros_like(carry)

    def tile(t, _):
        rowsel = side1_ref[...]
        b = wide_rows(pay_ref, t, plan.at_bc, states, plan.bc).astype(F32)
        bd = (b * inner[pl.ds(t, 1), :]).astype(BF16)
        bdt = b * dts[pl.ds(t, 1), :]
        left = jnp.concatenate([rowsel * bd[n : n + 1] for n in range(states)], axis=0)
        v = pay_ref[t, 0 : plan.half, :].astype(F32)
        if plan.half < LANES:
            v = jnp.concatenate([v, jnp.zeros((LANES - plan.half, LANES), F32)], axis=0)
        v = v.T
        v = jnp.concatenate([v[:HALF], v[HALF:]], axis=1).astype(BF16)
        fall = down[pl.ds(t * cp, cp), :]
        falls = jnp.concatenate([fall * bdt[n : n + 1] for n in range(states)], axis=0).astype(BF16)
        before = carry[...]
        before_low = before.astype(BF16)
        edge_ref[t] = before_low
        passed = jnp.concatenate([bottom[t]] * states, axis=0) * diag_ref[...]
        top_ref[t] = (nt_dot(v, falls) + mm(before_low, passed)).astype(BF16)
        kept_row = kept[pl.ds(t, 1), :]
        kept_row = jnp.concatenate([kept_row] * (plan.edge // LANES), axis=1)
        carry[...] = before * kept_row + nt_dot(v, left)
        return 0

    lax.fori_loop(0, tiles, tile, 0, unroll=unroll_of(plan))


def cells_kernel(plan, pay_ref, edge_ref, top_ref, side_ref, above_ref, colsel_ref, out_ref):
    states = plan.states

    def tile(t, _):
        c = wide_rows(pay_ref, t, plan.at_bc + states, states, plan.bc)
        side = side_ref[t]
        left = jnp.concatenate([side * c[n : n + 1] for n in range(states)], axis=0)
        ca = c.astype(F32) * above_ref[pl.ds(t, 1), :]
        colsel = colsel_ref[...].astype(F32)
        down = jnp.concatenate([colsel * ca[n : n + 1] for n in range(states)], axis=0).astype(BF16)
        y = mm(edge_ref[t], left) + mm(top_ref[t], down)
        y = jnp.concatenate([y[:, :LANES], y[:, LANES:]], axis=0).T
        out_ref[t] = y[: plan.half].astype(BF16)
        return 0

    lax.fori_loop(0, plan.devices, tile, 0, unroll=unroll_of(plan))


def scan_calls(plan, consts, row_axis, col_axis, pay, rate_x, rate_y):
    tiles, rp, cp = plan.devices, plan.row_pad, plan.col_pad
    names = ("to1", "to2", "from1", "from2", "side1", "side2", "sidemask", "down1", "down2")
    maps = [consts[k] for k in names + ("downmask", "keep", "pick", "diag")]
    shapes = [
        ((tiles, HALF, plan.edge), BF16),
        ((tiles, HALF, plan.top), BF16),
        ((tiles, rp, 2 * LANES), BF16),
        ((tiles, 2 * LANES), F32),
    ]
    edges, tops, side, above = pl.pallas_call(
        functools.partial(edges_kernel, plan, col_axis),
        grid=(1,),
        in_specs=[SMEM, SMEM, full(pay.shape)] + [full(x.shape) for x in maps],
        out_specs=[full(s) for s, _ in shapes],
        out_shape=[jax.ShapeDtypeStruct(s, d) for s, d in shapes],
        scratch_shapes=[
            pltpu.VMEM((tiles, 2 * LANES), F32),
            pltpu.VMEM((tiles, 2 * LANES), F32),
            pltpu.VMEM((tiles, LANES), F32),
            pltpu.VMEM((tiles * rp, 2 * LANES), BF16),
            pltpu.VMEM((tiles * rp, 2 * LANES), BF16),
            pltpu.VMEM((tiles * cp, 2 * LANES), F32),
            pltpu.VMEM((tiles * cp, 2 * LANES), F32),
            pltpu.VMEM((tiles * cp, 2 * LANES), F32),
            pltpu.VMEM((tiles, rp, LANES), BF16),
            pltpu.VMEM((HALF, plan.edge), F32),
        ],
        name="edges",
    )(rate_x, rate_y, pay, *maps)

    count = lax.axis_size(row_axis)
    chain = [(r, r + 1) for r in range(count - 1)]
    entry = lax.ppermute(tops, row_axis, chain)
    if count > 2:
        keep = jnp.dot(above.astype(BF16), consts["pick"], preferred_element_type=F32)[:, None, :]
        for _ in range(count - 2):
            entry = lax.ppermute(
                (tops.astype(F32) + keep * entry.astype(F32)).astype(BF16), row_axis, chain
            )

    args = (pay, edges, entry, side, above, consts["down2"])
    shape = (tiles, plan.half, LANES)
    return pl.pallas_call(
        functools.partial(cells_kernel, plan),
        grid=(1,),
        in_specs=[full(x.shape) for x in args],
        out_specs=full(shape),
        out_shape=jax.ShapeDtypeStruct(shape, BF16),
        name="cells",
    )(*args)


def finish_kernel(plan, y_ref, own_ref, z_ref, gain_ref, t_ref, rowj_ref, rowi_ref, w_ref, out_ref, full_ref):
    group, half, cells = plan.group, plan.half, plan.cells
    per = LANES // group
    lane = lax.broadcasted_iota(jnp.int32, (half, LANES), 1)
    for block in range(plan.width // LANES):
        for k, (lo, hi) in enumerate(((0, half), (half, cells))):
            joined = None
            for d in range(per):
                part = y_ref[block * per + d].astype(F32)
                shift = (d * group - k * HALF) % LANES
                if shift:
                    part = pltpu.roll(part, shift, 1)
                joined = part if joined is None else jnp.where(lane < d * group, joined, part)
            full_ref[lo:hi, block * LANES : (block + 1) * LANES] = joined[: hi - lo]
    y = full_ref[...] + own_ref[...].astype(F32)
    y = y.astype(BF16).astype(F32)
    z = z_ref[...].astype(F32)
    gated = y * (z * (1.0 / (1.0 + jnp.exp(-z))))
    scale = lax.rsqrt(jnp.mean(gated * gated, axis=-1, keepdims=True) + norm_eps)
    normed = (gated * scale * gain_ref[...]).astype(BF16)
    full_ref[...] = mm(normed, w_ref[...]) * cell_mask_of(t_ref, rowj_ref, rowi_ref)
    for i in range(plan.rows):
        out_ref[i] = full_ref[i * plan.col_pad : i * plan.col_pad + plan.cols, :].astype(BF16)


def finish(plan, consts, y, own, z, gain, tissue, w_out):
    args = (y, own, z, gain, tissue.T, consts["rowj"], consts["rowi"], w_out)
    shape = (plan.rows, plan.cols, w_out.shape[1])
    assert w_out.shape[1] == plan.width
    return pl.pallas_call(
        functools.partial(finish_kernel, plan),
        grid=(1,),
        in_specs=[full(a.shape) for a in args],
        out_specs=full(shape),
        out_shape=jax.ShapeDtypeStruct(shape, BF16),
        scratch_shapes=[pltpu.VMEM((plan.cells, plan.width), F32)],
        name="finish",
    )(*args)


def per_device(slide, tissue, w_in, w_bcd, dt_bias, rate_x, rate_y, d_skip, norm_gain, w_out):
    rows, cols, model_width = slide.shape
    width = w_out.shape[0]
    heads = dt_bias.shape[0]
    states = (w_bcd.shape[1] - heads) // 2
    plan = Plan(rows, cols, states, heads, width, lax.axis_size("col"))
    consts = plan.constants()
    v, pay, table, x = project(plan, consts, slide, w_in, w_bcd, tissue, dt_bias)
    pay = lax.all_to_all(pay, "col", 0, 0, tiled=True)
    own = own_tile(plan, consts, v, table, rate_x, rate_y, d_skip)
    z = jnp.dot(x, w_in[:, width:], preferred_element_type=F32).astype(BF16)
    y = scan_calls(plan, consts, "row", "col", pay, rate_x, rate_y)
    y = lax.all_to_all(y, "col", 0, 0, tiled=True)
    return finish(plan, consts, y, own, z, norm_gain.reshape(1, width), tissue, w_out)


def solution(mesh):
    placed = (
        P(("slides", "row"), "col", None),
        P(("slides", "row"), "col"),
        P(),
        P(),
        P(),
        P(),
        P(),
        P(),
        P(),
        P(),
    )
    return jax.shard_map(
        per_device,
        mesh=mesh,
        in_specs=placed,
        out_specs=P(("slides", "row"), "col", None),
        check_vma=False,
    )
```

```python
import functools

import jax
import jax.numpy as jnp
import numpy as np
from jax import lax
from jax.experimental import pallas as pl
from jax.experimental.pallas import tpu as pltpu
from jax.sharding import PartitionSpec as P

norm_eps = 1e-05
LANES = 128
HALF = LANES // 2
F32 = jnp.float32
BF16 = jnp.bfloat16


def round_up(value, step):
    return -(-value // step) * step


def mm(a, b):
    return jnp.dot(a, b, preferred_element_type=F32)


def nt_dot(a, b):
    return lax.dot_general(a, b, (((1,), (1,)), ((), ())), preferred_element_type=F32)


def tn_dot(a, b):
    return lax.dot_general(a, b, (((0,), (0,)), ((), ())), preferred_element_type=F32)


class Plan:
    def __init__(self, rows, cols, states, heads, width, devices):
        self.rows, self.cols, self.states, self.heads = rows, cols, states, heads
        self.width = width
        self.parts = 2 if devices % 2 == 0 and devices > 2 else 1
        self.devices = devices // self.parts
        self.group = width // self.devices
        self.slot = min(self.group, HALF)
        self.slots = self.group // self.slot
        self.work = self.slots * self.devices
        self.head_width = width // heads
        self.col_pad = round_up(cols, 8)
        self.upper = -(-rows // 2)
        self.half = round_up(self.upper * self.col_pad, 8)
        self.cells = rows * self.col_pad
        self.row_pad = 32
        self.edge = states * self.row_pad
        self.top = states * self.col_pad
        self.bc = 2 * states
        self.at_bc = self.slots * self.half
        self.at_dt = self.at_bc + 2 * self.bc
        self.message = round_up(self.at_dt + 2 * self.slots, 8)
        assert self.head_width % self.slot == 0 and self.group % self.slot == 0
        assert LANES % self.head_width == 0 and self.half <= LANES
        assert rows <= self.row_pad and self.cells - self.half <= self.half
        assert states % 16 == 0 and self.edge % LANES == 0 and heads % 8 == 0

    def segments(self):
        return [list(range(p * self.devices, (p + 1) * self.devices)) for p in range(self.parts)]

    def lanes(self):
        at = np.arange(2 * LANES)
        cell = np.where(at < LANES, at, at - LANES + self.half)
        live = np.where(at < LANES, at < self.half, cell < self.cells)
        i, j = cell // self.col_pad, cell % self.col_pad
        return i, j, live & (j < self.cols)

    def constants(self):
        i, j, real = self.lanes()
        both = real[:, None] & real[None]
        cell = np.arange(self.cells)
        ci, cj = cell // self.col_pad, cell % self.col_pad
        creal = cj < self.cols
        le = np.arange(self.row_pad)
        lj = np.arange(self.col_pad)
        n = np.arange(self.states)
        edge = np.tile(le, LANES // self.row_pad)
        out = {}
        out["to1"] = (j[:, None] <= j[None]) & both
        out["to2"] = (j[:, None] == j[None]) & (i[:, None] <= i[None]) & both
        out["from1"] = (i[:, None] == i[None]) & (j[:, None] > j[None]) & both
        out["from2"] = (i[:, None] > i[None]) & both
        out["side1"] = (i[None] == le[:, None]) & real[None]
        out["side2"] = (i[None] > le[:, None]) & real[None]
        out["sidemask"] = (i[None] >= le[:, None]) & (le < self.rows)[:, None] & real[None]
        out["down1"] = (j[None] <= lj[:, None]) & real[None]
        out["down2"] = (j[None] == lj[:, None]) & real[None]
        out["downmask"] = (j[None] <= lj[:, None]) & (lj < self.cols)[:, None] & real[None]
        out["keep"] = (i[:, None] == edge[None]) & real[:, None]
        out["pick"] = (
            (i == self.rows - 1)[:, None] & real[:, None] & (j[:, None] == np.tile(lj, self.states)[None])
        )
        out["diag"] = np.repeat(n, self.row_pad)[:, None] == np.repeat(n, self.col_pad)[None]
        cboth = creal[:, None] & real[None]
        out["own1"] = (j[None] <= cj[:, None]) & cboth
        out["own2"] = (j[None] == cj[:, None]) & (i[None] <= ci[:, None]) & cboth
        out["ownmask"] = (i[None] <= ci[:, None]) & (j[None] <= cj[:, None]) & cboth
        out["lanei"] = (np.arange(self.rows)[:, None] == i[None]) & real[None]
        out["lanej"] = (np.arange(self.cols)[:, None] == j[None]) & real[None]
        return {k: jnp.asarray(x.astype(np.float32), BF16) for k, x in out.items()}


def full(shape):
    return pl.BlockSpec(shape, lambda *_: (0,) * len(shape))


SMEM = pl.BlockSpec(memory_space=pltpu.SMEM)


def cell_mask_of(plan, t_ref):
    t = t_ref[...].astype(F32).astype(BF16)
    cell = lax.broadcasted_iota(jnp.int32, (plan.cells, plan.cols), 0)
    col = lax.broadcasted_iota(jnp.int32, (plan.cells, plan.cols), 1)
    pick = (lax.rem(cell, plan.col_pad) == col).astype(F32).astype(BF16)
    cell = lax.broadcasted_iota(jnp.int32, (plan.cells, plan.rows), 0)
    row = lax.broadcasted_iota(jnp.int32, (plan.cells, plan.rows), 1)
    return jnp.sum(jnp.where(lax.div(cell, plan.col_pad) == row, mm(pick, t), 0.0), axis=1, keepdims=True)


def project_kernel(
    plan, tile, bias_ref, x_ref, w_ref, wt_ref, t_ref, lanei_ref, lanej_ref,
    v_ref, pay_ref, rows_ref, flat_ref, wide, keep,
):
    step = pl.program_id(0)
    group, states, cells, heads = plan.group, plan.states, plan.cells, plan.heads
    half, rest = plan.half, plan.cells - plan.half

    @pl.when(step == 0)
    def _():
        wide[...] = jnp.zeros_like(wide)
        for i in range(plan.rows):
            wide[i * plan.col_pad : i * plan.col_pad + plan.cols, :] = x_ref[i].astype(F32)
        flat_ref[...] = wide[...].astype(BF16)
        keep[...] = jnp.broadcast_to(cell_mask_of(plan, t_ref), keep.shape)
        t = t_ref[...].astype(F32).astype(BF16)
        m = jnp.sum(mm(t, lanei_ref[...]) * lanej_ref[...].astype(F32), axis=0, keepdims=True)
        x = flat_ref[...]
        table = nt_dot(wt_ref[...], x)
        ext = jnp.concatenate([table, jnp.zeros((table.shape[0], 2 * LANES - cells), F32)], axis=1)
        lane = lax.broadcasted_iota(jnp.int32, (table.shape[0], LANES), 1)
        lo, hi = ext[:, :LANES], ext[:, LANES:]
        shift = half % LANES
        if shift:
            moved = jnp.where(
                lane < LANES - shift, pltpu.roll(lo, LANES - shift, 1), pltpu.roll(hi, LANES - shift, 1)
            )
        else:
            moved = hi
        table = jnp.concatenate([jnp.where(lane < half, lo, 0.0), jnp.where(lane < rest, moved, 0.0)], axis=1)
        z = table[2 * states :]
        at = lax.broadcasted_iota(jnp.int32, z.shape, 0)
        for h in range(heads):
            z = jnp.where(at == h, z + bias_ref[h], z)
        soft = m * (jnp.maximum(z, 0.0) + jnp.log1p(jnp.exp(-jnp.abs(z))))
        rows_ref[...] = jnp.concatenate([table[: 2 * states], soft], axis=0).astype(BF16).astype(F32)
        v_ref[...] = jnp.zeros_like(v_ref)

    v = mm(flat_ref[...], w_ref[...]).astype(BF16).astype(F32) * keep[:, :1]
    low = v.astype(BF16)
    v_ref[0:half, :] = low[:half]
    v_ref[LANES : LANES + rest, :] = low[half:]
    lane = lax.broadcasted_iota(jnp.int32, (half, LANES), 1)
    bc = rows_ref[0 : 2 * states, :].astype(BF16)
    for k in range(tile // group):
        dts = []
        for s in range(plan.slots):
            offset = k * group + s * plan.slot
            base = offset // LANES * LANES
            at = offset % LANES
            first = v[:half, base : base + LANES]
            last = v[half:, base : base + LANES]
            if rest < half:
                last = jnp.concatenate([last, jnp.zeros((half - rest, LANES), F32)], axis=0)
            if at:
                first = pltpu.roll(first, LANES - at, 1)
            if at != HALF:
                last = pltpu.roll(last, (HALF - at) % LANES, 1)
            both = jnp.where(lane < HALF, first, last)
            if plan.slot < HALF:
                both = jnp.where(lane % HALF < plan.slot, both, 0.0)
            pay_ref[k, s * half : (s + 1) * half, :] = both.astype(BF16)
            head = (step * tile + offset) // plan.head_width
            dt = rows_ref[pl.ds(2 * states + head, 1), :]
            dts += [dt[:, :LANES], dt[:, LANES:]]
        pay_ref[k, plan.at_bc : plan.at_bc + plan.bc, :] = bc[:, :LANES]
        pay_ref[k, plan.at_bc + plan.bc : plan.at_dt, :] = bc[:, LANES:]
        spare = plan.message - plan.at_dt - len(dts)
        dts += [jnp.zeros((spare, LANES), F32)] if spare else []
        pay_ref[k, plan.at_dt : plan.message, :] = jnp.concatenate(dts, axis=0).astype(BF16)


def project(plan, consts, slide, w_in, w_bcd, tissue, dt_bias):
    tile = plan.width // 2
    picks = [consts[k] for k in ("lanei", "lanej")]
    wt, t = w_bcd.T, tissue.T
    depth = slide.shape[2]
    count = 2 * plan.states + plan.heads
    return pl.pallas_call(
        functools.partial(project_kernel, plan, tile),
        grid=(plan.width // tile,),
        in_specs=[
            SMEM,
            full(slide.shape),
            pl.BlockSpec((depth, tile), lambda s: (0, s)),
            full(wt.shape),
            full(t.shape),
        ]
        + [full(x.shape) for x in picks],
        out_specs=[
            pl.BlockSpec((2 * LANES, tile), lambda s: (0, s)),
            pl.BlockSpec((tile // plan.group, plan.message, LANES), lambda s: (s, 0, 0)),
            full((count, 2 * LANES)),
            full((plan.cells, depth)),
        ],
        out_shape=[
            jax.ShapeDtypeStruct((2 * LANES, plan.width), BF16),
            jax.ShapeDtypeStruct((plan.devices, plan.message, LANES), BF16),
            jax.ShapeDtypeStruct((count, 2 * LANES), F32),
            jax.ShapeDtypeStruct((plan.cells, depth), BF16),
        ],
        scratch_shapes=[pltpu.VMEM((plan.cells, depth), F32), pltpu.VMEM((plan.cells, LANES), F32)],
        name="project",
    )(dt_bias, slide, w_in, wt, t, *picks)


def own_kernel(
    plan, rx_ref, ry_ref, skip_ref, v_ref, rows_ref, own1_ref, own2_ref, from1_ref, from2_ref,
    mask_ref, out_ref, pair,
):
    states, cells, half = plan.states, plan.cells, plan.half
    b = rows_ref[0:states, :].astype(BF16)
    c = rows_ref[states : 2 * states, :].astype(BF16)
    pairs = tn_dot(c, b)
    pairs = jnp.concatenate([pairs[:half], pairs[LANES : LANES + cells - half]], axis=0)
    pair[...] = pairs * mask_ref[...].astype(F32)
    lane = lax.broadcasted_iota(jnp.int32, (cells, LANES), 1)
    per = LANES // plan.head_width
    for block in range(plan.width // LANES):
        v = v_ref[:, block * LANES : (block + 1) * LANES]
        vc = jnp.concatenate([v[:half], v[LANES : LANES + cells - half]], axis=0).astype(F32)
        total = None
        for k in range(per):
            h = block * per + k
            dt = rows_ref[2 * states + h : 2 * states + h + 1, :]
            low = dt.astype(BF16)
            x = mm(own1_ref[...] * low, from1_ref[...])
            y = mm(own2_ref[...] * low, from2_ref[...])
            weight = jnp.exp(-(rx_ref[h] * x + ry_ref[h] * y)) * pair[...] * dt
            part = mm(weight.astype(BF16), v) + skip_ref[h] * vc
            total = part if total is None else jnp.where(lane < k * plan.head_width, total, part)
        out_ref[:, block * LANES : (block + 1) * LANES] = total.astype(BF16)


def own_tile(plan, consts, v, rows, rate_x, rate_y, d_skip):
    maps = [consts[k] for k in ("own1", "own2", "from1", "from2", "ownmask")]
    args = [v, rows] + maps
    return pl.pallas_call(
        functools.partial(own_kernel, plan),
        grid=(1,),
        in_specs=[SMEM, SMEM, SMEM] + [full(x.shape) for x in args],
        out_specs=full((plan.cells, plan.width)),
        out_shape=jax.ShapeDtypeStruct((plan.cells, plan.width), BF16),
        scratch_shapes=[pltpu.VMEM((plan.cells, 2 * LANES), F32)],
        compiler_params=pltpu.CompilerParams(vmem_limit_bytes=24 * 2**20),
        name="own",
    )(rate_x, rate_y, d_skip, *args)


def my_head(plan, axis, slot):
    place = lax.rem(lax.axis_index(axis), plan.devices)
    return (place * plan.group + slot * plan.slot) // plan.head_width


def wide_rows(pay_ref, t, at, count, gap):
    return jnp.concatenate([pay_ref[t, at : at + count, :], pay_ref[t, at + gap : at + gap + count, :]], axis=1)


def turned(plan, pay_ref, t, s):
    v = pay_ref[t, s * plan.half : (s + 1) * plan.half, :].astype(F32)
    if plan.half < LANES:
        v = jnp.concatenate([v, jnp.zeros((LANES - plan.half, LANES), F32)], axis=0)
    v = v.T
    return jnp.concatenate([v[:HALF], v[HALF:]], axis=1).astype(BF16)


def repeat_lanes(row, count):
    return jnp.concatenate([row] * count, axis=1)


def load_steps(plan, pay_ref, dts):
    for t in range(plan.devices):
        rows = pay_ref[t, plan.at_dt : plan.message, :].astype(F32)
        for s in range(plan.slots):
            w = s * plan.devices + t
            dts[w : w + 1, :LANES] = rows[2 * s : 2 * s + 1]
            dts[w : w + 1, LANES:] = rows[2 * s + 1 : 2 * s + 2]


def slot_rates(plan, axis, ref, shape):
    rate = jnp.full(shape, ref[my_head(plan, axis, 0)], F32)
    at = lax.broadcasted_iota(jnp.int32, shape, 0)
    for s in range(1, plan.slots):
        rate = jnp.where(at >= s * (shape[0] // plan.slots), ref[my_head(plan, axis, s)], rate)
    return rate


def edges_kernel(
    plan, axis, rx_ref, pay_ref, from1_ref, side1_ref, keep_ref, edge_ref, upto_ref, last_ref,
    dts, inner, kept,
):
    states, tiles = plan.states, plan.devices
    load_steps(plan, pay_ref, dts)
    dt = dts[...]
    low = dt.astype(BF16)
    rate = slot_rates(plan, axis, rx_ref, (plan.work, 2 * LANES))
    inner[...] = jnp.exp(-rate * mm(low, from1_ref[...])) * dt
    kept[...] = jnp.exp(-rate[:, :LANES] * mm(low, keep_ref[...]))
    rowsel = side1_ref[...]
    width = plan.edge // LANES
    for s in range(plan.slots):
        held = jnp.zeros((HALF, plan.edge), F32)
        product = jnp.ones((1, LANES), F32)
        for t in range(tiles):
            w = s * tiles + t
            b = wide_rows(pay_ref, t, plan.at_bc, states, plan.bc).astype(F32)
            bd = (b * inner[w : w + 1, :]).astype(BF16)
            left = jnp.concatenate([rowsel * bd[n : n + 1] for n in range(states)], axis=0)
            edge_ref[w] = held.astype(BF16)
            upto_ref[w : w + 1, :] = product
            now = kept[w : w + 1, :]
            held = held * repeat_lanes(now, width) + nt_dot(turned(plan, pay_ref, t, s), left)
            product = product * now
        last_ref[s] = held.astype(BF16)


def maps_kernel(
    plan, axis, rx_ref, ry_ref, pay_ref, to1_ref, to2_ref, from1_ref, from2_ref, side1_ref, side2_ref,
    sidemask_ref, down1_ref, down2_ref, downmask_ref, pick_ref,
    side_ref, above_ref, bottom_ref, top_ref, dts, s1, s2, d1, d2, down,
):
    states, tiles, rp, cp, work = plan.states, plan.devices, plan.row_pad, plan.col_pad, plan.work
    load_steps(plan, pay_ref, dts)
    low = dts[...].astype(BF16)
    rate_y = slot_rates(plan, axis, ry_ref, (work, 2 * LANES))
    above_ref[...] = jnp.exp(-rate_y * mm(low, to2_ref[...]))
    for w in range(work):
        row = low[w : w + 1]
        s1[w * rp : (w + 1) * rp, :] = side1_ref[...] * row
        s2[w * rp : (w + 1) * rp, :] = side2_ref[...] * row
        rf = dts[w : w + 1, :]
        d1[w * cp : (w + 1) * cp, :] = down1_ref[...].astype(F32) * rf
        d2[w * cp : (w + 1) * cp, :] = down2_ref[...].astype(F32) * rf
    mask = sidemask_ref[...].astype(F32)
    x, y = mm(s1[...], to1_ref[...]), mm(s2[...], to2_ref[...])
    for w in range(work):
        head = my_head(plan, axis, w // tiles)
        at = slice(w * rp, (w + 1) * rp)
        side_ref[w] = (jnp.exp(-(rx_ref[head] * x[at] + ry_ref[head] * y[at])) * mask).astype(BF16)
        bottom_ref[w] = mm(side_ref[w], pick_ref[...]).astype(BF16)
    x, y = mm(d1[...].astype(BF16), from1_ref[...]), mm(d2[...].astype(BF16), from2_ref[...])
    mask = downmask_ref[...].astype(F32)
    for w in range(work):
        head = my_head(plan, axis, w // tiles)
        at = slice(w * cp, (w + 1) * cp)
        fall = jnp.exp(-(rx_ref[head] * x[at] + ry_ref[head] * y[at])) * mask * dts[w : w + 1, :]
        b = wide_rows(pay_ref, w % tiles, plan.at_bc, states, plan.bc).astype(F32)
        falls = jnp.concatenate([fall * b[n : n + 1] for n in range(states)], axis=0).astype(BF16)
        top_ref[w] = nt_dot(turned(plan, pay_ref, w % tiles, w // tiles), falls)


def join_kernel(plan, edge_ref, upto_ref, entry_ref, bottom_ref, top_ref, diag_ref, whole_ref, out_ref):
    width = plan.edge // LANES
    for w in range(plan.work):
        entry = entry_ref[w // plan.devices].astype(F32)
        whole = edge_ref[w].astype(F32) + entry * repeat_lanes(upto_ref[w : w + 1, :], width)
        whole = whole.astype(BF16)
        whole_ref[w] = whole
        passed = jnp.concatenate([bottom_ref[w]] * plan.states, axis=0) * diag_ref[...]
        out_ref[w] = (top_ref[w] + mm(whole, passed)).astype(BF16)


def cells_kernel(plan, pay_ref, edge_ref, top_ref, side_ref, above_ref, colsel_ref, out_ref):
    states, tiles = plan.states, plan.devices
    colsel = colsel_ref[...].astype(F32)
    for w in range(plan.work):
        t, s = w % tiles, w // tiles
        c = wide_rows(pay_ref, t, plan.at_bc + states, states, plan.bc)
        side = side_ref[w]
        left = jnp.concatenate([side * c[n : n + 1] for n in range(states)], axis=0)
        ca = c.astype(F32) * above_ref[w : w + 1, :]
        down = jnp.concatenate([colsel * ca[n : n + 1] for n in range(states)], axis=0).astype(BF16)
        y = mm(edge_ref[w], left) + mm(top_ref[w], down)
        y = jnp.concatenate([y[:, :LANES], y[:, LANES:]], axis=0).T
        out_ref[t, s * plan.half : (s + 1) * plan.half, :] = y[: plan.half].astype(BF16)


def call(kernel, name, smem, args, outs, scratch=(), mib=24):
    return pl.pallas_call(
        kernel,
        grid=(1,),
        in_specs=[SMEM] * len(smem) + [full(x.shape) for x in args],
        out_specs=[full(s) for s, _ in outs],
        out_shape=[jax.ShapeDtypeStruct(s, d) for s, d in outs],
        scratch_shapes=[pltpu.VMEM(s, d) for s, d in scratch],
        compiler_params=pltpu.CompilerParams(vmem_limit_bytes=mib * 2**20),
        name=name,
    )(*smem, *args)


def scan_calls(plan, consts, row_axis, col_axis, pay, rate_x, rate_y):
    work, rp, cp, wide = plan.work, plan.row_pad, plan.col_pad, 2 * LANES
    names = ("from1", "side1", "keep")
    edges, upto, last = call(
        functools.partial(edges_kernel, plan, col_axis),
        "edges",
        [rate_x],
        [pay] + [consts[k] for k in names],
        [((work, HALF, plan.edge), BF16), ((work, LANES), F32), ((plan.slots, HALF, plan.edge), BF16)],
        [((work, wide), F32), ((work, wide), F32), ((work, LANES), F32)],
    )
    if plan.parts > 1:
        hops = [(k, k + plan.devices) for k in range(plan.devices)]
        entry = lax.ppermute(last, col_axis, hops)
    else:
        entry = jnp.zeros_like(last)
    names = ("to1", "to2", "from1", "from2", "side1", "side2", "sidemask", "down1", "down2", "downmask", "pick")
    side, above, bottom, tops = call(
        functools.partial(maps_kernel, plan, col_axis),
        "maps",
        [rate_x, rate_y],
        [pay] + [consts[k] for k in names],
        [
            ((work, rp, wide), BF16),
            ((work, wide), F32),
            ((work, rp, LANES), BF16),
            ((work, HALF, plan.top), F32),
        ],
        [
            ((work, wide), F32),
            ((work * rp, wide), BF16),
            ((work * rp, wide), BF16),
            ((work * cp, wide), F32),
            ((work * cp, wide), F32),
            ((work * cp, wide), F32),
        ],
    )
    edges, tops = call(
        functools.partial(join_kernel, plan),
        "join",
        [],
        [edges, upto, entry, bottom, tops, consts["diag"]],
        [((work, HALF, plan.edge), BF16), ((work, HALF, plan.top), BF16)],
    )
    count = lax.axis_size(row_axis)
    chain = [(r, r + 1) for r in range(count - 1)]
    entry = lax.ppermute(tops, row_axis, chain)
    if count > 2:
        keep = jnp.dot(above.astype(BF16), consts["pick"], preferred_element_type=F32)[:, None, :]
        for _ in range(count - 2):
            entry = lax.ppermute(
                (tops.astype(F32) + keep * entry.astype(F32)).astype(BF16), row_axis, chain
            )
    return call(
        functools.partial(cells_kernel, plan),
        "cells",
        [],
        [pay, edges, entry, side, above, consts["down2"]],
        [((plan.devices, plan.slots * plan.half, LANES), BF16)],
    )[0]


def finish_kernel(plan, y_ref, own_ref, z_ref, gain_ref, t_ref, w_ref, out_ref, full_ref):
    half, cells = plan.half, plan.cells
    slot, slots = plan.slot, plan.slots
    per = LANES // slot
    lane = lax.broadcasted_iota(jnp.int32, (half, LANES), 1)
    for block in range(plan.width // LANES):
        for k, (lo, hi) in enumerate(((0, half), (half, cells))):
            joined = None
            for d in range(per):
                at = block * per + d
                part = y_ref[at // slots, at % slots * half : (at % slots + 1) * half, :].astype(F32)
                shift = (d * slot - k * HALF) % LANES
                if shift:
                    part = pltpu.roll(part, shift, 1)
                joined = part if joined is None else jnp.where(lane < d * slot, joined, part)
            full_ref[lo:hi, block * LANES : (block + 1) * LANES] = joined[: hi - lo]
    y = full_ref[...] + own_ref[...].astype(F32)
    y = y.astype(BF16).astype(F32)
    z = z_ref[...].astype(F32)
    gated = y * (z * (1.0 / (1.0 + jnp.exp(-z))))
    scale = lax.rsqrt(jnp.mean(gated * gated, axis=-1, keepdims=True) + norm_eps)
    normed = (gated * scale * gain_ref[...]).astype(BF16)
    full_ref[...] = mm(normed, w_ref[...]) * cell_mask_of(plan, t_ref)
    for i in range(plan.rows):
        out_ref[i] = full_ref[i * plan.col_pad : i * plan.col_pad + plan.cols, :].astype(BF16)


def finish(plan, consts, y, own, z, gain, tissue, w_out):
    args = (y, own, z, gain, tissue.T, w_out)
    shape = (plan.rows, plan.cols, w_out.shape[1])
    assert w_out.shape[1] == plan.width
    return pl.pallas_call(
        functools.partial(finish_kernel, plan),
        grid=(1,),
        in_specs=[full(a.shape) for a in args],
        out_specs=full(shape),
        out_shape=jax.ShapeDtypeStruct(shape, BF16),
        scratch_shapes=[pltpu.VMEM((plan.cells, plan.width), F32)],
        compiler_params=pltpu.CompilerParams(vmem_limit_bytes=24 * 2**20),
        name="finish",
    )(*args)


def per_device(slide, tissue, w_in, w_bcd, dt_bias, rate_x, rate_y, d_skip, norm_gain, w_out):
    rows, cols, model_width = slide.shape
    width = w_out.shape[0]
    heads = dt_bias.shape[0]
    states = (w_bcd.shape[1] - heads) // 2
    plan = Plan(rows, cols, states, heads, width, lax.axis_size("col"))
    consts = plan.constants()
    v, pay, table, x = project(plan, consts, slide, w_in, w_bcd, tissue, dt_bias)
    groups = plan.segments()
    pay = lax.all_to_all(pay, "col", 0, 0, tiled=True, axis_index_groups=groups)
    own = own_tile(plan, consts, v, table, rate_x, rate_y, d_skip)
    z = jnp.dot(x, w_in[:, width:], preferred_element_type=F32).astype(BF16)
    y = scan_calls(plan, consts, "row", "col", pay, rate_x, rate_y)
    y = lax.all_to_all(y, "col", 0, 0, tiled=True, axis_index_groups=groups)
    return finish(plan, consts, y, own, z, norm_gain.reshape(1, width), tissue, w_out)


def solution(mesh):
    placed = (
        P(("slides", "row"), "col", None),
        P(("slides", "row"), "col"),
        P(),
        P(),
        P(),
        P(),
        P(),
        P(),
        P(),
        P(),
    )
    return jax.shard_map(
        per_device,
        mesh=mesh,
        in_specs=placed,
        out_specs=P(("slides", "row"), "col", None),
        check_vma=False,
    )
```

```python
import functools

import jax
import jax.numpy as jnp
import numpy as np
from jax import lax
from jax.experimental import pallas as pl
from jax.experimental.pallas import tpu as pltpu
from jax.sharding import PartitionSpec as P

norm_eps = 1e-05
LANES = 128
HALF = LANES // 2
F32 = jnp.float32
BF16 = jnp.bfloat16


def round_up(value, step):
    return -(-value // step) * step


def in_hbm(x):
    return pltpu.with_memory_space_constraint(x, pltpu.HBM)


def mm(a, b):
    return jnp.dot(a, b, preferred_element_type=F32)


def nt_dot(a, b):
    return lax.dot_general(a, b, (((1,), (1,)), ((), ())), preferred_element_type=F32)


def tn_dot(a, b):
    return lax.dot_general(a, b, (((0,), (0,)), ((), ())), preferred_element_type=F32)


class Plan:
    def __init__(self, rows, cols, states, heads, width, devices):
        self.rows, self.cols, self.states, self.heads = rows, cols, states, heads
        self.width = width
        self.parts = 2 if devices % 2 == 0 and devices > 2 else 1
        self.devices = devices // self.parts
        self.group = width // self.devices
        self.slot = min(self.group, HALF)
        self.slots = self.group // self.slot
        self.work = self.slots * self.devices
        self.head_width = width // heads
        self.col_pad = round_up(cols, 8)
        self.upper = -(-rows // 2)
        self.half = round_up(self.upper * self.col_pad, 8)
        self.cells = rows * self.col_pad
        self.row_pad = 32
        self.edge = states * self.row_pad
        self.top = states * self.col_pad
        self.bc = 2 * states
        self.at_bc = self.slots * self.half
        self.at_dt = self.at_bc + 2 * self.bc
        self.message = round_up(self.at_dt + 2 * self.slots, 8)
        assert self.head_width % self.slot == 0 and self.group % self.slot == 0
        assert LANES % self.head_width == 0 and self.half <= LANES
        assert rows <= self.row_pad and self.cells - self.half <= self.half
        assert states % 16 == 0 and self.edge % LANES == 0 and heads % 8 == 0

    def segments(self):
        return [list(range(p * self.devices, (p + 1) * self.devices)) for p in range(self.parts)]

    def lanes(self):
        at = np.arange(2 * LANES)
        cell = np.where(at < LANES, at, at - LANES + self.half)
        live = np.where(at < LANES, at < self.half, cell < self.cells)
        i, j = cell // self.col_pad, cell % self.col_pad
        return i, j, live & (j < self.cols)

    def constants(self):
        i, j, real = self.lanes()
        both = real[:, None] & real[None]
        cell = np.arange(self.cells)
        ci, cj = cell // self.col_pad, cell % self.col_pad
        creal = cj < self.cols
        le = np.arange(self.row_pad)
        lj = np.arange(self.col_pad)
        n = np.arange(self.states)
        edge = np.tile(le, LANES // self.row_pad)
        out = {}
        out["to1"] = (j[:, None] <= j[None]) & both
        out["to2"] = (j[:, None] == j[None]) & (i[:, None] <= i[None]) & both
        out["from1"] = (i[:, None] == i[None]) & (j[:, None] > j[None]) & both
        out["from2"] = (i[:, None] > i[None]) & both
        out["side1"] = (i[None] == le[:, None]) & real[None]
        out["side2"] = (i[None] > le[:, None]) & real[None]
        out["sidemask"] = (i[None] >= le[:, None]) & (le < self.rows)[:, None] & real[None]
        out["down1"] = (j[None] <= lj[:, None]) & real[None]
        out["down2"] = (j[None] == lj[:, None]) & real[None]
        out["downmask"] = (j[None] <= lj[:, None]) & (lj < self.cols)[:, None] & real[None]
        out["keep"] = (i[:, None] == edge[None]) & real[:, None]
        out["pick"] = (
            (i == self.rows - 1)[:, None] & real[:, None] & (j[:, None] == np.tile(lj, self.states)[None])
        )
        out["diag"] = np.repeat(n, self.row_pad)[:, None] == np.repeat(n, self.col_pad)[None]
        cboth = creal[:, None] & real[None]
        out["own1"] = (j[None] <= cj[:, None]) & cboth
        out["own2"] = (j[None] == cj[:, None]) & (i[None] <= ci[:, None]) & cboth
        out["ownmask"] = (i[None] <= ci[:, None]) & (j[None] <= cj[:, None]) & cboth
        out["lanei"] = (np.arange(self.rows)[:, None] == i[None]) & real[None]
        out["lanej"] = (np.arange(self.cols)[:, None] == j[None]) & real[None]
        return {k: in_hbm(jnp.asarray(x.astype(np.float32), BF16)) for k, x in out.items()}


def full(shape):
    return pl.BlockSpec(shape, lambda *_: (0,) * len(shape))


HBM = pl.BlockSpec(memory_space=pltpu.HBM)
SMEM = pl.BlockSpec(memory_space=pltpu.SMEM)


def cell_mask_of(plan, t_ref):
    t = t_ref[...].astype(F32).astype(BF16)
    cell = lax.broadcasted_iota(jnp.int32, (plan.cells, plan.cols), 0)
    col = lax.broadcasted_iota(jnp.int32, (plan.cells, plan.cols), 1)
    pick = (lax.rem(cell, plan.col_pad) == col).astype(F32).astype(BF16)
    cell = lax.broadcasted_iota(jnp.int32, (plan.cells, plan.rows), 0)
    row = lax.broadcasted_iota(jnp.int32, (plan.cells, plan.rows), 1)
    return jnp.sum(jnp.where(lax.div(cell, plan.col_pad) == row, mm(pick, t), 0.0), axis=1, keepdims=True)


def project_kernel(
    plan, chunks, bias_ref, x_hbm, w_hbm, wt_ref, t_ref, lanei_ref, lanej_ref,
    v_ref, pay_ref, rows_ref, flat_ref, x_ref, w_ref, wide, x_sem, w_sems,
):
    group, states, cells, heads = plan.group, plan.states, plan.cells, plan.heads
    half, rest = plan.half, plan.cells - plan.half
    tile = plan.width // chunks
    x_copy = pltpu.make_async_copy(x_hbm, x_ref, x_sem)
    x_copy.start()
    copies = [
        pltpu.make_async_copy(w_hbm.at[:, k * tile : (k + 1) * tile], w_ref.at[k], w_sems.at[k])
        for k in range(chunks)
    ]
    for copy in copies:
        copy.start()
    keep = cell_mask_of(plan, t_ref)
    t = t_ref[...].astype(F32).astype(BF16)
    m = jnp.sum(mm(t, lanei_ref[...]) * lanej_ref[...].astype(F32), axis=0, keepdims=True)
    wide[...] = jnp.zeros_like(wide)
    v_ref[half:LANES, :] = jnp.zeros((LANES - half, plan.width), BF16)
    v_ref[LANES + rest :, :] = jnp.zeros((LANES - rest, plan.width), BF16)

    x_copy.wait()
    for i in range(plan.rows):
        wide[i * plan.col_pad : i * plan.col_pad + plan.cols, :] = x_ref[i].astype(F32)
    x = wide[...].astype(BF16)
    flat_ref[...] = x
    table = nt_dot(wt_ref[...], x)
    ext = jnp.concatenate([table, jnp.zeros((table.shape[0], 2 * LANES - cells), F32)], axis=1)
    lane = lax.broadcasted_iota(jnp.int32, (table.shape[0], LANES), 1)
    lo, hi = ext[:, :LANES], ext[:, LANES:]
    shift = half % LANES
    if shift:
        moved = jnp.where(
            lane < LANES - shift, pltpu.roll(lo, LANES - shift, 1), pltpu.roll(hi, LANES - shift, 1)
        )
    else:
        moved = hi
    table = jnp.concatenate([jnp.where(lane < half, lo, 0.0), jnp.where(lane < rest, moved, 0.0)], axis=1)
    z = table[2 * states :]
    at = lax.broadcasted_iota(jnp.int32, z.shape, 0)
    for h in range(heads):
        z = jnp.where(at == h, z + bias_ref[h], z)
    soft = m * (jnp.maximum(z, 0.0) + jnp.log1p(jnp.exp(-jnp.abs(z))))
    table = jnp.concatenate([table[: 2 * states], soft], axis=0).astype(BF16)
    rows_ref[...] = table.astype(F32)
    bc = table[: 2 * states]
    steps = rows_ref[2 * states :, :]

    lane = lax.broadcasted_iota(jnp.int32, (half, LANES), 1)
    for chunk in range(chunks):
        copies[chunk].wait()
        v = mm(flat_ref[...], w_ref[chunk]).astype(BF16).astype(F32) * keep
        low = v.astype(BF16)
        v_ref[0:half, chunk * tile : (chunk + 1) * tile] = low[:half]
        v_ref[LANES : LANES + rest, chunk * tile : (chunk + 1) * tile] = low[half:]
        for k in range(tile // group):
            dest = chunk * (tile // group) + k
            dts = []
            for s in range(plan.slots):
                offset = k * group + s * plan.slot
                base = offset // LANES * LANES
                at = offset % LANES
                first = v[:half, base : base + LANES]
                last = v[half:, base : base + LANES]
                if rest < half:
                    last = jnp.concatenate([last, jnp.zeros((half - rest, LANES), F32)], axis=0)
                if at:
                    first = pltpu.roll(first, LANES - at, 1)
                if at != HALF:
                    last = pltpu.roll(last, (HALF - at) % LANES, 1)
                both = jnp.where(lane < HALF, first, last)
                if plan.slot < HALF:
                    both = jnp.where(lane % HALF < plan.slot, both, 0.0)
                pay_ref[dest, s * half : (s + 1) * half, :] = both.astype(BF16)
                head = (chunk * tile + offset) // plan.head_width
                dts += [steps[head : head + 1, :LANES], steps[head : head + 1, LANES:]]
            pay_ref[dest, plan.at_bc : plan.at_bc + plan.bc, :] = bc[:, :LANES]
            pay_ref[dest, plan.at_bc + plan.bc : plan.at_dt, :] = bc[:, LANES:]
            spare = plan.message - plan.at_dt - len(dts)
            dts += [jnp.zeros((spare, LANES), F32)] if spare else []
            pay_ref[dest, plan.at_dt : plan.message, :] = jnp.concatenate(dts, axis=0).astype(BF16)


def project(plan, consts, slide, w_in, w_bcd, tissue, dt_bias):
    chunks = 4
    tile = plan.width // chunks
    depth = slide.shape[2]
    args = [in_hbm(w_bcd.T), in_hbm(tissue.T), consts["lanei"], consts["lanej"]]
    count = 2 * plan.states + plan.heads
    assert plan.width % chunks == 0 and tile % plan.group == 0 and tile % LANES == 0
    outs = [
        ((2 * LANES, plan.width), BF16),
        ((plan.devices, plan.message, LANES), BF16),
        ((count, 2 * LANES), F32),
        ((plan.cells, depth), BF16),
    ]
    return pl.pallas_call(
        functools.partial(project_kernel, plan, chunks),
        grid=(1,),
        in_specs=[SMEM, HBM, HBM] + [full(x.shape) for x in args],
        out_specs=[full(s) for s, _ in outs],
        out_shape=[jax.ShapeDtypeStruct(s, d) for s, d in outs],
        scratch_shapes=[
            pltpu.VMEM(slide.shape, BF16),
            pltpu.VMEM((chunks, depth, tile), BF16),
            pltpu.VMEM((plan.cells, depth), F32),
            pltpu.SemaphoreType.DMA,
            pltpu.SemaphoreType.DMA((chunks,)),
        ],
        compiler_params=pltpu.CompilerParams(vmem_limit_bytes=24 * 2**20),
        name="project",
    )(in_hbm(dt_bias), in_hbm(slide), in_hbm(w_in), *args)


def home_kernel(
    plan, rx_ref, ry_ref, skip_ref, w_hbm, v_ref, rows_ref, flat_ref, t_ref, gain_ref,
    own1_ref, own2_ref, from1_ref, from2_ref, mask_ref, out_ref, gate_ref, gain_out, pair, w_ref, sem,
):
    states, cells, half = plan.states, plan.cells, plan.half
    copy = pltpu.make_async_copy(w_hbm.at[:, plan.width :], w_ref, sem)
    copy.start()
    gain_out[...] = gain_ref[...]
    b = rows_ref[0:states, :].astype(BF16)
    c = rows_ref[states : 2 * states, :].astype(BF16)
    pairs = tn_dot(c, b)
    pairs = jnp.concatenate([pairs[:half], pairs[LANES : LANES + cells - half]], axis=0)
    pair[...] = pairs * mask_ref[...].astype(F32)
    lane = lax.broadcasted_iota(jnp.int32, (cells, LANES), 1)
    per = LANES // plan.head_width
    for block in range(plan.width // LANES):
        v = v_ref[:, block * LANES : (block + 1) * LANES]
        vc = jnp.concatenate([v[:half], v[LANES : LANES + cells - half]], axis=0).astype(F32)
        total = None
        for k in range(per):
            h = block * per + k
            dt = rows_ref[2 * states + h : 2 * states + h + 1, :]
            low = dt.astype(BF16)
            x = mm(own1_ref[...] * low, from1_ref[...])
            y = mm(own2_ref[...] * low, from2_ref[...])
            weight = jnp.exp(-(rx_ref[h] * x + ry_ref[h] * y)) * pair[...] * dt
            part = mm(weight.astype(BF16), v) + skip_ref[h] * vc
            total = part if total is None else jnp.where(lane < k * plan.head_width, total, part)
        out_ref[:, block * LANES : (block + 1) * LANES] = total.astype(BF16)
    keep = cell_mask_of(plan, t_ref)
    copy.wait()
    tile = 2 * LANES
    for block in range(plan.width // tile):
        at = slice(block * tile, (block + 1) * tile)
        z = mm(flat_ref[...], w_ref[:, at]).astype(BF16).astype(F32)
        gate_ref[:, at] = (z * (1.0 / (1.0 + jnp.exp(-z))) * keep).astype(BF16)


def home(plan, consts, v, rows, flat, w_in, tissue, gain, rate_x, rate_y, d_skip):
    maps = [consts[k] for k in ("own1", "own2", "from1", "from2", "ownmask")]
    args = [v, rows, flat, in_hbm(tissue.T), in_hbm(gain)] + maps
    outs = [((plan.cells, plan.width), BF16), ((plan.cells, plan.width), BF16), (gain.shape, F32)]
    return pl.pallas_call(
        functools.partial(home_kernel, plan),
        grid=(1,),
        in_specs=[SMEM, SMEM, SMEM, HBM] + [full(x.shape) for x in args],
        out_specs=[full(s) for s, _ in outs],
        out_shape=[jax.ShapeDtypeStruct(s, d) for s, d in outs],
        scratch_shapes=[
            pltpu.VMEM((plan.cells, 2 * LANES), F32),
            pltpu.VMEM((w_in.shape[0], w_in.shape[1] - plan.width), BF16),
            pltpu.SemaphoreType.DMA,
        ],
        compiler_params=pltpu.CompilerParams(vmem_limit_bytes=24 * 2**20),
        name="home",
    )(in_hbm(rate_x), in_hbm(rate_y), in_hbm(d_skip), in_hbm(w_in), *args)


def my_head(plan, axis, slot):
    place = lax.rem(lax.axis_index(axis), plan.devices)
    return (place * plan.group + slot * plan.slot) // plan.head_width


def wide_rows(pay_ref, t, at, count, gap):
    return jnp.concatenate([pay_ref[t, at : at + count, :], pay_ref[t, at + gap : at + gap + count, :]], axis=1)


def turned(plan, pay_ref, t, s):
    v = pay_ref[t, s * plan.half : (s + 1) * plan.half, :].astype(F32)
    if plan.half < LANES:
        v = jnp.concatenate([v, jnp.zeros((LANES - plan.half, LANES), F32)], axis=0)
    v = v.T
    return jnp.concatenate([v[:HALF], v[HALF:]], axis=1).astype(BF16)


def repeat_lanes(row, count):
    return jnp.concatenate([row] * count, axis=1)


def load_steps(plan, pay_ref, dts):
    for t in range(plan.devices):
        rows = pay_ref[t, plan.at_dt : plan.message, :].astype(F32)
        for s in range(plan.slots):
            w = s * plan.devices + t
            dts[w : w + 1, :LANES] = rows[2 * s : 2 * s + 1]
            dts[w : w + 1, LANES:] = rows[2 * s + 1 : 2 * s + 2]


def slot_rates(plan, axis, ref, shape):
    rate = jnp.full(shape, ref[my_head(plan, axis, 0)], F32)
    at = lax.broadcasted_iota(jnp.int32, shape, 0)
    for s in range(1, plan.slots):
        rate = jnp.where(at >= s * (shape[0] // plan.slots), ref[my_head(plan, axis, s)], rate)
    return rate


def edges_kernel(
    plan, axis, rx_ref, pay_ref, from1_ref, side1_ref, keep_ref, edge_ref, upto_ref, last_ref,
    dts, inner, kept,
):
    states, tiles = plan.states, plan.devices
    load_steps(plan, pay_ref, dts)
    dt = dts[...]
    low = dt.astype(BF16)
    rate = slot_rates(plan, axis, rx_ref, (plan.work, 2 * LANES))
    inner[...] = jnp.exp(-rate * mm(low, from1_ref[...])) * dt
    kept[...] = jnp.exp(-rate[:, :LANES] * mm(low, keep_ref[...]))
    rowsel = side1_ref[...]
    width = plan.edge // LANES
    for s in range(plan.slots):
        held = jnp.zeros((HALF, plan.edge), F32)
        product = jnp.ones((1, LANES), F32)
        for t in range(tiles):
            w = s * tiles + t
            b = wide_rows(pay_ref, t, plan.at_bc, states, plan.bc).astype(F32)
            bd = (b * inner[w : w + 1, :]).astype(BF16)
            left = jnp.concatenate([rowsel * bd[n : n + 1] for n in range(states)], axis=0)
            edge_ref[w] = held.astype(BF16)
            upto_ref[w : w + 1, :] = product
            now = kept[w : w + 1, :]
            held = held * repeat_lanes(now, width) + nt_dot(turned(plan, pay_ref, t, s), left)
            product = product * now
        last_ref[s] = held.astype(BF16)


def maps_kernel(
    plan, axis, rx_ref, ry_ref, pay_ref, to1_ref, to2_ref, from1_ref, from2_ref, side1_ref, side2_ref,
    sidemask_ref, down1_ref, down2_ref, downmask_ref, pick_ref,
    side_ref, above_ref, bottom_ref, top_ref, dts, s1, s2, d1, d2, down,
):
    states, tiles, rp, cp, work = plan.states, plan.devices, plan.row_pad, plan.col_pad, plan.work
    load_steps(plan, pay_ref, dts)
    low = dts[...].astype(BF16)
    rate_y = slot_rates(plan, axis, ry_ref, (work, 2 * LANES))
    above_ref[...] = jnp.exp(-rate_y * mm(low, to2_ref[...]))
    for w in range(work):
        row = low[w : w + 1]
        s1[w * rp : (w + 1) * rp, :] = side1_ref[...] * row
        s2[w * rp : (w + 1) * rp, :] = side2_ref[...] * row
        rf = dts[w : w + 1, :]
        d1[w * cp : (w + 1) * cp, :] = down1_ref[...].astype(F32) * rf
        d2[w * cp : (w + 1) * cp, :] = down2_ref[...].astype(F32) * rf
    mask = sidemask_ref[...].astype(F32)
    x, y = mm(s1[...], to1_ref[...]), mm(s2[...], to2_ref[...])
    for w in range(work):
        head = my_head(plan, axis, w // tiles)
        at = slice(w * rp, (w + 1) * rp)
        side_ref[w] = (jnp.exp(-(rx_ref[head] * x[at] + ry_ref[head] * y[at])) * mask).astype(BF16)
        bottom_ref[w] = mm(side_ref[w], pick_ref[...]).astype(BF16)
    x, y = mm(d1[...].astype(BF16), from1_ref[...]), mm(d2[...].astype(BF16), from2_ref[...])
    mask = downmask_ref[...].astype(F32)
    for w in range(work):
        head = my_head(plan, axis, w // tiles)
        at = slice(w * cp, (w + 1) * cp)
        fall = jnp.exp(-(rx_ref[head] * x[at] + ry_ref[head] * y[at])) * mask * dts[w : w + 1, :]
        b = wide_rows(pay_ref, w % tiles, plan.at_bc, states, plan.bc).astype(F32)
        falls = jnp.concatenate([fall * b[n : n + 1] for n in range(states)], axis=0).astype(BF16)
        top_ref[w] = nt_dot(turned(plan, pay_ref, w % tiles, w // tiles), falls)


def join_kernel(plan, edge_ref, upto_ref, entry_ref, bottom_ref, top_ref, diag_ref, whole_ref, out_ref):
    width = plan.edge // LANES
    for w in range(plan.work):
        entry = entry_ref[w // plan.devices].astype(F32)
        whole = edge_ref[w].astype(F32) + entry * repeat_lanes(upto_ref[w : w + 1, :], width)
        whole = whole.astype(BF16)
        whole_ref[w] = whole
        passed = jnp.concatenate([bottom_ref[w]] * plan.states, axis=0) * diag_ref[...]
        out_ref[w] = (top_ref[w] + mm(whole, passed)).astype(BF16)


def cells_kernel(plan, pay_ref, edge_ref, top_ref, side_ref, above_ref, colsel_ref, out_ref):
    states, tiles = plan.states, plan.devices
    colsel = colsel_ref[...].astype(F32)
    for w in range(plan.work):
        t, s = w % tiles, w // tiles
        c = wide_rows(pay_ref, t, plan.at_bc + states, states, plan.bc)
        side = side_ref[w]
        left = jnp.concatenate([side * c[n : n + 1] for n in range(states)], axis=0)
        ca = c.astype(F32) * above_ref[w : w + 1, :]
        down = jnp.concatenate([colsel * ca[n : n + 1] for n in range(states)], axis=0).astype(BF16)
        y = mm(edge_ref[w], left) + mm(top_ref[w], down)
        y = jnp.concatenate([y[:, :LANES], y[:, LANES:]], axis=0).T
        out_ref[t, s * plan.half : (s + 1) * plan.half, :] = y[: plan.half].astype(BF16)


def call(kernel, name, smem, args, outs, scratch=(), mib=24):
    return pl.pallas_call(
        kernel,
        grid=(1,),
        in_specs=[SMEM] * len(smem) + [full(x.shape) for x in args],
        out_specs=[full(s) for s, _ in outs],
        out_shape=[jax.ShapeDtypeStruct(s, d) for s, d in outs],
        scratch_shapes=[pltpu.VMEM(s, d) for s, d in scratch],
        compiler_params=pltpu.CompilerParams(vmem_limit_bytes=mib * 2**20),
        name=name,
    )(*[in_hbm(x) for x in smem], *args)


def scan_calls(plan, consts, row_axis, col_axis, pay, rate_x, rate_y):
    work, rp, cp, wide = plan.work, plan.row_pad, plan.col_pad, 2 * LANES
    names = ("from1", "side1", "keep")
    edges, upto, last = call(
        functools.partial(edges_kernel, plan, col_axis),
        "edges",
        [rate_x],
        [pay] + [consts[k] for k in names],
        [((work, HALF, plan.edge), BF16), ((work, LANES), F32), ((plan.slots, HALF, plan.edge), BF16)],
        [((work, wide), F32), ((work, wide), F32), ((work, LANES), F32)],
    )
    if plan.parts > 1:
        hops = [(k, k + plan.devices) for k in range(plan.devices)]
        entry = lax.ppermute(last, col_axis, hops)
    else:
        entry = jnp.zeros_like(last)
    names = ("to1", "to2", "from1", "from2", "side1", "side2", "sidemask", "down1", "down2", "downmask", "pick")
    side, above, bottom, tops = call(
        functools.partial(maps_kernel, plan, col_axis),
        "maps",
        [rate_x, rate_y],
        [pay] + [consts[k] for k in names],
        [
            ((work, rp, wide), BF16),
            ((work, wide), F32),
            ((work, rp, LANES), BF16),
            ((work, HALF, plan.top), F32),
        ],
        [
            ((work, wide), F32),
            ((work * rp, wide), BF16),
            ((work * rp, wide), BF16),
            ((work * cp, wide), F32),
            ((work * cp, wide), F32),
            ((work * cp, wide), F32),
        ],
    )
    edges, tops = call(
        functools.partial(join_kernel, plan),
        "join",
        [],
        [edges, upto, entry, bottom, tops, consts["diag"]],
        [((work, HALF, plan.edge), BF16), ((work, HALF, plan.top), BF16)],
    )
    count = lax.axis_size(row_axis)
    chain = [(r, r + 1) for r in range(count - 1)]
    entry = lax.ppermute(tops, row_axis, chain)
    if count > 2:
        keep = jnp.dot(above.astype(BF16), consts["pick"], preferred_element_type=F32)[:, None, :]
        for _ in range(count - 2):
            entry = lax.ppermute(
                (tops.astype(F32) + keep * entry.astype(F32)).astype(BF16), row_axis, chain
            )
    return call(
        functools.partial(cells_kernel, plan),
        "cells",
        [],
        [pay, edges, entry, side, above, consts["down2"]],
        [((plan.devices, plan.slots * plan.half, LANES), BF16)],
    )[0]


def finish_kernel(plan, y_ref, own_ref, gate_ref, gain_ref, w_ref, out_ref, full_ref):
    half, cells = plan.half, plan.cells
    slot, slots = plan.slot, plan.slots
    per = LANES // slot
    lane = lax.broadcasted_iota(jnp.int32, (half, LANES), 1)
    for block in range(plan.width // LANES):
        for k, (lo, hi) in enumerate(((0, half), (half, cells))):
            joined = None
            for d in range(per):
                at = block * per + d
                part = y_ref[at // slots, at % slots * half : (at % slots + 1) * half, :].astype(F32)
                shift = (d * slot - k * HALF) % LANES
                if shift:
                    part = pltpu.roll(part, shift, 1)
                joined = part if joined is None else jnp.where(lane < d * slot, joined, part)
            full_ref[lo:hi, block * LANES : (block + 1) * LANES] = joined[: hi - lo]
    y = full_ref[...] + own_ref[...].astype(F32)
    y = y.astype(BF16).astype(F32)
    gated = y * gate_ref[...].astype(F32)
    scale = lax.rsqrt(jnp.mean(gated * gated, axis=-1, keepdims=True) + norm_eps)
    normed = (gated * scale * gain_ref[...]).astype(BF16)
    full_ref[...] = mm(normed, w_ref[...])
    for i in range(plan.rows):
        out_ref[i] = full_ref[i * plan.col_pad : i * plan.col_pad + plan.cols, :].astype(BF16)


def finish(plan, y, own, gate, gain, w_out):
    args = (y, own, gate, gain, w_out)
    shape = (plan.rows, plan.cols, w_out.shape[1])
    assert w_out.shape[1] == plan.width
    return call(
        functools.partial(finish_kernel, plan), "finish", [], args, [(shape, BF16)], [((plan.cells, plan.width), F32)]
    )[0]


def per_device(slide, tissue, w_in, w_bcd, dt_bias, rate_x, rate_y, d_skip, norm_gain, w_out):
    rows, cols, model_width = slide.shape
    width = w_out.shape[0]
    heads = dt_bias.shape[0]
    states = (w_bcd.shape[1] - heads) // 2
    plan = Plan(rows, cols, states, heads, width, lax.axis_size("col"))
    consts = plan.constants()
    v, pay, table, x = project(plan, consts, slide, w_in, w_bcd, tissue, dt_bias)
    groups = plan.segments()
    pay = lax.all_to_all(pay, "col", 0, 0, tiled=True, axis_index_groups=groups)
    gain = norm_gain.reshape(1, width)
    own, gate, gain = home(plan, consts, v, table, x, w_in, tissue, gain, rate_x, rate_y, d_skip)
    pay, own, gate, gain = lax.optimization_barrier((pay, own, gate, gain))
    y = scan_calls(plan, consts, "row", "col", pay, rate_x, rate_y)
    y = lax.all_to_all(y, "col", 0, 0, tiled=True, axis_index_groups=groups)
    return finish(plan, y, own, gate, gain, w_out)


def solution(mesh):
    placed = (
        P(("slides", "row"), "col", None),
        P(("slides", "row"), "col"),
        P(),
        P(),
        P(),
        P(),
        P(),
        P(),
        P(),
        P(),
    )
    return jax.shard_map(
        per_device,
        mesh=mesh,
        in_specs=placed,
        out_specs=P(("slides", "row"), "col", None),
        check_vma=False,
    )
```

```python
import functools

import jax
import jax.numpy as jnp
import numpy as np
from jax import lax
from jax.experimental import pallas as pl
from jax.experimental.pallas import tpu as pltpu
from jax.sharding import PartitionSpec as P

norm_eps = 1e-05
LANES = 128
HALF = LANES // 2
F32 = jnp.float32
BF16 = jnp.bfloat16


def round_up(value, step):
    return -(-value // step) * step


def in_hbm(x):
    return pltpu.with_memory_space_constraint(x, pltpu.HBM)


def mm(a, b):
    return jnp.dot(a, b, preferred_element_type=F32)


def nt_dot(a, b):
    return lax.dot_general(a, b, (((1,), (1,)), ((), ())), preferred_element_type=F32)


def tn_dot(a, b):
    return lax.dot_general(a, b, (((0,), (0,)), ((), ())), preferred_element_type=F32)


class Plan:
    def __init__(self, rows, cols, states, heads, width, devices):
        self.rows, self.cols, self.states, self.heads = rows, cols, states, heads
        self.width = width
        self.parts = 2 if devices % 2 == 0 and devices > 2 else 1
        self.devices = devices // self.parts
        self.group = width // self.devices
        self.slot = min(self.group, HALF)
        self.slots = self.group // self.slot
        self.work = self.slots * self.devices
        self.head_width = width // heads
        self.col_pad = round_up(cols, 8)
        self.upper = -(-rows // 2)
        self.half = round_up(self.upper * self.col_pad, 8)
        self.cells = rows * self.col_pad
        self.edge = rows * states
        self.top = states * self.col_pad
        self.bc = 2 * states
        self.at_bc = self.slots * self.half
        self.at_dt = self.at_bc + 2 * self.bc
        self.message = round_up(self.at_dt + 2 * self.slots, 8)
        assert self.head_width % self.slot == 0 and self.group % self.slot == 0
        assert LANES % self.head_width == 0 and self.half <= LANES
        assert self.cells - self.half <= self.half
        assert states % 16 == 0 and heads % 8 == 0

    def segments(self):
        return [list(range(p * self.devices, (p + 1) * self.devices)) for p in range(self.parts)]

    def lanes(self):
        at = np.arange(2 * LANES)
        cell = np.where(at < LANES, at, at - LANES + self.half)
        live = np.where(at < LANES, at < self.half, cell < self.cells)
        i, j = cell // self.col_pad, cell % self.col_pad
        return i, j, live & (j < self.cols)

    def constants(self):
        i, j, real = self.lanes()
        both = real[:, None] & real[None]
        cell = np.arange(self.cells)
        ci, cj = cell // self.col_pad, cell % self.col_pad
        creal = cj < self.cols
        le = np.arange(round_up(self.rows, 8))
        lj = np.arange(self.col_pad)
        out = {}
        out["to1"] = (j[:, None] <= j[None]) & both
        out["to2"] = (j[:, None] == j[None]) & (i[:, None] <= i[None]) & both
        out["from1"] = (i[:, None] == i[None]) & (j[:, None] > j[None]) & both
        out["from2"] = (i[:, None] > i[None]) & both
        out["side1"] = (i[None] == le[:, None]) & real[None]
        out["side2"] = (i[None] > le[:, None]) & real[None]
        out["sidemask"] = (i[None] >= le[:, None]) & (le < self.rows)[:, None] & real[None]
        out["down1"] = (j[None] <= lj[:, None]) & real[None]
        out["down2"] = (j[None] == lj[:, None]) & real[None]
        out["downmask"] = (j[None] <= lj[:, None]) & (lj < self.cols)[:, None] & real[None]
        out["pick"] = (
            (i == self.rows - 1)[:, None] & real[:, None] & (j[:, None] == np.tile(lj, self.states)[None])
        )
        cboth = creal[:, None] & real[None]
        out["own1"] = (j[None] <= cj[:, None]) & cboth
        out["own2"] = (j[None] == cj[:, None]) & (i[None] <= ci[:, None]) & cboth
        out["ownmask"] = (i[None] <= ci[:, None]) & (j[None] <= cj[:, None]) & cboth
        out["lanei"] = (np.arange(self.rows)[:, None] == i[None]) & real[None]
        out["lanej"] = (np.arange(self.cols)[:, None] == j[None]) & real[None]
        return {k: in_hbm(jnp.asarray(x.astype(np.float32), BF16)) for k, x in out.items()}


def full(shape):
    return pl.BlockSpec(shape, lambda *_: (0,) * len(shape))


HBM = pl.BlockSpec(memory_space=pltpu.HBM)
SMEM = pl.BlockSpec(memory_space=pltpu.SMEM)


def cell_mask_of(plan, t_ref):
    t = t_ref[...].astype(F32).astype(BF16)
    cell = lax.broadcasted_iota(jnp.int32, (plan.cells, plan.cols), 0)
    col = lax.broadcasted_iota(jnp.int32, (plan.cells, plan.cols), 1)
    pick = (lax.rem(cell, plan.col_pad) == col).astype(F32).astype(BF16)
    cell = lax.broadcasted_iota(jnp.int32, (plan.cells, plan.rows), 0)
    row = lax.broadcasted_iota(jnp.int32, (plan.cells, plan.rows), 1)
    return jnp.sum(jnp.where(lax.div(cell, plan.col_pad) == row, mm(pick, t), 0.0), axis=1, keepdims=True)


def project_kernel(
    plan, chunks, bias_hbm, x_hbm, w_hbm, wt_hbm, t_hbm, lanei_hbm, lanej_hbm,
    v_ref, pay_hbm, rows_ref, flat_ref,
    bias_ref, x_ref, w_ref, wt_ref, t_ref, lanei_ref, lanej_ref, pay_ref, wide, sems, w_sems, out_sems,
):
    group, states, cells, heads = plan.group, plan.states, plan.cells, plan.heads
    half, rest = plan.half, plan.cells - plan.half
    tile = plan.width // chunks
    pairs = (
        (x_hbm, x_ref), (t_hbm, t_ref), (wt_hbm, wt_ref), (lanei_hbm, lanei_ref), (lanej_hbm, lanej_ref),
        (bias_hbm, bias_ref),
    )
    loads = [pltpu.make_async_copy(a, b, sems.at[k]) for k, (a, b) in enumerate(pairs)]
    copies = [
        pltpu.make_async_copy(w_hbm.at[:, k * tile : (k + 1) * tile], w_ref.at[k], w_sems.at[k])
        for k in range(chunks)
    ]
    for copy in loads + copies:
        copy.start()
    wide[...] = jnp.zeros_like(wide)
    v_ref[half:LANES, :] = jnp.zeros((LANES - half, plan.width), BF16)
    v_ref[LANES + rest :, :] = jnp.zeros((LANES - rest, plan.width), BF16)

    loads[0].wait()
    for i in range(plan.rows):
        wide[i * plan.col_pad : i * plan.col_pad + plan.cols, :] = x_ref[i].astype(F32)
    x = wide[...].astype(BF16)
    flat_ref[...] = x
    for copy in loads[1:]:
        copy.wait()
    keep = cell_mask_of(plan, t_ref)
    t = t_ref[...].astype(F32).astype(BF16)
    m = jnp.sum(mm(t, lanei_ref[...]) * lanej_ref[...].astype(F32), axis=0, keepdims=True)
    table = nt_dot(wt_ref[...], x)
    ext = jnp.concatenate([table, jnp.zeros((table.shape[0], 2 * LANES - cells), F32)], axis=1)
    lane = lax.broadcasted_iota(jnp.int32, (table.shape[0], LANES), 1)
    lo, hi = ext[:, :LANES], ext[:, LANES:]
    shift = half % LANES
    if shift:
        moved = jnp.where(
            lane < LANES - shift, pltpu.roll(lo, LANES - shift, 1), pltpu.roll(hi, LANES - shift, 1)
        )
    else:
        moved = hi
    table = jnp.concatenate([jnp.where(lane < half, lo, 0.0), jnp.where(lane < rest, moved, 0.0)], axis=1)
    z = table[2 * states :]
    at = lax.broadcasted_iota(jnp.int32, z.shape, 0)
    for h in range(heads):
        z = jnp.where(at == h, z + bias_ref[h], z)
    soft = m * (jnp.maximum(z, 0.0) + jnp.log1p(jnp.exp(-jnp.abs(z))))
    table = jnp.concatenate([table[: 2 * states], soft], axis=0).astype(BF16)
    rows_ref[...] = table.astype(F32)
    bc = table[: 2 * states]
    steps = rows_ref[2 * states :, :]

    lane = lax.broadcasted_iota(jnp.int32, (half, LANES), 1)
    sent = []
    for chunk in range(chunks):
        copies[chunk].wait()
        v = mm(flat_ref[...], w_ref[chunk]).astype(BF16).astype(F32) * keep
        low = v.astype(BF16)
        v_ref[0:half, chunk * tile : (chunk + 1) * tile] = low[:half]
        v_ref[LANES : LANES + rest, chunk * tile : (chunk + 1) * tile] = low[half:]
        per = tile // group
        for k in range(per):
            dest = chunk * per + k
            dts = []
            for s in range(plan.slots):
                offset = k * group + s * plan.slot
                base = offset // LANES * LANES
                at = offset % LANES
                first = v[:half, base : base + LANES]
                last = v[half:, base : base + LANES]
                if rest < half:
                    last = jnp.concatenate([last, jnp.zeros((half - rest, LANES), F32)], axis=0)
                if at:
                    first = pltpu.roll(first, LANES - at, 1)
                if at != HALF:
                    last = pltpu.roll(last, (HALF - at) % LANES, 1)
                both = jnp.where(lane < HALF, first, last)
                if plan.slot < HALF:
                    both = jnp.where(lane % HALF < plan.slot, both, 0.0)
                pay_ref[dest, s * half : (s + 1) * half, :] = both.astype(BF16)
                head = (chunk * tile + offset) // plan.head_width
                dts += [steps[head : head + 1, :LANES], steps[head : head + 1, LANES:]]
            pay_ref[dest, plan.at_bc : plan.at_bc + plan.bc, :] = bc[:, :LANES]
            pay_ref[dest, plan.at_bc + plan.bc : plan.at_dt, :] = bc[:, LANES:]
            spare = plan.message - plan.at_dt - len(dts)
            dts += [jnp.zeros((spare, LANES), F32)] if spare else []
            pay_ref[dest, plan.at_dt : plan.message, :] = jnp.concatenate(dts, axis=0).astype(BF16)
        at = slice(chunk * per, (chunk + 1) * per)
        sent.append(pltpu.make_async_copy(pay_ref.at[at], pay_hbm.at[at], out_sems.at[chunk]))
        sent[-1].start()
    for copy in sent:
        copy.wait()


def project(plan, consts, slide, w_in, w_bcd, tissue, dt_bias):
    chunks = 4
    tile = plan.width // chunks
    depth = slide.shape[2]
    args = [dt_bias, slide, w_in, w_bcd.T, tissue.T, consts["lanei"], consts["lanej"]]
    count = 2 * plan.states + plan.heads
    assert plan.width % chunks == 0 and tile % plan.group == 0 and tile % LANES == 0
    message = (plan.devices, plan.message, LANES)
    outs = [((2 * LANES, plan.width), BF16), (message, BF16), ((count, 2 * LANES), F32), ((plan.cells, depth), BF16)]
    specs = [full(s) for s, _ in outs]
    specs[1] = HBM
    return pl.pallas_call(
        functools.partial(project_kernel, plan, chunks),
        grid=(1,),
        in_specs=[HBM] * len(args),
        out_specs=specs,
        out_shape=[jax.ShapeDtypeStruct(s, d) for s, d in outs],
        scratch_shapes=[
            pltpu.SMEM(dt_bias.shape, F32),
            pltpu.VMEM(slide.shape, BF16),
            pltpu.VMEM((chunks, depth, tile), BF16),
        ]
        + [pltpu.VMEM(x.shape, x.dtype) for x in args[3:]]
        + [
            pltpu.VMEM(message, BF16),
            pltpu.VMEM((plan.cells, depth), F32),
            pltpu.SemaphoreType.DMA((6,)),
            pltpu.SemaphoreType.DMA((chunks,)),
            pltpu.SemaphoreType.DMA((chunks,)),
        ],
        compiler_params=pltpu.CompilerParams(vmem_limit_bytes=24 * 2**20),
        name="project",
    )(*[in_hbm(x) for x in args])


def home_kernel(
    plan, rx_ref, ry_ref, skip_ref, w_hbm, v_ref, rows_ref, flat_ref, t_ref, gain_ref,
    own1_ref, own2_ref, from1_ref, from2_ref, mask_ref, out_ref, gate_ref, gain_out, pair, w_ref, sem,
):
    states, cells, half = plan.states, plan.cells, plan.half
    copy = pltpu.make_async_copy(w_hbm.at[:, plan.width :], w_ref, sem)
    copy.start()
    gain_out[...] = gain_ref[...]
    b = rows_ref[0:states, :].astype(BF16)
    c = rows_ref[states : 2 * states, :].astype(BF16)
    pairs = tn_dot(c, b)
    pairs = jnp.concatenate([pairs[:half], pairs[LANES : LANES + cells - half]], axis=0)
    pair[...] = pairs * mask_ref[...].astype(F32)
    lane = lax.broadcasted_iota(jnp.int32, (cells, LANES), 1)
    per = LANES // plan.head_width
    for block in range(plan.width // LANES):
        v = v_ref[:, block * LANES : (block + 1) * LANES]
        vc = jnp.concatenate([v[:half], v[LANES : LANES + cells - half]], axis=0).astype(F32)
        total = None
        for k in range(per):
            h = block * per + k
            dt = rows_ref[2 * states + h : 2 * states + h + 1, :]
            low = dt.astype(BF16)
            x = mm(own1_ref[...] * low, from1_ref[...])
            y = mm(own2_ref[...] * low, from2_ref[...])
            weight = jnp.exp(-(rx_ref[h] * x + ry_ref[h] * y)) * pair[...] * dt
            part = mm(weight.astype(BF16), v) + skip_ref[h] * vc
            total = part if total is None else jnp.where(lane < k * plan.head_width, total, part)
        out_ref[:, block * LANES : (block + 1) * LANES] = total.astype(BF16)
    keep = cell_mask_of(plan, t_ref)
    copy.wait()
    tile = 2 * LANES
    for block in range(plan.width // tile):
        at = slice(block * tile, (block + 1) * tile)
        z = mm(flat_ref[...], w_ref[:, at]).astype(BF16).astype(F32)
        gate_ref[:, at] = (z * (1.0 / (1.0 + jnp.exp(-z))) * keep).astype(BF16)


def home(plan, consts, v, rows, flat, w_in, tissue, gain, rate_x, rate_y, d_skip):
    args = [in_hbm(w_in), v, rows, flat, in_hbm(tissue.T), in_hbm(gain)]
    args += [consts[k] for k in ("own1", "own2", "from1", "from2", "ownmask")]
    outs = [((plan.cells, plan.width), BF16), ((plan.cells, plan.width), BF16), (gain.shape, F32)]
    return pl.pallas_call(
        functools.partial(home_kernel, plan),
        grid=(1,),
        in_specs=[SMEM, SMEM, SMEM, HBM] + [full(x.shape) for x in args[1:]],
        out_specs=[full(s) for s, _ in outs],
        out_shape=[jax.ShapeDtypeStruct(s, d) for s, d in outs],
        scratch_shapes=[
            pltpu.VMEM((plan.cells, 2 * LANES), F32),
            pltpu.VMEM((w_in.shape[0], w_in.shape[1] - plan.width), BF16),
            pltpu.SemaphoreType.DMA,
        ],
        compiler_params=pltpu.CompilerParams(vmem_limit_bytes=24 * 2**20),
        name="home",
    )(in_hbm(rate_x), in_hbm(rate_y), in_hbm(d_skip), *args)


def ones(mask):
    return jnp.where(mask, 1.0, 0.0).astype(BF16)


def places(plan, shape, axis):
    at = lax.broadcasted_iota(jnp.int32, shape, axis)
    late = at >= LANES
    at = jnp.where(late, at - LANES, at)
    i = lax.div(at, plan.col_pad)
    j = at - i * plan.col_pad
    real = (at < jnp.where(late, plan.cells - plan.half, plan.half)) & (j < plan.cols)
    return jnp.where(late, i + plan.upper, i), j, real


def my_head(plan, axis, slot):
    place = lax.rem(lax.axis_index(axis), plan.devices)
    return (place * plan.group + slot * plan.slot) // plan.head_width


def wide_rows(pay_ref, t, at, count, gap):
    return jnp.concatenate([pay_ref[t, at : at + count, :], pay_ref[t, at + gap : at + gap + count, :]], axis=1)


def turned(plan, pay_ref, t, s):
    v = pay_ref[t, s * plan.half : (s + 1) * plan.half, :].astype(F32)
    if plan.half < LANES:
        v = jnp.concatenate([v, jnp.zeros((LANES - plan.half, LANES), F32)], axis=0)
    v = v.T
    return jnp.concatenate([v[:HALF], v[HALF:]], axis=1).astype(BF16)


def load_steps(plan, pay_ref, dts):
    for t in range(plan.devices):
        rows = pay_ref[t, plan.at_dt : plan.message, :].astype(F32)
        for s in range(plan.slots):
            w = s * plan.devices + t
            dts[w : w + 1, :LANES] = rows[2 * s : 2 * s + 1]
            dts[w : w + 1, LANES:] = rows[2 * s + 1 : 2 * s + 2]


def slot_rates(plan, axis, rate_ref):
    at = lax.broadcasted_iota(jnp.int32, (plan.work, 1), 0)
    rate = jnp.full((plan.work, 1), rate_ref[my_head(plan, axis, 0)], F32)
    for s in range(1, plan.slots):
        rate = jnp.where(at >= s * plan.devices, rate_ref[my_head(plan, axis, s)], rate)
    return rate


def edges_kernel(plan, axis, rx_hbm, pay_ref, edge_ref, upto_ref, last_ref, rx_ref, dts, inner, kept, sem):
    states, tiles, wide = plan.states, plan.devices, 2 * LANES
    copy = pltpu.make_async_copy(rx_hbm, rx_ref, sem)
    copy.start()
    load_steps(plan, pay_ref, dts)
    i, j, real = places(plan, (wide, wide), 0)
    ti, tj, treal = places(plan, (wide, wide), 1)
    from1 = ones((i == ti) & (j > tj) & real & treal)
    edge_row = lax.div(lax.broadcasted_iota(jnp.int32, (wide, plan.edge), 1), states)
    i, _, real = places(plan, (wide, plan.edge), 0)
    keep = ones((i == edge_row) & real)
    ti, _, treal = places(plan, (plan.rows, wide), 1)
    rowsel = ones((ti == lax.broadcasted_iota(jnp.int32, (plan.rows, wide), 0)) & treal)
    dt = dts[...]
    low = dt.astype(BF16)
    inside, across = mm(low, from1), mm(low, keep)
    copy.wait()
    rate = slot_rates(plan, axis, rx_ref)
    inner[...] = jnp.exp(-rate * inside) * dt
    kept[...] = jnp.exp(-rate * across)
    for s in range(plan.slots):
        held = jnp.zeros((HALF, plan.edge), F32)
        product = jnp.ones((1, plan.edge), F32)
        for t in range(tiles):
            w = s * tiles + t
            b = wide_rows(pay_ref, t, plan.at_bc, states, plan.bc).astype(F32)
            bd = (b * inner[w : w + 1, :]).astype(BF16)
            left = jnp.concatenate([bd * rowsel[i : i + 1] for i in range(plan.rows)], axis=0)
            edge_ref[w] = held.astype(BF16)
            upto_ref[w : w + 1, :] = product
            now = kept[w : w + 1, :]
            held = held * now + nt_dot(turned(plan, pay_ref, t, s), left)
            product = product * now
        last_ref[s] = held.astype(BF16)


def maps_kernel(
    plan, axis, rx_ref, ry_ref, pay_ref, to1_ref, to2_ref, from1_ref, from2_ref, side1_ref, side2_ref,
    sidemask_ref, down1_ref, down2_ref, downmask_ref, pick_ref,
    side_ref, above_ref, bottom_ref, top_ref, dts, s1, s2, d1, d2,
):
    states, tiles, cp, work = plan.states, plan.devices, plan.col_pad, plan.work
    rp = side1_ref.shape[0]
    load_steps(plan, pay_ref, dts)
    low = dts[...].astype(BF16)
    above_ref[...] = jnp.exp(-slot_rates(plan, axis, ry_ref) * mm(low, to2_ref[...]))
    for w in range(work):
        rf = dts[w : w + 1, :]
        s1[w * rp : (w + 1) * rp, :] = side1_ref[...].astype(F32) * rf
        s2[w * rp : (w + 1) * rp, :] = side2_ref[...].astype(F32) * rf
        d1[w * cp : (w + 1) * cp, :] = down1_ref[...].astype(F32) * rf
        d2[w * cp : (w + 1) * cp, :] = down2_ref[...].astype(F32) * rf
    mask = sidemask_ref[...].astype(F32)
    x, y = mm(s1[...].astype(BF16), to1_ref[...]), mm(s2[...].astype(BF16), to2_ref[...])
    for w in range(work):
        head = my_head(plan, axis, w // tiles)
        rx, ry = rx_ref[head], ry_ref[head]
        at = slice(w * rp, (w + 1) * rp)
        side = (jnp.exp(-(rx * x[at] + ry * y[at])) * mask).astype(BF16)
        side_ref[w] = side
        bottom_ref[w] = mm(side, pick_ref[...]).astype(BF16)
    x, y = mm(d1[...].astype(BF16), from1_ref[...]), mm(d2[...].astype(BF16), from2_ref[...])
    mask = downmask_ref[...].astype(F32)
    for w in range(work):
        s, t = w // tiles, w % tiles
        head = my_head(plan, axis, s)
        rx, ry = rx_ref[head], ry_ref[head]
        at = slice(w * cp, (w + 1) * cp)
        fall = jnp.exp(-(rx * x[at] + ry * y[at])) * mask * dts[w : w + 1, :]
        b = wide_rows(pay_ref, t, plan.at_bc, states, plan.bc).astype(F32)
        falls = jnp.concatenate([fall * b[n : n + 1] for n in range(states)], axis=0).astype(BF16)
        top_ref[w] = nt_dot(turned(plan, pay_ref, t, s), falls)


def join_kernel(plan, edge_ref, upto_ref, entry_ref, bottom_ref, top_ref, whole_ref, out_ref):
    shape = (plan.states, plan.top)
    n = lax.broadcasted_iota(jnp.int32, shape, 0)
    diag = ones(n == lax.div(lax.broadcasted_iota(jnp.int32, shape, 1), plan.col_pad))
    for w in range(plan.work):
        entry = entry_ref[w // plan.devices].astype(F32)
        whole = (edge_ref[w].astype(F32) + entry * upto_ref[w : w + 1, :]).astype(BF16)
        whole_ref[w] = whole
        bottom = bottom_ref[w]
        passed = jnp.concatenate([diag * bottom[i : i + 1] for i in range(plan.rows)], axis=0)
        out_ref[w] = (top_ref[w] + mm(whole, passed)).astype(BF16)


def cells_kernel(plan, pay_ref, edge_ref, top_ref, side_ref, above_ref, out_ref):
    states, tiles = plan.states, plan.devices
    shape = (plan.col_pad, 2 * LANES)
    _, tj, treal = places(plan, shape, 1)
    colsel = jnp.where((tj == lax.broadcasted_iota(jnp.int32, shape, 0)) & treal, 1.0, 0.0)
    for w in range(plan.work):
        t, s = w % tiles, w // tiles
        c = wide_rows(pay_ref, t, plan.at_bc + states, states, plan.bc)
        side = side_ref[w]
        left = jnp.concatenate([c * side[i : i + 1] for i in range(plan.rows)], axis=0)
        ca = c.astype(F32) * above_ref[w : w + 1, :]
        down = jnp.concatenate([colsel * ca[n : n + 1] for n in range(states)], axis=0).astype(BF16)
        y = mm(edge_ref[w], left) + mm(top_ref[w], down)
        y = jnp.concatenate([y[:, :LANES], y[:, LANES:]], axis=0).T
        out_ref[t, s * plan.half : (s + 1) * plan.half, :] = y[: plan.half].astype(BF16)


def call(kernel, name, args, outs, scratch=(), specs=()):
    specs = list(specs) + [full(x.shape) for x in args[len(specs) :]]
    return pl.pallas_call(
        kernel,
        grid=(1,),
        in_specs=specs,
        out_specs=[full(s) for s, _ in outs],
        out_shape=[jax.ShapeDtypeStruct(s, d) for s, d in outs],
        scratch_shapes=[x if not isinstance(x, tuple) else pltpu.VMEM(*x) for x in scratch],
        compiler_params=pltpu.CompilerParams(vmem_limit_bytes=24 * 2**20),
        name=name,
    )(*args)


def scan_calls(plan, consts, row_axis, col_axis, pay, rate_x, rate_y):
    work, cp, wide = plan.work, plan.col_pad, 2 * LANES
    rp = consts["side1"].shape[0]
    rate_x, rate_y = in_hbm(rate_x), in_hbm(rate_y)
    edges, upto, last = call(
        functools.partial(edges_kernel, plan, col_axis),
        "edges",
        [rate_x, pay],
        [((work, HALF, plan.edge), BF16), ((work, plan.edge), F32), ((plan.slots, HALF, plan.edge), BF16)],
        [
            pltpu.SMEM(rate_x.shape, F32),
            ((work, wide), F32),
            ((work, wide), F32),
            ((work, plan.edge), F32),
            pltpu.SemaphoreType.DMA,
        ],
        [HBM],
    )
    if plan.parts > 1:
        hops = [(k, k + plan.devices) for k in range(plan.devices)]
        entry = lax.ppermute(last, col_axis, hops)
    else:
        entry = jnp.zeros_like(last)
    names = ("to1", "to2", "from1", "from2", "side1", "side2", "sidemask", "down1", "down2", "downmask", "pick")
    side, above, bottom, tops = call(
        functools.partial(maps_kernel, plan, col_axis),
        "maps",
        [rate_x, rate_y, pay] + [consts[k] for k in names],
        [
            ((work, rp, wide), BF16),
            ((work, wide), F32),
            ((work, rp, LANES), BF16),
            ((work, HALF, plan.top), F32),
        ],
        [((work, wide), F32)] + [((work * rp, wide), F32)] * 2 + [((work * cp, wide), F32)] * 2,
        [SMEM, SMEM],
    )
    edges, tops = call(
        functools.partial(join_kernel, plan),
        "join",
        [edges, upto, entry, bottom, tops],
        [((work, HALF, plan.edge), BF16), ((work, HALF, plan.top), BF16)],
    )
    count = lax.axis_size(row_axis)
    chain = [(r, r + 1) for r in range(count - 1)]
    entry = lax.ppermute(tops, row_axis, chain)
    if count > 2:
        keep = jnp.dot(above.astype(BF16), consts["pick"], preferred_element_type=F32)[:, None, :]
        for _ in range(count - 2):
            entry = lax.ppermute(
                (tops.astype(F32) + keep * entry.astype(F32)).astype(BF16), row_axis, chain
            )
    return call(
        functools.partial(cells_kernel, plan),
        "cells",
        [pay, edges, entry, side, above],
        [((plan.devices, plan.slots * plan.half, LANES), BF16)],
    )[0]


def finish_kernel(plan, y_ref, own_ref, gate_ref, gain_ref, w_ref, out_ref, full_ref):
    half, cells = plan.half, plan.cells
    slot, slots = plan.slot, plan.slots
    per = LANES // slot
    lane = lax.broadcasted_iota(jnp.int32, (half, LANES), 1)
    for block in range(plan.width // LANES):
        for k, (lo, hi) in enumerate(((0, half), (half, cells))):
            joined = None
            for d in range(per):
                at = block * per + d
                part = y_ref[at // slots, at % slots * half : (at % slots + 1) * half, :].astype(F32)
                shift = (d * slot - k * HALF) % LANES
                if shift:
                    part = pltpu.roll(part, shift, 1)
                joined = part if joined is None else jnp.where(lane < d * slot, joined, part)
            full_ref[lo:hi, block * LANES : (block + 1) * LANES] = joined[: hi - lo]
    y = full_ref[...] + own_ref[...].astype(F32)
    y = y.astype(BF16).astype(F32)
    gated = y * gate_ref[...].astype(F32)
    scale = lax.rsqrt(jnp.mean(gated * gated, axis=-1, keepdims=True) + norm_eps)
    normed = (gated * scale * gain_ref[...]).astype(BF16)
    full_ref[...] = mm(normed, w_ref[...])
    for i in range(plan.rows):
        out_ref[i] = full_ref[i * plan.col_pad : i * plan.col_pad + plan.cols, :].astype(BF16)


def finish(plan, y, own, gate, gain, w_out):
    args = (y, own, gate, gain, w_out)
    shape = (plan.rows, plan.cols, w_out.shape[1])
    assert w_out.shape[1] == plan.width
    return call(
        functools.partial(finish_kernel, plan), "finish", args, [(shape, BF16)], [((plan.cells, plan.width), F32)]
    )[0]


def per_device(slide, tissue, w_in, w_bcd, dt_bias, rate_x, rate_y, d_skip, norm_gain, w_out):
    rows, cols, model_width = slide.shape
    width = w_out.shape[0]
    heads = dt_bias.shape[0]
    states = (w_bcd.shape[1] - heads) // 2
    plan = Plan(rows, cols, states, heads, width, lax.axis_size("col"))
    consts = plan.constants()
    v, pay, table, x = project(plan, consts, slide, w_in, w_bcd, tissue, dt_bias)
    groups = plan.segments()
    pay = lax.all_to_all(pay, "col", 0, 0, tiled=True, axis_index_groups=groups)
    gain = norm_gain.reshape(1, width)
    own, gate, gain = home(plan, consts, v, table, x, w_in, tissue, gain, rate_x, rate_y, d_skip)
    pay, own, gate, gain = lax.optimization_barrier((pay, own, gate, gain))
    y = scan_calls(plan, consts, "row", "col", pay, rate_x, rate_y)
    y = lax.all_to_all(y, "col", 0, 0, tiled=True, axis_index_groups=groups)
    return finish(plan, y, own, gate, gain, w_out)


def solution(mesh):
    placed = (
        P(("slides", "row"), "col", None),
        P(("slides", "row"), "col"),
        P(),
        P(),
        P(),
        P(),
        P(),
        P(),
        P(),
        P(),
    )
    return jax.shard_map(
        per_device,
        mesh=mesh,
        in_specs=placed,
        out_specs=P(("slides", "row"), "col", None),
        check_vma=False,
    )
```

```python
import functools

import jax
import jax.numpy as jnp
import numpy as np
from jax import lax
from jax.experimental import pallas as pl
from jax.experimental.pallas import tpu as pltpu
from jax.sharding import PartitionSpec as P

norm_eps = 1e-05
LANES = 128
HALF = LANES // 2
F32 = jnp.float32
BF16 = jnp.bfloat16


def round_up(value, step):
    return -(-value // step) * step


def in_hbm(x):
    return pltpu.with_memory_space_constraint(x, pltpu.HBM)


def mm(a, b):
    return jnp.dot(a, b, preferred_element_type=F32)


def nt_dot(a, b):
    return lax.dot_general(a, b, (((1,), (1,)), ((), ())), preferred_element_type=F32)


def tn_dot(a, b):
    return lax.dot_general(a, b, (((0,), (0,)), ((), ())), preferred_element_type=F32)


class Plan:
    def __init__(self, rows, cols, states, heads, width, devices):
        self.rows, self.cols, self.states, self.heads = rows, cols, states, heads
        self.width = width
        self.parts = 2 if devices % 2 == 0 and devices > 2 else 1
        self.devices = devices // self.parts
        self.group = width // self.devices
        self.slot = min(self.group, HALF)
        self.slots = self.group // self.slot
        self.work = self.slots * self.devices
        self.head_width = width // heads
        self.col_pad = round_up(cols, 8)
        self.upper = -(-rows // 2)
        self.half = round_up(self.upper * self.col_pad, 8)
        self.cells = rows * self.col_pad
        self.edge = rows * states
        self.top = states * self.col_pad
        self.bc = 2 * states
        self.at_bc = self.slots * self.half
        self.at_dt = self.at_bc + 2 * self.bc
        self.at_rate = self.at_dt + 2 * self.slots
        self.message = round_up(self.at_rate + 1, 8)
        self.tail = self.edge % LANES
        self.solid = self.edge // LANES
        self.share = LANES // self.tail if self.tail else 1
        self.packed = self.slots * self.solid + (-(-self.slots // self.share) if self.tail else 0)
        assert self.head_width % self.slot == 0 and self.group % self.slot == 0
        assert LANES % self.head_width == 0 and self.half <= LANES
        assert self.cells - self.half <= self.half
        assert states % 16 == 0 and heads % 8 == 0

    def segments(self):
        return [list(range(p * self.devices, (p + 1) * self.devices)) for p in range(self.parts)]

    def lanes(self):
        at = np.arange(2 * LANES)
        cell = np.where(at < LANES, at, at - LANES + self.half)
        live = np.where(at < LANES, at < self.half, cell < self.cells)
        i, j = cell // self.col_pad, cell % self.col_pad
        return i, j, live & (j < self.cols)

    def constants(self):
        i, j, real = self.lanes()
        both = real[:, None] & real[None]
        cell = np.arange(self.cells)
        ci, cj = cell // self.col_pad, cell % self.col_pad
        creal = cj < self.cols
        le = np.arange(round_up(self.rows, 8))
        lj = np.arange(self.col_pad)
        out = {}
        out["to1"] = (j[:, None] <= j[None]) & both
        out["to2"] = (j[:, None] == j[None]) & (i[:, None] <= i[None]) & both
        out["from1"] = (i[:, None] == i[None]) & (j[:, None] > j[None]) & both
        out["from2"] = (i[:, None] > i[None]) & both
        out["side1"] = (i[None] == le[:, None]) & real[None]
        out["side2"] = (i[None] > le[:, None]) & real[None]
        out["sidemask"] = (i[None] >= le[:, None]) & (le < self.rows)[:, None] & real[None]
        out["down1"] = (j[None] <= lj[:, None]) & real[None]
        out["down2"] = (j[None] == lj[:, None]) & real[None]
        out["downmask"] = (j[None] <= lj[:, None]) & (lj < self.cols)[:, None] & real[None]
        out["pick"] = (
            (i == self.rows - 1)[:, None] & real[:, None] & (j[:, None] == np.tile(lj, self.states)[None])
        )
        cboth = creal[:, None] & real[None]
        out["own1"] = (j[None] <= cj[:, None]) & cboth
        out["own2"] = (j[None] == cj[:, None]) & (i[None] <= ci[:, None]) & cboth
        out["ownmask"] = (i[None] <= ci[:, None]) & (j[None] <= cj[:, None]) & cboth
        out["lanei"] = (np.arange(self.rows)[:, None] == i[None]) & real[None]
        out["lanej"] = (np.arange(self.cols)[:, None] == j[None]) & real[None]
        return {k: in_hbm(jnp.asarray(x.astype(np.float32), BF16)) for k, x in out.items()}


def full(shape):
    return pl.BlockSpec(shape, lambda *_: (0,) * len(shape))


HBM = pl.BlockSpec(memory_space=pltpu.HBM)
SMEM = pl.BlockSpec(memory_space=pltpu.SMEM)


def cell_mask_of(plan, t_ref):
    t = t_ref[...].astype(F32).astype(BF16)
    cell = lax.broadcasted_iota(jnp.int32, (plan.cells, plan.cols), 0)
    col = lax.broadcasted_iota(jnp.int32, (plan.cells, plan.cols), 1)
    pick = (lax.rem(cell, plan.col_pad) == col).astype(F32).astype(BF16)
    cell = lax.broadcasted_iota(jnp.int32, (plan.cells, plan.rows), 0)
    row = lax.broadcasted_iota(jnp.int32, (plan.cells, plan.rows), 1)
    return jnp.sum(jnp.where(lax.div(cell, plan.col_pad) == row, mm(pick, t), 0.0), axis=1, keepdims=True)


def rate_row(heads_of, rx_ref, ry_ref):
    at = lax.broadcasted_iota(jnp.int32, (1, LANES), 1)
    rate = jnp.zeros((1, LANES), F32)
    part = jnp.zeros((1, LANES), jnp.int32)
    for s, head in enumerate(heads_of):
        for k, ref in enumerate((rx_ref, ry_ref)):
            first = 8 * s + 3 * k
            here = (at >= first) & (at < first + 3)
            rate = jnp.where(here, ref[head], rate)
            part = jnp.where(here, at - first, part)
    high = rate.astype(BF16).astype(F32)
    middle = (rate - high).astype(BF16).astype(F32)
    low = rate - high - middle
    return jnp.where(part == 0, high, jnp.where(part == 1, middle, low))


def project_kernel(
    plan, chunks, bias_hbm, rx_hbm, ry_hbm, x_hbm, w_hbm, wt_hbm, t_hbm, lanei_hbm, lanej_hbm,
    v_ref, pay_hbm, rows_ref, flat_ref,
    bias_ref, rx_ref, ry_ref, x_ref, w_ref, wt_ref, t_ref, lanei_ref, lanej_ref, pay_ref, wide, sems, w_sems, out_sems,
):
    group, states, cells, heads = plan.group, plan.states, plan.cells, plan.heads
    half, rest = plan.half, plan.cells - plan.half
    tile = plan.width // chunks
    pairs = (
        (x_hbm, x_ref), (t_hbm, t_ref), (wt_hbm, wt_ref), (lanei_hbm, lanei_ref), (lanej_hbm, lanej_ref),
        (bias_hbm, bias_ref), (rx_hbm, rx_ref), (ry_hbm, ry_ref),
    )
    loads = [pltpu.make_async_copy(a, b, sems.at[k]) for k, (a, b) in enumerate(pairs)]
    copies = [
        pltpu.make_async_copy(w_hbm.at[:, k * tile : (k + 1) * tile], w_ref.at[k], w_sems.at[k])
        for k in range(chunks)
    ]
    for copy in loads + copies:
        copy.start()
    wide[...] = jnp.zeros_like(wide)
    v_ref[half:LANES, :] = jnp.zeros((LANES - half, plan.width), BF16)
    v_ref[LANES + rest :, :] = jnp.zeros((LANES - rest, plan.width), BF16)

    loads[0].wait()
    for i in range(plan.rows):
        wide[i * plan.col_pad : i * plan.col_pad + plan.cols, :] = x_ref[i].astype(F32)
    x = wide[...].astype(BF16)
    flat_ref[...] = x
    for copy in loads[1:]:
        copy.wait()
    keep = cell_mask_of(plan, t_ref)
    t = t_ref[...].astype(F32).astype(BF16)
    m = jnp.sum(mm(t, lanei_ref[...]) * lanej_ref[...].astype(F32), axis=0, keepdims=True)
    table = nt_dot(wt_ref[...], x)
    ext = jnp.concatenate([table, jnp.zeros((table.shape[0], 2 * LANES - cells), F32)], axis=1)
    lane = lax.broadcasted_iota(jnp.int32, (table.shape[0], LANES), 1)
    lo, hi = ext[:, :LANES], ext[:, LANES:]
    shift = half % LANES
    if shift:
        moved = jnp.where(
            lane < LANES - shift, pltpu.roll(lo, LANES - shift, 1), pltpu.roll(hi, LANES - shift, 1)
        )
    else:
        moved = hi
    table = jnp.concatenate([jnp.where(lane < half, lo, 0.0), jnp.where(lane < rest, moved, 0.0)], axis=1)
    z = table[2 * states :]
    at = lax.broadcasted_iota(jnp.int32, z.shape, 0)
    for h in range(heads):
        z = jnp.where(at == h, z + bias_ref[h], z)
    soft = m * (jnp.maximum(z, 0.0) + jnp.log1p(jnp.exp(-jnp.abs(z))))
    table = jnp.concatenate([table[: 2 * states], soft], axis=0).astype(BF16)
    rows_ref[...] = table.astype(F32)
    bc = table[: 2 * states]
    steps = rows_ref[2 * states :, :]

    lane = lax.broadcasted_iota(jnp.int32, (half, LANES), 1)
    sent = []
    for chunk in range(chunks):
        copies[chunk].wait()
        v = mm(flat_ref[...], w_ref[chunk]).astype(BF16).astype(F32) * keep
        low = v.astype(BF16)
        v_ref[0:half, chunk * tile : (chunk + 1) * tile] = low[:half]
        v_ref[LANES : LANES + rest, chunk * tile : (chunk + 1) * tile] = low[half:]
        per = tile // group
        for k in range(per):
            dest = chunk * per + k
            dts, heads_of = [], []
            for s in range(plan.slots):
                offset = k * group + s * plan.slot
                base = offset // LANES * LANES
                at = offset % LANES
                first = v[:half, base : base + LANES]
                last = v[half:, base : base + LANES]
                if rest < half:
                    last = jnp.concatenate([last, jnp.zeros((half - rest, LANES), F32)], axis=0)
                if at:
                    first = pltpu.roll(first, LANES - at, 1)
                if at != HALF:
                    last = pltpu.roll(last, (HALF - at) % LANES, 1)
                both = jnp.where(lane < HALF, first, last)
                if plan.slot < HALF:
                    both = jnp.where(lane % HALF < plan.slot, both, 0.0)
                pay_ref[dest, s * half : (s + 1) * half, :] = both.astype(BF16)
                head = (chunk * tile + offset) // plan.head_width
                heads_of.append(head)
                dts += [steps[head : head + 1, :LANES], steps[head : head + 1, LANES:]]
            dts.append(rate_row(heads_of, rx_ref, ry_ref))
            pay_ref[dest, plan.at_bc : plan.at_bc + plan.bc, :] = bc[:, :LANES]
            pay_ref[dest, plan.at_bc + plan.bc : plan.at_dt, :] = bc[:, LANES:]
            spare = plan.message - plan.at_dt - len(dts)
            dts += [jnp.zeros((spare, LANES), F32)] if spare else []
            pay_ref[dest, plan.at_dt : plan.message, :] = jnp.concatenate(dts, axis=0).astype(BF16)
        at = slice(chunk * per, (chunk + 1) * per)
        sent.append(pltpu.make_async_copy(pay_ref.at[at], pay_hbm.at[at], out_sems.at[chunk]))
        sent[-1].start()
    for copy in sent:
        copy.wait()


def project(plan, consts, slide, w_in, w_bcd, tissue, dt_bias, rate_x, rate_y):
    chunks = 4
    tile = plan.width // chunks
    depth = slide.shape[2]
    args = [dt_bias, rate_x, rate_y, slide, w_in, w_bcd.T, tissue.T, consts["lanei"], consts["lanej"]]
    count = 2 * plan.states + plan.heads
    assert plan.width % chunks == 0 and tile % plan.group == 0 and tile % LANES == 0
    message = (plan.devices, plan.message, LANES)
    outs = [((2 * LANES, plan.width), BF16), (message, BF16), ((count, 2 * LANES), F32), ((plan.cells, depth), BF16)]
    specs = [full(s) for s, _ in outs]
    specs[1] = HBM
    return pl.pallas_call(
        functools.partial(project_kernel, plan, chunks),
        grid=(1,),
        in_specs=[HBM] * len(args),
        out_specs=specs,
        out_shape=[jax.ShapeDtypeStruct(s, d) for s, d in outs],
        scratch_shapes=[
            pltpu.SMEM(dt_bias.shape, F32),
            pltpu.SMEM(rate_x.shape, F32),
            pltpu.SMEM(rate_y.shape, F32),
            pltpu.VMEM(slide.shape, BF16),
            pltpu.VMEM((chunks, depth, tile), BF16),
        ]
        + [pltpu.VMEM(x.shape, x.dtype) for x in args[5:]]
        + [
            pltpu.VMEM(message, BF16),
            pltpu.VMEM((plan.cells, depth), F32),
            pltpu.SemaphoreType.DMA((8,)),
            pltpu.SemaphoreType.DMA((chunks,)),
            pltpu.SemaphoreType.DMA((chunks,)),
        ],
        compiler_params=pltpu.CompilerParams(vmem_limit_bytes=24 * 2**20),
        name="project",
    )(*[in_hbm(x) for x in args])


def home_kernel(
    plan, rx_ref, ry_ref, skip_ref, w_hbm, v_ref, rows_ref, flat_ref, t_ref, gain_ref,
    own1_ref, own2_ref, from1_ref, from2_ref, mask_ref, out_ref, gate_hbm, gain_out, pair, w_ref, gate_ref, sem, gate_sem,
):
    states, cells, half = plan.states, plan.cells, plan.half
    copy = pltpu.make_async_copy(w_hbm.at[:, plan.width :], w_ref, sem)
    copy.start()
    gain_out[...] = gain_ref[...]
    b = rows_ref[0:states, :].astype(BF16)
    c = rows_ref[states : 2 * states, :].astype(BF16)
    pairs = tn_dot(c, b)
    pairs = jnp.concatenate([pairs[:half], pairs[LANES : LANES + cells - half]], axis=0)
    pair[...] = pairs * mask_ref[...].astype(F32)
    lane = lax.broadcasted_iota(jnp.int32, (cells, LANES), 1)
    per = LANES // plan.head_width
    for block in range(plan.width // LANES):
        v = v_ref[:, block * LANES : (block + 1) * LANES]
        vc = jnp.concatenate([v[:half], v[LANES : LANES + cells - half]], axis=0).astype(F32)
        total = None
        for k in range(per):
            h = block * per + k
            dt = rows_ref[2 * states + h : 2 * states + h + 1, :]
            low = dt.astype(BF16)
            x = mm(own1_ref[...] * low, from1_ref[...])
            y = mm(own2_ref[...] * low, from2_ref[...])
            weight = jnp.exp(-(rx_ref[h] * x + ry_ref[h] * y)) * pair[...] * dt
            part = mm(weight.astype(BF16), v) + skip_ref[h] * vc
            total = part if total is None else jnp.where(lane < k * plan.head_width, total, part)
        out_ref[:, block * LANES : (block + 1) * LANES] = total.astype(BF16)
    keep = cell_mask_of(plan, t_ref)
    copy.wait()
    tile = 2 * LANES
    for block in range(plan.width // tile):
        at = slice(block * tile, (block + 1) * tile)
        z = mm(flat_ref[...], w_ref[:, at]).astype(BF16).astype(F32)
        gate_ref[:, at] = (z * (1.0 / (1.0 + jnp.exp(-z))) * keep).astype(BF16)
    copy = pltpu.make_async_copy(gate_ref, gate_hbm, gate_sem)
    copy.start()
    copy.wait()


def home(plan, consts, v, rows, flat, w_in, tissue, gain, rate_x, rate_y, d_skip):
    args = [in_hbm(w_in), v, rows, flat, in_hbm(tissue.T), in_hbm(gain)]
    args += [consts[k] for k in ("own1", "own2", "from1", "from2", "ownmask")]
    outs = [((plan.cells, plan.width), BF16), ((plan.cells, plan.width), BF16), (gain.shape, F32)]
    return pl.pallas_call(
        functools.partial(home_kernel, plan),
        grid=(1,),
        in_specs=[SMEM, SMEM, SMEM, HBM] + [full(x.shape) for x in args[1:]],
        out_specs=[full(outs[0][0]), HBM, full(outs[2][0])],
        out_shape=[jax.ShapeDtypeStruct(s, d) for s, d in outs],
        scratch_shapes=[
            pltpu.VMEM((plan.cells, 2 * LANES), F32),
            pltpu.VMEM((w_in.shape[0], w_in.shape[1] - plan.width), BF16),
            pltpu.VMEM((plan.cells, plan.width), BF16),
            pltpu.SemaphoreType.DMA,
            pltpu.SemaphoreType.DMA,
        ],
        compiler_params=pltpu.CompilerParams(vmem_limit_bytes=24 * 2**20),
        name="home",
    )(in_hbm(rate_x), in_hbm(rate_y), in_hbm(d_skip), *args)


def ones(mask):
    return jnp.where(mask, 1.0, 0.0).astype(BF16)


def places(plan, shape, axis):
    at = lax.broadcasted_iota(jnp.int32, shape, axis)
    late = at >= LANES
    at = jnp.where(late, at - LANES, at)
    i = lax.div(at, plan.col_pad)
    j = at - i * plan.col_pad
    real = (at < jnp.where(late, plan.cells - plan.half, plan.half)) & (j < plan.cols)
    return jnp.where(late, i + plan.upper, i), j, real


def wide_rows(pay_ref, t, at, count, gap):
    return jnp.concatenate([pay_ref[t, at : at + count, :], pay_ref[t, at + gap : at + gap + count, :]], axis=1)


def turned(plan, pay_ref, t, s):
    v = pay_ref[t, s * plan.half : (s + 1) * plan.half, :].astype(F32)
    if plan.half < LANES:
        v = jnp.concatenate([v, jnp.zeros((LANES - plan.half, LANES), F32)], axis=0)
    v = v.T
    return jnp.concatenate([v[:HALF], v[HALF:]], axis=1).astype(BF16)


def load_steps(plan, pay_ref, dts):
    for t in range(plan.devices):
        rows = pay_ref[t, plan.at_dt : plan.message, :].astype(F32)
        for s in range(plan.slots):
            w = s * plan.devices + t
            dts[w : w + 1, :LANES] = rows[2 * s : 2 * s + 1]
            dts[w : w + 1, LANES:] = rows[2 * s + 1 : 2 * s + 2]


def rates_of(plan, pay_ref, kind):
    row = pay_ref[0, plan.at_dt : plan.message, :].astype(F32)[plan.at_rate - plan.at_dt : plan.at_rate - plan.at_dt + 1]
    at = lax.broadcasted_iota(jnp.int32, (1, LANES), 1)
    first = [8 * s + 3 * kind for s in range(plan.slots)]
    return [jnp.sum(jnp.where((at >= f) & (at < f + 3), row, 0.0), axis=1, keepdims=True) for f in first]


def slot_rates(plan, pay_ref, kind):
    return jnp.concatenate(
        [jnp.broadcast_to(r, (plan.devices, 1)) for r in rates_of(plan, pay_ref, kind)], axis=0
    )


def pack_edges(plan, out_ref, held):
    for s in range(plan.slots):
        for k in range(plan.solid):
            out_ref[s * plan.solid + k] = held[s][:, k * LANES : (k + 1) * LANES].astype(BF16)
    if plan.tail:
        first = plan.slots * plan.solid
        for k in range(plan.packed - first):
            parts = [x[:, plan.solid * LANES :] for x in held[k * plan.share : (k + 1) * plan.share]]
            spare = LANES - plan.tail * len(parts)
            parts += [jnp.zeros((HALF, spare), F32)] if spare else []
            out_ref[first + k] = jnp.concatenate(parts, axis=1).astype(BF16)


def unpack_edges(plan, ref, s):
    parts = [ref[s * plan.solid + k].astype(F32) for k in range(plan.solid)]
    if plan.tail:
        last = ref[plan.slots * plan.solid + s // plan.share].astype(F32)
        at = s % plan.share * plan.tail
        parts.append(last[:, at : at + plan.tail])
    return jnp.concatenate(parts, axis=1)


def edges_kernel(plan, pay_ref, edge_ref, upto_ref, last_ref, dts, inner, kept):
    states, tiles, wide = plan.states, plan.devices, 2 * LANES
    load_steps(plan, pay_ref, dts)
    i, j, real = places(plan, (wide, wide), 0)
    ti, tj, treal = places(plan, (wide, wide), 1)
    from1 = ones((i == ti) & (j > tj) & real & treal)
    edge_row = lax.div(lax.broadcasted_iota(jnp.int32, (wide, plan.edge), 1), states)
    i, _, real = places(plan, (wide, plan.edge), 0)
    keep = ones((i == edge_row) & real)
    ti, _, treal = places(plan, (plan.rows, wide), 1)
    rowsel = ones((ti == lax.broadcasted_iota(jnp.int32, (plan.rows, wide), 0)) & treal)
    dt = dts[...]
    low = dt.astype(BF16)
    rate = slot_rates(plan, pay_ref, 0)
    inner[...] = jnp.exp(-rate * mm(low, from1)) * dt
    kept[...] = jnp.exp(-rate * mm(low, keep))
    ends = []
    for s in range(plan.slots):
        held = jnp.zeros((HALF, plan.edge), F32)
        product = jnp.ones((1, plan.edge), F32)
        for t in range(tiles):
            w = s * tiles + t
            b = wide_rows(pay_ref, t, plan.at_bc, states, plan.bc).astype(F32)
            bd = (b * inner[w : w + 1, :]).astype(BF16)
            left = jnp.concatenate([bd * rowsel[i : i + 1] for i in range(plan.rows)], axis=0)
            edge_ref[w] = held.astype(BF16)
            upto_ref[w : w + 1, :] = product
            now = kept[w : w + 1, :]
            held = held * now + nt_dot(turned(plan, pay_ref, t, s), left)
            product = product * now
        ends.append(held)
    pack_edges(plan, last_ref, ends)


def maps_kernel(
    plan, pay_ref, edge_ref, to1_ref, to2_ref, from1_ref, from2_ref, side1_ref, side2_ref,
    sidemask_ref, down1_ref, down2_ref, downmask_ref, pick_ref,
    side_ref, above_ref, passed_ref, top_ref, dts, s1, s2, d1, d2,
):
    states, tiles, cp, work = plan.states, plan.devices, plan.col_pad, plan.work
    rp = side1_ref.shape[0]
    load_steps(plan, pay_ref, dts)
    low = dts[...].astype(BF16)
    above_ref[...] = jnp.exp(-slot_rates(plan, pay_ref, 1) * mm(low, to2_ref[...]))
    rates_x, rates_y = rates_of(plan, pay_ref, 0), rates_of(plan, pay_ref, 1)
    for w in range(work):
        rf = dts[w : w + 1, :]
        s1[w * rp : (w + 1) * rp, :] = side1_ref[...].astype(F32) * rf
        s2[w * rp : (w + 1) * rp, :] = side2_ref[...].astype(F32) * rf
        d1[w * cp : (w + 1) * cp, :] = down1_ref[...].astype(F32) * rf
        d2[w * cp : (w + 1) * cp, :] = down2_ref[...].astype(F32) * rf
    mask = sidemask_ref[...].astype(F32)
    x, y = mm(s1[...].astype(BF16), to1_ref[...]), mm(s2[...].astype(BF16), to2_ref[...])
    shape = (states, plan.top)
    n = lax.broadcasted_iota(jnp.int32, shape, 0)
    diag = ones(n == lax.div(lax.broadcasted_iota(jnp.int32, shape, 1), cp))
    for w in range(work):
        s = w // tiles
        at = slice(w * rp, (w + 1) * rp)
        side = (jnp.exp(-(rates_x[s] * x[at] + rates_y[s] * y[at])) * mask).astype(BF16)
        side_ref[w] = side
        bottom = mm(side, pick_ref[...]).astype(BF16)
        passed_ref[w] = jnp.concatenate([diag * bottom[i : i + 1] for i in range(plan.rows)], axis=0)
    x, y = mm(d1[...].astype(BF16), from1_ref[...]), mm(d2[...].astype(BF16), from2_ref[...])
    mask = downmask_ref[...].astype(F32)
    for w in range(work):
        s, t = w // tiles, w % tiles
        at = slice(w * cp, (w + 1) * cp)
        fall = jnp.exp(-(rates_x[s] * x[at] + rates_y[s] * y[at])) * mask * dts[w : w + 1, :]
        b = wide_rows(pay_ref, t, plan.at_bc, states, plan.bc).astype(F32)
        falls = jnp.concatenate([fall * b[n : n + 1] for n in range(states)], axis=0).astype(BF16)
        top_ref[w] = nt_dot(turned(plan, pay_ref, t, s), falls) + mm(edge_ref[w], passed_ref[w])


def join_kernel(plan, upto_ref, entry_ref, passed_ref, top_ref, out_ref):
    for s in range(plan.slots):
        entry = unpack_edges(plan, entry_ref, s)
        for t in range(plan.devices):
            w = s * plan.devices + t
            late = (entry * upto_ref[w : w + 1, :]).astype(BF16)
            out_ref[w] = (top_ref[w] + mm(late, passed_ref[w])).astype(BF16)


def sides_kernel(plan, pay_ref, edge_ref, upto_ref, entry_ref, side_ref, above_ref, y_ref, down_ref):
    states, tiles = plan.states, plan.devices
    shape = (plan.col_pad, 2 * LANES)
    _, tj, treal = places(plan, shape, 1)
    colsel = jnp.where((tj == lax.broadcasted_iota(jnp.int32, shape, 0)) & treal, 1.0, 0.0)
    for s in range(plan.slots):
        entry = unpack_edges(plan, entry_ref, s)
        for t in range(tiles):
            w = s * tiles + t
            c = wide_rows(pay_ref, t, plan.at_bc + states, states, plan.bc)
            side = side_ref[w]
            left = jnp.concatenate([c * side[i : i + 1] for i in range(plan.rows)], axis=0)
            whole = (edge_ref[w].astype(F32) + entry * upto_ref[w : w + 1, :]).astype(BF16)
            y_ref[w] = mm(whole, left)
            ca = c.astype(F32) * above_ref[w : w + 1, :]
            down_ref[w] = jnp.concatenate([colsel * ca[n : n + 1] for n in range(states)], axis=0).astype(BF16)


def cells_kernel(plan, y_ref, down_ref, top_ref, out_ref):
    for w in range(plan.work):
        t, s = w % plan.devices, w // plan.devices
        y = y_ref[w] + mm(top_ref[w], down_ref[w])
        y = jnp.concatenate([y[:, :LANES], y[:, LANES:]], axis=0).T
        out_ref[t, s * plan.half : (s + 1) * plan.half, :] = y[: plan.half].astype(BF16)


def call(kernel, name, args, outs, scratch=(), out_specs=None):
    return pl.pallas_call(
        kernel,
        grid=(1,),
        in_specs=[full(x.shape) for x in args],
        out_specs=out_specs or [full(s) for s, _ in outs],
        out_shape=[jax.ShapeDtypeStruct(s, d) for s, d in outs],
        scratch_shapes=[x if not isinstance(x, tuple) else pltpu.VMEM(*x) for x in scratch],
        compiler_params=pltpu.CompilerParams(vmem_limit_bytes=24 * 2**20),
        name=name,
    )(*args)


def scan_calls(plan, consts, row_axis, col_axis, pay):
    work, cp, wide = plan.work, plan.col_pad, 2 * LANES
    rp = consts["side1"].shape[0]
    edges, upto, last = call(
        functools.partial(edges_kernel, plan),
        "edges",
        [pay],
        [((work, HALF, plan.edge), BF16), ((work, plan.edge), F32), ((plan.packed, HALF, LANES), BF16)],
        [((work, wide), F32), ((work, wide), F32), ((work, plan.edge), F32)],
    )
    if plan.parts > 1:
        hops = [(k, k + plan.devices) for k in range(plan.devices)]
        entry = lax.ppermute(last, col_axis, hops)
    else:
        entry = jnp.zeros_like(last)
    names = ("to1", "to2", "from1", "from2", "side1", "side2", "sidemask", "down1", "down2", "downmask", "pick")
    side, above, passed, tops = call(
        functools.partial(maps_kernel, plan),
        "maps",
        [pay, edges] + [consts[k] for k in names],
        [
            ((work, rp, wide), BF16),
            ((work, wide), F32),
            ((work, plan.edge, plan.top), BF16),
            ((work, HALF, plan.top), F32),
        ],
        [((work, wide), F32)] + [((work * rp, wide), F32)] * 2 + [((work * cp, wide), F32)] * 2,
    )
    edge_entry = entry
    tops = call(
        functools.partial(join_kernel, plan),
        "join",
        [upto, entry, passed, tops],
        [((work, HALF, plan.top), BF16)],
    )[0]
    count = lax.axis_size(row_axis)
    chain = [(r, r + 1) for r in range(count - 1)]
    entry = lax.ppermute(tops, row_axis, chain)
    if count > 2:
        keep = jnp.dot(above.astype(BF16), consts["pick"], preferred_element_type=F32)[:, None, :]
        for _ in range(count - 2):
            entry = lax.ppermute(
                (tops.astype(F32) + keep * entry.astype(F32)).astype(BF16), row_axis, chain
            )
    y, down = call(
        functools.partial(sides_kernel, plan),
        "sides",
        [pay, edges, upto, edge_entry, side, above],
        [((work, HALF, wide), F32), ((work, plan.top, wide), BF16)],
    )
    return call(
        functools.partial(cells_kernel, plan),
        "cells",
        [y, down, entry],
        [((plan.devices, plan.slots * plan.half, LANES), BF16)],
    )[0]


def finish_kernel(plan, y_ref, own_ref, gate_ref, gain_ref, w_ref, out_hbm, full_ref, out_ref, sems):
    half, cells = plan.half, plan.cells
    slot, slots = plan.slot, plan.slots
    per = LANES // slot
    lane = lax.broadcasted_iota(jnp.int32, (half, LANES), 1)
    copies = []
    for k, (lo, hi) in enumerate(((0, half), (half, cells))):
        for block in range(plan.width // LANES):
            joined = None
            for d in range(per):
                at = block * per + d
                part = y_ref[at // slots, at % slots * half : (at % slots + 1) * half, :].astype(F32)
                shift = (d * slot - k * HALF) % LANES
                if shift:
                    part = pltpu.roll(part, shift, 1)
                joined = part if joined is None else jnp.where(lane < d * slot, joined, part)
            full_ref[lo:hi, block * LANES : (block + 1) * LANES] = joined[: hi - lo]
        y = full_ref[lo:hi, :] + own_ref[lo:hi, :].astype(F32)
        y = y.astype(BF16).astype(F32)
        gated = y * gate_ref[lo:hi, :].astype(F32)
        scale = lax.rsqrt(jnp.mean(gated * gated, axis=-1, keepdims=True) + norm_eps)
        normed = (gated * scale * gain_ref[...]).astype(BF16)
        full_ref[lo:hi, :] = mm(normed, w_ref[...])
        first, last = lo // plan.col_pad, hi // plan.col_pad
        for i in range(first, last):
            out_ref[i] = full_ref[i * plan.col_pad : i * plan.col_pad + plan.cols, :].astype(BF16)
        copies.append(pltpu.make_async_copy(out_ref.at[first:last], out_hbm.at[first:last], sems.at[k]))
        copies[-1].start()
    for copy in copies:
        copy.wait()


def finish(plan, y, own, gate, gain, w_out):
    args = (y, own, gate, gain, w_out)
    shape = (plan.rows, plan.cols, w_out.shape[1])
    assert w_out.shape[1] == plan.width
    return call(
        functools.partial(finish_kernel, plan),
        "finish",
        args,
        [(shape, BF16)],
        [((plan.cells, plan.width), F32), (shape, BF16), pltpu.SemaphoreType.DMA((2,))],
        [HBM],
    )[0]


def per_device(slide, tissue, w_in, w_bcd, dt_bias, rate_x, rate_y, d_skip, norm_gain, w_out):
    rows, cols, model_width = slide.shape
    width = w_out.shape[0]
    heads = dt_bias.shape[0]
    states = (w_bcd.shape[1] - heads) // 2
    plan = Plan(rows, cols, states, heads, width, lax.axis_size("col"))
    consts = plan.constants()
    v, pay, table, x = project(plan, consts, slide, w_in, w_bcd, tissue, dt_bias, rate_x, rate_y)
    groups = plan.segments()
    pay = lax.all_to_all(pay, "col", 0, 0, tiled=True, axis_index_groups=groups)
    gain = norm_gain.reshape(1, width)
    own, gate, gain = home(plan, consts, v, table, x, w_in, tissue, gain, rate_x, rate_y, d_skip)
    pay, own, gate, gain = lax.optimization_barrier((pay, own, gate, gain))
    y = scan_calls(plan, consts, "row", "col", pay)
    y = lax.all_to_all(y, "col", 0, 0, tiled=True, axis_index_groups=groups)
    return finish(plan, y, own, gate, gain, w_out)


def solution(mesh):
    placed = (
        P(("slides", "row"), "col", None),
        P(("slides", "row"), "col"),
        P(),
        P(),
        P(),
        P(),
        P(),
        P(),
        P(),
        P(),
    )
    return jax.shard_map(
        per_device,
        mesh=mesh,
        in_specs=placed,
        out_specs=P(("slides", "row"), "col", None),
        check_vma=False,
    )
```

```python
import functools

import jax
import jax.numpy as jnp
import numpy as np
from jax import lax
from jax.experimental import pallas as pl
from jax.experimental.pallas import tpu as pltpu
from jax.sharding import PartitionSpec as P

norm_eps = 1e-05
LANES = 128
HALF = LANES // 2
F32 = jnp.float32
BF16 = jnp.bfloat16


def round_up(value, step):
    return -(-value // step) * step


def in_hbm(x):
    return pltpu.with_memory_space_constraint(x, pltpu.HBM)


def mm(a, b):
    return jnp.dot(a, b, preferred_element_type=F32)


def nt_dot(a, b):
    return lax.dot_general(a, b, (((1,), (1,)), ((), ())), preferred_element_type=F32)


def tn_dot(a, b):
    return lax.dot_general(a, b, (((0,), (0,)), ((), ())), preferred_element_type=F32)


class Plan:
    def __init__(self, rows, cols, states, heads, width, devices):
        self.rows, self.cols, self.states, self.heads = rows, cols, states, heads
        self.width = width
        self.parts = 2 if devices % 2 == 0 and devices > 2 else 1
        self.devices = devices // self.parts
        self.group = width // self.devices
        self.slot = min(self.group, HALF)
        self.slots = self.group // self.slot
        self.work = self.slots * self.devices
        self.head_width = width // heads
        self.col_pad = round_up(cols, 8)
        self.upper = -(-rows // 2)
        self.half = round_up(self.upper * self.col_pad, 8)
        self.cells = rows * self.col_pad
        self.edge = rows * states
        self.top = states * self.col_pad
        self.bc = 2 * states
        self.at_bc = self.slots * self.half
        self.at_dt = self.at_bc + 2 * self.bc
        self.at_rate = self.at_dt + 2 * self.slots
        self.message = round_up(self.at_rate + 1, 8)
        self.tail = self.edge % LANES
        self.solid = self.edge // LANES
        self.share = LANES // self.tail if self.tail else 1
        self.packed = self.slots * self.solid + (-(-self.slots // self.share) if self.tail else 0)
        assert self.head_width % self.slot == 0 and self.group % self.slot == 0
        assert LANES % self.head_width == 0 and self.half <= LANES
        assert self.cells - self.half <= self.half
        assert states % 16 == 0 and heads % 8 == 0

    def segments(self):
        return [list(range(p * self.devices, (p + 1) * self.devices)) for p in range(self.parts)]

    def lanes(self):
        at = np.arange(2 * LANES)
        cell = np.where(at < LANES, at, at - LANES + self.half)
        live = np.where(at < LANES, at < self.half, cell < self.cells)
        i, j = cell // self.col_pad, cell % self.col_pad
        return i, j, live & (j < self.cols)

    def constants(self):
        i, j, real = self.lanes()
        both = real[:, None] & real[None]
        cell = np.arange(self.cells)
        ci, cj = cell // self.col_pad, cell % self.col_pad
        creal = cj < self.cols
        le = np.arange(round_up(self.rows, 8))
        lj = np.arange(self.col_pad)
        out = {}
        out["to1"] = (j[:, None] <= j[None]) & both
        out["to2"] = (j[:, None] == j[None]) & (i[:, None] <= i[None]) & both
        out["from1"] = (i[:, None] == i[None]) & (j[:, None] > j[None]) & both
        out["from2"] = (i[:, None] > i[None]) & both
        out["side1"] = (i[None] == le[:, None]) & real[None]
        out["side2"] = (i[None] > le[:, None]) & real[None]
        out["sidemask"] = (i[None] >= le[:, None]) & (le < self.rows)[:, None] & real[None]
        out["down1"] = (j[None] <= lj[:, None]) & real[None]
        out["down2"] = (j[None] == lj[:, None]) & real[None]
        out["downmask"] = (j[None] <= lj[:, None]) & (lj < self.cols)[:, None] & real[None]
        out["pick"] = (
            (i == self.rows - 1)[:, None] & real[:, None] & (j[:, None] == np.tile(lj, self.states)[None])
        )
        cboth = creal[:, None] & real[None]
        out["own1"] = (j[None] <= cj[:, None]) & cboth
        out["own2"] = (j[None] == cj[:, None]) & (i[None] <= ci[:, None]) & cboth
        out["ownmask"] = (i[None] <= ci[:, None]) & (j[None] <= cj[:, None]) & cboth
        out["lanei"] = (np.arange(self.rows)[:, None] == i[None]) & real[None]
        out["lanej"] = (np.arange(self.cols)[:, None] == j[None]) & real[None]
        return {k: in_hbm(jnp.asarray(x.astype(np.float32), BF16)) for k, x in out.items()}


def full(shape):
    return pl.BlockSpec(shape, lambda *_: (0,) * len(shape))


HBM = pl.BlockSpec(memory_space=pltpu.HBM)
SMEM = pl.BlockSpec(memory_space=pltpu.SMEM)


def cell_mask_of(plan, t_ref):
    t = t_ref[...].astype(F32).astype(BF16)
    cell = lax.broadcasted_iota(jnp.int32, (plan.cells, plan.cols), 0)
    col = lax.broadcasted_iota(jnp.int32, (plan.cells, plan.cols), 1)
    pick = (lax.rem(cell, plan.col_pad) == col).astype(F32).astype(BF16)
    cell = lax.broadcasted_iota(jnp.int32, (plan.cells, plan.rows), 0)
    row = lax.broadcasted_iota(jnp.int32, (plan.cells, plan.rows), 1)
    return jnp.sum(jnp.where(lax.div(cell, plan.col_pad) == row, mm(pick, t), 0.0), axis=1, keepdims=True)


def rate_row(heads_of, rx_ref, ry_ref):
    at = lax.broadcasted_iota(jnp.int32, (1, LANES), 1)
    rate = jnp.zeros((1, LANES), F32)
    part = jnp.zeros((1, LANES), jnp.int32)
    for s, head in enumerate(heads_of):
        for k, ref in enumerate((rx_ref, ry_ref)):
            first = 8 * s + 3 * k
            here = (at >= first) & (at < first + 3)
            rate = jnp.where(here, ref[head], rate)
            part = jnp.where(here, at - first, part)
    high = rate.astype(BF16).astype(F32)
    middle = (rate - high).astype(BF16).astype(F32)
    low = rate - high - middle
    return jnp.where(part == 0, high, jnp.where(part == 1, middle, low))


def project_kernel(
    plan, chunks, bias_hbm, rx_hbm, ry_hbm, x_hbm, w_hbm, wt_hbm, t_hbm, lanei_hbm, lanej_hbm,
    v_ref, pay_hbm, rows_ref, flat_ref,
    bias_ref, rx_ref, ry_ref, x_ref, w_ref, wt_ref, t_ref, lanei_ref, lanej_ref, pay_ref, wide, sems, w_sems, out_sems,
):
    group, states, cells, heads = plan.group, plan.states, plan.cells, plan.heads
    half, rest = plan.half, plan.cells - plan.half
    tile = plan.width // chunks
    pairs = (
        (x_hbm, x_ref), (t_hbm, t_ref), (wt_hbm, wt_ref), (lanei_hbm, lanei_ref), (lanej_hbm, lanej_ref),
        (bias_hbm, bias_ref), (rx_hbm, rx_ref), (ry_hbm, ry_ref),
    )
    loads = [pltpu.make_async_copy(a, b, sems.at[k]) for k, (a, b) in enumerate(pairs)]
    copies = [
        pltpu.make_async_copy(w_hbm.at[:, k * tile : (k + 1) * tile], w_ref.at[k], w_sems.at[k])
        for k in range(chunks)
    ]
    for copy in loads + copies:
        copy.start()
    wide[...] = jnp.zeros_like(wide)
    v_ref[half:LANES, :] = jnp.zeros((LANES - half, plan.width), BF16)
    v_ref[LANES + rest :, :] = jnp.zeros((LANES - rest, plan.width), BF16)

    loads[0].wait()
    for i in range(plan.rows):
        wide[i * plan.col_pad : i * plan.col_pad + plan.cols, :] = x_ref[i].astype(F32)
    x = wide[...].astype(BF16)
    flat_ref[...] = x
    for copy in loads[1:]:
        copy.wait()
    keep = cell_mask_of(plan, t_ref)
    t = t_ref[...].astype(F32).astype(BF16)
    m = jnp.sum(mm(t, lanei_ref[...]) * lanej_ref[...].astype(F32), axis=0, keepdims=True)
    table = nt_dot(wt_ref[...], x)
    ext = jnp.concatenate([table, jnp.zeros((table.shape[0], 2 * LANES - cells), F32)], axis=1)
    lane = lax.broadcasted_iota(jnp.int32, (table.shape[0], LANES), 1)
    lo, hi = ext[:, :LANES], ext[:, LANES:]
    shift = half % LANES
    if shift:
        moved = jnp.where(
            lane < LANES - shift, pltpu.roll(lo, LANES - shift, 1), pltpu.roll(hi, LANES - shift, 1)
        )
    else:
        moved = hi
    table = jnp.concatenate([jnp.where(lane < half, lo, 0.0), jnp.where(lane < rest, moved, 0.0)], axis=1)
    z = table[2 * states :]
    at = lax.broadcasted_iota(jnp.int32, z.shape, 0)
    for h in range(heads):
        z = jnp.where(at == h, z + bias_ref[h], z)
    soft = m * (jnp.maximum(z, 0.0) + jnp.log1p(jnp.exp(-jnp.abs(z))))
    table = jnp.concatenate([table[: 2 * states], soft], axis=0).astype(BF16)
    rows_ref[...] = table.astype(F32)
    bc = table[: 2 * states]
    steps = rows_ref[2 * states :, :]

    lane = lax.broadcasted_iota(jnp.int32, (half, LANES), 1)
    sent = []
    for chunk in range(chunks):
        copies[chunk].wait()
        v = mm(flat_ref[...], w_ref[chunk]).astype(BF16).astype(F32) * keep
        low = v.astype(BF16)
        v_ref[0:half, chunk * tile : (chunk + 1) * tile] = low[:half]
        v_ref[LANES : LANES + rest, chunk * tile : (chunk + 1) * tile] = low[half:]
        per = tile // group
        for k in range(per):
            dest = chunk * per + k
            dts, heads_of = [], []
            for s in range(plan.slots):
                offset = k * group + s * plan.slot
                base = offset // LANES * LANES
                at = offset % LANES
                first = v[:half, base : base + LANES]
                last = v[half:, base : base + LANES]
                if rest < half:
                    last = jnp.concatenate([last, jnp.zeros((half - rest, LANES), F32)], axis=0)
                if at:
                    first = pltpu.roll(first, LANES - at, 1)
                if at != HALF:
                    last = pltpu.roll(last, (HALF - at) % LANES, 1)
                both = jnp.where(lane < HALF, first, last)
                if plan.slot < HALF:
                    both = jnp.where(lane % HALF < plan.slot, both, 0.0)
                pay_ref[dest, s * half : (s + 1) * half, :] = both.astype(BF16)
                head = (chunk * tile + offset) // plan.head_width
                heads_of.append(head)
                dts += [steps[head : head + 1, :LANES], steps[head : head + 1, LANES:]]
            dts.append(rate_row(heads_of, rx_ref, ry_ref))
            pay_ref[dest, plan.at_bc : plan.at_bc + plan.bc, :] = bc[:, :LANES]
            pay_ref[dest, plan.at_bc + plan.bc : plan.at_dt, :] = bc[:, LANES:]
            spare = plan.message - plan.at_dt - len(dts)
            dts += [jnp.zeros((spare, LANES), F32)] if spare else []
            pay_ref[dest, plan.at_dt : plan.message, :] = jnp.concatenate(dts, axis=0).astype(BF16)
        at = slice(chunk * per, (chunk + 1) * per)
        sent.append(pltpu.make_async_copy(pay_ref.at[at], pay_hbm.at[at], out_sems.at[chunk]))
        sent[-1].start()
    for copy in sent:
        copy.wait()


def project(plan, consts, slide, w_in, w_bcd, tissue, dt_bias, rate_x, rate_y):
    chunks = 4
    tile = plan.width // chunks
    depth = slide.shape[2]
    args = [dt_bias, rate_x, rate_y, slide, w_in, w_bcd.T, tissue.T, consts["lanei"], consts["lanej"]]
    count = 2 * plan.states + plan.heads
    assert plan.width % chunks == 0 and tile % plan.group == 0 and tile % LANES == 0
    message = (plan.devices, plan.message, LANES)
    outs = [((2 * LANES, plan.width), BF16), (message, BF16), ((count, 2 * LANES), F32), ((plan.cells, depth), BF16)]
    specs = [full(s) for s, _ in outs]
    specs[1] = HBM
    return pl.pallas_call(
        functools.partial(project_kernel, plan, chunks),
        grid=(1,),
        in_specs=[HBM] * len(args),
        out_specs=specs,
        out_shape=[jax.ShapeDtypeStruct(s, d) for s, d in outs],
        scratch_shapes=[
            pltpu.SMEM(dt_bias.shape, F32),
            pltpu.SMEM(rate_x.shape, F32),
            pltpu.SMEM(rate_y.shape, F32),
            pltpu.VMEM(slide.shape, BF16),
            pltpu.VMEM((chunks, depth, tile), BF16),
        ]
        + [pltpu.VMEM(x.shape, x.dtype) for x in args[5:]]
        + [
            pltpu.VMEM(message, BF16),
            pltpu.VMEM((plan.cells, depth), F32),
            pltpu.SemaphoreType.DMA((8,)),
            pltpu.SemaphoreType.DMA((chunks,)),
            pltpu.SemaphoreType.DMA((chunks,)),
        ],
        compiler_params=pltpu.CompilerParams(vmem_limit_bytes=24 * 2**20),
        name="project",
    )(*[in_hbm(x) for x in args])


def home_kernel(
    plan, rx_ref, ry_ref, skip_ref, w_hbm, v_ref, rows_ref, flat_ref, t_ref, gain_ref,
    own1_ref, own2_ref, from1_ref, from2_ref, mask_ref, out_ref, gate_hbm, gain_out, pair, w_ref, gate_ref, sem, gate_sem,
):
    states, cells, half = plan.states, plan.cells, plan.half
    copy = pltpu.make_async_copy(w_hbm.at[:, plan.width :], w_ref, sem)
    copy.start()
    gain_out[...] = gain_ref[...]
    b = rows_ref[0:states, :].astype(BF16)
    c = rows_ref[states : 2 * states, :].astype(BF16)
    pairs = tn_dot(c, b)
    pairs = jnp.concatenate([pairs[:half], pairs[LANES : LANES + cells - half]], axis=0)
    pair[...] = pairs * mask_ref[...].astype(F32)
    lane = lax.broadcasted_iota(jnp.int32, (cells, LANES), 1)
    per = LANES // plan.head_width
    for block in range(plan.width // LANES):
        v = v_ref[:, block * LANES : (block + 1) * LANES]
        vc = jnp.concatenate([v[:half], v[LANES : LANES + cells - half]], axis=0).astype(F32)
        total = None
        for k in range(per):
            h = block * per + k
            dt = rows_ref[2 * states + h : 2 * states + h + 1, :]
            low = dt.astype(BF16)
            x = mm(own1_ref[...] * low, from1_ref[...])
            y = mm(own2_ref[...] * low, from2_ref[...])
            weight = jnp.exp(-(rx_ref[h] * x + ry_ref[h] * y)) * pair[...] * dt
            part = mm(weight.astype(BF16), v) + skip_ref[h] * vc
            total = part if total is None else jnp.where(lane < k * plan.head_width, total, part)
        out_ref[:, block * LANES : (block + 1) * LANES] = total.astype(BF16)
    keep = cell_mask_of(plan, t_ref)
    copy.wait()
    tile = 2 * LANES
    for block in range(plan.width // tile):
        at = slice(block * tile, (block + 1) * tile)
        z = mm(flat_ref[...], w_ref[:, at]).astype(BF16).astype(F32)
        gate_ref[:, at] = (z * (1.0 / (1.0 + jnp.exp(-z))) * keep).astype(BF16)
    copy = pltpu.make_async_copy(gate_ref, gate_hbm, gate_sem)
    copy.start()
    copy.wait()


def home(plan, consts, v, rows, flat, w_in, tissue, gain, rate_x, rate_y, d_skip):
    args = [in_hbm(w_in), v, rows, flat, in_hbm(tissue.T), in_hbm(gain)]
    args += [consts[k] for k in ("own1", "own2", "from1", "from2", "ownmask")]
    outs = [((plan.cells, plan.width), BF16), ((plan.cells, plan.width), BF16), (gain.shape, F32)]
    return pl.pallas_call(
        functools.partial(home_kernel, plan),
        grid=(1,),
        in_specs=[SMEM, SMEM, SMEM, HBM] + [full(x.shape) for x in args[1:]],
        out_specs=[full(outs[0][0]), HBM, full(outs[2][0])],
        out_shape=[jax.ShapeDtypeStruct(s, d) for s, d in outs],
        scratch_shapes=[
            pltpu.VMEM((plan.cells, 2 * LANES), F32),
            pltpu.VMEM((w_in.shape[0], w_in.shape[1] - plan.width), BF16),
            pltpu.VMEM((plan.cells, plan.width), BF16),
            pltpu.SemaphoreType.DMA,
            pltpu.SemaphoreType.DMA,
        ],
        compiler_params=pltpu.CompilerParams(vmem_limit_bytes=24 * 2**20),
        name="home",
    )(in_hbm(rate_x), in_hbm(rate_y), in_hbm(d_skip), *args)


def ones(mask):
    return jnp.where(mask, 1.0, 0.0).astype(BF16)


def places(plan, shape, axis):
    at = lax.broadcasted_iota(jnp.int32, shape, axis)
    late = at >= LANES
    at = jnp.where(late, at - LANES, at)
    i = lax.div(at, plan.col_pad)
    j = at - i * plan.col_pad
    real = (at < jnp.where(late, plan.cells - plan.half, plan.half)) & (j < plan.cols)
    return jnp.where(late, i + plan.upper, i), j, real


def wide_rows(pay_ref, t, at, count, gap):
    return jnp.concatenate([pay_ref[t, at : at + count, :], pay_ref[t, at + gap : at + gap + count, :]], axis=1)


def turned(plan, pay_ref, t, s):
    v = pay_ref[t, s * plan.half : (s + 1) * plan.half, :].astype(F32)
    if plan.half < LANES:
        v = jnp.concatenate([v, jnp.zeros((LANES - plan.half, LANES), F32)], axis=0)
    v = v.T
    return jnp.concatenate([v[:HALF], v[HALF:]], axis=1).astype(BF16)


def load_steps(plan, pay_ref, dts):
    for t in range(plan.devices):
        rows = pay_ref[t, plan.at_dt : plan.message, :].astype(F32)
        for s in range(plan.slots):
            w = s * plan.devices + t
            dts[w : w + 1, :LANES] = rows[2 * s : 2 * s + 1]
            dts[w : w + 1, LANES:] = rows[2 * s + 1 : 2 * s + 2]


def rates_of(plan, pay_ref, kind):
    row = pay_ref[0, plan.at_dt : plan.message, :].astype(F32)[plan.at_rate - plan.at_dt : plan.at_rate - plan.at_dt + 1]
    at = lax.broadcasted_iota(jnp.int32, (1, LANES), 1)
    first = [8 * s + 3 * kind for s in range(plan.slots)]
    return [jnp.sum(jnp.where((at >= f) & (at < f + 3), row, 0.0), axis=1, keepdims=True) for f in first]


def slot_rates(plan, pay_ref, kind):
    return jnp.concatenate(
        [jnp.broadcast_to(r, (plan.devices, 1)) for r in rates_of(plan, pay_ref, kind)], axis=0
    )


def pack_edges(plan, out_ref, held):
    for s in range(plan.slots):
        for k in range(plan.solid):
            out_ref[s * plan.solid + k] = held[s][:, k * LANES : (k + 1) * LANES].astype(BF16)
    if plan.tail:
        first = plan.slots * plan.solid
        for k in range(plan.packed - first):
            parts = [x[:, plan.solid * LANES :] for x in held[k * plan.share : (k + 1) * plan.share]]
            spare = LANES - plan.tail * len(parts)
            parts += [jnp.zeros((HALF, spare), F32)] if spare else []
            out_ref[first + k] = jnp.concatenate(parts, axis=1).astype(BF16)


def unpack_edges(plan, ref, s):
    parts = [ref[s * plan.solid + k].astype(F32) for k in range(plan.solid)]
    if plan.tail:
        last = ref[plan.slots * plan.solid + s // plan.share].astype(F32)
        at = s % plan.share * plan.tail
        parts.append(last[:, at : at + plan.tail])
    return jnp.concatenate(parts, axis=1)


def scan_edges(plan, pay_ref, dts, inner, kept, seen):
    states, tiles, wide = plan.states, plan.devices, 2 * LANES
    i, j, real = places(plan, (wide, wide), 0)
    ti, tj, treal = places(plan, (wide, wide), 1)
    from1 = ones((i == ti) & (j > tj) & real & treal)
    edge_row = lax.div(lax.broadcasted_iota(jnp.int32, (wide, plan.edge), 1), states)
    i, _, real = places(plan, (wide, plan.edge), 0)
    keep = ones((i == edge_row) & real)
    ti, _, treal = places(plan, (plan.rows, wide), 1)
    rowsel = ones((ti == lax.broadcasted_iota(jnp.int32, (plan.rows, wide), 0)) & treal)
    dt = dts[...]
    low = dt.astype(BF16)
    rate = slot_rates(plan, pay_ref, 0)
    inner[...] = jnp.exp(-rate * mm(low, from1)) * dt
    kept[...] = jnp.exp(-rate * mm(low, keep))
    ends = []
    for s in range(plan.slots):
        held = jnp.zeros((HALF, plan.edge), F32)
        product = jnp.ones((1, plan.edge), F32)
        for t in range(tiles):
            w = s * tiles + t
            seen(w, held, product)
            b = wide_rows(pay_ref, t, plan.at_bc, states, plan.bc).astype(F32)
            bd = (b * inner[w : w + 1, :]).astype(BF16)
            left = jnp.concatenate([bd * rowsel[i : i + 1] for i in range(plan.rows)], axis=0)
            now = kept[w : w + 1, :]
            held = held * now + nt_dot(turned(plan, pay_ref, t, s), left)
            product = product * now
        ends.append(held)
    return ends


def last_kernel(plan, axis, pay_ref, last_ref, dts, inner, kept):
    @pl.when(lax.axis_index(axis) < (plan.parts - 1) * plan.devices)
    def _():
        load_steps(plan, pay_ref, dts)
        pack_edges(plan, last_ref, scan_edges(plan, pay_ref, dts, inner, kept, lambda w, held, product: None))


def maps_kernel(
    plan, pay_ref, to1_ref, to2_ref, from1_ref, from2_ref, side1_ref, side2_ref,
    sidemask_ref, down1_ref, down2_ref, downmask_ref, pick_ref,
    side_ref, above_ref, passed_ref, top_ref, edge_ref, upto_ref, dts, inner, kept, s1, s2, d1, d2,
):
    states, tiles, cp, work = plan.states, plan.devices, plan.col_pad, plan.work
    rp = side1_ref.shape[0]
    load_steps(plan, pay_ref, dts)

    def seen(w, held, product):
        edge_ref[w] = held.astype(BF16)
        upto_ref[w : w + 1, :] = product

    scan_edges(plan, pay_ref, dts, inner, kept, seen)
    low = dts[...].astype(BF16)
    above_ref[...] = jnp.exp(-slot_rates(plan, pay_ref, 1) * mm(low, to2_ref[...]))
    rates_x, rates_y = rates_of(plan, pay_ref, 0), rates_of(plan, pay_ref, 1)
    for w in range(work):
        rf = dts[w : w + 1, :]
        s1[w * rp : (w + 1) * rp, :] = side1_ref[...].astype(F32) * rf
        s2[w * rp : (w + 1) * rp, :] = side2_ref[...].astype(F32) * rf
        d1[w * cp : (w + 1) * cp, :] = down1_ref[...].astype(F32) * rf
        d2[w * cp : (w + 1) * cp, :] = down2_ref[...].astype(F32) * rf
    mask = sidemask_ref[...].astype(F32)
    x, y = mm(s1[...].astype(BF16), to1_ref[...]), mm(s2[...].astype(BF16), to2_ref[...])
    shape = (states, plan.top)
    n = lax.broadcasted_iota(jnp.int32, shape, 0)
    diag = ones(n == lax.div(lax.broadcasted_iota(jnp.int32, shape, 1), cp))
    for w in range(work):
        s = w // tiles
        at = slice(w * rp, (w + 1) * rp)
        side = (jnp.exp(-(rates_x[s] * x[at] + rates_y[s] * y[at])) * mask).astype(BF16)
        side_ref[w] = side
        bottom = mm(side, pick_ref[...]).astype(BF16)
        passed_ref[w] = jnp.concatenate([diag * bottom[i : i + 1] for i in range(plan.rows)], axis=0)
    x, y = mm(d1[...].astype(BF16), from1_ref[...]), mm(d2[...].astype(BF16), from2_ref[...])
    mask = downmask_ref[...].astype(F32)
    for w in range(work):
        s, t = w // tiles, w % tiles
        at = slice(w * cp, (w + 1) * cp)
        fall = jnp.exp(-(rates_x[s] * x[at] + rates_y[s] * y[at])) * mask * dts[w : w + 1, :]
        b = wide_rows(pay_ref, t, plan.at_bc, states, plan.bc).astype(F32)
        falls = jnp.concatenate([fall * b[n : n + 1] for n in range(states)], axis=0).astype(BF16)
        top_ref[w] = nt_dot(turned(plan, pay_ref, t, s), falls) + mm(edge_ref[w], passed_ref[w])


def join_kernel(plan, upto_ref, entry_ref, passed_ref, top_ref, out_ref):
    for s in range(plan.slots):
        entry = unpack_edges(plan, entry_ref, s)
        for t in range(plan.devices):
            w = s * plan.devices + t
            late = (entry * upto_ref[w : w + 1, :]).astype(BF16)
            out_ref[w] = (top_ref[w] + mm(late, passed_ref[w])).astype(BF16)


def sides_kernel(plan, pay_ref, edge_ref, upto_ref, entry_ref, side_ref, above_ref, y_ref, down_ref):
    states, tiles = plan.states, plan.devices
    shape = (plan.col_pad, 2 * LANES)
    _, tj, treal = places(plan, shape, 1)
    colsel = jnp.where((tj == lax.broadcasted_iota(jnp.int32, shape, 0)) & treal, 1.0, 0.0)
    for s in range(plan.slots):
        entry = unpack_edges(plan, entry_ref, s)
        for t in range(tiles):
            w = s * tiles + t
            c = wide_rows(pay_ref, t, plan.at_bc + states, states, plan.bc)
            side = side_ref[w]
            left = jnp.concatenate([c * side[i : i + 1] for i in range(plan.rows)], axis=0)
            whole = (edge_ref[w].astype(F32) + entry * upto_ref[w : w + 1, :]).astype(BF16)
            y_ref[w] = mm(whole, left)
            ca = c.astype(F32) * above_ref[w : w + 1, :]
            down_ref[w] = jnp.concatenate([colsel * ca[n : n + 1] for n in range(states)], axis=0).astype(BF16)


def cells_kernel(plan, y_ref, down_ref, top_ref, out_ref):
    for w in range(plan.work):
        t, s = w % plan.devices, w // plan.devices
        y = y_ref[w] + mm(top_ref[w], down_ref[w])
        y = jnp.concatenate([y[:, :LANES], y[:, LANES:]], axis=0).T
        out_ref[t, s * plan.half : (s + 1) * plan.half, :] = y[: plan.half].astype(BF16)


def call(kernel, name, args, outs, scratch=(), out_specs=None):
    return pl.pallas_call(
        kernel,
        grid=(1,),
        in_specs=[full(x.shape) for x in args],
        out_specs=out_specs or [full(s) for s, _ in outs],
        out_shape=[jax.ShapeDtypeStruct(s, d) for s, d in outs],
        scratch_shapes=[x if not isinstance(x, tuple) else pltpu.VMEM(*x) for x in scratch],
        compiler_params=pltpu.CompilerParams(vmem_limit_bytes=24 * 2**20),
        name=name,
    )(*args)


def scan_calls(plan, consts, row_axis, col_axis, pay):
    work, cp, wide = plan.work, plan.col_pad, 2 * LANES
    rp = consts["side1"].shape[0]
    steps = [((work, wide), F32), ((work, wide), F32), ((work, plan.edge), F32)]
    shape = (plan.packed, HALF, LANES)
    if plan.parts > 1:
        last = call(functools.partial(last_kernel, plan, col_axis), "last", [pay], [(shape, BF16)], steps)[0]
        entry = lax.ppermute(last, col_axis, [(k, k + plan.devices) for k in range(plan.devices)])
    else:
        entry = jnp.zeros(shape, BF16)
    names = ("to1", "to2", "from1", "from2", "side1", "side2", "sidemask", "down1", "down2", "downmask", "pick")
    side, above, passed, tops, edges, upto = call(
        functools.partial(maps_kernel, plan),
        "maps",
        [pay] + [consts[k] for k in names],
        [
            ((work, rp, wide), BF16),
            ((work, wide), F32),
            ((work, plan.edge, plan.top), BF16),
            ((work, HALF, plan.top), F32),
            ((work, HALF, plan.edge), BF16),
            ((work, plan.edge), F32),
        ],
        steps + [((work * rp, wide), F32)] * 2 + [((work * cp, wide), F32)] * 2,
    )
    edge_entry = entry
    tops = call(
        functools.partial(join_kernel, plan),
        "join",
        [upto, entry, passed, tops],
        [((work, HALF, plan.top), BF16)],
    )[0]
    count = lax.axis_size(row_axis)
    chain = [(r, r + 1) for r in range(count - 1)]
    entry = lax.ppermute(tops, row_axis, chain)
    if count > 2:
        keep = jnp.dot(above.astype(BF16), consts["pick"], preferred_element_type=F32)[:, None, :]
        for _ in range(count - 2):
            entry = lax.ppermute(
                (tops.astype(F32) + keep * entry.astype(F32)).astype(BF16), row_axis, chain
            )
    y, down = call(
        functools.partial(sides_kernel, plan),
        "sides",
        [pay, edges, upto, edge_entry, side, above],
        [((work, HALF, wide), F32), ((work, plan.top, wide), BF16)],
    )
    return call(
        functools.partial(cells_kernel, plan),
        "cells",
        [y, down, entry],
        [((plan.devices, plan.slots * plan.half, LANES), BF16)],
    )[0]


def finish_kernel(plan, y_ref, own_ref, gate_ref, gain_ref, w_ref, out_hbm, full_ref, out_ref, sems):
    half, cells = plan.half, plan.cells
    slot, slots = plan.slot, plan.slots
    per = LANES // slot
    lane = lax.broadcasted_iota(jnp.int32, (half, LANES), 1)
    copies = []
    for k, (lo, hi) in enumerate(((0, half), (half, cells))):
        for block in range(plan.width // LANES):
            joined = None
            for d in range(per):
                at = block * per + d
                part = y_ref[at // slots, at % slots * half : (at % slots + 1) * half, :].astype(F32)
                shift = (d * slot - k * HALF) % LANES
                if shift:
                    part = pltpu.roll(part, shift, 1)
                joined = part if joined is None else jnp.where(lane < d * slot, joined, part)
            full_ref[lo:hi, block * LANES : (block + 1) * LANES] = joined[: hi - lo]
        y = full_ref[lo:hi, :] + own_ref[lo:hi, :].astype(F32)
        y = y.astype(BF16).astype(F32)
        gated = y * gate_ref[lo:hi, :].astype(F32)
        scale = lax.rsqrt(jnp.mean(gated * gated, axis=-1, keepdims=True) + norm_eps)
        normed = (gated * scale * gain_ref[...]).astype(BF16)
        full_ref[lo:hi, :] = mm(normed, w_ref[...])
        first, last = lo // plan.col_pad, hi // plan.col_pad
        for i in range(first, last):
            out_ref[i] = full_ref[i * plan.col_pad : i * plan.col_pad + plan.cols, :].astype(BF16)
        copies.append(pltpu.make_async_copy(out_ref.at[first:last], out_hbm.at[first:last], sems.at[k]))
        copies[-1].start()
    for copy in copies:
        copy.wait()


def finish(plan, y, own, gate, gain, w_out):
    args = (y, own, gate, gain, w_out)
    shape = (plan.rows, plan.cols, w_out.shape[1])
    assert w_out.shape[1] == plan.width
    return call(
        functools.partial(finish_kernel, plan),
        "finish",
        args,
        [(shape, BF16)],
        [((plan.cells, plan.width), F32), (shape, BF16), pltpu.SemaphoreType.DMA((2,))],
        [HBM],
    )[0]


def per_device(slide, tissue, w_in, w_bcd, dt_bias, rate_x, rate_y, d_skip, norm_gain, w_out):
    rows, cols, model_width = slide.shape
    width = w_out.shape[0]
    heads = dt_bias.shape[0]
    states = (w_bcd.shape[1] - heads) // 2
    plan = Plan(rows, cols, states, heads, width, lax.axis_size("col"))
    consts = plan.constants()
    v, pay, table, x = project(plan, consts, slide, w_in, w_bcd, tissue, dt_bias, rate_x, rate_y)
    groups = plan.segments()
    pay = lax.all_to_all(pay, "col", 0, 0, tiled=True, axis_index_groups=groups)
    gain = norm_gain.reshape(1, width)
    own, gate, gain = home(plan, consts, v, table, x, w_in, tissue, gain, rate_x, rate_y, d_skip)
    pay, own, gate, gain = lax.optimization_barrier((pay, own, gate, gain))
    y = scan_calls(plan, consts, "row", "col", pay)
    y = lax.all_to_all(y, "col", 0, 0, tiled=True, axis_index_groups=groups)
    return finish(plan, y, own, gate, gain, w_out)


def solution(mesh):
    placed = (
        P(("slides", "row"), "col", None),
        P(("slides", "row"), "col"),
        P(),
        P(),
        P(),
        P(),
        P(),
        P(),
        P(),
        P(),
    )
    return jax.shard_map(
        per_device,
        mesh=mesh,
        in_specs=placed,
        out_specs=P(("slides", "row"), "col", None),
        check_vma=False,
    )
```

```python
import functools

import jax
import jax.numpy as jnp
import numpy as np
from jax import lax
from jax.experimental import pallas as pl
from jax.experimental.pallas import tpu as pltpu
from jax.sharding import PartitionSpec as P

norm_eps = 1e-05
LANES = 128
HALF = LANES // 2
F32 = jnp.float32
BF16 = jnp.bfloat16


def round_up(value, step):
    return -(-value // step) * step


def in_hbm(x):
    return pltpu.with_memory_space_constraint(x, pltpu.HBM)


def mm(a, b):
    return jnp.dot(a, b, preferred_element_type=F32)


def nt_dot(a, b):
    return lax.dot_general(a, b, (((1,), (1,)), ((), ())), preferred_element_type=F32)


def tn_dot(a, b):
    return lax.dot_general(a, b, (((0,), (0,)), ((), ())), preferred_element_type=F32)


class Plan:
    def __init__(self, rows, cols, states, heads, width, devices):
        self.rows, self.cols, self.states, self.heads = rows, cols, states, heads
        self.width = width
        self.parts = 2 if devices % 2 == 0 and devices > 2 else 1
        self.devices = devices // self.parts
        self.group = width // self.devices
        self.slot = min(self.group, HALF)
        self.slots = self.group // self.slot
        self.work = self.slots * self.devices
        self.head_width = width // heads
        self.col_pad = round_up(cols, 8)
        self.upper = -(-rows // 2)
        self.half = round_up(self.upper * self.col_pad, 8)
        self.cells = rows * self.col_pad
        self.edge = rows * states
        self.top = states * self.col_pad
        self.bc = 2 * states
        self.at_bc = self.slots * self.half
        self.at_dt = self.at_bc + 2 * self.bc
        self.at_rate = self.at_dt + 2 * self.slots
        self.message = round_up(self.at_rate + 1, 8)
        self.tail = self.edge % LANES
        self.solid = self.edge // LANES
        self.share = LANES // self.tail if self.tail else 1
        self.packed = self.slots * self.solid + (-(-self.slots // self.share) if self.tail else 0)
        assert self.head_width % self.slot == 0 and self.group % self.slot == 0
        assert LANES % self.head_width == 0 and self.half <= LANES
        assert self.cells - self.half <= self.half
        assert states % 16 == 0 and heads % 8 == 0

    def segments(self):
        return [list(range(p * self.devices, (p + 1) * self.devices)) for p in range(self.parts)]

    def lanes(self):
        at = np.arange(2 * LANES)
        cell = np.where(at < LANES, at, at - LANES + self.half)
        live = np.where(at < LANES, at < self.half, cell < self.cells)
        i, j = cell // self.col_pad, cell % self.col_pad
        return i, j, live & (j < self.cols)

    def constants(self):
        i, j, real = self.lanes()
        both = real[:, None] & real[None]
        cell = np.arange(self.cells)
        ci, cj = cell // self.col_pad, cell % self.col_pad
        creal = cj < self.cols
        le = np.arange(round_up(self.rows, 8))
        lj = np.arange(self.col_pad)
        out = {}
        out["to1"] = (j[:, None] <= j[None]) & both
        out["to2"] = (j[:, None] == j[None]) & (i[:, None] <= i[None]) & both
        out["from1"] = (i[:, None] == i[None]) & (j[:, None] > j[None]) & both
        out["from2"] = (i[:, None] > i[None]) & both
        out["side1"] = (i[None] == le[:, None]) & real[None]
        out["side2"] = (i[None] > le[:, None]) & real[None]
        out["sidemask"] = (i[None] >= le[:, None]) & (le < self.rows)[:, None] & real[None]
        out["down1"] = (j[None] <= lj[:, None]) & real[None]
        out["down2"] = (j[None] == lj[:, None]) & real[None]
        out["downmask"] = (j[None] <= lj[:, None]) & (lj < self.cols)[:, None] & real[None]
        out["pick"] = (
            (i == self.rows - 1)[:, None] & real[:, None] & (j[:, None] == np.tile(lj, self.states)[None])
        )
        cboth = creal[:, None] & real[None]
        out["own1"] = (j[None] <= cj[:, None]) & cboth
        out["own2"] = (j[None] == cj[:, None]) & (i[None] <= ci[:, None]) & cboth
        out["ownmask"] = (i[None] <= ci[:, None]) & (j[None] <= cj[:, None]) & cboth
        out["lanei"] = (np.arange(self.rows)[:, None] == i[None]) & real[None]
        out["lanej"] = (np.arange(self.cols)[:, None] == j[None]) & real[None]
        return {k: in_hbm(jnp.asarray(x.astype(np.float32), BF16)) for k, x in out.items()}


def full(shape):
    return pl.BlockSpec(shape, lambda *_: (0,) * len(shape))


HBM = pl.BlockSpec(memory_space=pltpu.HBM)
SMEM = pl.BlockSpec(memory_space=pltpu.SMEM)


def cell_mask_of(plan, t_ref):
    t = t_ref[...].astype(F32).astype(BF16)
    cell = lax.broadcasted_iota(jnp.int32, (plan.cells, plan.cols), 0)
    col = lax.broadcasted_iota(jnp.int32, (plan.cells, plan.cols), 1)
    pick = (lax.rem(cell, plan.col_pad) == col).astype(F32).astype(BF16)
    cell = lax.broadcasted_iota(jnp.int32, (plan.cells, plan.rows), 0)
    row = lax.broadcasted_iota(jnp.int32, (plan.cells, plan.rows), 1)
    return jnp.sum(jnp.where(lax.div(cell, plan.col_pad) == row, mm(pick, t), 0.0), axis=1, keepdims=True)


def rate_row(heads_of, rx_ref, ry_ref):
    at = lax.broadcasted_iota(jnp.int32, (1, LANES), 1)
    rate = jnp.zeros((1, LANES), F32)
    part = jnp.zeros((1, LANES), jnp.int32)
    for s, head in enumerate(heads_of):
        for k, ref in enumerate((rx_ref, ry_ref)):
            first = 8 * s + 3 * k
            here = (at >= first) & (at < first + 3)
            rate = jnp.where(here, ref[head], rate)
            part = jnp.where(here, at - first, part)
    high = rate.astype(BF16).astype(F32)
    middle = (rate - high).astype(BF16).astype(F32)
    low = rate - high - middle
    return jnp.where(part == 0, high, jnp.where(part == 1, middle, low))


def project_kernel(
    plan, chunks, bias_hbm, rx_hbm, ry_hbm, x_hbm, w_hbm, wt_hbm, t_hbm, lanei_hbm, lanej_hbm,
    v_ref, pay_hbm, rows_ref, flat_ref,
    bias_ref, rx_ref, ry_ref, x_ref, w_ref, wt_ref, t_ref, lanei_ref, lanej_ref, pay_ref, wide, sems, w_sems, out_sems,
):
    group, states, cells, heads = plan.group, plan.states, plan.cells, plan.heads
    half, rest = plan.half, plan.cells - plan.half
    tile = plan.width // chunks
    pairs = (
        (x_hbm, x_ref), (t_hbm, t_ref), (wt_hbm, wt_ref), (lanei_hbm, lanei_ref), (lanej_hbm, lanej_ref),
        (bias_hbm, bias_ref), (rx_hbm, rx_ref), (ry_hbm, ry_ref),
    )
    loads = [pltpu.make_async_copy(a, b, sems.at[k]) for k, (a, b) in enumerate(pairs)]
    copies = [
        pltpu.make_async_copy(w_hbm.at[:, k * tile : (k + 1) * tile], w_ref.at[k], w_sems.at[k])
        for k in range(chunks)
    ]
    for copy in loads + copies:
        copy.start()
    wide[...] = jnp.zeros_like(wide)
    v_ref[half:LANES, :] = jnp.zeros((LANES - half, plan.width), BF16)
    v_ref[LANES + rest :, :] = jnp.zeros((LANES - rest, plan.width), BF16)

    loads[0].wait()
    for i in range(plan.rows):
        wide[i * plan.col_pad : i * plan.col_pad + plan.cols, :] = x_ref[i].astype(F32)
    x = wide[...].astype(BF16)
    flat_ref[...] = x
    for copy in loads[1:]:
        copy.wait()
    keep = cell_mask_of(plan, t_ref)
    t = t_ref[...].astype(F32).astype(BF16)
    m = jnp.sum(mm(t, lanei_ref[...]) * lanej_ref[...].astype(F32), axis=0, keepdims=True)
    table = nt_dot(wt_ref[...], x)
    ext = jnp.concatenate([table, jnp.zeros((table.shape[0], 2 * LANES - cells), F32)], axis=1)
    lane = lax.broadcasted_iota(jnp.int32, (table.shape[0], LANES), 1)
    lo, hi = ext[:, :LANES], ext[:, LANES:]
    shift = half % LANES
    if shift:
        moved = jnp.where(
            lane < LANES - shift, pltpu.roll(lo, LANES - shift, 1), pltpu.roll(hi, LANES - shift, 1)
        )
    else:
        moved = hi
    table = jnp.concatenate([jnp.where(lane < half, lo, 0.0), jnp.where(lane < rest, moved, 0.0)], axis=1)
    z = table[2 * states :]
    at = lax.broadcasted_iota(jnp.int32, z.shape, 0)
    for h in range(heads):
        z = jnp.where(at == h, z + bias_ref[h], z)
    soft = m * (jnp.maximum(z, 0.0) + jnp.log1p(jnp.exp(-jnp.abs(z))))
    table = jnp.concatenate([table[: 2 * states], soft], axis=0).astype(BF16)
    rows_ref[...] = table.astype(F32)
    bc = table[: 2 * states]
    steps = rows_ref[2 * states :, :]

    lane = lax.broadcasted_iota(jnp.int32, (half, LANES), 1)
    sent = []
    for chunk in range(chunks):
        copies[chunk].wait()
        v = mm(flat_ref[...], w_ref[chunk]).astype(BF16).astype(F32) * keep
        low = v.astype(BF16)
        v_ref[0:half, chunk * tile : (chunk + 1) * tile] = low[:half]
        v_ref[LANES : LANES + rest, chunk * tile : (chunk + 1) * tile] = low[half:]
        per = tile // group
        for k in range(per):
            dest = chunk * per + k
            dts, heads_of = [], []
            for s in range(plan.slots):
                offset = k * group + s * plan.slot
                base = offset // LANES * LANES
                at = offset % LANES
                first = v[:half, base : base + LANES]
                last = v[half:, base : base + LANES]
                if rest < half:
                    last = jnp.concatenate([last, jnp.zeros((half - rest, LANES), F32)], axis=0)
                if at:
                    first = pltpu.roll(first, LANES - at, 1)
                if at != HALF:
                    last = pltpu.roll(last, (HALF - at) % LANES, 1)
                both = jnp.where(lane < HALF, first, last)
                if plan.slot < HALF:
                    both = jnp.where(lane % HALF < plan.slot, both, 0.0)
                pay_ref[dest, s * half : (s + 1) * half, :] = both.astype(BF16)
                head = (chunk * tile + offset) // plan.head_width
                heads_of.append(head)
                dts += [steps[head : head + 1, :LANES], steps[head : head + 1, LANES:]]
            dts.append(rate_row(heads_of, rx_ref, ry_ref))
            pay_ref[dest, plan.at_bc : plan.at_bc + plan.bc, :] = bc[:, :LANES]
            pay_ref[dest, plan.at_bc + plan.bc : plan.at_dt, :] = bc[:, LANES:]
            spare = plan.message - plan.at_dt - len(dts)
            dts += [jnp.zeros((spare, LANES), F32)] if spare else []
            pay_ref[dest, plan.at_dt : plan.message, :] = jnp.concatenate(dts, axis=0).astype(BF16)
        at = slice(chunk * per, (chunk + 1) * per)
        sent.append(pltpu.make_async_copy(pay_ref.at[at], pay_hbm.at[at], out_sems.at[chunk]))
        sent[-1].start()
    for copy in sent:
        copy.wait()


def project(plan, consts, slide, w_in, w_bcd, tissue, dt_bias, rate_x, rate_y):
    chunks = 2
    tile = plan.width // chunks
    depth = slide.shape[2]
    args = [dt_bias, rate_x, rate_y, slide, w_in, w_bcd.T, tissue.T, consts["lanei"], consts["lanej"]]
    count = 2 * plan.states + plan.heads
    assert plan.width % chunks == 0 and tile % plan.group == 0 and tile % LANES == 0
    message = (plan.devices, plan.message, LANES)
    outs = [((2 * LANES, plan.width), BF16), (message, BF16), ((count, 2 * LANES), F32), ((plan.cells, depth), BF16)]
    specs = [full(s) for s, _ in outs]
    specs[1] = HBM
    return pl.pallas_call(
        functools.partial(project_kernel, plan, chunks),
        grid=(1,),
        in_specs=[HBM] * len(args),
        out_specs=specs,
        out_shape=[jax.ShapeDtypeStruct(s, d) for s, d in outs],
        scratch_shapes=[
            pltpu.SMEM(dt_bias.shape, F32),
            pltpu.SMEM(rate_x.shape, F32),
            pltpu.SMEM(rate_y.shape, F32),
            pltpu.VMEM(slide.shape, BF16),
            pltpu.VMEM((chunks, depth, tile), BF16),
        ]
        + [pltpu.VMEM(x.shape, x.dtype) for x in args[5:]]
        + [
            pltpu.VMEM(message, BF16),
            pltpu.VMEM((plan.cells, depth), F32),
            pltpu.SemaphoreType.DMA((8,)),
            pltpu.SemaphoreType.DMA((chunks,)),
            pltpu.SemaphoreType.DMA((chunks,)),
        ],
        compiler_params=pltpu.CompilerParams(vmem_limit_bytes=24 * 2**20),
        name="project",
    )(*[in_hbm(x) for x in args])


def home_kernel(
    plan, rx_ref, ry_ref, skip_ref, w_hbm, v_ref, rows_ref, flat_ref, t_ref, gain_ref,
    own1_ref, own2_ref, from1_ref, from2_ref, mask_ref, out_ref, gate_hbm, gain_out, pair, w_ref, gate_ref, sem, gate_sem,
):
    states, cells, half = plan.states, plan.cells, plan.half
    copy = pltpu.make_async_copy(w_hbm.at[:, plan.width :], w_ref, sem)
    copy.start()
    gain_out[...] = gain_ref[...]
    b = rows_ref[0:states, :].astype(BF16)
    c = rows_ref[states : 2 * states, :].astype(BF16)
    pairs = tn_dot(c, b)
    pairs = jnp.concatenate([pairs[:half], pairs[LANES : LANES + cells - half]], axis=0)
    pair[...] = pairs * mask_ref[...].astype(F32)
    lane = lax.broadcasted_iota(jnp.int32, (cells, LANES), 1)
    per = LANES // plan.head_width
    for block in range(plan.width // LANES):
        v = v_ref[:, block * LANES : (block + 1) * LANES]
        vc = jnp.concatenate([v[:half], v[LANES : LANES + cells - half]], axis=0).astype(F32)
        total = None
        for k in range(per):
            h = block * per + k
            dt = rows_ref[2 * states + h : 2 * states + h + 1, :]
            low = dt.astype(BF16)
            x = mm(own1_ref[...] * low, from1_ref[...])
            y = mm(own2_ref[...] * low, from2_ref[...])
            weight = jnp.exp(-(rx_ref[h] * x + ry_ref[h] * y)) * pair[...] * dt
            part = mm(weight.astype(BF16), v) + skip_ref[h] * vc
            total = part if total is None else jnp.where(lane < k * plan.head_width, total, part)
        out_ref[:, block * LANES : (block + 1) * LANES] = total.astype(BF16)
    keep = cell_mask_of(plan, t_ref)
    copy.wait()
    tile = 2 * LANES
    for block in range(plan.width // tile):
        at = slice(block * tile, (block + 1) * tile)
        z = mm(flat_ref[...], w_ref[:, at]).astype(BF16).astype(F32)
        gate_ref[:, at] = (z * (1.0 / (1.0 + jnp.exp(-z))) * keep).astype(BF16)
    copy = pltpu.make_async_copy(gate_ref, gate_hbm, gate_sem)
    copy.start()
    copy.wait()


def home(plan, consts, v, rows, flat, w_in, tissue, gain, rate_x, rate_y, d_skip):
    args = [in_hbm(w_in), v, rows, flat, in_hbm(tissue.T), in_hbm(gain)]
    args += [consts[k] for k in ("own1", "own2", "from1", "from2", "ownmask")]
    outs = [((plan.cells, plan.width), BF16), ((plan.cells, plan.width), BF16), (gain.shape, F32)]
    return pl.pallas_call(
        functools.partial(home_kernel, plan),
        grid=(1,),
        in_specs=[SMEM, SMEM, SMEM, HBM] + [full(x.shape) for x in args[1:]],
        out_specs=[full(outs[0][0]), HBM, full(outs[2][0])],
        out_shape=[jax.ShapeDtypeStruct(s, d) for s, d in outs],
        scratch_shapes=[
            pltpu.VMEM((plan.cells, 2 * LANES), F32),
            pltpu.VMEM((w_in.shape[0], w_in.shape[1] - plan.width), BF16),
            pltpu.VMEM((plan.cells, plan.width), BF16),
            pltpu.SemaphoreType.DMA,
            pltpu.SemaphoreType.DMA,
        ],
        compiler_params=pltpu.CompilerParams(vmem_limit_bytes=24 * 2**20),
        name="home",
    )(in_hbm(rate_x), in_hbm(rate_y), in_hbm(d_skip), *args)


def ones(mask):
    return jnp.where(mask, 1.0, 0.0).astype(BF16)


def places(plan, shape, axis):
    at = lax.broadcasted_iota(jnp.int32, shape, axis)
    late = at >= LANES
    at = jnp.where(late, at - LANES, at)
    i = lax.div(at, plan.col_pad)
    j = at - i * plan.col_pad
    real = (at < jnp.where(late, plan.cells - plan.half, plan.half)) & (j < plan.cols)
    return jnp.where(late, i + plan.upper, i), j, real


def wide_rows(pay_ref, t, at, count, gap):
    return jnp.concatenate([pay_ref[t, at : at + count, :], pay_ref[t, at + gap : at + gap + count, :]], axis=1)


def turned(plan, pay_ref, t, s):
    v = pay_ref[t, s * plan.half : (s + 1) * plan.half, :].astype(F32)
    if plan.half < LANES:
        v = jnp.concatenate([v, jnp.zeros((LANES - plan.half, LANES), F32)], axis=0)
    v = v.T
    return jnp.concatenate([v[:HALF], v[HALF:]], axis=1).astype(BF16)


def load_steps(plan, pay_ref, dts):
    for t in range(plan.devices):
        rows = pay_ref[t, plan.at_dt : plan.message, :].astype(F32)
        for s in range(plan.slots):
            w = s * plan.devices + t
            dts[w : w + 1, :LANES] = rows[2 * s : 2 * s + 1]
            dts[w : w + 1, LANES:] = rows[2 * s + 1 : 2 * s + 2]


def rates_of(plan, pay_ref, kind):
    row = pay_ref[0, plan.at_dt : plan.message, :].astype(F32)[plan.at_rate - plan.at_dt : plan.at_rate - plan.at_dt + 1]
    at = lax.broadcasted_iota(jnp.int32, (1, LANES), 1)
    first = [8 * s + 3 * kind for s in range(plan.slots)]
    return [jnp.sum(jnp.where((at >= f) & (at < f + 3), row, 0.0), axis=1, keepdims=True) for f in first]


def slot_rates(plan, pay_ref, kind):
    return jnp.concatenate(
        [jnp.broadcast_to(r, (plan.devices, 1)) for r in rates_of(plan, pay_ref, kind)], axis=0
    )


def pack_edges(plan, out_ref, held):
    for s in range(plan.slots):
        for k in range(plan.solid):
            out_ref[s * plan.solid + k] = held[s][:, k * LANES : (k + 1) * LANES].astype(BF16)
    if plan.tail:
        first = plan.slots * plan.solid
        for k in range(plan.packed - first):
            parts = [x[:, plan.solid * LANES :] for x in held[k * plan.share : (k + 1) * plan.share]]
            spare = LANES - plan.tail * len(parts)
            parts += [jnp.zeros((HALF, spare), F32)] if spare else []
            out_ref[first + k] = jnp.concatenate(parts, axis=1).astype(BF16)


def unpack_edges(plan, ref, s):
    parts = [ref[s * plan.solid + k].astype(F32) for k in range(plan.solid)]
    if plan.tail:
        last = ref[plan.slots * plan.solid + s // plan.share].astype(F32)
        at = s % plan.share * plan.tail
        parts.append(last[:, at : at + plan.tail])
    return jnp.concatenate(parts, axis=1)


def scan_edges(plan, pay_ref, dts, inner, kept, seen):
    states, tiles, wide = plan.states, plan.devices, 2 * LANES
    i, j, real = places(plan, (wide, wide), 0)
    ti, tj, treal = places(plan, (wide, wide), 1)
    from1 = ones((i == ti) & (j > tj) & real & treal)
    edge_row = lax.div(lax.broadcasted_iota(jnp.int32, (wide, plan.edge), 1), states)
    i, _, real = places(plan, (wide, plan.edge), 0)
    keep = ones((i == edge_row) & real)
    ti, _, treal = places(plan, (plan.rows, wide), 1)
    rowsel = ones((ti == lax.broadcasted_iota(jnp.int32, (plan.rows, wide), 0)) & treal)
    dt = dts[...]
    low = dt.astype(BF16)
    rate = slot_rates(plan, pay_ref, 0)
    inner[...] = jnp.exp(-rate * mm(low, from1)) * dt
    kept[...] = jnp.exp(-rate * mm(low, keep))
    ends = []
    for s in range(plan.slots):
        held = jnp.zeros((HALF, plan.edge), F32)
        product = jnp.ones((1, plan.edge), F32)
        for t in range(tiles):
            w = s * tiles + t
            seen(w, held, product)
            b = wide_rows(pay_ref, t, plan.at_bc, states, plan.bc).astype(F32)
            bd = (b * inner[w : w + 1, :]).astype(BF16)
            left = jnp.concatenate([bd * rowsel[i : i + 1] for i in range(plan.rows)], axis=0)
            now = kept[w : w + 1, :]
            held = held * now + nt_dot(turned(plan, pay_ref, t, s), left)
            product = product * now
        ends.append(held)
    return ends


def last_kernel(plan, axis, pay_ref, last_ref, dts, inner):
    @pl.when(lax.axis_index(axis) < (plan.parts - 1) * plan.devices)
    def _():
        states, tiles, wide = plan.states, plan.devices, 2 * LANES
        load_steps(plan, pay_ref, dts)
        i, j, real = places(plan, (wide, wide), 0)
        ti, tj, treal = places(plan, (wide, wide), 1)
        same = (i == ti) & real & treal
        ti, _, treal = places(plan, (plan.rows, wide), 1)
        rowsel = ones((ti == lax.broadcasted_iota(jnp.int32, (plan.rows, wide), 0)) & treal)
        low = dts[...].astype(BF16)
        rest, whole = mm(low, ones(same & (j > tj))), mm(low, ones(same))
        left = []
        for s in range(plan.slots):
            after = jnp.zeros((1, wide), F32)
            rows = []
            for t in reversed(range(tiles)):
                rows.append(after)
                after = after + whole[s * tiles + t : s * tiles + t + 1]
            left += rows[::-1]
        inner[...] = jnp.exp(-slot_rates(plan, pay_ref, 0) * (rest + jnp.concatenate(left, axis=0))) * dts[...]
        ends = []
        for s in range(plan.slots):
            held = None
            for t in range(tiles):
                w = s * tiles + t
                b = wide_rows(pay_ref, t, plan.at_bc, states, plan.bc).astype(F32)
                bd = (b * inner[w : w + 1, :]).astype(BF16)
                left = jnp.concatenate([bd * rowsel[i : i + 1] for i in range(plan.rows)], axis=0)
                part = nt_dot(turned(plan, pay_ref, t, s), left)
                held = part if held is None else held + part
            ends.append(held)
        pack_edges(plan, last_ref, ends)


def maps_kernel(
    plan, pay_ref, to1_ref, to2_ref, from1_ref, from2_ref, side1_ref, side2_ref,
    sidemask_ref, down1_ref, down2_ref, downmask_ref, pick_ref,
    side_ref, above_ref, passed_ref, top_ref, edge_ref, upto_ref, dts, inner, kept, s1, s2, d1, d2,
):
    states, tiles, cp, work = plan.states, plan.devices, plan.col_pad, plan.work
    rp = side1_ref.shape[0]
    load_steps(plan, pay_ref, dts)

    def seen(w, held, product):
        edge_ref[w] = held.astype(BF16)
        upto_ref[w : w + 1, :] = product

    scan_edges(plan, pay_ref, dts, inner, kept, seen)
    low = dts[...].astype(BF16)
    above_ref[...] = jnp.exp(-slot_rates(plan, pay_ref, 1) * mm(low, to2_ref[...]))
    rates_x, rates_y = rates_of(plan, pay_ref, 0), rates_of(plan, pay_ref, 1)
    for w in range(work):
        rf = dts[w : w + 1, :]
        s1[w * rp : (w + 1) * rp, :] = side1_ref[...].astype(F32) * rf
        s2[w * rp : (w + 1) * rp, :] = side2_ref[...].astype(F32) * rf
        d1[w * cp : (w + 1) * cp, :] = down1_ref[...].astype(F32) * rf
        d2[w * cp : (w + 1) * cp, :] = down2_ref[...].astype(F32) * rf
    mask = sidemask_ref[...].astype(F32)
    x, y = mm(s1[...].astype(BF16), to1_ref[...]), mm(s2[...].astype(BF16), to2_ref[...])
    shape = (states, plan.top)
    n = lax.broadcasted_iota(jnp.int32, shape, 0)
    diag = ones(n == lax.div(lax.broadcasted_iota(jnp.int32, shape, 1), cp))
    for w in range(work):
        s = w // tiles
        at = slice(w * rp, (w + 1) * rp)
        side = (jnp.exp(-(rates_x[s] * x[at] + rates_y[s] * y[at])) * mask).astype(BF16)
        side_ref[w] = side
        bottom = mm(side, pick_ref[...]).astype(BF16)
        passed_ref[w] = jnp.concatenate([diag * bottom[i : i + 1] for i in range(plan.rows)], axis=0)
    x, y = mm(d1[...].astype(BF16), from1_ref[...]), mm(d2[...].astype(BF16), from2_ref[...])
    mask = downmask_ref[...].astype(F32)
    for w in range(work):
        s, t = w // tiles, w % tiles
        at = slice(w * cp, (w + 1) * cp)
        fall = jnp.exp(-(rates_x[s] * x[at] + rates_y[s] * y[at])) * mask * dts[w : w + 1, :]
        b = wide_rows(pay_ref, t, plan.at_bc, states, plan.bc).astype(F32)
        falls = jnp.concatenate([fall * b[n : n + 1] for n in range(states)], axis=0).astype(BF16)
        top_ref[w] = nt_dot(turned(plan, pay_ref, t, s), falls) + mm(edge_ref[w], passed_ref[w])


def join_kernel(plan, upto_ref, entry_ref, passed_ref, top_ref, out_ref):
    for s in range(plan.slots):
        entry = unpack_edges(plan, entry_ref, s)
        for t in range(plan.devices):
            w = s * plan.devices + t
            late = (entry * upto_ref[w : w + 1, :]).astype(BF16)
            out_ref[w] = (top_ref[w] + mm(late, passed_ref[w])).astype(BF16)


def sides_kernel(plan, pay_ref, edge_ref, upto_ref, entry_ref, side_ref, above_ref, y_ref, down_ref):
    states, tiles = plan.states, plan.devices
    shape = (plan.col_pad, 2 * LANES)
    _, tj, treal = places(plan, shape, 1)
    colsel = jnp.where((tj == lax.broadcasted_iota(jnp.int32, shape, 0)) & treal, 1.0, 0.0)
    for s in range(plan.slots):
        entry = unpack_edges(plan, entry_ref, s)
        for t in range(tiles):
            w = s * tiles + t
            c = wide_rows(pay_ref, t, plan.at_bc + states, states, plan.bc)
            side = side_ref[w]
            left = jnp.concatenate([c * side[i : i + 1] for i in range(plan.rows)], axis=0)
            whole = (edge_ref[w].astype(F32) + entry * upto_ref[w : w + 1, :]).astype(BF16)
            y_ref[w] = mm(whole, left)
            ca = c.astype(F32) * above_ref[w : w + 1, :]
            down_ref[w] = jnp.concatenate([colsel * ca[n : n + 1] for n in range(states)], axis=0).astype(BF16)


def cells_kernel(plan, y_ref, down_ref, top_ref, out_ref):
    for w in range(plan.work):
        t, s = w % plan.devices, w // plan.devices
        y = y_ref[w] + mm(top_ref[w], down_ref[w])
        y = jnp.concatenate([y[:, :LANES], y[:, LANES:]], axis=0).T
        out_ref[t, s * plan.half : (s + 1) * plan.half, :] = y[: plan.half].astype(BF16)


def call(kernel, name, args, outs, scratch=(), out_specs=None):
    return pl.pallas_call(
        kernel,
        grid=(1,),
        in_specs=[full(x.shape) for x in args],
        out_specs=out_specs or [full(s) for s, _ in outs],
        out_shape=[jax.ShapeDtypeStruct(s, d) for s, d in outs],
        scratch_shapes=[x if not isinstance(x, tuple) else pltpu.VMEM(*x) for x in scratch],
        compiler_params=pltpu.CompilerParams(vmem_limit_bytes=24 * 2**20),
        name=name,
    )(*args)


def scan_calls(plan, consts, row_axis, col_axis, pay):
    work, cp, wide = plan.work, plan.col_pad, 2 * LANES
    rp = consts["side1"].shape[0]
    steps = [((work, wide), F32), ((work, wide), F32), ((work, plan.edge), F32)]
    shape = (plan.packed, HALF, LANES)
    if plan.parts > 1:
        last = call(functools.partial(last_kernel, plan, col_axis), "last", [pay], [(shape, BF16)], steps[:2])[0]
        entry = lax.ppermute(last, col_axis, [(k, k + plan.devices) for k in range(plan.devices)])
    else:
        entry = jnp.zeros(shape, BF16)
    names = ("to1", "to2", "from1", "from2", "side1", "side2", "sidemask", "down1", "down2", "downmask", "pick")
    side, above, passed, tops, edges, upto = call(
        functools.partial(maps_kernel, plan),
        "maps",
        [pay] + [consts[k] for k in names],
        [
            ((work, rp, wide), BF16),
            ((work, wide), F32),
            ((work, plan.edge, plan.top), BF16),
            ((work, HALF, plan.top), F32),
            ((work, HALF, plan.edge), BF16),
            ((work, plan.edge), F32),
        ],
        steps + [((work * rp, wide), F32)] * 2 + [((work * cp, wide), F32)] * 2,
    )
    edge_entry = entry
    tops = call(
        functools.partial(join_kernel, plan),
        "join",
        [upto, entry, passed, tops],
        [((work, HALF, plan.top), BF16)],
    )[0]
    count = lax.axis_size(row_axis)
    chain = [(r, r + 1) for r in range(count - 1)]
    entry = lax.ppermute(tops, row_axis, chain)
    if count > 2:
        keep = jnp.dot(above.astype(BF16), consts["pick"], preferred_element_type=F32)[:, None, :]
        for _ in range(count - 2):
            entry = lax.ppermute(
                (tops.astype(F32) + keep * entry.astype(F32)).astype(BF16), row_axis, chain
            )
    y, down = call(
        functools.partial(sides_kernel, plan),
        "sides",
        [pay, edges, upto, edge_entry, side, above],
        [((work, HALF, wide), F32), ((work, plan.top, wide), BF16)],
    )
    return call(
        functools.partial(cells_kernel, plan),
        "cells",
        [y, down, entry],
        [((plan.devices, plan.slots * plan.half, LANES), BF16)],
    )[0]


def finish_kernel(plan, y_ref, own_ref, gate_ref, gain_ref, w_ref, out_hbm, full_ref, out_ref, sems):
    half, cells = plan.half, plan.cells
    slot, slots = plan.slot, plan.slots
    per = LANES // slot
    lane = lax.broadcasted_iota(jnp.int32, (half, LANES), 1)
    for block in range(plan.width // LANES):
        for k, (lo, hi) in enumerate(((0, half), (half, cells))):
            joined = None
            for d in range(per):
                at = block * per + d
                part = y_ref[at // slots, at % slots * half : (at % slots + 1) * half, :].astype(F32)
                shift = (d * slot - k * HALF) % LANES
                if shift:
                    part = pltpu.roll(part, shift, 1)
                joined = part if joined is None else jnp.where(lane < d * slot, joined, part)
            at = slice(block * LANES, (block + 1) * LANES)
            y = joined[: hi - lo] + own_ref[lo:hi, at].astype(F32)
            full_ref[lo:hi, at] = y.astype(BF16).astype(F32) * gate_ref[lo:hi, at].astype(F32)
    gated = full_ref[...]
    scale = lax.rsqrt(jnp.mean(gated * gated, axis=-1, keepdims=True) + norm_eps)
    normed = (gated * scale * gain_ref[...]).astype(BF16)
    copies = []
    chunks = sems.shape[0]
    tile = w_ref.shape[1] // chunks
    for k in range(chunks):
        at = slice(k * tile, (k + 1) * tile)
        out = mm(normed, w_ref[:, at])
        for i in range(plan.rows):
            out_ref[i, :, at] = out[i * plan.col_pad : i * plan.col_pad + plan.cols].astype(BF16)
        copies.append(pltpu.make_async_copy(out_ref.at[:, :, at], out_hbm.at[:, :, at], sems.at[k]))
        copies[-1].start()
    for copy in copies:
        copy.wait()


def finish(plan, y, own, gate, gain, w_out):
    args = (y, own, gate, gain, w_out)
    shape = (plan.rows, plan.cols, w_out.shape[1])
    assert w_out.shape[1] == plan.width
    return call(
        functools.partial(finish_kernel, plan),
        "finish",
        args,
        [(shape, BF16)],
        [((plan.cells, plan.width), F32), (shape, BF16), pltpu.SemaphoreType.DMA((4,))],
        [HBM],
    )[0]


def per_device(slide, tissue, w_in, w_bcd, dt_bias, rate_x, rate_y, d_skip, norm_gain, w_out):
    rows, cols, model_width = slide.shape
    width = w_out.shape[0]
    heads = dt_bias.shape[0]
    states = (w_bcd.shape[1] - heads) // 2
    plan = Plan(rows, cols, states, heads, width, lax.axis_size("col"))
    consts = plan.constants()
    v, pay, table, x = project(plan, consts, slide, w_in, w_bcd, tissue, dt_bias, rate_x, rate_y)
    groups = plan.segments()
    pay = lax.all_to_all(pay, "col", 0, 0, tiled=True, axis_index_groups=groups)
    gain = norm_gain.reshape(1, width)
    own, gate, gain = home(plan, consts, v, table, x, w_in, tissue, gain, rate_x, rate_y, d_skip)
    pay, own, gate, gain = lax.optimization_barrier((pay, own, gate, gain))
    y = scan_calls(plan, consts, "row", "col", pay)
    y = lax.all_to_all(y, "col", 0, 0, tiled=True, axis_index_groups=groups)
    return finish(plan, y, own, gate, gain, w_out)


def solution(mesh):
    placed = (
        P(("slides", "row"), "col", None),
        P(("slides", "row"), "col"),
        P(),
        P(),
        P(),
        P(),
        P(),
        P(),
        P(),
        P(),
    )
    return jax.shard_map(
        per_device,
        mesh=mesh,
        in_specs=placed,
        out_specs=P(("slides", "row"), "col", None),
        check_vma=False,
    )
```

```python
import functools

import jax
import jax.numpy as jnp
import numpy as np
from jax import lax
from jax.experimental import pallas as pl
from jax.experimental.pallas import tpu as pltpu
from jax.sharding import PartitionSpec as P

norm_eps = 1e-05
LANES = 128
HALF = LANES // 2
F32 = jnp.float32
BF16 = jnp.bfloat16


def round_up(value, step):
    return -(-value // step) * step


def in_hbm(x):
    return pltpu.with_memory_space_constraint(x, pltpu.HBM)


def mm(a, b):
    return jnp.dot(a, b, preferred_element_type=F32)


def nt_dot(a, b):
    return lax.dot_general(a, b, (((1,), (1,)), ((), ())), preferred_element_type=F32)


def tn_dot(a, b):
    return lax.dot_general(a, b, (((0,), (0,)), ((), ())), preferred_element_type=F32)


class Plan:
    def __init__(self, rows, cols, states, heads, width, devices):
        self.rows, self.cols, self.states, self.heads = rows, cols, states, heads
        self.width = width
        self.parts = 2 if devices % 2 == 0 and devices > 2 else 1
        self.devices = devices // self.parts
        self.group = width // self.devices
        self.slot = min(self.group, HALF)
        self.slots = self.group // self.slot
        self.work = self.slots * self.devices
        self.head_width = width // heads
        self.col_pad = round_up(cols, 8)
        self.count = rows * cols
        self.half = self.count // 2 // 8 * 8
        self.cells = round_up(self.count, 8)
        self.stride = max(self.half, self.cells - self.half)
        self.edge = rows * states
        self.top = states * self.col_pad
        self.bc = 2 * states
        self.at_bc = self.slots * self.stride
        self.at_dt = self.at_bc + 2 * self.bc
        self.at_rate = self.at_dt + 2 * self.slots
        self.message = round_up(self.at_rate + 1, 8)
        self.tail = self.edge % LANES
        self.solid = self.edge // LANES
        self.share = LANES // self.tail if self.tail else 1
        self.packed = self.slots * self.solid + (-(-self.slots // self.share) if self.tail else 0)
        assert self.head_width % self.slot == 0 and self.group % self.slot == 0
        assert LANES % self.head_width == 0 and self.stride <= LANES
        assert states % 16 == 0 and heads % 8 == 0

    def segments(self):
        return [list(range(p * self.devices, (p + 1) * self.devices)) for p in range(self.parts)]

    def lanes(self):
        at = np.arange(2 * LANES)
        cell = np.where(at < LANES, at, at - LANES + self.half)
        live = np.where(at < LANES, at < self.half, cell < self.count)
        return cell // self.cols, cell % self.cols, live

    def constants(self):
        i, j, real = self.lanes()
        both = real[:, None] & real[None]
        cell = np.arange(self.cells)
        ci, cj = cell // self.cols, cell % self.cols
        creal = cell < self.count
        le = np.arange(round_up(self.rows, 8))
        lj = np.arange(self.col_pad)
        out = {}
        out["to1"] = (j[:, None] <= j[None]) & both
        out["to2"] = (j[:, None] == j[None]) & (i[:, None] <= i[None]) & both
        out["from1"] = (i[:, None] == i[None]) & (j[:, None] > j[None]) & both
        out["from2"] = (i[:, None] > i[None]) & both
        out["side1"] = (i[None] == le[:, None]) & real[None]
        out["side2"] = (i[None] > le[:, None]) & real[None]
        out["sidemask"] = (i[None] >= le[:, None]) & (le < self.rows)[:, None] & real[None]
        out["down1"] = (j[None] <= lj[:, None]) & real[None]
        out["down2"] = (j[None] == lj[:, None]) & real[None]
        out["downmask"] = (j[None] <= lj[:, None]) & (lj < self.cols)[:, None] & real[None]
        out["pick"] = (
            (i == self.rows - 1)[:, None] & real[:, None] & (j[:, None] == np.tile(lj, self.states)[None])
        )
        cboth = creal[:, None] & real[None]
        out["own1"] = (j[None] <= cj[:, None]) & cboth
        out["own2"] = (j[None] == cj[:, None]) & (i[None] <= ci[:, None]) & cboth
        out["ownmask"] = (i[None] <= ci[:, None]) & (j[None] <= cj[:, None]) & cboth
        out["lanei"] = (np.arange(self.rows)[:, None] == i[None]) & real[None]
        out["lanej"] = (np.arange(self.cols)[:, None] == j[None]) & real[None]
        return {k: in_hbm(jnp.asarray(x.astype(np.float32), BF16)) for k, x in out.items()}


def full(shape):
    return pl.BlockSpec(shape, lambda *_: (0,) * len(shape))


HBM = pl.BlockSpec(memory_space=pltpu.HBM)
SMEM = pl.BlockSpec(memory_space=pltpu.SMEM)


def split_cell(plan, cell):
    i = lax.shift_right_logical(cell * (-(-65536 // plan.cols)), 16)
    return i, cell - i * plan.cols


def cell_mask_of(plan, t_ref):
    t = t_ref[...].astype(F32).astype(BF16)
    shape = (plan.cells, plan.cols)
    _, j = split_cell(plan, lax.broadcasted_iota(jnp.int32, shape, 0))
    pick = ones(j == lax.broadcasted_iota(jnp.int32, shape, 1))
    shape = (plan.cells, plan.rows)
    i, _ = split_cell(plan, lax.broadcasted_iota(jnp.int32, shape, 0))
    here = i == lax.broadcasted_iota(jnp.int32, shape, 1)
    return jnp.sum(jnp.where(here, mm(pick, t), 0.0), axis=1, keepdims=True)


def rate_row(heads_of, rx_ref, ry_ref):
    at = lax.broadcasted_iota(jnp.int32, (1, LANES), 1)
    rate = jnp.zeros((1, LANES), F32)
    part = jnp.zeros((1, LANES), jnp.int32)
    for s, head in enumerate(heads_of):
        for k, ref in enumerate((rx_ref, ry_ref)):
            first = 8 * s + 3 * k
            here = (at >= first) & (at < first + 3)
            rate = jnp.where(here, ref[head], rate)
            part = jnp.where(here, at - first, part)
    high = rate.astype(BF16).astype(F32)
    middle = (rate - high).astype(BF16).astype(F32)
    low = rate - high - middle
    return jnp.where(part == 0, high, jnp.where(part == 1, middle, low))


def project_kernel(
    plan, chunks, bias_hbm, rx_hbm, ry_hbm, x_hbm, w_hbm, wt_hbm, t_hbm, lanei_hbm, lanej_hbm,
    v_ref, pay_hbm, rows_ref, flat_ref,
    bias_ref, rx_ref, ry_ref, x_ref, w_ref, wt_ref, t_ref, lanei_ref, lanej_ref, pay_ref, wide, sems, w_sems, out_sems,
):
    group, states, cells, heads = plan.group, plan.states, plan.cells, plan.heads
    half, rest = plan.half, plan.cells - plan.half
    tile = plan.width // chunks
    pairs = (
        (x_hbm, x_ref), (t_hbm, t_ref), (wt_hbm, wt_ref), (lanei_hbm, lanei_ref), (lanej_hbm, lanej_ref),
        (bias_hbm, bias_ref), (rx_hbm, rx_ref), (ry_hbm, ry_ref),
    )
    loads = [pltpu.make_async_copy(a, b, sems.at[k]) for k, (a, b) in enumerate(pairs)]
    copies = [
        pltpu.make_async_copy(w_hbm.at[:, k * tile : (k + 1) * tile], w_ref.at[k], w_sems.at[k])
        for k in range(chunks)
    ]
    for copy in loads + copies:
        copy.start()
    wide[...] = jnp.zeros_like(wide)
    v_ref[half:LANES, :] = jnp.zeros((LANES - half, plan.width), BF16)
    v_ref[LANES + rest :, :] = jnp.zeros((LANES - rest, plan.width), BF16)

    loads[0].wait()
    for i in range(plan.rows):
        wide[i * plan.cols : (i + 1) * plan.cols, :] = x_ref[i].astype(F32)
    x = wide[...].astype(BF16)
    flat_ref[...] = x
    for copy in loads[1:]:
        copy.wait()
    keep = cell_mask_of(plan, t_ref)
    t = t_ref[...].astype(F32).astype(BF16)
    m = jnp.sum(mm(t, lanei_ref[...]) * lanej_ref[...].astype(F32), axis=0, keepdims=True)
    table = nt_dot(wt_ref[...], x)
    ext = jnp.concatenate([table, jnp.zeros((table.shape[0], 2 * LANES - cells), F32)], axis=1)
    lane = lax.broadcasted_iota(jnp.int32, (table.shape[0], LANES), 1)
    lo, hi = ext[:, :LANES], ext[:, LANES:]
    shift = half % LANES
    if shift:
        moved = jnp.where(
            lane < LANES - shift, pltpu.roll(lo, LANES - shift, 1), pltpu.roll(hi, LANES - shift, 1)
        )
    else:
        moved = hi
    table = jnp.concatenate([jnp.where(lane < half, lo, 0.0), jnp.where(lane < plan.count - half, moved, 0.0)], axis=1)
    z = table[2 * states :]
    at = lax.broadcasted_iota(jnp.int32, z.shape, 0)
    for h in range(heads):
        z = jnp.where(at == h, z + bias_ref[h], z)
    soft = m * (jnp.maximum(z, 0.0) + jnp.log1p(jnp.exp(-jnp.abs(z))))
    table = jnp.concatenate([table[: 2 * states], soft], axis=0).astype(BF16)
    rows_ref[...] = table.astype(F32)
    bc = table[: 2 * states]
    steps = rows_ref[2 * states :, :]

    lane = lax.broadcasted_iota(jnp.int32, (plan.stride, LANES), 1)
    sent = []
    for chunk in range(chunks):
        copies[chunk].wait()
        v = mm(flat_ref[...], w_ref[chunk]).astype(BF16).astype(F32) * keep
        low = v.astype(BF16)
        v_ref[0:half, chunk * tile : (chunk + 1) * tile] = low[:half]
        v_ref[LANES : LANES + rest, chunk * tile : (chunk + 1) * tile] = low[half:]
        per = tile // group
        for k in range(per):
            dest = chunk * per + k
            dts, heads_of = [], []
            for s in range(plan.slots):
                offset = k * group + s * plan.slot
                base = offset // LANES * LANES
                at = offset % LANES
                first = v[:half, base : base + LANES]
                last = v[half:, base : base + LANES]
                if half < plan.stride:
                    first = jnp.concatenate([first, jnp.zeros((plan.stride - half, LANES), F32)], axis=0)
                if rest < plan.stride:
                    last = jnp.concatenate([last, jnp.zeros((plan.stride - rest, LANES), F32)], axis=0)
                if at:
                    first = pltpu.roll(first, LANES - at, 1)
                if at != HALF:
                    last = pltpu.roll(last, (HALF - at) % LANES, 1)
                both = jnp.where(lane < HALF, first, last)
                if plan.slot < HALF:
                    both = jnp.where(lane % HALF < plan.slot, both, 0.0)
                pay_ref[dest, s * plan.stride : (s + 1) * plan.stride, :] = both.astype(BF16)
                head = (chunk * tile + offset) // plan.head_width
                heads_of.append(head)
                dts += [steps[head : head + 1, :LANES], steps[head : head + 1, LANES:]]
            dts.append(rate_row(heads_of, rx_ref, ry_ref))
            pay_ref[dest, plan.at_bc : plan.at_bc + plan.bc, :] = bc[:, :LANES]
            pay_ref[dest, plan.at_bc + plan.bc : plan.at_dt, :] = bc[:, LANES:]
            spare = plan.message - plan.at_dt - len(dts)
            dts += [jnp.zeros((spare, LANES), F32)] if spare else []
            pay_ref[dest, plan.at_dt : plan.message, :] = jnp.concatenate(dts, axis=0).astype(BF16)
        at = slice(chunk * per, (chunk + 1) * per)
        sent.append(pltpu.make_async_copy(pay_ref.at[at], pay_hbm.at[at], out_sems.at[chunk]))
        sent[-1].start()
    for copy in sent:
        copy.wait()


def project(plan, consts, slide, w_in, w_bcd, tissue, dt_bias, rate_x, rate_y):
    chunks = 2
    tile = plan.width // chunks
    depth = slide.shape[2]
    args = [dt_bias, rate_x, rate_y, slide, w_in, w_bcd.T, tissue.T, consts["lanei"], consts["lanej"]]
    count = 2 * plan.states + plan.heads
    assert plan.width % chunks == 0 and tile % plan.group == 0 and tile % LANES == 0
    message = (plan.devices, plan.message, LANES)
    outs = [((2 * LANES, plan.width), BF16), (message, BF16), ((count, 2 * LANES), F32), ((plan.cells, depth), BF16)]
    specs = [full(s) for s, _ in outs]
    specs[1] = HBM
    return pl.pallas_call(
        functools.partial(project_kernel, plan, chunks),
        grid=(1,),
        in_specs=[HBM] * len(args),
        out_specs=specs,
        out_shape=[jax.ShapeDtypeStruct(s, d) for s, d in outs],
        scratch_shapes=[
            pltpu.SMEM(dt_bias.shape, F32),
            pltpu.SMEM(rate_x.shape, F32),
            pltpu.SMEM(rate_y.shape, F32),
            pltpu.VMEM(slide.shape, BF16),
            pltpu.VMEM((chunks, depth, tile), BF16),
        ]
        + [pltpu.VMEM(x.shape, x.dtype) for x in args[5:]]
        + [
            pltpu.VMEM(message, BF16),
            pltpu.VMEM((plan.cells, depth), F32),
            pltpu.SemaphoreType.DMA((8,)),
            pltpu.SemaphoreType.DMA((chunks,)),
            pltpu.SemaphoreType.DMA((chunks,)),
        ],
        compiler_params=pltpu.CompilerParams(vmem_limit_bytes=24 * 2**20),
        name="project",
    )(*[in_hbm(x) for x in args])


def home_kernel(
    plan, rx_ref, ry_ref, skip_ref, w_hbm, v_ref, rows_ref, flat_ref, t_ref, gain_ref,
    own1_ref, own2_ref, from1_ref, from2_ref, mask_ref, out_ref, gate_hbm, gain_out, pair, w_ref, gate_ref, sem, gate_sem,
):
    states, cells, half = plan.states, plan.cells, plan.half
    copy = pltpu.make_async_copy(w_hbm.at[:, plan.width :], w_ref, sem)
    copy.start()
    gain_out[...] = gain_ref[...]
    b = rows_ref[0:states, :].astype(BF16)
    c = rows_ref[states : 2 * states, :].astype(BF16)
    pairs = tn_dot(c, b)
    pairs = jnp.concatenate([pairs[:half], pairs[LANES : LANES + cells - half]], axis=0)
    pair[...] = pairs * mask_ref[...].astype(F32)
    lane = lax.broadcasted_iota(jnp.int32, (cells, LANES), 1)
    per = LANES // plan.head_width
    for block in range(plan.width // LANES):
        v = v_ref[:, block * LANES : (block + 1) * LANES]
        vc = jnp.concatenate([v[:half], v[LANES : LANES + cells - half]], axis=0).astype(F32)
        total = None
        for k in range(per):
            h = block * per + k
            dt = rows_ref[2 * states + h : 2 * states + h + 1, :]
            low = dt.astype(BF16)
            x = mm(own1_ref[...] * low, from1_ref[...])
            y = mm(own2_ref[...] * low, from2_ref[...])
            weight = jnp.exp(-(rx_ref[h] * x + ry_ref[h] * y)) * pair[...] * dt
            part = mm(weight.astype(BF16), v) + skip_ref[h] * vc
            total = part if total is None else jnp.where(lane < k * plan.head_width, total, part)
        out_ref[:, block * LANES : (block + 1) * LANES] = total.astype(BF16)
    keep = cell_mask_of(plan, t_ref)
    copy.wait()
    tile = 2 * LANES
    for block in range(plan.width // tile):
        at = slice(block * tile, (block + 1) * tile)
        z = mm(flat_ref[...], w_ref[:, at]).astype(BF16).astype(F32)
        gate_ref[:, at] = (z * (1.0 / (1.0 + jnp.exp(-z))) * keep).astype(BF16)
    copy = pltpu.make_async_copy(gate_ref, gate_hbm, gate_sem)
    copy.start()
    copy.wait()


def home(plan, consts, v, rows, flat, w_in, tissue, gain, rate_x, rate_y, d_skip):
    args = [in_hbm(w_in), v, rows, flat, in_hbm(tissue.T), in_hbm(gain)]
    args += [consts[k] for k in ("own1", "own2", "from1", "from2", "ownmask")]
    outs = [((plan.cells, plan.width), BF16), ((plan.cells, plan.width), BF16), (gain.shape, F32)]
    return pl.pallas_call(
        functools.partial(home_kernel, plan),
        grid=(1,),
        in_specs=[SMEM, SMEM, SMEM, HBM] + [full(x.shape) for x in args[1:]],
        out_specs=[full(outs[0][0]), HBM, full(outs[2][0])],
        out_shape=[jax.ShapeDtypeStruct(s, d) for s, d in outs],
        scratch_shapes=[
            pltpu.VMEM((plan.cells, 2 * LANES), F32),
            pltpu.VMEM((w_in.shape[0], w_in.shape[1] - plan.width), BF16),
            pltpu.VMEM((plan.cells, plan.width), BF16),
            pltpu.SemaphoreType.DMA,
            pltpu.SemaphoreType.DMA,
        ],
        compiler_params=pltpu.CompilerParams(vmem_limit_bytes=24 * 2**20),
        name="home",
    )(in_hbm(rate_x), in_hbm(rate_y), in_hbm(d_skip), *args)


def ones(mask):
    return jnp.where(mask, 1.0, 0.0).astype(BF16)


def places(plan, shape, axis):
    at = lax.broadcasted_iota(jnp.int32, shape, axis)
    late = at >= LANES
    cell = jnp.where(late, at - (LANES - plan.half), at)
    i, j = split_cell(plan, cell)
    return i, j, cell < jnp.where(late, plan.count, plan.half)


def wide_rows(pay_ref, t, at, count, gap):
    return jnp.concatenate([pay_ref[t, at : at + count, :], pay_ref[t, at + gap : at + gap + count, :]], axis=1)


def turned(plan, pay_ref, t, s):
    v = pay_ref[t, s * plan.stride : (s + 1) * plan.stride, :].astype(F32)
    if plan.stride < LANES:
        v = jnp.concatenate([v, jnp.zeros((LANES - plan.stride, LANES), F32)], axis=0)
    v = v.T
    return jnp.concatenate([v[:HALF], v[HALF:]], axis=1).astype(BF16)


def load_steps(plan, pay_ref, dts):
    for t in range(plan.devices):
        rows = pay_ref[t, plan.at_dt : plan.message, :].astype(F32)
        for s in range(plan.slots):
            w = s * plan.devices + t
            dts[w : w + 1, :LANES] = rows[2 * s : 2 * s + 1]
            dts[w : w + 1, LANES:] = rows[2 * s + 1 : 2 * s + 2]


def rates_of(plan, pay_ref, kind):
    row = pay_ref[0, plan.at_dt : plan.message, :].astype(F32)[plan.at_rate - plan.at_dt : plan.at_rate - plan.at_dt + 1]
    at = lax.broadcasted_iota(jnp.int32, (1, LANES), 1)
    first = [8 * s + 3 * kind for s in range(plan.slots)]
    return [jnp.sum(jnp.where((at >= f) & (at < f + 3), row, 0.0), axis=1, keepdims=True) for f in first]


def slot_rates(plan, pay_ref, kind):
    return jnp.concatenate(
        [jnp.broadcast_to(r, (plan.devices, 1)) for r in rates_of(plan, pay_ref, kind)], axis=0
    )


def pack_edges(plan, out_ref, held):
    for s in range(plan.slots):
        for k in range(plan.solid):
            out_ref[s * plan.solid + k] = held[s][:, k * LANES : (k + 1) * LANES].astype(BF16)
    if plan.tail:
        first = plan.slots * plan.solid
        for k in range(plan.packed - first):
            parts = [x[:, plan.solid * LANES :] for x in held[k * plan.share : (k + 1) * plan.share]]
            spare = LANES - plan.tail * len(parts)
            parts += [jnp.zeros((HALF, spare), F32)] if spare else []
            out_ref[first + k] = jnp.concatenate(parts, axis=1).astype(BF16)


def unpack_edges(plan, ref, s):
    parts = [ref[s * plan.solid + k].astype(F32) for k in range(plan.solid)]
    if plan.tail:
        last = ref[plan.slots * plan.solid + s // plan.share].astype(F32)
        at = s % plan.share * plan.tail
        parts.append(last[:, at : at + plan.tail])
    return jnp.concatenate(parts, axis=1)


def scan_edges(plan, pay_ref, dts, inner, kept, seen):
    states, tiles, wide = plan.states, plan.devices, 2 * LANES
    i, j, real = places(plan, (wide, wide), 0)
    ti, tj, treal = places(plan, (wide, wide), 1)
    from1 = ones((i == ti) & (j > tj) & real & treal)
    edge_row = lax.div(lax.broadcasted_iota(jnp.int32, (wide, plan.edge), 1), states)
    i, _, real = places(plan, (wide, plan.edge), 0)
    keep = ones((i == edge_row) & real)
    ti, _, treal = places(plan, (plan.rows, wide), 1)
    rowsel = ones((ti == lax.broadcasted_iota(jnp.int32, (plan.rows, wide), 0)) & treal)
    dt = dts[...]
    low = dt.astype(BF16)
    rate = slot_rates(plan, pay_ref, 0)
    inner[...] = jnp.exp(-rate * mm(low, from1)) * dt
    kept[...] = jnp.exp(-rate * mm(low, keep))
    ends = []
    for s in range(plan.slots):
        held = jnp.zeros((HALF, plan.edge), F32)
        product = jnp.ones((1, plan.edge), F32)
        for t in range(tiles):
            w = s * tiles + t
            seen(w, held, product)
            b = wide_rows(pay_ref, t, plan.at_bc, states, plan.bc).astype(F32)
            bd = (b * inner[w : w + 1, :]).astype(BF16)
            left = jnp.concatenate([bd * rowsel[i : i + 1] for i in range(plan.rows)], axis=0)
            now = kept[w : w + 1, :]
            held = held * now + nt_dot(turned(plan, pay_ref, t, s), left)
            product = product * now
        ends.append(held)
    return ends


def last_kernel(plan, axis, pay_ref, last_ref, dts, inner):
    @pl.when(lax.axis_index(axis) < (plan.parts - 1) * plan.devices)
    def _():
        states, tiles, wide = plan.states, plan.devices, 2 * LANES
        load_steps(plan, pay_ref, dts)
        i, j, real = places(plan, (wide, wide), 0)
        ti, tj, treal = places(plan, (wide, wide), 1)
        same = (i == ti) & real & treal
        ti, _, treal = places(plan, (plan.rows, wide), 1)
        rowsel = ones((ti == lax.broadcasted_iota(jnp.int32, (plan.rows, wide), 0)) & treal)
        low = dts[...].astype(BF16)
        rest, whole = mm(low, ones(same & (j > tj))), mm(low, ones(same))
        left = []
        for s in range(plan.slots):
            after = jnp.zeros((1, wide), F32)
            rows = []
            for t in reversed(range(tiles)):
                rows.append(after)
                after = after + whole[s * tiles + t : s * tiles + t + 1]
            left += rows[::-1]
        inner[...] = jnp.exp(-slot_rates(plan, pay_ref, 0) * (rest + jnp.concatenate(left, axis=0))) * dts[...]
        ends = []
        for s in range(plan.slots):
            held = None
            for t in range(tiles):
                w = s * tiles + t
                b = wide_rows(pay_ref, t, plan.at_bc, states, plan.bc).astype(F32)
                bd = (b * inner[w : w + 1, :]).astype(BF16)
                left = jnp.concatenate([bd * rowsel[i : i + 1] for i in range(plan.rows)], axis=0)
                part = nt_dot(turned(plan, pay_ref, t, s), left)
                held = part if held is None else held + part
            ends.append(held)
        pack_edges(plan, last_ref, ends)


def maps_kernel(
    plan, pay_ref, to1_ref, to2_ref, from1_ref, from2_ref, side1_ref, side2_ref,
    sidemask_ref, down1_ref, down2_ref, downmask_ref, pick_ref,
    side_ref, above_ref, passed_ref, top_ref, edge_ref, upto_ref, dts, inner, kept, s1, s2, d1, d2,
):
    states, tiles, cp, work = plan.states, plan.devices, plan.col_pad, plan.work
    rp = side1_ref.shape[0]
    load_steps(plan, pay_ref, dts)

    def seen(w, held, product):
        edge_ref[w] = held.astype(BF16)
        upto_ref[w : w + 1, :] = product

    scan_edges(plan, pay_ref, dts, inner, kept, seen)
    low = dts[...].astype(BF16)
    above_ref[...] = jnp.exp(-slot_rates(plan, pay_ref, 1) * mm(low, to2_ref[...]))
    rates_x, rates_y = rates_of(plan, pay_ref, 0), rates_of(plan, pay_ref, 1)
    for w in range(work):
        rf = dts[w : w + 1, :]
        s1[w * rp : (w + 1) * rp, :] = side1_ref[...].astype(F32) * rf
        s2[w * rp : (w + 1) * rp, :] = side2_ref[...].astype(F32) * rf
        d1[w * cp : (w + 1) * cp, :] = down1_ref[...].astype(F32) * rf
        d2[w * cp : (w + 1) * cp, :] = down2_ref[...].astype(F32) * rf
    mask = sidemask_ref[...].astype(F32)
    x, y = mm(s1[...].astype(BF16), to1_ref[...]), mm(s2[...].astype(BF16), to2_ref[...])
    shape = (states, plan.top)
    n = lax.broadcasted_iota(jnp.int32, shape, 0)
    diag = ones(n == lax.div(lax.broadcasted_iota(jnp.int32, shape, 1), cp))
    for w in range(work):
        s = w // tiles
        at = slice(w * rp, (w + 1) * rp)
        side = (jnp.exp(-(rates_x[s] * x[at] + rates_y[s] * y[at])) * mask).astype(BF16)
        side_ref[w] = side
        bottom = mm(side, pick_ref[...]).astype(BF16)
        passed_ref[w] = jnp.concatenate([diag * bottom[i : i + 1] for i in range(plan.rows)], axis=0)
    x, y = mm(d1[...].astype(BF16), from1_ref[...]), mm(d2[...].astype(BF16), from2_ref[...])
    mask = downmask_ref[...].astype(F32)
    for w in range(work):
        s, t = w // tiles, w % tiles
        at = slice(w * cp, (w + 1) * cp)
        fall = jnp.exp(-(rates_x[s] * x[at] + rates_y[s] * y[at])) * mask * dts[w : w + 1, :]
        b = wide_rows(pay_ref, t, plan.at_bc, states, plan.bc).astype(F32)
        falls = jnp.concatenate([fall * b[n : n + 1] for n in range(states)], axis=0).astype(BF16)
        top_ref[w] = nt_dot(turned(plan, pay_ref, t, s), falls) + mm(edge_ref[w], passed_ref[w])


def join_kernel(plan, upto_ref, entry_ref, passed_ref, top_ref, out_ref):
    for s in range(plan.slots):
        entry = unpack_edges(plan, entry_ref, s)
        for t in range(plan.devices):
            w = s * plan.devices + t
            late = (entry * upto_ref[w : w + 1, :]).astype(BF16)
            out_ref[w] = (top_ref[w] + mm(late, passed_ref[w])).astype(BF16)


def sides_kernel(plan, pay_ref, edge_ref, upto_ref, entry_ref, side_ref, above_ref, y_ref, down_ref):
    states, tiles = plan.states, plan.devices
    shape = (plan.col_pad, 2 * LANES)
    _, tj, treal = places(plan, shape, 1)
    colsel = jnp.where((tj == lax.broadcasted_iota(jnp.int32, shape, 0)) & treal, 1.0, 0.0)
    for s in range(plan.slots):
        entry = unpack_edges(plan, entry_ref, s)
        for t in range(tiles):
            w = s * tiles + t
            c = wide_rows(pay_ref, t, plan.at_bc + states, states, plan.bc)
            side = side_ref[w]
            left = jnp.concatenate([c * side[i : i + 1] for i in range(plan.rows)], axis=0)
            whole = (edge_ref[w].astype(F32) + entry * upto_ref[w : w + 1, :]).astype(BF16)
            y_ref[w] = mm(whole, left)
            ca = c.astype(F32) * above_ref[w : w + 1, :]
            down_ref[w] = jnp.concatenate([colsel * ca[n : n + 1] for n in range(states)], axis=0).astype(BF16)


def cells_kernel(plan, y_ref, down_ref, top_ref, out_ref):
    for w in range(plan.work):
        t, s = w % plan.devices, w // plan.devices
        y = y_ref[w] + mm(top_ref[w], down_ref[w])
        y = jnp.concatenate([y[:, :LANES], y[:, LANES:]], axis=0).T
        out_ref[t, s * plan.stride : (s + 1) * plan.stride, :] = y[: plan.stride].astype(BF16)


def call(kernel, name, args, outs, scratch=(), out_specs=None):
    return pl.pallas_call(
        kernel,
        grid=(1,),
        in_specs=[full(x.shape) for x in args],
        out_specs=out_specs or [full(s) for s, _ in outs],
        out_shape=[jax.ShapeDtypeStruct(s, d) for s, d in outs],
        scratch_shapes=[x if not isinstance(x, tuple) else pltpu.VMEM(*x) for x in scratch],
        compiler_params=pltpu.CompilerParams(vmem_limit_bytes=24 * 2**20),
        name=name,
    )(*args)


def scan_calls(plan, consts, row_axis, col_axis, pay):
    work, cp, wide = plan.work, plan.col_pad, 2 * LANES
    rp = consts["side1"].shape[0]
    steps = [((work, wide), F32), ((work, wide), F32), ((work, plan.edge), F32)]
    shape = (plan.packed, HALF, LANES)
    if plan.parts > 1:
        last = call(functools.partial(last_kernel, plan, col_axis), "last", [pay], [(shape, BF16)], steps[:2])[0]
        entry = lax.ppermute(last, col_axis, [(k, k + plan.devices) for k in range(plan.devices)])
    else:
        entry = jnp.zeros(shape, BF16)
    names = ("to1", "to2", "from1", "from2", "side1", "side2", "sidemask", "down1", "down2", "downmask", "pick")
    side, above, passed, tops, edges, upto = call(
        functools.partial(maps_kernel, plan),
        "maps",
        [pay] + [consts[k] for k in names],
        [
            ((work, rp, wide), BF16),
            ((work, wide), F32),
            ((work, plan.edge, plan.top), BF16),
            ((work, HALF, plan.top), F32),
            ((work, HALF, plan.edge), BF16),
            ((work, plan.edge), F32),
        ],
        steps + [((work * rp, wide), F32)] * 2 + [((work * cp, wide), F32)] * 2,
    )
    edge_entry = entry
    tops = call(
        functools.partial(join_kernel, plan),
        "join",
        [upto, entry, passed, tops],
        [((work, HALF, plan.top), BF16)],
    )[0]
    count = lax.axis_size(row_axis)
    chain = [(r, r + 1) for r in range(count - 1)]
    entry = lax.ppermute(tops, row_axis, chain)
    if count > 2:
        keep = jnp.dot(above.astype(BF16), consts["pick"], preferred_element_type=F32)[:, None, :]
        for _ in range(count - 2):
            entry = lax.ppermute(
                (tops.astype(F32) + keep * entry.astype(F32)).astype(BF16), row_axis, chain
            )
    y, down = call(
        functools.partial(sides_kernel, plan),
        "sides",
        [pay, edges, upto, edge_entry, side, above],
        [((work, HALF, wide), F32), ((work, plan.top, wide), BF16)],
    )
    return call(
        functools.partial(cells_kernel, plan),
        "cells",
        [y, down, entry],
        [((plan.devices, plan.slots * plan.stride, LANES), BF16)],
    )[0]


def finish_kernel(plan, y_ref, own_ref, gate_ref, gain_ref, w_ref, out_hbm, full_ref, out_ref, sems):
    half, cells, stride = plan.half, plan.cells, plan.stride
    slot, slots = plan.slot, plan.slots
    per = LANES // slot
    lane = lax.broadcasted_iota(jnp.int32, (stride, LANES), 1)
    for block in range(plan.width // LANES):
        for k, (lo, hi) in enumerate(((0, half), (half, cells))):
            joined = None
            for d in range(per):
                at = block * per + d
                part = y_ref[at // slots, at % slots * stride : (at % slots + 1) * stride, :].astype(F32)
                shift = (d * slot - k * HALF) % LANES
                if shift:
                    part = pltpu.roll(part, shift, 1)
                joined = part if joined is None else jnp.where(lane < d * slot, joined, part)
            at = slice(block * LANES, (block + 1) * LANES)
            y = joined[: hi - lo] + own_ref[lo:hi, at].astype(F32)
            full_ref[lo:hi, at] = y.astype(BF16).astype(F32) * gate_ref[lo:hi, at].astype(F32)
    gated = full_ref[...]
    scale = lax.rsqrt(jnp.mean(gated * gated, axis=-1, keepdims=True) + norm_eps)
    normed = (gated * scale * gain_ref[...]).astype(BF16)
    copies = []
    chunks = sems.shape[0]
    tile = w_ref.shape[1] // chunks
    for k in range(chunks):
        at = slice(k * tile, (k + 1) * tile)
        out = mm(normed, w_ref[:, at])
        for i in range(plan.rows):
            out_ref[i, :, at] = out[i * plan.cols : (i + 1) * plan.cols].astype(BF16)
        copies.append(pltpu.make_async_copy(out_ref.at[:, :, at], out_hbm.at[:, :, at], sems.at[k]))
        copies[-1].start()
    for copy in copies:
        copy.wait()


def finish(plan, y, own, gate, gain, w_out):
    args = (y, own, gate, gain, w_out)
    shape = (plan.rows, plan.cols, w_out.shape[1])
    assert w_out.shape[1] == plan.width
    return call(
        functools.partial(finish_kernel, plan),
        "finish",
        args,
        [(shape, BF16)],
        [((plan.cells, plan.width), F32), (shape, BF16), pltpu.SemaphoreType.DMA((4,))],
        [HBM],
    )[0]


def per_device(slide, tissue, w_in, w_bcd, dt_bias, rate_x, rate_y, d_skip, norm_gain, w_out):
    rows, cols, model_width = slide.shape
    width = w_out.shape[0]
    heads = dt_bias.shape[0]
    states = (w_bcd.shape[1] - heads) // 2
    plan = Plan(rows, cols, states, heads, width, lax.axis_size("col"))
    consts = plan.constants()
    v, pay, table, x = project(plan, consts, slide, w_in, w_bcd, tissue, dt_bias, rate_x, rate_y)
    groups = plan.segments()
    pay = lax.all_to_all(pay, "col", 0, 0, tiled=True, axis_index_groups=groups)
    gain = norm_gain.reshape(1, width)
    own, gate, gain = home(plan, consts, v, table, x, w_in, tissue, gain, rate_x, rate_y, d_skip)
    pay, own, gate, gain = lax.optimization_barrier((pay, own, gate, gain))
    y = scan_calls(plan, consts, "row", "col", pay)
    y = lax.all_to_all(y, "col", 0, 0, tiled=True, axis_index_groups=groups)
    return finish(plan, y, own, gate, gain, w_out)


def solution(mesh):
    placed = (
        P(("slides", "row"), "col", None),
        P(("slides", "row"), "col"),
        P(),
        P(),
        P(),
        P(),
        P(),
        P(),
        P(),
        P(),
    )
    return jax.shard_map(
        per_device,
        mesh=mesh,
        in_specs=placed,
        out_specs=P(("slides", "row"), "col", None),
        check_vma=False,
    )
```

```python
import functools

import jax
import jax.numpy as jnp
import numpy as np
from jax import lax
from jax.experimental import pallas as pl
from jax.experimental.pallas import tpu as pltpu
from jax.sharding import PartitionSpec as P

norm_eps = 1e-05
LANES = 128
HALF = LANES // 2
F32 = jnp.float32
BF16 = jnp.bfloat16


def round_up(value, step):
    return -(-value // step) * step


def in_hbm(x):
    return pltpu.with_memory_space_constraint(x, pltpu.HBM)


def mm(a, b):
    return jnp.dot(a, b, preferred_element_type=F32)


def nt_dot(a, b):
    return lax.dot_general(a, b, (((1,), (1,)), ((), ())), preferred_element_type=F32)


def tn_dot(a, b):
    return lax.dot_general(a, b, (((0,), (0,)), ((), ())), preferred_element_type=F32)


class Plan:
    def __init__(self, rows, cols, states, heads, width, devices):
        self.rows, self.cols, self.states, self.heads = rows, cols, states, heads
        self.width = width
        self.parts = 2 if devices % 2 == 0 and devices > 2 else 1
        self.devices = devices // self.parts
        self.group = width // self.devices
        self.slot = min(self.group, HALF)
        self.slots = self.group // self.slot
        self.work = self.slots * self.devices
        self.head_width = width // heads
        self.col_pad = round_up(cols, 8)
        self.count = rows * cols
        self.half = self.count // 2 // 8 * 8
        self.cells = round_up(self.count, 8)
        self.stride = max(self.half, self.cells - self.half)
        self.edge = rows * states
        self.top = states * self.col_pad
        self.bc = 2 * states
        self.at_bc = self.slots * self.stride
        self.at_dt = self.at_bc + 2 * self.bc
        self.at_rate = self.at_dt + 2 * self.slots
        self.message = round_up(self.at_rate + 1, 8)
        self.tail = self.edge % LANES
        self.solid = self.edge // LANES
        self.share = LANES // self.tail if self.tail else 1
        self.packed = self.slots * self.solid + (-(-self.slots // self.share) if self.tail else 0)
        assert self.head_width % self.slot == 0 and self.group % self.slot == 0
        assert LANES % self.head_width == 0 and self.stride <= LANES
        assert states % 16 == 0 and heads % 8 == 0

    def segments(self):
        return [list(range(p * self.devices, (p + 1) * self.devices)) for p in range(self.parts)]

    def lanes(self):
        at = np.arange(2 * LANES)
        cell = np.where(at < LANES, at, at - LANES + self.half)
        live = np.where(at < LANES, at < self.half, cell < self.count)
        return cell // self.cols, cell % self.cols, live

    def constants(self):
        i, j, real = self.lanes()
        both = real[:, None] & real[None]
        cell = np.arange(self.cells)
        ci, cj = cell // self.cols, cell % self.cols
        creal = cell < self.count
        le = np.arange(round_up(self.rows, 8))
        lj = np.arange(self.col_pad)
        out = {}
        out["to1"] = (j[:, None] <= j[None]) & both
        out["to2"] = (j[:, None] == j[None]) & (i[:, None] <= i[None]) & both
        out["from1"] = (i[:, None] == i[None]) & (j[:, None] > j[None]) & both
        out["from2"] = (i[:, None] > i[None]) & both
        out["side1"] = (i[None] == le[:, None]) & real[None]
        out["side2"] = (i[None] > le[:, None]) & real[None]
        out["sidemask"] = (i[None] >= le[:, None]) & (le < self.rows)[:, None] & real[None]
        out["down1"] = (j[None] <= lj[:, None]) & real[None]
        out["down2"] = (j[None] == lj[:, None]) & real[None]
        out["downmask"] = (j[None] <= lj[:, None]) & (lj < self.cols)[:, None] & real[None]
        out["pick"] = (
            (i == self.rows - 1)[:, None] & real[:, None] & (j[:, None] == np.tile(lj, self.states)[None])
        )
        cboth = creal[:, None] & real[None]
        out["own1"] = (j[None] <= cj[:, None]) & cboth
        out["own2"] = (j[None] == cj[:, None]) & (i[None] <= ci[:, None]) & cboth
        out["ownmask"] = (i[None] <= ci[:, None]) & (j[None] <= cj[:, None]) & cboth
        out["lanei"] = (np.arange(self.rows)[:, None] == i[None]) & real[None]
        out["lanej"] = (np.arange(self.cols)[:, None] == j[None]) & real[None]
        return {k: in_hbm(jnp.asarray(x.astype(np.float32), BF16)) for k, x in out.items()}


def full(shape):
    return pl.BlockSpec(shape, lambda *_: (0,) * len(shape))


HBM = pl.BlockSpec(memory_space=pltpu.HBM)
SMEM = pl.BlockSpec(memory_space=pltpu.SMEM)


def split_cell(plan, cell):
    i = lax.shift_right_logical(cell * (-(-65536 // plan.cols)), 16)
    return i, cell - i * plan.cols


def cell_mask_of(plan, t_ref):
    t = t_ref[...].astype(F32).astype(BF16)
    shape = (plan.cells, plan.cols)
    _, j = split_cell(plan, lax.broadcasted_iota(jnp.int32, shape, 0))
    pick = ones(j == lax.broadcasted_iota(jnp.int32, shape, 1))
    shape = (plan.cells, plan.rows)
    i, _ = split_cell(plan, lax.broadcasted_iota(jnp.int32, shape, 0))
    here = i == lax.broadcasted_iota(jnp.int32, shape, 1)
    return jnp.sum(jnp.where(here, mm(pick, t), 0.0), axis=1, keepdims=True)


def rate_row(heads_of, rx_ref, ry_ref):
    at = lax.broadcasted_iota(jnp.int32, (1, LANES), 1)
    rate = jnp.zeros((1, LANES), F32)
    part = jnp.zeros((1, LANES), jnp.int32)
    for s, head in enumerate(heads_of):
        for k, ref in enumerate((rx_ref, ry_ref)):
            first = 8 * s + 3 * k
            here = (at >= first) & (at < first + 3)
            rate = jnp.where(here, ref[head], rate)
            part = jnp.where(here, at - first, part)
    high = rate.astype(BF16).astype(F32)
    middle = (rate - high).astype(BF16).astype(F32)
    low = rate - high - middle
    return jnp.where(part == 0, high, jnp.where(part == 1, middle, low))


def project_kernel(
    plan, chunks, bias_hbm, rx_hbm, ry_hbm, x_hbm, w_hbm, wt_hbm, t_hbm, lanei_hbm, lanej_hbm,
    v_ref, pay_hbm, rows_ref, flat_ref,
    bias_ref, rx_ref, ry_ref, x_ref, w_ref, wt_ref, t_ref, lanei_ref, lanej_ref, pay_ref, wide, sems, w_sems, out_sems,
):
    group, states, cells, heads = plan.group, plan.states, plan.cells, plan.heads
    half, rest = plan.half, plan.cells - plan.half
    tile = plan.width // chunks
    pairs = (
        (x_hbm, x_ref), (t_hbm, t_ref), (wt_hbm, wt_ref), (lanei_hbm, lanei_ref), (lanej_hbm, lanej_ref),
        (bias_hbm, bias_ref), (rx_hbm, rx_ref), (ry_hbm, ry_ref),
    )
    loads = [pltpu.make_async_copy(a, b, sems.at[k]) for k, (a, b) in enumerate(pairs)]
    copies = [
        pltpu.make_async_copy(w_hbm.at[:, k * tile : (k + 1) * tile], w_ref.at[k], w_sems.at[k])
        for k in range(chunks)
    ]
    for copy in loads + copies:
        copy.start()
    wide[...] = jnp.zeros_like(wide)
    v_ref[half:LANES, :] = jnp.zeros((LANES - half, plan.width), BF16)
    v_ref[LANES + rest :, :] = jnp.zeros((LANES - rest, plan.width), BF16)

    loads[0].wait()
    for i in range(plan.rows):
        wide[i * plan.cols : (i + 1) * plan.cols, :] = x_ref[i].astype(F32)
    x = wide[...].astype(BF16)
    flat_ref[...] = x
    for copy in loads[1:]:
        copy.wait()
    keep = cell_mask_of(plan, t_ref)
    t = t_ref[...].astype(F32).astype(BF16)
    m = jnp.sum(mm(t, lanei_ref[...]) * lanej_ref[...].astype(F32), axis=0, keepdims=True)
    table = nt_dot(wt_ref[...], x)
    ext = jnp.concatenate([table, jnp.zeros((table.shape[0], 2 * LANES - cells), F32)], axis=1)
    lane = lax.broadcasted_iota(jnp.int32, (table.shape[0], LANES), 1)
    lo, hi = ext[:, :LANES], ext[:, LANES:]
    shift = half % LANES
    if shift:
        moved = jnp.where(
            lane < LANES - shift, pltpu.roll(lo, LANES - shift, 1), pltpu.roll(hi, LANES - shift, 1)
        )
    else:
        moved = hi
    table = jnp.concatenate([jnp.where(lane < half, lo, 0.0), jnp.where(lane < plan.count - half, moved, 0.0)], axis=1)
    z = table[2 * states :]
    at = lax.broadcasted_iota(jnp.int32, z.shape, 0)
    for h in range(heads):
        z = jnp.where(at == h, z + bias_ref[h], z)
    soft = m * (jnp.maximum(z, 0.0) + jnp.log1p(jnp.exp(-jnp.abs(z))))
    table = jnp.concatenate([table[: 2 * states], soft], axis=0).astype(BF16)
    rows_ref[...] = table.astype(F32)
    bc = table[: 2 * states]
    steps = rows_ref[2 * states :, :]

    lane = lax.broadcasted_iota(jnp.int32, (plan.stride, LANES), 1)
    sent = []
    for chunk in range(chunks):
        copies[chunk].wait()
        v = mm(flat_ref[...], w_ref[chunk]).astype(BF16).astype(F32) * keep
        low = v.astype(BF16)
        v_ref[0:half, chunk * tile : (chunk + 1) * tile] = low[:half]
        v_ref[LANES : LANES + rest, chunk * tile : (chunk + 1) * tile] = low[half:]
        per = tile // group
        for k in range(per):
            dest = chunk * per + k
            dts, heads_of = [], []
            for s in range(plan.slots):
                offset = k * group + s * plan.slot
                base = offset // LANES * LANES
                at = offset % LANES
                first = v[:half, base : base + LANES]
                last = v[half:, base : base + LANES]
                if half < plan.stride:
                    first = jnp.concatenate([first, jnp.zeros((plan.stride - half, LANES), F32)], axis=0)
                if rest < plan.stride:
                    last = jnp.concatenate([last, jnp.zeros((plan.stride - rest, LANES), F32)], axis=0)
                if at:
                    first = pltpu.roll(first, LANES - at, 1)
                if at != HALF:
                    last = pltpu.roll(last, (HALF - at) % LANES, 1)
                both = jnp.where(lane < HALF, first, last)
                if plan.slot < HALF:
                    both = jnp.where(lane % HALF < plan.slot, both, 0.0)
                pay_ref[dest, s * plan.stride : (s + 1) * plan.stride, :] = both.astype(BF16)
                head = (chunk * tile + offset) // plan.head_width
                heads_of.append(head)
                dts += [steps[head : head + 1, :LANES], steps[head : head + 1, LANES:]]
            dts.append(rate_row(heads_of, rx_ref, ry_ref))
            pay_ref[dest, plan.at_bc : plan.at_bc + plan.bc, :] = bc[:, :LANES]
            pay_ref[dest, plan.at_bc + plan.bc : plan.at_dt, :] = bc[:, LANES:]
            spare = plan.message - plan.at_dt - len(dts)
            dts += [jnp.zeros((spare, LANES), F32)] if spare else []
            pay_ref[dest, plan.at_dt : plan.message, :] = jnp.concatenate(dts, axis=0).astype(BF16)
        at = slice(chunk * per, (chunk + 1) * per)
        sent.append(pltpu.make_async_copy(pay_ref.at[at], pay_hbm.at[at], out_sems.at[chunk]))
        sent[-1].start()
    for copy in sent:
        copy.wait()


def project(plan, consts, slide, w_in, w_bcd, tissue, dt_bias, rate_x, rate_y):
    chunks = 2
    tile = plan.width // chunks
    depth = slide.shape[2]
    args = [dt_bias, rate_x, rate_y, slide, w_in, w_bcd.T, tissue.T, consts["lanei"], consts["lanej"]]
    count = 2 * plan.states + plan.heads
    assert plan.width % chunks == 0 and tile % plan.group == 0 and tile % LANES == 0
    message = (plan.devices, plan.message, LANES)
    outs = [((2 * LANES, plan.width), BF16), (message, BF16), ((count, 2 * LANES), F32), ((plan.cells, depth), BF16)]
    specs = [full(s) for s, _ in outs]
    specs[1] = HBM
    return pl.pallas_call(
        functools.partial(project_kernel, plan, chunks),
        grid=(1,),
        in_specs=[HBM] * len(args),
        out_specs=specs,
        out_shape=[jax.ShapeDtypeStruct(s, d) for s, d in outs],
        scratch_shapes=[
            pltpu.SMEM(dt_bias.shape, F32),
            pltpu.SMEM(rate_x.shape, F32),
            pltpu.SMEM(rate_y.shape, F32),
            pltpu.VMEM(slide.shape, BF16),
            pltpu.VMEM((chunks, depth, tile), BF16),
        ]
        + [pltpu.VMEM(x.shape, x.dtype) for x in args[5:]]
        + [
            pltpu.VMEM(message, BF16),
            pltpu.VMEM((plan.cells, depth), F32),
            pltpu.SemaphoreType.DMA((8,)),
            pltpu.SemaphoreType.DMA((chunks,)),
            pltpu.SemaphoreType.DMA((chunks,)),
        ],
        compiler_params=pltpu.CompilerParams(vmem_limit_bytes=24 * 2**20),
        name="project",
    )(*[in_hbm(x) for x in args])


def home_kernel(
    plan, rx_ref, ry_ref, skip_ref, w_hbm, v_ref, rows_ref, flat_ref, t_ref, gain_ref,
    own1_ref, own2_ref, from1_ref, from2_ref, mask_ref, out_ref, gate_hbm, gain_out, pair, w_ref, gate_ref, sem, gate_sem,
):
    states, cells, half = plan.states, plan.cells, plan.half
    copy = pltpu.make_async_copy(w_hbm.at[:, plan.width :], w_ref, sem)
    copy.start()
    gain_out[...] = gain_ref[...]
    b = rows_ref[0:states, :].astype(BF16)
    c = rows_ref[states : 2 * states, :].astype(BF16)
    pairs = tn_dot(c, b)
    pairs = jnp.concatenate([pairs[:half], pairs[LANES : LANES + cells - half]], axis=0)
    pair[...] = pairs * mask_ref[...].astype(F32)
    lane = lax.broadcasted_iota(jnp.int32, (cells, LANES), 1)
    per = LANES // plan.head_width
    for block in range(plan.width // LANES):
        v = v_ref[:, block * LANES : (block + 1) * LANES]
        vc = jnp.concatenate([v[:half], v[LANES : LANES + cells - half]], axis=0).astype(F32)
        total = None
        for k in range(per):
            h = block * per + k
            dt = rows_ref[2 * states + h : 2 * states + h + 1, :]
            low = dt.astype(BF16)
            x = mm(own1_ref[...] * low, from1_ref[...])
            y = mm(own2_ref[...] * low, from2_ref[...])
            weight = jnp.exp(-(rx_ref[h] * x + ry_ref[h] * y)) * pair[...] * dt
            part = mm(weight.astype(BF16), v) + skip_ref[h] * vc
            total = part if total is None else jnp.where(lane < k * plan.head_width, total, part)
        out_ref[:, block * LANES : (block + 1) * LANES] = total.astype(BF16)
    keep = cell_mask_of(plan, t_ref)
    copy.wait()
    tile = 2 * LANES
    for block in range(plan.width // tile):
        at = slice(block * tile, (block + 1) * tile)
        z = mm(flat_ref[...], w_ref[:, at]).astype(BF16).astype(F32)
        gate_ref[:, at] = (z * (1.0 / (1.0 + jnp.exp(-z))) * keep).astype(BF16)
    copy = pltpu.make_async_copy(gate_ref, gate_hbm, gate_sem)
    copy.start()
    copy.wait()


def home(plan, consts, v, rows, flat, w_in, tissue, gain, rate_x, rate_y, d_skip):
    args = [in_hbm(w_in), v, rows, flat, in_hbm(tissue.T), in_hbm(gain)]
    args += [consts[k] for k in ("own1", "own2", "from1", "from2", "ownmask")]
    outs = [((plan.cells, plan.width), BF16), ((plan.cells, plan.width), BF16), (gain.shape, F32)]
    return pl.pallas_call(
        functools.partial(home_kernel, plan),
        grid=(1,),
        in_specs=[SMEM, SMEM, SMEM, HBM] + [full(x.shape) for x in args[1:]],
        out_specs=[full(outs[0][0]), HBM, full(outs[2][0])],
        out_shape=[jax.ShapeDtypeStruct(s, d) for s, d in outs],
        scratch_shapes=[
            pltpu.VMEM((plan.cells, 2 * LANES), F32),
            pltpu.VMEM((w_in.shape[0], w_in.shape[1] - plan.width), BF16),
            pltpu.VMEM((plan.cells, plan.width), BF16),
            pltpu.SemaphoreType.DMA,
            pltpu.SemaphoreType.DMA,
        ],
        compiler_params=pltpu.CompilerParams(vmem_limit_bytes=24 * 2**20),
        name="home",
    )(in_hbm(rate_x), in_hbm(rate_y), in_hbm(d_skip), *args)


def ones(mask):
    return jnp.where(mask, 1.0, 0.0).astype(BF16)


def places(plan, shape, axis):
    at = lax.broadcasted_iota(jnp.int32, shape, axis)
    late = at >= LANES
    cell = jnp.where(late, at - (LANES - plan.half), at)
    i, j = split_cell(plan, cell)
    return i, j, cell < jnp.where(late, plan.count, plan.half)


def wide_rows(pay_ref, t, at, count, gap):
    return jnp.concatenate([pay_ref[t, at : at + count, :], pay_ref[t, at + gap : at + gap + count, :]], axis=1)


def turned(plan, pay_ref, t, s):
    v = pay_ref[t, s * plan.stride : (s + 1) * plan.stride, :].astype(F32)
    if plan.stride < LANES:
        v = jnp.concatenate([v, jnp.zeros((LANES - plan.stride, LANES), F32)], axis=0)
    v = v.T
    return jnp.concatenate([v[:HALF], v[HALF:]], axis=1).astype(BF16)


def load_steps(plan, pay_ref, dts):
    for t in range(plan.devices):
        rows = pay_ref[t, plan.at_dt : plan.message, :].astype(F32)
        for s in range(plan.slots):
            w = s * plan.devices + t
            dts[w : w + 1, :LANES] = rows[2 * s : 2 * s + 1]
            dts[w : w + 1, LANES:] = rows[2 * s + 1 : 2 * s + 2]


def rates_of(plan, pay_ref, kind):
    row = pay_ref[0, plan.at_dt : plan.message, :].astype(F32)[plan.at_rate - plan.at_dt : plan.at_rate - plan.at_dt + 1]
    at = lax.broadcasted_iota(jnp.int32, (1, LANES), 1)
    first = [8 * s + 3 * kind for s in range(plan.slots)]
    return [jnp.sum(jnp.where((at >= f) & (at < f + 3), row, 0.0), axis=1, keepdims=True) for f in first]


def slot_rates(plan, pay_ref, kind):
    return jnp.concatenate(
        [jnp.broadcast_to(r, (plan.devices, 1)) for r in rates_of(plan, pay_ref, kind)], axis=0
    )


def pack_edges(plan, out_ref, held):
    for s in range(plan.slots):
        for k in range(plan.solid):
            out_ref[s * plan.solid + k] = held[s][:, k * LANES : (k + 1) * LANES].astype(BF16)
    if plan.tail:
        first = plan.slots * plan.solid
        for k in range(plan.packed - first):
            parts = [x[:, plan.solid * LANES :] for x in held[k * plan.share : (k + 1) * plan.share]]
            spare = LANES - plan.tail * len(parts)
            parts += [jnp.zeros((HALF, spare), F32)] if spare else []
            out_ref[first + k] = jnp.concatenate(parts, axis=1).astype(BF16)


def unpack_edges(plan, ref, s):
    parts = [ref[s * plan.solid + k].astype(F32) for k in range(plan.solid)]
    if plan.tail:
        last = ref[plan.slots * plan.solid + s // plan.share].astype(F32)
        at = s % plan.share * plan.tail
        parts.append(last[:, at : at + plan.tail])
    return jnp.concatenate(parts, axis=1)


def scan_edges(plan, pay_ref, dts, inner, kept, seen):
    states, tiles, wide = plan.states, plan.devices, 2 * LANES
    i, j, real = places(plan, (wide, wide), 0)
    ti, tj, treal = places(plan, (wide, wide), 1)
    from1 = ones((i == ti) & (j > tj) & real & treal)
    edge_row = lax.div(lax.broadcasted_iota(jnp.int32, (wide, plan.edge), 1), states)
    i, _, real = places(plan, (wide, plan.edge), 0)
    keep = ones((i == edge_row) & real)
    ti, _, treal = places(plan, (plan.rows, wide), 1)
    rowsel = ones((ti == lax.broadcasted_iota(jnp.int32, (plan.rows, wide), 0)) & treal)
    dt = dts[...]
    low = dt.astype(BF16)
    rate = slot_rates(plan, pay_ref, 0)
    inner[...] = jnp.exp(-rate * mm(low, from1)) * dt
    kept[...] = jnp.exp(-rate * mm(low, keep))
    ends = []
    for s in range(plan.slots):
        held = jnp.zeros((HALF, plan.edge), F32)
        product = jnp.ones((1, plan.edge), F32)
        for t in range(tiles):
            w = s * tiles + t
            seen(w, held, product)
            b = wide_rows(pay_ref, t, plan.at_bc, states, plan.bc).astype(F32)
            bd = (b * inner[w : w + 1, :]).astype(BF16)
            left = jnp.concatenate([bd * rowsel[i : i + 1] for i in range(plan.rows)], axis=0)
            now = kept[w : w + 1, :]
            held = held * now + nt_dot(turned(plan, pay_ref, t, s), left)
            product = product * now
        ends.append(held)
    return ends


def last_kernel(plan, axis, pay_ref, last_ref, dts, inner):
    @pl.when(lax.axis_index(axis) < (plan.parts - 1) * plan.devices)
    def _():
        states, tiles, wide = plan.states, plan.devices, 2 * LANES
        load_steps(plan, pay_ref, dts)
        i, j, real = places(plan, (wide, wide), 0)
        ti, tj, treal = places(plan, (wide, wide), 1)
        same = (i == ti) & real & treal
        ti, _, treal = places(plan, (plan.rows, wide), 1)
        rowsel = ones((ti == lax.broadcasted_iota(jnp.int32, (plan.rows, wide), 0)) & treal)
        low = dts[...].astype(BF16)
        rest, whole = mm(low, ones(same & (j > tj))), mm(low, ones(same))
        left = []
        for s in range(plan.slots):
            after = jnp.zeros((1, wide), F32)
            rows = []
            for t in reversed(range(tiles)):
                rows.append(after)
                after = after + whole[s * tiles + t : s * tiles + t + 1]
            left += rows[::-1]
        inner[...] = jnp.exp(-slot_rates(plan, pay_ref, 0) * (rest + jnp.concatenate(left, axis=0))) * dts[...]
        ends = []
        for s in range(plan.slots):
            held = None
            for t in range(tiles):
                w = s * tiles + t
                b = wide_rows(pay_ref, t, plan.at_bc, states, plan.bc).astype(F32)
                bd = (b * inner[w : w + 1, :]).astype(BF16)
                left = jnp.concatenate([bd * rowsel[i : i + 1] for i in range(plan.rows)], axis=0)
                part = nt_dot(turned(plan, pay_ref, t, s), left)
                held = part if held is None else held + part
            ends.append(held)
        pack_edges(plan, last_ref, ends)


def scan_kernel(plan, pay_ref, last_ref, edge_ref, upto_ref, again_ref, dts, inner, kept):
    again_ref[...] = last_ref[...]
    load_steps(plan, pay_ref, dts)

    def seen(w, held, product):
        edge_ref[w] = held.astype(BF16)
        upto_ref[w : w + 1, :] = product

    scan_edges(plan, pay_ref, dts, inner, kept, seen)


def maps_kernel(
    plan, pay_ref, edge_ref, to1_ref, to2_ref, from1_ref, from2_ref, side1_ref, side2_ref,
    sidemask_ref, down1_ref, down2_ref, downmask_ref, pick_ref,
    side_ref, above_ref, passed_ref, top_ref, dts, s1, s2, d1, d2,
):
    states, tiles, cp, work = plan.states, plan.devices, plan.col_pad, plan.work
    rp = side1_ref.shape[0]
    load_steps(plan, pay_ref, dts)
    low = dts[...].astype(BF16)
    above_ref[...] = jnp.exp(-slot_rates(plan, pay_ref, 1) * mm(low, to2_ref[...]))
    rates_x, rates_y = rates_of(plan, pay_ref, 0), rates_of(plan, pay_ref, 1)
    for w in range(work):
        rf = dts[w : w + 1, :]
        s1[w * rp : (w + 1) * rp, :] = side1_ref[...].astype(F32) * rf
        s2[w * rp : (w + 1) * rp, :] = side2_ref[...].astype(F32) * rf
        d1[w * cp : (w + 1) * cp, :] = down1_ref[...].astype(F32) * rf
        d2[w * cp : (w + 1) * cp, :] = down2_ref[...].astype(F32) * rf
    mask = sidemask_ref[...].astype(F32)
    x, y = mm(s1[...].astype(BF16), to1_ref[...]), mm(s2[...].astype(BF16), to2_ref[...])
    shape = (states, plan.top)
    n = lax.broadcasted_iota(jnp.int32, shape, 0)
    diag = ones(n == lax.div(lax.broadcasted_iota(jnp.int32, shape, 1), cp))
    for w in range(work):
        s = w // tiles
        at = slice(w * rp, (w + 1) * rp)
        side = (jnp.exp(-(rates_x[s] * x[at] + rates_y[s] * y[at])) * mask).astype(BF16)
        side_ref[w] = side
        bottom = mm(side, pick_ref[...]).astype(BF16)
        passed_ref[w] = jnp.concatenate([diag * bottom[i : i + 1] for i in range(plan.rows)], axis=0)
    x, y = mm(d1[...].astype(BF16), from1_ref[...]), mm(d2[...].astype(BF16), from2_ref[...])
    mask = downmask_ref[...].astype(F32)
    for w in range(work):
        s, t = w // tiles, w % tiles
        at = slice(w * cp, (w + 1) * cp)
        fall = jnp.exp(-(rates_x[s] * x[at] + rates_y[s] * y[at])) * mask * dts[w : w + 1, :]
        b = wide_rows(pay_ref, t, plan.at_bc, states, plan.bc).astype(F32)
        falls = jnp.concatenate([fall * b[n : n + 1] for n in range(states)], axis=0).astype(BF16)
        top_ref[w] = nt_dot(turned(plan, pay_ref, t, s), falls) + mm(edge_ref[w], passed_ref[w])


def join_kernel(plan, upto_ref, entry_ref, passed_ref, top_ref, out_ref):
    for s in range(plan.slots):
        entry = unpack_edges(plan, entry_ref, s)
        for t in range(plan.devices):
            w = s * plan.devices + t
            late = (entry * upto_ref[w : w + 1, :]).astype(BF16)
            out_ref[w] = (top_ref[w] + mm(late, passed_ref[w])).astype(BF16)


def sides_kernel(plan, pay_ref, edge_ref, upto_ref, first_ref, second_ref, side_ref, above_ref, y_ref, down_ref):
    states, tiles = plan.states, plan.devices
    shape = (plan.col_pad, 2 * LANES)
    _, tj, treal = places(plan, shape, 1)
    colsel = jnp.where((tj == lax.broadcasted_iota(jnp.int32, shape, 0)) & treal, 1.0, 0.0)
    for s in range(plan.slots):
        entry = unpack_edges(plan, first_ref, s) + unpack_edges(plan, second_ref, s)
        for t in range(tiles):
            w = s * tiles + t
            c = wide_rows(pay_ref, t, plan.at_bc + states, states, plan.bc)
            side = side_ref[w]
            left = jnp.concatenate([c * side[i : i + 1] for i in range(plan.rows)], axis=0)
            whole = (edge_ref[w].astype(F32) + entry * upto_ref[w : w + 1, :]).astype(BF16)
            y_ref[w] = mm(whole, left)
            ca = c.astype(F32) * above_ref[w : w + 1, :]
            down_ref[w] = jnp.concatenate([colsel * ca[n : n + 1] for n in range(states)], axis=0).astype(BF16)


def cells_kernel(plan, y_ref, down_ref, top_ref, out_ref):
    for w in range(plan.work):
        t, s = w % plan.devices, w // plan.devices
        y = y_ref[w] + mm(top_ref[w], down_ref[w])
        y = jnp.concatenate([y[:, :LANES], y[:, LANES:]], axis=0).T
        out_ref[t, s * plan.stride : (s + 1) * plan.stride, :] = y[: plan.stride].astype(BF16)


def call(kernel, args, outs, scratch=(), out_specs=None):
    return pl.pallas_call(
        kernel,
        grid=(1,),
        in_specs=[full(x.shape) for x in args],
        out_specs=out_specs or [full(s) for s, _ in outs],
        out_shape=[jax.ShapeDtypeStruct(s, d) for s, d in outs],
        scratch_shapes=[x if not isinstance(x, tuple) else pltpu.VMEM(*x) for x in scratch],
        compiler_params=pltpu.CompilerParams(vmem_limit_bytes=24 * 2**20),
    )(*args)


def scan_calls(plan, consts, row_axis, col_axis, pay):
    work, cp, wide = plan.work, plan.col_pad, 2 * LANES
    rp = consts["side1"].shape[0]
    steps = [((work, wide), F32), ((work, wide), F32), ((work, plan.edge), F32)]
    shape = (plan.packed, HALF, LANES)
    count, across = lax.axis_size(row_axis), plan.parts * plan.devices
    axes = (row_axis, col_axis)
    hops = [[(r * across + k, r * across + k + plan.devices) for k in range(plan.devices)] for r in range(count)]
    early, late = hops[:-1], hops[-1:]
    if count > 2:
        early, late = hops, []
    if plan.parts > 1:
        last = call(functools.partial(last_kernel, plan, col_axis), [pay], [(shape, BF16)], steps[:2])[0]
        first = lax.ppermute(last, axes, sum(early, []))
    else:
        last = first = jnp.zeros(shape, BF16)
    edges, upto, again = call(
        functools.partial(scan_kernel, plan),
        [pay, last],
        [((work, HALF, plan.edge), BF16), ((work, plan.edge), F32), (shape, BF16)],
        steps,
    )
    if plan.parts > 1 and late:
        second = lax.ppermute(again, axes, sum(late, []))
    else:
        second = jnp.zeros(shape, BF16)
    names = ("to1", "to2", "from1", "from2", "side1", "side2", "sidemask", "down1", "down2", "downmask", "pick")
    side, above, passed, tops = call(
        functools.partial(maps_kernel, plan),
        [pay, edges] + [consts[k] for k in names],
        [
            ((work, rp, wide), BF16),
            ((work, wide), F32),
            ((work, plan.edge, plan.top), BF16),
            ((work, HALF, plan.top), F32),
        ],
        [((work, wide), F32)] + [((work * rp, wide), F32)] * 2 + [((work * cp, wide), F32)] * 2,
    )
    tops = call(functools.partial(join_kernel, plan), [upto, first, passed, tops], [((work, HALF, plan.top), BF16)])[0]
    chain = [(r, r + 1) for r in range(count - 1)]
    entry = lax.ppermute(tops, row_axis, chain)
    if count > 2:
        keep = jnp.dot(above.astype(BF16), consts["pick"], preferred_element_type=F32)[:, None, :]
        for _ in range(count - 2):
            entry = lax.ppermute(
                (tops.astype(F32) + keep * entry.astype(F32)).astype(BF16), row_axis, chain
            )
    y, down = call(
        functools.partial(sides_kernel, plan),
        [pay, edges, upto, first, second, side, above],
        [((work, HALF, wide), F32), ((work, plan.top, wide), BF16)],
    )
    return call(
        functools.partial(cells_kernel, plan),
        [y, down, entry],
        [((plan.devices, plan.slots * plan.stride, LANES), BF16)],
    )[0]


def finish_kernel(plan, y_ref, own_ref, gate_ref, gain_ref, w_ref, out_hbm, full_ref, out_ref, sems):
    half, cells, stride = plan.half, plan.cells, plan.stride
    slot, slots = plan.slot, plan.slots
    per = LANES // slot
    lane = lax.broadcasted_iota(jnp.int32, (stride, LANES), 1)
    for block in range(plan.width // LANES):
        for k, (lo, hi) in enumerate(((0, half), (half, cells))):
            joined = None
            for d in range(per):
                at = block * per + d
                part = y_ref[at // slots, at % slots * stride : (at % slots + 1) * stride, :].astype(F32)
                shift = (d * slot - k * HALF) % LANES
                if shift:
                    part = pltpu.roll(part, shift, 1)
                joined = part if joined is None else jnp.where(lane < d * slot, joined, part)
            at = slice(block * LANES, (block + 1) * LANES)
            y = joined[: hi - lo] + own_ref[lo:hi, at].astype(F32)
            full_ref[lo:hi, at] = y.astype(BF16).astype(F32) * gate_ref[lo:hi, at].astype(F32)
    gated = full_ref[...]
    scale = lax.rsqrt(jnp.mean(gated * gated, axis=-1, keepdims=True) + norm_eps)
    normed = (gated * scale * gain_ref[...]).astype(BF16)
    copies = []
    chunks = sems.shape[0]
    tile = w_ref.shape[1] // chunks
    for k in range(chunks):
        at = slice(k * tile, (k + 1) * tile)
        out = mm(normed, w_ref[:, at])
        for i in range(plan.rows):
            out_ref[i, :, at] = out[i * plan.cols : (i + 1) * plan.cols].astype(BF16)
        copies.append(pltpu.make_async_copy(out_ref.at[:, :, at], out_hbm.at[:, :, at], sems.at[k]))
        copies[-1].start()
    for copy in copies:
        copy.wait()


def finish(plan, y, own, gate, gain, w_out):
    args = (y, own, gate, gain, w_out)
    shape = (plan.rows, plan.cols, w_out.shape[1])
    assert w_out.shape[1] == plan.width
    return call(
        functools.partial(finish_kernel, plan),
        args,
        [(shape, BF16)],
        [((plan.cells, plan.width), F32), (shape, BF16), pltpu.SemaphoreType.DMA((4,))],
        [HBM],
    )[0]


def per_device(slide, tissue, w_in, w_bcd, dt_bias, rate_x, rate_y, d_skip, norm_gain, w_out):
    rows, cols, _ = slide.shape
    width = w_out.shape[0]
    heads = dt_bias.shape[0]
    states = (w_bcd.shape[1] - heads) // 2
    plan = Plan(rows, cols, states, heads, width, lax.axis_size("col"))
    consts = plan.constants()
    v, pay, table, x = project(plan, consts, slide, w_in, w_bcd, tissue, dt_bias, rate_x, rate_y)
    groups = plan.segments()
    pay = lax.all_to_all(pay, "col", 0, 0, tiled=True, axis_index_groups=groups)
    gain = norm_gain.reshape(1, width)
    own, gate, gain = home(plan, consts, v, table, x, w_in, tissue, gain, rate_x, rate_y, d_skip)
    pay, own, gate, gain = lax.optimization_barrier((pay, own, gate, gain))
    y = scan_calls(plan, consts, "row", "col", pay)
    y = lax.all_to_all(y, "col", 0, 0, tiled=True, axis_index_groups=groups)
    return finish(plan, y, own, gate, gain, w_out)


def solution(mesh):
    placed = (
        P(("slides", "row"), "col", None),
        P(("slides", "row"), "col"),
        P(),
        P(),
        P(),
        P(),
        P(),
        P(),
        P(),
        P(),
    )
    return jax.shard_map(
        per_device,
        mesh=mesh,
        in_specs=placed,
        out_specs=P(("slides", "row"), "col", None),
        check_vma=False,
    )
```

```python
import functools

import jax
import jax.numpy as jnp
import numpy as np
from jax import lax
from jax.experimental import pallas as pl
from jax.experimental.pallas import tpu as pltpu
from jax.sharding import PartitionSpec as P

norm_eps = 1e-05
LANES = 128
HALF = LANES // 2
F32 = jnp.float32
BF16 = jnp.bfloat16


def round_up(value, step):
    return -(-value // step) * step


def in_hbm(x):
    return pltpu.with_memory_space_constraint(x, pltpu.HBM)


def mm(a, b):
    return jnp.dot(a, b, preferred_element_type=F32)


def nt_dot(a, b):
    return lax.dot_general(a, b, (((1,), (1,)), ((), ())), preferred_element_type=F32)


def tn_dot(a, b):
    return lax.dot_general(a, b, (((0,), (0,)), ((), ())), preferred_element_type=F32)


class Plan:
    def __init__(self, rows, cols, states, heads, width, devices):
        self.rows, self.cols, self.states, self.heads = rows, cols, states, heads
        self.width = width
        self.parts = 2 if devices % 2 == 0 and devices > 2 else 1
        self.devices = devices // self.parts
        self.group = width // self.devices
        self.slot = min(self.group, HALF)
        self.slots = self.group // self.slot
        self.work = self.slots * self.devices
        self.head_width = width // heads
        self.col_pad = round_up(cols, 8)
        self.count = rows * cols
        self.half = self.count // 2 // 8 * 8
        self.cells = round_up(self.count, 8)
        self.edge = rows * states
        self.top = states * self.col_pad
        self.bc = 2 * states
        self.at_bc = self.cells
        self.at_dt = self.at_bc + 2 * self.bc
        self.at_rate = self.at_dt + 2 * self.slots
        self.message = round_up(self.at_rate + 1, 8)
        self.tail = self.edge % LANES
        self.solid = self.edge // LANES
        self.share = LANES // self.tail if self.tail else 1
        self.packed = self.slots * self.solid + (-(-self.slots // self.share) if self.tail else 0)
        assert self.head_width % self.slot == 0 and self.group % self.slot == 0
        assert LANES % self.head_width == 0 and LANES % self.group == 0
        assert self.cells - self.half <= LANES
        assert states % 16 == 0 and heads % 8 == 0

    def segments(self):
        return [list(range(p * self.devices, (p + 1) * self.devices)) for p in range(self.parts)]

    def lanes(self):
        at = np.arange(2 * LANES)
        cell = np.where(at < LANES, at, at - LANES + self.half)
        live = np.where(at < LANES, at < self.half, cell < self.count)
        return cell // self.cols, cell % self.cols, live

    def constants(self):
        i, j, real = self.lanes()
        both = real[:, None] & real[None]
        cell = np.arange(self.cells)
        ci, cj = cell // self.cols, cell % self.cols
        creal = cell < self.count
        le = np.arange(round_up(self.rows, 8))
        lj = np.arange(self.col_pad)
        out = {}
        out["to1"] = (j[:, None] <= j[None]) & both
        out["to2"] = (j[:, None] == j[None]) & (i[:, None] <= i[None]) & both
        out["from1"] = (i[:, None] == i[None]) & (j[:, None] > j[None]) & both
        out["from2"] = (i[:, None] > i[None]) & both
        out["side1"] = (i[None] == le[:, None]) & real[None]
        out["side2"] = (i[None] > le[:, None]) & real[None]
        out["sidemask"] = (i[None] >= le[:, None]) & (le < self.rows)[:, None] & real[None]
        out["down1"] = (j[None] <= lj[:, None]) & real[None]
        out["down2"] = (j[None] == lj[:, None]) & real[None]
        out["downmask"] = (j[None] <= lj[:, None]) & (lj < self.cols)[:, None] & real[None]
        out["pick"] = (
            (i == self.rows - 1)[:, None] & real[:, None] & (j[:, None] == np.tile(lj, self.states)[None])
        )
        cboth = creal[:, None] & real[None]
        out["own1"] = (j[None] <= cj[:, None]) & cboth
        out["own2"] = (j[None] == cj[:, None]) & (i[None] <= ci[:, None]) & cboth
        out["ownmask"] = (i[None] <= ci[:, None]) & (j[None] <= cj[:, None]) & cboth
        out["lanei"] = (np.arange(self.rows)[:, None] == i[None]) & real[None]
        out["lanej"] = (np.arange(self.cols)[:, None] == j[None]) & real[None]
        return {k: in_hbm(jnp.asarray(x.astype(np.float32), BF16)) for k, x in out.items()}


def full(shape):
    return pl.BlockSpec(shape, lambda *_: (0,) * len(shape))


HBM = pl.BlockSpec(memory_space=pltpu.HBM)
SMEM = pl.BlockSpec(memory_space=pltpu.SMEM)


def split_cell(plan, cell):
    i = lax.shift_right_logical(cell * (-(-65536 // plan.cols)), 16)
    return i, cell - i * plan.cols


def cell_mask_of(plan, t_ref):
    t = t_ref[...].astype(F32).astype(BF16)
    shape = (plan.cells, plan.cols)
    _, j = split_cell(plan, lax.broadcasted_iota(jnp.int32, shape, 0))
    pick = ones(j == lax.broadcasted_iota(jnp.int32, shape, 1))
    shape = (plan.cells, plan.rows)
    i, _ = split_cell(plan, lax.broadcasted_iota(jnp.int32, shape, 0))
    here = i == lax.broadcasted_iota(jnp.int32, shape, 1)
    return jnp.sum(jnp.where(here, mm(pick, t), 0.0), axis=1, keepdims=True)


def rate_row(heads_of, rx_ref, ry_ref):
    at = lax.broadcasted_iota(jnp.int32, (1, LANES), 1)
    rate = jnp.zeros((1, LANES), F32)
    part = jnp.zeros((1, LANES), jnp.int32)
    for s, head in enumerate(heads_of):
        for k, ref in enumerate((rx_ref, ry_ref)):
            first = 8 * s + 3 * k
            here = (at >= first) & (at < first + 3)
            rate = jnp.where(here, ref[head], rate)
            part = jnp.where(here, at - first, part)
    high = rate.astype(BF16).astype(F32)
    middle = (rate - high).astype(BF16).astype(F32)
    low = rate - high - middle
    return jnp.where(part == 0, high, jnp.where(part == 1, middle, low))


def project_kernel(
    plan, chunks, bias_hbm, rx_hbm, ry_hbm, x_hbm, w_hbm, wt_hbm, t_hbm, lanei_hbm, lanej_hbm,
    v_ref, pay_hbm, rows_ref, flat_ref,
    bias_ref, rx_ref, ry_ref, x_ref, w_ref, wt_ref, t_ref, lanei_ref, lanej_ref, pay_ref, wide, sems, w_sems, out_sems,
):
    group, states, cells, heads = plan.group, plan.states, plan.cells, plan.heads
    half, rest = plan.half, plan.cells - plan.half
    tile = plan.width // chunks
    pairs = (
        (x_hbm, x_ref), (t_hbm, t_ref), (wt_hbm, wt_ref), (lanei_hbm, lanei_ref), (lanej_hbm, lanej_ref),
        (bias_hbm, bias_ref), (rx_hbm, rx_ref), (ry_hbm, ry_ref),
    )
    loads = [pltpu.make_async_copy(a, b, sems.at[k]) for k, (a, b) in enumerate(pairs)]
    copies = [
        pltpu.make_async_copy(w_hbm.at[:, k * tile : (k + 1) * tile], w_ref.at[k], w_sems.at[k])
        for k in range(chunks)
    ]
    for copy in loads + copies:
        copy.start()
    wide[...] = jnp.zeros_like(wide)
    v_ref[half:LANES, :] = jnp.zeros((LANES - half, plan.width), BF16)
    v_ref[LANES + rest :, :] = jnp.zeros((LANES - rest, plan.width), BF16)

    loads[0].wait()
    for i in range(plan.rows):
        wide[i * plan.cols : (i + 1) * plan.cols, :] = x_ref[i].astype(F32)
    x = wide[...].astype(BF16)
    flat_ref[...] = x
    for copy in loads[1:]:
        copy.wait()
    keep = cell_mask_of(plan, t_ref)
    t = t_ref[...].astype(F32).astype(BF16)
    m = jnp.sum(mm(t, lanei_ref[...]) * lanej_ref[...].astype(F32), axis=0, keepdims=True)
    table = nt_dot(wt_ref[...], x)
    ext = jnp.concatenate([table, jnp.zeros((table.shape[0], 2 * LANES - cells), F32)], axis=1)
    lane = lax.broadcasted_iota(jnp.int32, (table.shape[0], LANES), 1)
    lo, hi = ext[:, :LANES], ext[:, LANES:]
    shift = half % LANES
    if shift:
        moved = jnp.where(
            lane < LANES - shift, pltpu.roll(lo, LANES - shift, 1), pltpu.roll(hi, LANES - shift, 1)
        )
    else:
        moved = hi
    table = jnp.concatenate([jnp.where(lane < half, lo, 0.0), jnp.where(lane < plan.count - half, moved, 0.0)], axis=1)
    z = table[2 * states :]
    at = lax.broadcasted_iota(jnp.int32, z.shape, 0)
    for h in range(heads):
        z = jnp.where(at == h, z + bias_ref[h], z)
    soft = m * (jnp.maximum(z, 0.0) + jnp.log1p(jnp.exp(-jnp.abs(z))))
    table = jnp.concatenate([table[: 2 * states], soft], axis=0).astype(BF16)
    rows_ref[...] = table.astype(F32)
    bc = table[: 2 * states]
    steps = rows_ref[2 * states :, :]

    lane = lax.broadcasted_iota(jnp.int32, (cells, LANES), 1)
    sent = []
    for chunk in range(chunks):
        copies[chunk].wait()
        v = mm(flat_ref[...], w_ref[chunk]).astype(BF16).astype(F32) * keep
        low = v.astype(BF16)
        v_ref[0:half, chunk * tile : (chunk + 1) * tile] = low[:half]
        v_ref[LANES : LANES + rest, chunk * tile : (chunk + 1) * tile] = low[half:]
        per = tile // group
        for k in range(per):
            dest = chunk * per + k
            base, at = k * group // LANES * LANES, k * group % LANES
            mine = v[:, base : base + LANES]
            if at:
                mine = pltpu.roll(mine, LANES - at, 1)
            if group < LANES:
                mine = jnp.where(lane < group, mine, 0.0)
            pay_ref[dest, 0:cells, :] = mine.astype(BF16)
            dts, heads_of = [], []
            for s in range(plan.slots):
                head = (chunk * tile + k * group + s * plan.slot) // plan.head_width
                heads_of.append(head)
                dts += [steps[head : head + 1, :LANES], steps[head : head + 1, LANES:]]
            dts.append(rate_row(heads_of, rx_ref, ry_ref))
            pay_ref[dest, plan.at_bc : plan.at_bc + plan.bc, :] = bc[:, :LANES]
            pay_ref[dest, plan.at_bc + plan.bc : plan.at_dt, :] = bc[:, LANES:]
            spare = plan.message - plan.at_dt - len(dts)
            dts += [jnp.zeros((spare, LANES), F32)] if spare else []
            pay_ref[dest, plan.at_dt : plan.message, :] = jnp.concatenate(dts, axis=0).astype(BF16)
        at = slice(chunk * per, (chunk + 1) * per)
        sent.append(pltpu.make_async_copy(pay_ref.at[at], pay_hbm.at[at], out_sems.at[chunk]))
        sent[-1].start()
    for copy in sent:
        copy.wait()


def project(plan, consts, slide, w_in, w_bcd, tissue, dt_bias, rate_x, rate_y):
    chunks = 2
    tile = plan.width // chunks
    depth = slide.shape[2]
    args = [dt_bias, rate_x, rate_y, slide, w_in, w_bcd.T, tissue.T, consts["lanei"], consts["lanej"]]
    count = 2 * plan.states + plan.heads
    assert plan.width % chunks == 0 and tile % plan.group == 0 and tile % LANES == 0
    message = (plan.devices, plan.message, LANES)
    outs = [((2 * LANES, plan.width), BF16), (message, BF16), ((count, 2 * LANES), F32), ((plan.cells, depth), BF16)]
    specs = [full(s) for s, _ in outs]
    specs[1] = HBM
    return pl.pallas_call(
        functools.partial(project_kernel, plan, chunks),
        grid=(1,),
        in_specs=[HBM] * len(args),
        out_specs=specs,
        out_shape=[jax.ShapeDtypeStruct(s, d) for s, d in outs],
        scratch_shapes=[
            pltpu.SMEM(dt_bias.shape, F32),
            pltpu.SMEM(rate_x.shape, F32),
            pltpu.SMEM(rate_y.shape, F32),
            pltpu.VMEM(slide.shape, BF16),
            pltpu.VMEM((chunks, depth, tile), BF16),
        ]
        + [pltpu.VMEM(x.shape, x.dtype) for x in args[5:]]
        + [
            pltpu.VMEM(message, BF16),
            pltpu.VMEM((plan.cells, depth), F32),
            pltpu.SemaphoreType.DMA((8,)),
            pltpu.SemaphoreType.DMA((chunks,)),
            pltpu.SemaphoreType.DMA((chunks,)),
        ],
        compiler_params=pltpu.CompilerParams(vmem_limit_bytes=24 * 2**20),
        name="project",
    )(*[in_hbm(x) for x in args])


def home_kernel(
    plan, rx_ref, ry_ref, skip_ref, w_hbm, v_ref, rows_ref, flat_ref, t_ref, gain_ref,
    own1_ref, own2_ref, from1_ref, from2_ref, mask_ref, out_ref, gate_hbm, gain_out, pair, w_ref, gate_ref, sem, gate_sem,
):
    states, cells, half = plan.states, plan.cells, plan.half
    copy = pltpu.make_async_copy(w_hbm.at[:, plan.width :], w_ref, sem)
    copy.start()
    gain_out[...] = gain_ref[...]
    b = rows_ref[0:states, :].astype(BF16)
    c = rows_ref[states : 2 * states, :].astype(BF16)
    pairs = tn_dot(c, b)
    pairs = jnp.concatenate([pairs[:half], pairs[LANES : LANES + cells - half]], axis=0)
    pair[...] = pairs * mask_ref[...].astype(F32)
    lane = lax.broadcasted_iota(jnp.int32, (cells, LANES), 1)
    per = LANES // plan.head_width
    for block in range(plan.width // LANES):
        v = v_ref[:, block * LANES : (block + 1) * LANES]
        vc = jnp.concatenate([v[:half], v[LANES : LANES + cells - half]], axis=0).astype(F32)
        total = None
        for k in range(per):
            h = block * per + k
            dt = rows_ref[2 * states + h : 2 * states + h + 1, :]
            low = dt.astype(BF16)
            x = mm(own1_ref[...] * low, from1_ref[...])
            y = mm(own2_ref[...] * low, from2_ref[...])
            weight = jnp.exp(-(rx_ref[h] * x + ry_ref[h] * y)) * pair[...] * dt
            part = mm(weight.astype(BF16), v) + skip_ref[h] * vc
            total = part if total is None else jnp.where(lane < k * plan.head_width, total, part)
        out_ref[:, block * LANES : (block + 1) * LANES] = total.astype(BF16)
    keep = cell_mask_of(plan, t_ref)
    copy.wait()
    tile = 2 * LANES
    for block in range(plan.width // tile):
        at = slice(block * tile, (block + 1) * tile)
        z = mm(flat_ref[...], w_ref[:, at]).astype(BF16).astype(F32)
        gate_ref[:, at] = (z * (1.0 / (1.0 + jnp.exp(-z))) * keep).astype(BF16)
    copy = pltpu.make_async_copy(gate_ref, gate_hbm, gate_sem)
    copy.start()
    copy.wait()


def home(plan, consts, v, rows, flat, w_in, tissue, gain, rate_x, rate_y, d_skip):
    args = [in_hbm(w_in), v, rows, flat, in_hbm(tissue.T), in_hbm(gain)]
    args += [consts[k] for k in ("own1", "own2", "from1", "from2", "ownmask")]
    outs = [((plan.cells, plan.width), BF16), ((plan.cells, plan.width), BF16), (gain.shape, F32)]
    return pl.pallas_call(
        functools.partial(home_kernel, plan),
        grid=(1,),
        in_specs=[SMEM, SMEM, SMEM, HBM] + [full(x.shape) for x in args[1:]],
        out_specs=[full(outs[0][0]), HBM, full(outs[2][0])],
        out_shape=[jax.ShapeDtypeStruct(s, d) for s, d in outs],
        scratch_shapes=[
            pltpu.VMEM((plan.cells, 2 * LANES), F32),
            pltpu.VMEM((w_in.shape[0], w_in.shape[1] - plan.width), BF16),
            pltpu.VMEM((plan.cells, plan.width), BF16),
            pltpu.SemaphoreType.DMA,
            pltpu.SemaphoreType.DMA,
        ],
        compiler_params=pltpu.CompilerParams(vmem_limit_bytes=24 * 2**20),
        name="home",
    )(in_hbm(rate_x), in_hbm(rate_y), in_hbm(d_skip), *args)


def ones(mask):
    return jnp.where(mask, 1.0, 0.0).astype(BF16)


def places(plan, shape, axis):
    at = lax.broadcasted_iota(jnp.int32, shape, axis)
    late = at >= LANES
    cell = jnp.where(late, at - (LANES - plan.half), at)
    i, j = split_cell(plan, cell)
    return i, j, cell < jnp.where(late, plan.count, plan.half)


def wide_rows(pay_ref, t, at, count, gap):
    return jnp.concatenate([pay_ref[t, at : at + count, :], pay_ref[t, at + gap : at + gap + count, :]], axis=1)


def turn_all(plan, pay_ref, turned):
    for t in range(plan.devices):
        sides = []
        for lo, hi in ((0, plan.half), (plan.half, plan.cells)):
            v = pay_ref[t, lo:hi, :].astype(F32)
            if hi - lo < LANES:
                v = jnp.concatenate([v, jnp.zeros((LANES - hi + lo, LANES), F32)], axis=0)
            sides.append(v.T)
        v = jnp.concatenate(sides, axis=1).astype(BF16)
        for s in range(plan.slots):
            turned[s * plan.devices + t] = v[s * HALF : (s + 1) * HALF]


def load_steps(plan, pay_ref, dts):
    for t in range(plan.devices):
        rows = pay_ref[t, plan.at_dt : plan.message, :].astype(F32)
        for s in range(plan.slots):
            w = s * plan.devices + t
            dts[w : w + 1, :LANES] = rows[2 * s : 2 * s + 1]
            dts[w : w + 1, LANES:] = rows[2 * s + 1 : 2 * s + 2]


def rates_of(plan, pay_ref, kind):
    row = pay_ref[0, plan.at_dt : plan.message, :].astype(F32)[plan.at_rate - plan.at_dt : plan.at_rate - plan.at_dt + 1]
    at = lax.broadcasted_iota(jnp.int32, (1, LANES), 1)
    first = [8 * s + 3 * kind for s in range(plan.slots)]
    return [jnp.sum(jnp.where((at >= f) & (at < f + 3), row, 0.0), axis=1, keepdims=True) for f in first]


def slot_rates(plan, pay_ref, kind):
    return jnp.concatenate(
        [jnp.broadcast_to(r, (plan.devices, 1)) for r in rates_of(plan, pay_ref, kind)], axis=0
    )


def pack_edges(plan, out_ref, held):
    for s in range(plan.slots):
        for k in range(plan.solid):
            out_ref[s * plan.solid + k] = held[s][:, k * LANES : (k + 1) * LANES].astype(BF16)
    if plan.tail:
        first = plan.slots * plan.solid
        for k in range(plan.packed - first):
            parts = [x[:, plan.solid * LANES :] for x in held[k * plan.share : (k + 1) * plan.share]]
            spare = LANES - plan.tail * len(parts)
            parts += [jnp.zeros((HALF, spare), F32)] if spare else []
            out_ref[first + k] = jnp.concatenate(parts, axis=1).astype(BF16)


def unpack_edges(plan, ref, s):
    parts = [ref[s * plan.solid + k].astype(F32) for k in range(plan.solid)]
    if plan.tail:
        last = ref[plan.slots * plan.solid + s // plan.share].astype(F32)
        at = s % plan.share * plan.tail
        parts.append(last[:, at : at + plan.tail])
    return jnp.concatenate(parts, axis=1)


def scan_edges(plan, pay_ref, turned, dts, inner, kept, seen):
    states, tiles, wide = plan.states, plan.devices, 2 * LANES
    i, j, real = places(plan, (wide, wide), 0)
    ti, tj, treal = places(plan, (wide, wide), 1)
    from1 = ones((i == ti) & (j > tj) & real & treal)
    edge_row = lax.div(lax.broadcasted_iota(jnp.int32, (wide, plan.edge), 1), states)
    i, _, real = places(plan, (wide, plan.edge), 0)
    keep = ones((i == edge_row) & real)
    ti, _, treal = places(plan, (plan.rows, wide), 1)
    rowsel = ones((ti == lax.broadcasted_iota(jnp.int32, (plan.rows, wide), 0)) & treal)
    dt = dts[...]
    low = dt.astype(BF16)
    rate = slot_rates(plan, pay_ref, 0)
    inner[...] = jnp.exp(-rate * mm(low, from1)) * dt
    kept[...] = jnp.exp(-rate * mm(low, keep))
    ends = []
    for s in range(plan.slots):
        held = jnp.zeros((HALF, plan.edge), F32)
        product = jnp.ones((1, plan.edge), F32)
        for t in range(tiles):
            w = s * tiles + t
            seen(w, held, product)
            b = wide_rows(pay_ref, t, plan.at_bc, states, plan.bc).astype(F32)
            bd = (b * inner[w : w + 1, :]).astype(BF16)
            left = jnp.concatenate([bd * rowsel[i : i + 1] for i in range(plan.rows)], axis=0)
            now = kept[w : w + 1, :]
            held = held * now + nt_dot(turned[w], left)
            product = product * now
        ends.append(held)
    return ends


def last_kernel(plan, axis, pay_ref, last_ref, turned, dts, inner):
    @pl.when(lax.axis_index(axis) < (plan.parts - 1) * plan.devices)
    def _():
        states, tiles, wide = plan.states, plan.devices, 2 * LANES
        turn_all(plan, pay_ref, turned)
        load_steps(plan, pay_ref, dts)
        i, j, real = places(plan, (wide, wide), 0)
        ti, tj, treal = places(plan, (wide, wide), 1)
        same = (i == ti) & real & treal
        ti, _, treal = places(plan, (plan.rows, wide), 1)
        rowsel = ones((ti == lax.broadcasted_iota(jnp.int32, (plan.rows, wide), 0)) & treal)
        low = dts[...].astype(BF16)
        rest, whole = mm(low, ones(same & (j > tj))), mm(low, ones(same))
        left = []
        for s in range(plan.slots):
            after = jnp.zeros((1, wide), F32)
            rows = []
            for t in reversed(range(tiles)):
                rows.append(after)
                after = after + whole[s * tiles + t : s * tiles + t + 1]
            left += rows[::-1]
        inner[...] = jnp.exp(-slot_rates(plan, pay_ref, 0) * (rest + jnp.concatenate(left, axis=0))) * dts[...]
        ends = []
        for s in range(plan.slots):
            held = None
            for t in range(tiles):
                w = s * tiles + t
                b = wide_rows(pay_ref, t, plan.at_bc, states, plan.bc).astype(F32)
                bd = (b * inner[w : w + 1, :]).astype(BF16)
                left = jnp.concatenate([bd * rowsel[i : i + 1] for i in range(plan.rows)], axis=0)
                part = nt_dot(turned[w], left)
                held = part if held is None else held + part
            ends.append(held)
        pack_edges(plan, last_ref, ends)


def maps_kernel(
    plan, pay_ref, to1_ref, to2_ref, from1_ref, from2_ref, side1_ref, side2_ref,
    sidemask_ref, down1_ref, down2_ref, downmask_ref, pick_ref,
    side_ref, above_ref, passed_ref, top_ref, edge_ref, upto_ref, turned, dts, inner, kept, s1, s2, d1, d2,
):
    states, tiles, cp, work = plan.states, plan.devices, plan.col_pad, plan.work
    rp = side1_ref.shape[0]
    turn_all(plan, pay_ref, turned)
    load_steps(plan, pay_ref, dts)

    def seen(w, held, product):
        edge_ref[w] = held.astype(BF16)
        upto_ref[w : w + 1, :] = product

    scan_edges(plan, pay_ref, turned, dts, inner, kept, seen)
    low = dts[...].astype(BF16)
    above_ref[...] = jnp.exp(-slot_rates(plan, pay_ref, 1) * mm(low, to2_ref[...]))
    rates_x, rates_y = rates_of(plan, pay_ref, 0), rates_of(plan, pay_ref, 1)
    for w in range(work):
        rf = dts[w : w + 1, :]
        s1[w * rp : (w + 1) * rp, :] = side1_ref[...].astype(F32) * rf
        s2[w * rp : (w + 1) * rp, :] = side2_ref[...].astype(F32) * rf
        d1[w * cp : (w + 1) * cp, :] = down1_ref[...].astype(F32) * rf
        d2[w * cp : (w + 1) * cp, :] = down2_ref[...].astype(F32) * rf
    mask = sidemask_ref[...].astype(F32)
    x, y = mm(s1[...].astype(BF16), to1_ref[...]), mm(s2[...].astype(BF16), to2_ref[...])
    shape = (states, plan.top)
    n = lax.broadcasted_iota(jnp.int32, shape, 0)
    diag = ones(n == lax.div(lax.broadcasted_iota(jnp.int32, shape, 1), cp))
    for w in range(work):
        s = w // tiles
        at = slice(w * rp, (w + 1) * rp)
        side = (jnp.exp(-(rates_x[s] * x[at] + rates_y[s] * y[at])) * mask).astype(BF16)
        side_ref[w] = side
        bottom = mm(side, pick_ref[...]).astype(BF16)
        passed_ref[w] = jnp.concatenate([diag * bottom[i : i + 1] for i in range(plan.rows)], axis=0)
    x, y = mm(d1[...].astype(BF16), from1_ref[...]), mm(d2[...].astype(BF16), from2_ref[...])
    mask = downmask_ref[...].astype(F32)
    for w in range(work):
        s, t = w // tiles, w % tiles
        at = slice(w * cp, (w + 1) * cp)
        fall = jnp.exp(-(rates_x[s] * x[at] + rates_y[s] * y[at])) * mask * dts[w : w + 1, :]
        b = wide_rows(pay_ref, t, plan.at_bc, states, plan.bc).astype(F32)
        falls = jnp.concatenate([fall * b[n : n + 1] for n in range(states)], axis=0).astype(BF16)
        top_ref[w] = nt_dot(turned[w], falls) + mm(edge_ref[w], passed_ref[w])


def join_kernel(plan, upto_ref, entry_ref, passed_ref, top_ref, out_ref):
    for s in range(plan.slots):
        entry = unpack_edges(plan, entry_ref, s)
        for t in range(plan.devices):
            w = s * plan.devices + t
            late = (entry * upto_ref[w : w + 1, :]).astype(BF16)
            out_ref[w] = (top_ref[w] + mm(late, passed_ref[w])).astype(BF16)


def sides_kernel(plan, pay_ref, edge_ref, upto_ref, entry_ref, side_ref, above_ref, y_ref, down_ref):
    states, tiles = plan.states, plan.devices
    shape = (plan.col_pad, 2 * LANES)
    _, tj, treal = places(plan, shape, 1)
    colsel = jnp.where((tj == lax.broadcasted_iota(jnp.int32, shape, 0)) & treal, 1.0, 0.0)
    for s in range(plan.slots):
        entry = unpack_edges(plan, entry_ref, s)
        for t in range(tiles):
            w = s * tiles + t
            c = wide_rows(pay_ref, t, plan.at_bc + states, states, plan.bc)
            side = side_ref[w]
            left = jnp.concatenate([c * side[i : i + 1] for i in range(plan.rows)], axis=0)
            whole = (edge_ref[w].astype(F32) + entry * upto_ref[w : w + 1, :]).astype(BF16)
            y_ref[w] = mm(whole, left)
            ca = c.astype(F32) * above_ref[w : w + 1, :]
            down_ref[w] = jnp.concatenate([colsel * ca[n : n + 1] for n in range(states)], axis=0).astype(BF16)


def cells_kernel(plan, y_ref, down_ref, top_ref, out_ref):
    tiles = plan.devices
    for t in range(tiles):
        ys = [y_ref[w] + mm(top_ref[w], down_ref[w]) for w in range(t, plan.work, tiles)]
        if plan.slots == 1:
            ys.append(jnp.zeros_like(ys[0]))
        y = jnp.concatenate(ys, axis=0)
        for k, (lo, hi) in enumerate(((0, plan.half), (plan.half, plan.cells))):
            out_ref[t, lo:hi, :] = y[:, k * LANES : (k + 1) * LANES].T[: hi - lo].astype(BF16)


def call(kernel, name, args, outs, scratch=(), out_specs=None):
    return pl.pallas_call(
        kernel,
        grid=(1,),
        in_specs=[full(x.shape) for x in args],
        out_specs=out_specs or [full(s) for s, _ in outs],
        out_shape=[jax.ShapeDtypeStruct(s, d) for s, d in outs],
        scratch_shapes=[x if not isinstance(x, tuple) else pltpu.VMEM(*x) for x in scratch],
        compiler_params=pltpu.CompilerParams(vmem_limit_bytes=24 * 2**20),
        name=name,
    )(*args)


def scan_calls(plan, consts, row_axis, col_axis, pay):
    work, cp, wide = plan.work, plan.col_pad, 2 * LANES
    rp = consts["side1"].shape[0]
    steps = [((work, HALF, wide), BF16), ((work, wide), F32), ((work, wide), F32), ((work, plan.edge), F32)]
    shape = (plan.packed, HALF, LANES)
    if plan.parts > 1:
        last = call(functools.partial(last_kernel, plan, col_axis), "last", [pay], [(shape, BF16)], steps[:3])[0]
        entry = lax.ppermute(last, col_axis, [(k, k + plan.devices) for k in range(plan.devices)])
    else:
        entry = jnp.zeros(shape, BF16)
    names = ("to1", "to2", "from1", "from2", "side1", "side2", "sidemask", "down1", "down2", "downmask", "pick")
    side, above, passed, tops, edges, upto = call(
        functools.partial(maps_kernel, plan),
        "maps",
        [pay] + [consts[k] for k in names],
        [
            ((work, rp, wide), BF16),
            ((work, wide), F32),
            ((work, plan.edge, plan.top), BF16),
            ((work, HALF, plan.top), F32),
            ((work, HALF, plan.edge), BF16),
            ((work, plan.edge), F32),
        ],
        steps + [((work * rp, wide), F32)] * 2 + [((work * cp, wide), F32)] * 2,
    )
    edge_entry = entry
    tops = call(
        functools.partial(join_kernel, plan),
        "join",
        [upto, entry, passed, tops],
        [((work, HALF, plan.top), BF16)],
    )[0]
    count = lax.axis_size(row_axis)
    chain = [(r, r + 1) for r in range(count - 1)]
    entry = lax.ppermute(tops, row_axis, chain)
    if count > 2:
        keep = jnp.dot(above.astype(BF16), consts["pick"], preferred_element_type=F32)[:, None, :]
        for _ in range(count - 2):
            entry = lax.ppermute(
                (tops.astype(F32) + keep * entry.astype(F32)).astype(BF16), row_axis, chain
            )
    y, down = call(
        functools.partial(sides_kernel, plan),
        "sides",
        [pay, edges, upto, edge_entry, side, above],
        [((work, HALF, wide), F32), ((work, plan.top, wide), BF16)],
    )
    return call(
        functools.partial(cells_kernel, plan),
        "cells",
        [y, down, entry],
        [((plan.devices, plan.cells, LANES), BF16)],
    )[0]


def finish_kernel(plan, y_ref, own_ref, gate_ref, gain_ref, w_ref, out_hbm, full_ref, out_ref, sems):
    group = plan.group
    per = LANES // group
    lane = lax.broadcasted_iota(jnp.int32, (plan.cells, LANES), 1)
    for block in range(plan.width // LANES):
        joined = None
        for d in range(per):
            part = y_ref[block * per + d].astype(F32)
            if d:
                part = pltpu.roll(part, d * group, 1)
            joined = part if joined is None else jnp.where(lane < d * group, joined, part)
        at = slice(block * LANES, (block + 1) * LANES)
        y = joined + own_ref[:, at].astype(F32)
        full_ref[:, at] = y.astype(BF16).astype(F32) * gate_ref[:, at].astype(F32)
    gated = full_ref[...]
    scale = lax.rsqrt(jnp.mean(gated * gated, axis=-1, keepdims=True) + norm_eps)
    normed = (gated * scale * gain_ref[...]).astype(BF16)
    copies = []
    chunks = sems.shape[0]
    tile = w_ref.shape[1] // chunks
    for k in range(chunks):
        at = slice(k * tile, (k + 1) * tile)
        out = mm(normed, w_ref[:, at])
        for i in range(plan.rows):
            out_ref[i, :, at] = out[i * plan.cols : (i + 1) * plan.cols].astype(BF16)
        copies.append(pltpu.make_async_copy(out_ref.at[:, :, at], out_hbm.at[:, :, at], sems.at[k]))
        copies[-1].start()
    for copy in copies:
        copy.wait()


def finish(plan, y, own, gate, gain, w_out):
    args = (y, own, gate, gain, w_out)
    shape = (plan.rows, plan.cols, w_out.shape[1])
    assert w_out.shape[1] == plan.width
    return call(
        functools.partial(finish_kernel, plan),
        "finish",
        args,
        [(shape, BF16)],
        [((plan.cells, plan.width), F32), (shape, BF16), pltpu.SemaphoreType.DMA((4,))],
        [HBM],
    )[0]


def per_device(slide, tissue, w_in, w_bcd, dt_bias, rate_x, rate_y, d_skip, norm_gain, w_out):
    rows, cols, model_width = slide.shape
    width = w_out.shape[0]
    heads = dt_bias.shape[0]
    states = (w_bcd.shape[1] - heads) // 2
    plan = Plan(rows, cols, states, heads, width, lax.axis_size("col"))
    consts = plan.constants()
    v, pay, table, x = project(plan, consts, slide, w_in, w_bcd, tissue, dt_bias, rate_x, rate_y)
    groups = plan.segments()
    pay = lax.all_to_all(pay, "col", 0, 0, tiled=True, axis_index_groups=groups)
    gain = norm_gain.reshape(1, width)
    own, gate, gain = home(plan, consts, v, table, x, w_in, tissue, gain, rate_x, rate_y, d_skip)
    pay, own, gate, gain = lax.optimization_barrier((pay, own, gate, gain))
    y = scan_calls(plan, consts, "row", "col", pay)
    y = lax.all_to_all(y, "col", 0, 0, tiled=True, axis_index_groups=groups)
    return finish(plan, y, own, gate, gain, w_out)


def solution(mesh):
    placed = (
        P(("slides", "row"), "col", None),
        P(("slides", "row"), "col"),
        P(),
        P(),
        P(),
        P(),
        P(),
        P(),
        P(),
        P(),
    )
    return jax.shard_map(
        per_device,
        mesh=mesh,
        in_specs=placed,
        out_specs=P(("slides", "row"), "col", None),
        check_vma=False,
    )
```

```python
import functools

import jax
import jax.numpy as jnp
import numpy as np
from jax import lax
from jax.experimental import pallas as pl
from jax.experimental.pallas import tpu as pltpu
from jax.sharding import PartitionSpec as P

norm_eps = 1e-05
LANES = 128
HALF = LANES // 2
F32 = jnp.float32
BF16 = jnp.bfloat16


def round_up(value, step):
    return -(-value // step) * step


def in_hbm(x):
    return pltpu.with_memory_space_constraint(x, pltpu.HBM)


def mm(a, b):
    return jnp.dot(a, b, preferred_element_type=F32)


def nt_dot(a, b):
    return lax.dot_general(a, b, (((1,), (1,)), ((), ())), preferred_element_type=F32)


def tn_dot(a, b):
    return lax.dot_general(a, b, (((0,), (0,)), ((), ())), preferred_element_type=F32)


class Plan:
    def __init__(self, rows, cols, states, heads, width, devices):
        self.rows, self.cols, self.states, self.heads = rows, cols, states, heads
        self.width = width
        self.parts = 2 if devices % 2 == 0 and devices > 2 else 1
        self.devices = devices // self.parts
        self.group = width // self.devices
        self.slot = min(self.group, HALF)
        self.slots = self.group // self.slot
        self.work = self.slots * self.devices
        self.head_width = width // heads
        self.col_pad = round_up(cols, 8)
        self.count = rows * cols
        self.half = self.count // 2 // 8 * 8
        self.cells = round_up(self.count, 8)
        self.edge = rows * states
        self.top = states * self.col_pad
        self.bc = 2 * states
        self.at_bc = self.cells
        self.at_dt = self.at_bc + 2 * self.bc
        self.at_rate = self.at_dt + 2 * self.slots
        self.message = round_up(self.at_rate + 1, 8)
        self.tail = self.edge % LANES
        self.solid = self.edge // LANES
        self.share = LANES // self.tail if self.tail else 1
        self.packed = self.slots * self.solid + (-(-self.slots // self.share) if self.tail else 0)
        assert self.head_width % self.slot == 0 and self.group % self.slot == 0
        assert LANES % self.head_width == 0 and LANES % self.group == 0
        assert self.cells - self.half <= LANES
        assert states % 16 == 0 and heads % 8 == 0

    def segments(self):
        return [list(range(p * self.devices, (p + 1) * self.devices)) for p in range(self.parts)]

    def lanes(self):
        at = np.arange(2 * LANES)
        cell = np.where(at < LANES, at, at - LANES + self.half)
        live = np.where(at < LANES, at < self.half, cell < self.count)
        return cell // self.cols, cell % self.cols, live

    def constants(self):
        i, j, real = self.lanes()
        both = real[:, None] & real[None]
        cell = np.arange(self.cells)
        ci, cj = cell // self.cols, cell % self.cols
        creal = cell < self.count
        le = np.arange(round_up(self.rows, 8))
        lj = np.arange(self.col_pad)
        out = {}
        out["to1"] = (j[:, None] <= j[None]) & both
        out["to2"] = (j[:, None] == j[None]) & (i[:, None] <= i[None]) & both
        out["from1"] = (i[:, None] == i[None]) & (j[:, None] > j[None]) & both
        out["from2"] = (i[:, None] > i[None]) & both
        out["side1"] = (i[None] == le[:, None]) & real[None]
        out["side2"] = (i[None] > le[:, None]) & real[None]
        out["sidemask"] = (i[None] >= le[:, None]) & (le < self.rows)[:, None] & real[None]
        out["down1"] = (j[None] <= lj[:, None]) & real[None]
        out["down2"] = (j[None] == lj[:, None]) & real[None]
        out["downmask"] = (j[None] <= lj[:, None]) & (lj < self.cols)[:, None] & real[None]
        out["pick"] = (
            (i == self.rows - 1)[:, None] & real[:, None] & (j[:, None] == np.tile(lj, self.states)[None])
        )
        cboth = creal[:, None] & real[None]
        out["own1"] = (j[None] <= cj[:, None]) & cboth
        out["own2"] = (j[None] == cj[:, None]) & (i[None] <= ci[:, None]) & cboth
        out["ownmask"] = (i[None] <= ci[:, None]) & (j[None] <= cj[:, None]) & cboth
        out["lanei"] = (np.arange(self.rows)[:, None] == i[None]) & real[None]
        out["lanej"] = (np.arange(self.cols)[:, None] == j[None]) & real[None]
        return {k: in_hbm(jnp.asarray(x.astype(np.float32), BF16)) for k, x in out.items()}


def full(shape):
    return pl.BlockSpec(shape, lambda *_: (0,) * len(shape))


HBM = pl.BlockSpec(memory_space=pltpu.HBM)
SMEM = pl.BlockSpec(memory_space=pltpu.SMEM)


def split_cell(plan, cell):
    i = lax.shift_right_logical(cell * (-(-65536 // plan.cols)), 16)
    return i, cell - i * plan.cols


def cell_mask_of(plan, t_ref):
    t = t_ref[...].astype(F32).astype(BF16)
    shape = (plan.cells, plan.cols)
    _, j = split_cell(plan, lax.broadcasted_iota(jnp.int32, shape, 0))
    pick = ones(j == lax.broadcasted_iota(jnp.int32, shape, 1))
    shape = (plan.cells, plan.rows)
    i, _ = split_cell(plan, lax.broadcasted_iota(jnp.int32, shape, 0))
    here = i == lax.broadcasted_iota(jnp.int32, shape, 1)
    return jnp.sum(jnp.where(here, mm(pick, t), 0.0), axis=1, keepdims=True)


def rate_row(heads_of, rx_ref, ry_ref):
    at = lax.broadcasted_iota(jnp.int32, (1, LANES), 1)
    rate = jnp.zeros((1, LANES), F32)
    part = jnp.zeros((1, LANES), jnp.int32)
    for s, head in enumerate(heads_of):
        for k, ref in enumerate((rx_ref, ry_ref)):
            first = 8 * s + 3 * k
            here = (at >= first) & (at < first + 3)
            rate = jnp.where(here, ref[head], rate)
            part = jnp.where(here, at - first, part)
    high = rate.astype(BF16).astype(F32)
    middle = (rate - high).astype(BF16).astype(F32)
    low = rate - high - middle
    return jnp.where(part == 0, high, jnp.where(part == 1, middle, low))


def project_kernel(
    plan, chunks, bias_hbm, rx_hbm, ry_hbm, x_hbm, w_hbm, wt_hbm, t_hbm, lanei_hbm, lanej_hbm,
    v_ref, pay_hbm, rows_ref, flat_ref,
    bias_ref, rx_ref, ry_ref, x_ref, w_ref, wt_ref, t_ref, lanei_ref, lanej_ref, pay_ref, wide, sems, w_sems, out_sems,
):
    group, states, cells, heads = plan.group, plan.states, plan.cells, plan.heads
    half, rest = plan.half, plan.cells - plan.half
    tile = plan.width // chunks
    pairs = (
        (x_hbm, x_ref), (t_hbm, t_ref), (wt_hbm, wt_ref), (lanei_hbm, lanei_ref), (lanej_hbm, lanej_ref),
        (bias_hbm, bias_ref), (rx_hbm, rx_ref), (ry_hbm, ry_ref),
    )
    loads = [pltpu.make_async_copy(a, b, sems.at[k]) for k, (a, b) in enumerate(pairs)]
    copies = [
        pltpu.make_async_copy(w_hbm.at[:, k * tile : (k + 1) * tile], w_ref.at[k], w_sems.at[k])
        for k in range(chunks)
    ]
    for copy in loads + copies:
        copy.start()
    wide[...] = jnp.zeros_like(wide)
    v_ref[half:LANES, :] = jnp.zeros((LANES - half, plan.width), BF16)
    v_ref[LANES + rest :, :] = jnp.zeros((LANES - rest, plan.width), BF16)

    loads[0].wait()
    for i in range(plan.rows):
        wide[i * plan.cols : (i + 1) * plan.cols, :] = x_ref[i].astype(F32)
    x = wide[...].astype(BF16)
    flat_ref[...] = x
    for copy in loads[1:]:
        copy.wait()
    keep = cell_mask_of(plan, t_ref)
    t = t_ref[...].astype(F32).astype(BF16)
    m = jnp.sum(mm(t, lanei_ref[...]) * lanej_ref[...].astype(F32), axis=0, keepdims=True)
    table = nt_dot(wt_ref[...], x)
    ext = jnp.concatenate([table, jnp.zeros((table.shape[0], 2 * LANES - cells), F32)], axis=1)
    lane = lax.broadcasted_iota(jnp.int32, (table.shape[0], LANES), 1)
    lo, hi = ext[:, :LANES], ext[:, LANES:]
    shift = half % LANES
    if shift:
        moved = jnp.where(
            lane < LANES - shift, pltpu.roll(lo, LANES - shift, 1), pltpu.roll(hi, LANES - shift, 1)
        )
    else:
        moved = hi
    table = jnp.concatenate([jnp.where(lane < half, lo, 0.0), jnp.where(lane < plan.count - half, moved, 0.0)], axis=1)
    z = table[2 * states :]
    at = lax.broadcasted_iota(jnp.int32, z.shape, 0)
    for h in range(heads):
        z = jnp.where(at == h, z + bias_ref[h], z)
    soft = m * (jnp.maximum(z, 0.0) + jnp.log1p(jnp.exp(-jnp.abs(z))))
    table = jnp.concatenate([table[: 2 * states], soft], axis=0).astype(BF16)
    rows_ref[...] = table.astype(F32)
    bc = table[: 2 * states]
    steps = rows_ref[2 * states :, :]

    lane = lax.broadcasted_iota(jnp.int32, (cells, LANES), 1)
    sent = []
    for chunk in range(chunks):
        copies[chunk].wait()
        v = mm(flat_ref[...], w_ref[chunk]).astype(BF16).astype(F32) * keep
        low = v.astype(BF16)
        v_ref[0:half, chunk * tile : (chunk + 1) * tile] = low[:half]
        v_ref[LANES : LANES + rest, chunk * tile : (chunk + 1) * tile] = low[half:]
        per = tile // group
        for k in range(per):
            dest = chunk * per + k
            base, at = k * group // LANES * LANES, k * group % LANES
            mine = v[:, base : base + LANES]
            if at:
                mine = pltpu.roll(mine, LANES - at, 1)
            if group < LANES:
                mine = jnp.where(lane < group, mine, 0.0)
            pay_ref[dest, 0:cells, :] = mine.astype(BF16)
            dts, heads_of = [], []
            for s in range(plan.slots):
                head = (chunk * tile + k * group + s * plan.slot) // plan.head_width
                heads_of.append(head)
                dts += [steps[head : head + 1, :LANES], steps[head : head + 1, LANES:]]
            dts.append(rate_row(heads_of, rx_ref, ry_ref))
            pay_ref[dest, plan.at_bc : plan.at_bc + plan.bc, :] = bc[:, :LANES]
            pay_ref[dest, plan.at_bc + plan.bc : plan.at_dt, :] = bc[:, LANES:]
            spare = plan.message - plan.at_dt - len(dts)
            dts += [jnp.zeros((spare, LANES), F32)] if spare else []
            pay_ref[dest, plan.at_dt : plan.message, :] = jnp.concatenate(dts, axis=0).astype(BF16)
        at = slice(chunk * per, (chunk + 1) * per)
        sent.append(pltpu.make_async_copy(pay_ref.at[at], pay_hbm.at[at], out_sems.at[chunk]))
        sent[-1].start()
    for copy in sent:
        copy.wait()


def project(plan, consts, slide, w_in, w_bcd, tissue, dt_bias, rate_x, rate_y):
    chunks = 2
    tile = plan.width // chunks
    depth = slide.shape[2]
    args = [dt_bias, rate_x, rate_y, slide, w_in, w_bcd.T, tissue.T, consts["lanei"], consts["lanej"]]
    count = 2 * plan.states + plan.heads
    assert plan.width % chunks == 0 and tile % plan.group == 0 and tile % LANES == 0
    message = (plan.devices, plan.message, LANES)
    outs = [((2 * LANES, plan.width), BF16), (message, BF16), ((count, 2 * LANES), F32), ((plan.cells, depth), BF16)]
    specs = [full(s) for s, _ in outs]
    specs[1] = HBM
    return pl.pallas_call(
        functools.partial(project_kernel, plan, chunks),
        grid=(1,),
        in_specs=[HBM] * len(args),
        out_specs=specs,
        out_shape=[jax.ShapeDtypeStruct(s, d) for s, d in outs],
        scratch_shapes=[
            pltpu.SMEM(dt_bias.shape, F32),
            pltpu.SMEM(rate_x.shape, F32),
            pltpu.SMEM(rate_y.shape, F32),
            pltpu.VMEM(slide.shape, BF16),
            pltpu.VMEM((chunks, depth, tile), BF16),
        ]
        + [pltpu.VMEM(x.shape, x.dtype) for x in args[5:]]
        + [
            pltpu.VMEM(message, BF16),
            pltpu.VMEM((plan.cells, depth), F32),
            pltpu.SemaphoreType.DMA((8,)),
            pltpu.SemaphoreType.DMA((chunks,)),
            pltpu.SemaphoreType.DMA((chunks,)),
        ],
        compiler_params=pltpu.CompilerParams(vmem_limit_bytes=24 * 2**20),
        name="project",
    )(*[in_hbm(x) for x in args])


def home_kernel(
    plan, rx_ref, ry_ref, skip_ref, w_hbm, v_ref, rows_ref, flat_ref, t_ref, gain_ref,
    own1_ref, own2_ref, from1_ref, from2_ref, mask_ref, out_ref, gate_hbm, gain_out, pair, w_ref, gate_ref, sem, gate_sem,
):
    states, cells, half = plan.states, plan.cells, plan.half
    copy = pltpu.make_async_copy(w_hbm.at[:, plan.width :], w_ref, sem)
    copy.start()
    gain_out[...] = gain_ref[...]
    b = rows_ref[0:states, :].astype(BF16)
    c = rows_ref[states : 2 * states, :].astype(BF16)
    pairs = tn_dot(c, b)
    pairs = jnp.concatenate([pairs[:half], pairs[LANES : LANES + cells - half]], axis=0)
    pair[...] = pairs * mask_ref[...].astype(F32)
    lane = lax.broadcasted_iota(jnp.int32, (cells, LANES), 1)
    per = LANES // plan.head_width
    for block in range(plan.width // LANES):
        v = v_ref[:, block * LANES : (block + 1) * LANES]
        vc = jnp.concatenate([v[:half], v[LANES : LANES + cells - half]], axis=0).astype(F32)
        total = None
        for k in range(per):
            h = block * per + k
            dt = rows_ref[2 * states + h : 2 * states + h + 1, :]
            low = dt.astype(BF16)
            x = mm(own1_ref[...] * low, from1_ref[...])
            y = mm(own2_ref[...] * low, from2_ref[...])
            weight = jnp.exp(-(rx_ref[h] * x + ry_ref[h] * y)) * pair[...] * dt
            part = mm(weight.astype(BF16), v) + skip_ref[h] * vc
            total = part if total is None else jnp.where(lane < k * plan.head_width, total, part)
        out_ref[:, block * LANES : (block + 1) * LANES] = total.astype(BF16)
    keep = cell_mask_of(plan, t_ref)
    copy.wait()
    tile = 2 * LANES
    for block in range(plan.width // tile):
        at = slice(block * tile, (block + 1) * tile)
        z = mm(flat_ref[...], w_ref[:, at]).astype(BF16).astype(F32)
        gate_ref[:, at] = (z * (1.0 / (1.0 + jnp.exp(-z))) * keep).astype(BF16)
    copy = pltpu.make_async_copy(gate_ref, gate_hbm, gate_sem)
    copy.start()
    copy.wait()


def home(plan, consts, v, rows, flat, w_in, tissue, gain, rate_x, rate_y, d_skip):
    args = [in_hbm(w_in), v, rows, flat, in_hbm(tissue.T), in_hbm(gain)]
    args += [consts[k] for k in ("own1", "own2", "from1", "from2", "ownmask")]
    outs = [((plan.cells, plan.width), BF16), ((plan.cells, plan.width), BF16), (gain.shape, F32)]
    return pl.pallas_call(
        functools.partial(home_kernel, plan),
        grid=(1,),
        in_specs=[SMEM, SMEM, SMEM, HBM] + [full(x.shape) for x in args[1:]],
        out_specs=[full(outs[0][0]), HBM, full(outs[2][0])],
        out_shape=[jax.ShapeDtypeStruct(s, d) for s, d in outs],
        scratch_shapes=[
            pltpu.VMEM((plan.cells, 2 * LANES), F32),
            pltpu.VMEM((w_in.shape[0], w_in.shape[1] - plan.width), BF16),
            pltpu.VMEM((plan.cells, plan.width), BF16),
            pltpu.SemaphoreType.DMA,
            pltpu.SemaphoreType.DMA,
        ],
        compiler_params=pltpu.CompilerParams(vmem_limit_bytes=24 * 2**20),
        name="home",
    )(in_hbm(rate_x), in_hbm(rate_y), in_hbm(d_skip), *args)


def ones(mask):
    return jnp.where(mask, 1.0, 0.0).astype(BF16)


def places(plan, shape, axis):
    at = lax.broadcasted_iota(jnp.int32, shape, axis)
    late = at >= LANES
    cell = jnp.where(late, at - (LANES - plan.half), at)
    i, j = split_cell(plan, cell)
    return i, j, cell < jnp.where(late, plan.count, plan.half)


def wide_rows(pay_ref, t, at, count, gap):
    return jnp.concatenate([pay_ref[t, at : at + count, :], pay_ref[t, at + gap : at + gap + count, :]], axis=1)


def turn_all(plan, pay_ref, turned):
    for t in range(plan.devices):
        sides = []
        for lo, hi in ((0, plan.half), (plan.half, plan.cells)):
            v = pay_ref[t, lo:hi, :].astype(F32)
            if hi - lo < LANES:
                v = jnp.concatenate([v, jnp.zeros((LANES - hi + lo, LANES), F32)], axis=0)
            sides.append(v.T)
        v = jnp.concatenate(sides, axis=1).astype(BF16)
        for s in range(plan.slots):
            turned[s * plan.devices + t] = v[s * HALF : (s + 1) * HALF]


def load_steps(plan, pay_ref, dts):
    for t in range(plan.devices):
        rows = pay_ref[t, plan.at_dt : plan.message, :].astype(F32)
        for s in range(plan.slots):
            w = s * plan.devices + t
            dts[w : w + 1, :LANES] = rows[2 * s : 2 * s + 1]
            dts[w : w + 1, LANES:] = rows[2 * s + 1 : 2 * s + 2]


def rates_of(plan, pay_ref, kind):
    row = pay_ref[0, plan.at_dt : plan.message, :].astype(F32)[plan.at_rate - plan.at_dt : plan.at_rate - plan.at_dt + 1]
    at = lax.broadcasted_iota(jnp.int32, (1, LANES), 1)
    first = [8 * s + 3 * kind for s in range(plan.slots)]
    return [jnp.sum(jnp.where((at >= f) & (at < f + 3), row, 0.0), axis=1, keepdims=True) for f in first]


def slot_rates(plan, pay_ref, kind):
    return jnp.concatenate(
        [jnp.broadcast_to(r, (plan.devices, 1)) for r in rates_of(plan, pay_ref, kind)], axis=0
    )


def pack_edges(plan, out_ref, held):
    for s in range(plan.slots):
        for k in range(plan.solid):
            out_ref[s * plan.solid + k] = held[s][:, k * LANES : (k + 1) * LANES].astype(BF16)
    if plan.tail:
        first = plan.slots * plan.solid
        for k in range(plan.packed - first):
            parts = [x[:, plan.solid * LANES :] for x in held[k * plan.share : (k + 1) * plan.share]]
            spare = LANES - plan.tail * len(parts)
            parts += [jnp.zeros((HALF, spare), F32)] if spare else []
            out_ref[first + k] = jnp.concatenate(parts, axis=1).astype(BF16)


def unpack_edges(plan, ref, s):
    parts = [ref[s * plan.solid + k].astype(F32) for k in range(plan.solid)]
    if plan.tail:
        last = ref[plan.slots * plan.solid + s // plan.share].astype(F32)
        at = s % plan.share * plan.tail
        parts.append(last[:, at : at + plan.tail])
    return jnp.concatenate(parts, axis=1)


def scan_edges(plan, pay_ref, turned, dts, inner, kept, seen):
    states, tiles, wide = plan.states, plan.devices, 2 * LANES
    i, j, real = places(plan, (wide, wide), 0)
    ti, tj, treal = places(plan, (wide, wide), 1)
    from1 = ones((i == ti) & (j > tj) & real & treal)
    edge_row = lax.div(lax.broadcasted_iota(jnp.int32, (wide, plan.edge), 1), states)
    i, _, real = places(plan, (wide, plan.edge), 0)
    keep = ones((i == edge_row) & real)
    ti, _, treal = places(plan, (plan.rows, wide), 1)
    rowsel = ones((ti == lax.broadcasted_iota(jnp.int32, (plan.rows, wide), 0)) & treal)
    dt = dts[...]
    low = dt.astype(BF16)
    rate = slot_rates(plan, pay_ref, 0)
    inner[...] = jnp.exp(-rate * mm(low, from1)) * dt
    kept[...] = jnp.exp(-rate * mm(low, keep))
    ends = []
    for s in range(plan.slots):
        held = jnp.zeros((HALF, plan.edge), F32)
        product = jnp.ones((1, plan.edge), F32)
        for t in range(tiles):
            w = s * tiles + t
            seen(w, held, product)
            b = wide_rows(pay_ref, t, plan.at_bc, states, plan.bc).astype(F32)
            bd = (b * inner[w : w + 1, :]).astype(BF16)
            left = jnp.concatenate([bd * rowsel[i : i + 1] for i in range(plan.rows)], axis=0)
            now = kept[w : w + 1, :]
            held = held * now + nt_dot(turned[w], left)
            product = product * now
        ends.append(held)
    return ends


def last_kernel(plan, axis, pay_ref, last_ref, turned, dts, inner):
    @pl.when(lax.axis_index(axis) < (plan.parts - 1) * plan.devices)
    def _():
        states, tiles, wide = plan.states, plan.devices, 2 * LANES
        turn_all(plan, pay_ref, turned)
        load_steps(plan, pay_ref, dts)
        i, j, real = places(plan, (wide, wide), 0)
        ti, tj, treal = places(plan, (wide, wide), 1)
        same = (i == ti) & real & treal
        ti, _, treal = places(plan, (plan.rows, wide), 1)
        rowsel = ones((ti == lax.broadcasted_iota(jnp.int32, (plan.rows, wide), 0)) & treal)
        low = dts[...].astype(BF16)
        rest, whole = mm(low, ones(same & (j > tj))), mm(low, ones(same))
        left = []
        for s in range(plan.slots):
            after = jnp.zeros((1, wide), F32)
            rows = []
            for t in reversed(range(tiles)):
                rows.append(after)
                after = after + whole[s * tiles + t : s * tiles + t + 1]
            left += rows[::-1]
        inner[...] = jnp.exp(-slot_rates(plan, pay_ref, 0) * (rest + jnp.concatenate(left, axis=0))) * dts[...]
        ends = []
        for s in range(plan.slots):
            held = None
            for t in range(tiles):
                w = s * tiles + t
                b = wide_rows(pay_ref, t, plan.at_bc, states, plan.bc).astype(F32)
                bd = (b * inner[w : w + 1, :]).astype(BF16)
                left = jnp.concatenate([bd * rowsel[i : i + 1] for i in range(plan.rows)], axis=0)
                part = nt_dot(turned[w], left)
                held = part if held is None else held + part
            ends.append(held)
        pack_edges(plan, last_ref, ends)


map_names = ("to1", "to2", "from1", "from2", "side1", "side2", "sidemask", "down1", "down2", "downmask", "pick")


def maps_kernel(plan, pay_ref, *refs):
    count = len(map_names)
    maps, refs = refs[:count], refs[count:]
    passed_ref, top_ref, upto_ref, y_ref, left_ref, down_ref = refs[:6]
    turned, dts, inner, kept, s1, s2, d1, d2, edge_ref, side_ref, above_ref = refs[6:17]
    held, sems = refs[17 : 17 + count], refs[17 + count]
    copies = [pltpu.make_async_copy(a, b, sems.at[k]) for k, (a, b) in enumerate(zip(maps, held))]
    for copy in copies:
        copy.start()
    to1_ref, to2_ref, from1_ref, from2_ref, side1_ref, side2_ref = held[:6]
    sidemask_ref, down1_ref, down2_ref, downmask_ref, pick_ref = held[6:]
    states, tiles, cp, work = plan.states, plan.devices, plan.col_pad, plan.work
    rp = side1_ref.shape[0]
    turn_all(plan, pay_ref, turned)
    load_steps(plan, pay_ref, dts)

    def seen(w, held, product):
        edge_ref[w] = held.astype(BF16)
        upto_ref[w : w + 1, :] = product

    scan_edges(plan, pay_ref, turned, dts, inner, kept, seen)
    for copy in copies:
        copy.wait()
    low = dts[...].astype(BF16)
    above_ref[...] = jnp.exp(-slot_rates(plan, pay_ref, 1) * mm(low, to2_ref[...]))
    rates_x, rates_y = rates_of(plan, pay_ref, 0), rates_of(plan, pay_ref, 1)
    for w in range(work):
        rf = dts[w : w + 1, :]
        s1[w * rp : (w + 1) * rp, :] = side1_ref[...].astype(F32) * rf
        s2[w * rp : (w + 1) * rp, :] = side2_ref[...].astype(F32) * rf
        d1[w * cp : (w + 1) * cp, :] = down1_ref[...].astype(F32) * rf
        d2[w * cp : (w + 1) * cp, :] = down2_ref[...].astype(F32) * rf
    mask = sidemask_ref[...].astype(F32)
    x, y = mm(s1[...].astype(BF16), to1_ref[...]), mm(s2[...].astype(BF16), to2_ref[...])
    shape = (states, plan.top)
    n = lax.broadcasted_iota(jnp.int32, shape, 0)
    diag = ones(n == lax.div(lax.broadcasted_iota(jnp.int32, shape, 1), cp))
    for w in range(work):
        s = w // tiles
        at = slice(w * rp, (w + 1) * rp)
        side = (jnp.exp(-(rates_x[s] * x[at] + rates_y[s] * y[at])) * mask).astype(BF16)
        side_ref[w] = side
        bottom = mm(side, pick_ref[...]).astype(BF16)
        passed_ref[w] = jnp.concatenate([diag * bottom[i : i + 1] for i in range(plan.rows)], axis=0)
    x, y = mm(d1[...].astype(BF16), from1_ref[...]), mm(d2[...].astype(BF16), from2_ref[...])
    mask = downmask_ref[...].astype(F32)
    for w in range(work):
        s, t = w // tiles, w % tiles
        at = slice(w * cp, (w + 1) * cp)
        fall = jnp.exp(-(rates_x[s] * x[at] + rates_y[s] * y[at])) * mask * dts[w : w + 1, :]
        b = wide_rows(pay_ref, t, plan.at_bc, states, plan.bc).astype(F32)
        falls = jnp.concatenate([fall * b[n : n + 1] for n in range(states)], axis=0).astype(BF16)
        top_ref[w] = nt_dot(turned[w], falls) + mm(edge_ref[w], passed_ref[w])
    colsel = down2_ref[...].astype(F32)
    for w in range(work):
        c = wide_rows(pay_ref, w % tiles, plan.at_bc + states, states, plan.bc)
        side = side_ref[w]
        left = jnp.concatenate([c * side[i : i + 1] for i in range(plan.rows)], axis=0)
        left_ref[w] = left
        y_ref[w] = mm(edge_ref[w], left)
        ca = c.astype(F32) * above_ref[w : w + 1, :]
        down_ref[w] = jnp.concatenate([colsel * ca[n : n + 1] for n in range(states)], axis=0).astype(BF16)


def join_kernel(plan, upto_ref, entry_ref, passed_ref, top_ref, out_ref, late_ref):
    for s in range(plan.slots):
        entry = unpack_edges(plan, entry_ref, s)
        for t in range(plan.devices):
            w = s * plan.devices + t
            late = (entry * upto_ref[w : w + 1, :]).astype(BF16)
            late_ref[w] = late
            out_ref[w] = (top_ref[w] + mm(late, passed_ref[w])).astype(BF16)


def sides_kernel(plan, y_ref, left_ref, late_ref, out_ref):
    for w in range(plan.work):
        out_ref[w] = y_ref[w] + mm(late_ref[w], left_ref[w])


def cells_kernel(plan, y_ref, down_ref, top_ref, out_ref):
    tiles = plan.devices
    for t in range(tiles):
        ys = [y_ref[w] + mm(top_ref[w], down_ref[w]) for w in range(t, plan.work, tiles)]
        if plan.slots == 1:
            ys.append(jnp.zeros_like(ys[0]))
        y = jnp.concatenate(ys, axis=0)
        for k, (lo, hi) in enumerate(((0, plan.half), (plan.half, plan.cells))):
            out_ref[t, lo:hi, :] = y[:, k * LANES : (k + 1) * LANES].T[: hi - lo].astype(BF16)


def call(kernel, name, args, outs, scratch=(), out_specs=None, in_specs=None):
    return pl.pallas_call(
        kernel,
        grid=(1,),
        in_specs=in_specs or [full(x.shape) for x in args],
        out_specs=out_specs or [full(s) for s, _ in outs],
        out_shape=[jax.ShapeDtypeStruct(s, d) for s, d in outs],
        scratch_shapes=[x if not isinstance(x, tuple) else pltpu.VMEM(*x) for x in scratch],
        compiler_params=pltpu.CompilerParams(vmem_limit_bytes=24 * 2**20),
        name=name,
    )(*args)


def scan_calls(plan, consts, row_axis, col_axis, pay, rate_y):
    work, cp, wide = plan.work, plan.col_pad, 2 * LANES
    rp = consts["side1"].shape[0]
    steps = [((work, HALF, wide), BF16), ((work, wide), F32), ((work, wide), F32), ((work, plan.edge), F32)]
    shape = (plan.packed, HALF, LANES)
    if plan.parts > 1:
        last = call(functools.partial(last_kernel, plan, col_axis), "last", [pay], [(shape, BF16)], steps[:3])[0]
        entry = lax.ppermute(last, col_axis, [(k, k + plan.devices) for k in range(plan.devices)])
    else:
        entry = jnp.zeros(shape, BF16)
    maps = [consts[k] for k in map_names]
    passed, tops, upto, y, left, down = call(
        functools.partial(maps_kernel, plan),
        "maps",
        [pay] + maps,
        [
            ((work, plan.edge, plan.top), BF16),
            ((work, HALF, plan.top), F32),
            ((work, plan.edge), F32),
            ((work, HALF, wide), F32),
            ((work, plan.edge, wide), BF16),
            ((work, plan.top, wide), BF16),
        ],
        steps
        + [((work * rp, wide), F32)] * 2
        + [((work * cp, wide), F32)] * 2
        + [((work, HALF, plan.edge), BF16), ((work, rp, wide), BF16), ((work, wide), F32)]
        + [(x.shape, BF16) for x in maps]
        + [pltpu.SemaphoreType.DMA((len(maps),))],
        in_specs=[full(pay.shape)] + [HBM] * len(maps),
    )
    tops, late = call(
        functools.partial(join_kernel, plan),
        "join",
        [upto, entry, passed, tops],
        [((work, HALF, plan.top), BF16), ((work, HALF, plan.edge), BF16)],
    )
    count = lax.axis_size(row_axis)
    chain = [(r, r + 1) for r in range(count - 1)]
    entry = lax.ppermute(tops, row_axis, chain)
    if count > 2:
        place = lax.rem(lax.axis_index(col_axis), plan.devices) * plan.group
        spread = jnp.tile(consts["down2"].T, (1, plan.states))
        keep = []
        for s in range(plan.slots):
            dt = pay[:, plan.at_dt + 2 * s : plan.at_dt + 2 * s + 2].reshape(plan.devices, wide)
            rate = rate_y[(place + s * plan.slot) // plan.head_width]
            keep.append(jnp.exp(-rate * jnp.dot(dt, spread, preferred_element_type=F32)))
        keep = jnp.concatenate(keep, axis=0)[:, None, :]
        for _ in range(count - 2):
            entry = lax.ppermute(
                (tops.astype(F32) + keep * entry.astype(F32)).astype(BF16), row_axis, chain
            )
    y = call(
        functools.partial(sides_kernel, plan), "sides", [y, left, late], [((work, HALF, wide), F32)]
    )[0]
    return call(
        functools.partial(cells_kernel, plan),
        "cells",
        [y, down, entry],
        [((plan.devices, plan.cells, LANES), BF16)],
    )[0]


def finish_kernel(plan, y_ref, own_ref, gate_ref, gain_ref, w_ref, out_hbm, full_ref, out_ref, sems):
    group = plan.group
    per = LANES // group
    lane = lax.broadcasted_iota(jnp.int32, (plan.cells, LANES), 1)
    for block in range(plan.width // LANES):
        joined = None
        for d in range(per):
            part = y_ref[block * per + d].astype(F32)
            if d:
                part = pltpu.roll(part, d * group, 1)
            joined = part if joined is None else jnp.where(lane < d * group, joined, part)
        at = slice(block * LANES, (block + 1) * LANES)
        y = joined + own_ref[:, at].astype(F32)
        full_ref[:, at] = y.astype(BF16).astype(F32) * gate_ref[:, at].astype(F32)
    gated = full_ref[...]
    scale = lax.rsqrt(jnp.mean(gated * gated, axis=-1, keepdims=True) + norm_eps)
    normed = (gated * scale * gain_ref[...]).astype(BF16)
    copies = []
    chunks = sems.shape[0]
    tile = w_ref.shape[1] // chunks
    for k in range(chunks):
        at = slice(k * tile, (k + 1) * tile)
        out = mm(normed, w_ref[:, at])
        for i in range(plan.rows):
            out_ref[i, :, at] = out[i * plan.cols : (i + 1) * plan.cols].astype(BF16)
        copies.append(pltpu.make_async_copy(out_ref.at[:, :, at], out_hbm.at[:, :, at], sems.at[k]))
        copies[-1].start()
    for copy in copies:
        copy.wait()


def finish(plan, y, own, gate, gain, w_out):
    args = (y, own, gate, gain, w_out)
    shape = (plan.rows, plan.cols, w_out.shape[1])
    assert w_out.shape[1] == plan.width
    return call(
        functools.partial(finish_kernel, plan),
        "finish",
        args,
        [(shape, BF16)],
        [((plan.cells, plan.width), F32), (shape, BF16), pltpu.SemaphoreType.DMA((4,))],
        [HBM],
    )[0]


def per_device(slide, tissue, w_in, w_bcd, dt_bias, rate_x, rate_y, d_skip, norm_gain, w_out):
    rows, cols, model_width = slide.shape
    width = w_out.shape[0]
    heads = dt_bias.shape[0]
    states = (w_bcd.shape[1] - heads) // 2
    plan = Plan(rows, cols, states, heads, width, lax.axis_size("col"))
    consts = plan.constants()
    v, pay, table, x = project(plan, consts, slide, w_in, w_bcd, tissue, dt_bias, rate_x, rate_y)
    groups = plan.segments()
    pay = lax.all_to_all(pay, "col", 0, 0, tiled=True, axis_index_groups=groups)
    gain = norm_gain.reshape(1, width)
    own, gate, gain = home(plan, consts, v, table, x, w_in, tissue, gain, rate_x, rate_y, d_skip)
    pay, own, gate, gain = lax.optimization_barrier((pay, own, gate, gain))
    y = scan_calls(plan, consts, "row", "col", pay, rate_y)
    y = lax.all_to_all(y, "col", 0, 0, tiled=True, axis_index_groups=groups)
    return finish(plan, y, own, gate, gain, w_out)


def solution(mesh):
    placed = (
        P(("slides", "row"), "col", None),
        P(("slides", "row"), "col"),
        P(),
        P(),
        P(),
        P(),
        P(),
        P(),
        P(),
        P(),
    )
    return jax.shard_map(
        per_device,
        mesh=mesh,
        in_specs=placed,
        out_specs=P(("slides", "row"), "col", None),
        check_vma=False,
    )
```

```python
import functools

import jax
import jax.numpy as jnp
import numpy as np
from jax import lax
from jax.experimental import pallas as pl
from jax.experimental.pallas import tpu as pltpu
from jax.sharding import PartitionSpec as P

norm_eps = 1e-05
LANES = 128
HALF = LANES // 2
F32 = jnp.float32
BF16 = jnp.bfloat16


def round_up(value, step):
    return -(-value // step) * step


def in_hbm(x):
    return pltpu.with_memory_space_constraint(x, pltpu.HBM)


def mm(a, b):
    return jnp.dot(a, b, preferred_element_type=F32)


def nt_dot(a, b):
    return lax.dot_general(a, b, (((1,), (1,)), ((), ())), preferred_element_type=F32)


def tn_dot(a, b):
    return lax.dot_general(a, b, (((0,), (0,)), ((), ())), preferred_element_type=F32)


class Plan:
    def __init__(self, rows, cols, states, heads, width, devices):
        self.rows, self.cols, self.states, self.heads = rows, cols, states, heads
        self.width = width
        self.parts = 2 if devices % 2 == 0 and devices > 2 else 1
        self.devices = devices // self.parts
        self.group = width // self.devices
        self.slot = min(self.group, HALF)
        self.slots = self.group // self.slot
        self.work = self.slots * self.devices
        self.head_width = width // heads
        self.col_pad = round_up(cols, 8)
        self.count = rows * cols
        self.half = self.count // 2 // 8 * 8
        self.cells = round_up(self.count, 8)
        self.edge = rows * states
        self.top = states * self.col_pad
        self.bc = 2 * states
        self.at_bc = self.cells
        self.at_dt = self.at_bc + 2 * self.bc
        self.at_rate = self.at_dt + 2 * self.slots
        self.message = round_up(self.at_rate + 1, 8)
        self.tail = self.edge % LANES
        self.solid = self.edge // LANES
        self.share = LANES // self.tail if self.tail else 1
        self.packed = self.slots * self.solid + (-(-self.slots // self.share) if self.tail else 0)
        assert self.head_width % self.slot == 0 and self.group % self.slot == 0
        assert LANES % self.head_width == 0 and LANES % self.group == 0
        assert self.cells - self.half <= LANES
        assert states % 16 == 0 and heads % 8 == 0

    def segments(self):
        return [list(range(p * self.devices, (p + 1) * self.devices)) for p in range(self.parts)]

    def lanes(self):
        at = np.arange(2 * LANES)
        cell = np.where(at < LANES, at, at - LANES + self.half)
        live = np.where(at < LANES, at < self.half, cell < self.count)
        return cell // self.cols, cell % self.cols, live

    def constants(self):
        i, j, real = self.lanes()
        both = real[:, None] & real[None]
        cell = np.arange(self.cells)
        ci, cj = cell // self.cols, cell % self.cols
        creal = cell < self.count
        le = np.arange(round_up(self.rows, 8))
        lj = np.arange(self.col_pad)
        out = {}
        out["to1"] = (j[:, None] <= j[None]) & both
        out["to2"] = (j[:, None] == j[None]) & (i[:, None] <= i[None]) & both
        out["from1"] = (i[:, None] == i[None]) & (j[:, None] > j[None]) & both
        out["from2"] = (i[:, None] > i[None]) & both
        out["side1"] = (i[None] == le[:, None]) & real[None]
        out["side2"] = (i[None] > le[:, None]) & real[None]
        out["sidemask"] = (i[None] >= le[:, None]) & (le < self.rows)[:, None] & real[None]
        out["down1"] = (j[None] <= lj[:, None]) & real[None]
        out["down2"] = (j[None] == lj[:, None]) & real[None]
        out["downmask"] = (j[None] <= lj[:, None]) & (lj < self.cols)[:, None] & real[None]
        out["pick"] = (
            (i == self.rows - 1)[:, None] & real[:, None] & (j[:, None] == np.tile(lj, self.states)[None])
        )
        cboth = creal[:, None] & real[None]
        out["own1"] = (j[None] <= cj[:, None]) & cboth
        out["own2"] = (j[None] == cj[:, None]) & (i[None] <= ci[:, None]) & cboth
        out["ownmask"] = (i[None] <= ci[:, None]) & (j[None] <= cj[:, None]) & cboth
        out["lanei"] = (np.arange(self.rows)[:, None] == i[None]) & real[None]
        out["lanej"] = (np.arange(self.cols)[:, None] == j[None]) & real[None]
        return {k: in_hbm(jnp.asarray(x.astype(np.float32), BF16)) for k, x in out.items()}


def full(shape):
    return pl.BlockSpec(shape, lambda *_: (0,) * len(shape))


HBM = pl.BlockSpec(memory_space=pltpu.HBM)
SMEM = pl.BlockSpec(memory_space=pltpu.SMEM)


def split_cell(plan, cell):
    i = lax.shift_right_logical(cell * (-(-65536 // plan.cols)), 16)
    return i, cell - i * plan.cols


def cell_mask_of(plan, t_ref):
    t = t_ref[...].astype(F32).astype(BF16)
    shape = (plan.cells, plan.cols)
    _, j = split_cell(plan, lax.broadcasted_iota(jnp.int32, shape, 0))
    pick = ones(j == lax.broadcasted_iota(jnp.int32, shape, 1))
    shape = (plan.cells, plan.rows)
    i, _ = split_cell(plan, lax.broadcasted_iota(jnp.int32, shape, 0))
    here = i == lax.broadcasted_iota(jnp.int32, shape, 1)
    return jnp.sum(jnp.where(here, mm(pick, t), 0.0), axis=1, keepdims=True)


def rate_row(heads_of, rx_ref, ry_ref):
    at = lax.broadcasted_iota(jnp.int32, (1, LANES), 1)
    rate = jnp.zeros((1, LANES), F32)
    part = jnp.zeros((1, LANES), jnp.int32)
    for s, head in enumerate(heads_of):
        for k, ref in enumerate((rx_ref, ry_ref)):
            first = 8 * s + 3 * k
            here = (at >= first) & (at < first + 3)
            rate = jnp.where(here, ref[head], rate)
            part = jnp.where(here, at - first, part)
    high = rate.astype(BF16).astype(F32)
    middle = (rate - high).astype(BF16).astype(F32)
    low = rate - high - middle
    return jnp.where(part == 0, high, jnp.where(part == 1, middle, low))


def project_kernel(
    plan, chunks, bias_hbm, rx_hbm, ry_hbm, x_hbm, w_hbm, wt_hbm, t_hbm, lanei_hbm, lanej_hbm,
    v_ref, pay_hbm, rows_ref, flat_ref,
    bias_ref, rx_ref, ry_ref, x_ref, w_ref, wt_ref, t_ref, lanei_ref, lanej_ref, pay_ref, wide, sems, w_sems, out_sems,
):
    group, states, cells, heads = plan.group, plan.states, plan.cells, plan.heads
    half, rest = plan.half, plan.cells - plan.half
    tile = plan.width // chunks
    pairs = (
        (x_hbm, x_ref), (t_hbm, t_ref), (wt_hbm, wt_ref), (lanei_hbm, lanei_ref), (lanej_hbm, lanej_ref),
        (bias_hbm, bias_ref), (rx_hbm, rx_ref), (ry_hbm, ry_ref),
    )
    loads = [pltpu.make_async_copy(a, b, sems.at[k]) for k, (a, b) in enumerate(pairs)]
    copies = [
        pltpu.make_async_copy(w_hbm.at[:, k * tile : (k + 1) * tile], w_ref.at[k], w_sems.at[k])
        for k in range(chunks)
    ]
    for copy in loads + copies:
        copy.start()
    wide[...] = jnp.zeros_like(wide)
    v_ref[half:LANES, :] = jnp.zeros((LANES - half, plan.width), BF16)
    v_ref[LANES + rest :, :] = jnp.zeros((LANES - rest, plan.width), BF16)

    loads[0].wait()
    for i in range(plan.rows):
        wide[i * plan.cols : (i + 1) * plan.cols, :] = x_ref[i].astype(F32)
    x = wide[...].astype(BF16)
    flat_ref[...] = x
    for copy in loads[1:]:
        copy.wait()
    keep = cell_mask_of(plan, t_ref)
    t = t_ref[...].astype(F32).astype(BF16)
    m = jnp.sum(mm(t, lanei_ref[...]) * lanej_ref[...].astype(F32), axis=0, keepdims=True)
    table = nt_dot(wt_ref[...], x)
    ext = jnp.concatenate([table, jnp.zeros((table.shape[0], 2 * LANES - cells), F32)], axis=1)
    lane = lax.broadcasted_iota(jnp.int32, (table.shape[0], LANES), 1)
    lo, hi = ext[:, :LANES], ext[:, LANES:]
    shift = half % LANES
    if shift:
        moved = jnp.where(
            lane < LANES - shift, pltpu.roll(lo, LANES - shift, 1), pltpu.roll(hi, LANES - shift, 1)
        )
    else:
        moved = hi
    table = jnp.concatenate([jnp.where(lane < half, lo, 0.0), jnp.where(lane < plan.count - half, moved, 0.0)], axis=1)
    z = table[2 * states :]
    at = lax.broadcasted_iota(jnp.int32, z.shape, 0)
    for h in range(heads):
        z = jnp.where(at == h, z + bias_ref[h], z)
    soft = m * (jnp.maximum(z, 0.0) + jnp.log1p(jnp.exp(-jnp.abs(z))))
    table = jnp.concatenate([table[: 2 * states], soft], axis=0).astype(BF16)
    rows_ref[...] = table.astype(F32)
    bc = table[: 2 * states]
    steps = rows_ref[2 * states :, :]

    lane = lax.broadcasted_iota(jnp.int32, (cells, LANES), 1)
    sent = []
    for chunk in range(chunks):
        copies[chunk].wait()
        v = mm(flat_ref[...], w_ref[chunk]).astype(BF16).astype(F32) * keep
        low = v.astype(BF16)
        v_ref[0:half, chunk * tile : (chunk + 1) * tile] = low[:half]
        v_ref[LANES : LANES + rest, chunk * tile : (chunk + 1) * tile] = low[half:]
        per = tile // group
        for k in range(per):
            dest = chunk * per + k
            base, at = k * group // LANES * LANES, k * group % LANES
            mine = v[:, base : base + LANES]
            if at:
                mine = pltpu.roll(mine, LANES - at, 1)
            if group < LANES:
                mine = jnp.where(lane < group, mine, 0.0)
            pay_ref[dest, 0:cells, :] = mine.astype(BF16)
            dts, heads_of = [], []
            for s in range(plan.slots):
                head = (chunk * tile + k * group + s * plan.slot) // plan.head_width
                heads_of.append(head)
                dts += [steps[head : head + 1, :LANES], steps[head : head + 1, LANES:]]
            dts.append(rate_row(heads_of, rx_ref, ry_ref))
            pay_ref[dest, plan.at_bc : plan.at_bc + plan.bc, :] = bc[:, :LANES]
            pay_ref[dest, plan.at_bc + plan.bc : plan.at_dt, :] = bc[:, LANES:]
            spare = plan.message - plan.at_dt - len(dts)
            dts += [jnp.zeros((spare, LANES), F32)] if spare else []
            pay_ref[dest, plan.at_dt : plan.message, :] = jnp.concatenate(dts, axis=0).astype(BF16)
            sent.append(pltpu.make_async_copy(pay_ref.at[dest], pay_hbm.at[dest], out_sems.at[dest]))
            sent[-1].start()
    for copy in sent:
        copy.wait()


def project(plan, consts, slide, w_in, w_bcd, tissue, dt_bias, rate_x, rate_y):
    chunks = 2
    tile = plan.width // chunks
    depth = slide.shape[2]
    args = [dt_bias, rate_x, rate_y, slide, w_in, w_bcd.T, tissue.T, consts["lanei"], consts["lanej"]]
    count = 2 * plan.states + plan.heads
    assert plan.width % chunks == 0 and tile % plan.group == 0 and tile % LANES == 0
    message = (plan.devices, plan.message, LANES)
    outs = [((2 * LANES, plan.width), BF16), (message, BF16), ((count, 2 * LANES), F32), ((plan.cells, depth), BF16)]
    specs = [full(s) for s, _ in outs]
    specs[1] = HBM
    return pl.pallas_call(
        functools.partial(project_kernel, plan, chunks),
        grid=(1,),
        in_specs=[HBM] * len(args),
        out_specs=specs,
        out_shape=[jax.ShapeDtypeStruct(s, d) for s, d in outs],
        scratch_shapes=[
            pltpu.SMEM(dt_bias.shape, F32),
            pltpu.SMEM(rate_x.shape, F32),
            pltpu.SMEM(rate_y.shape, F32),
            pltpu.VMEM(slide.shape, BF16),
            pltpu.VMEM((chunks, depth, tile), BF16),
        ]
        + [pltpu.VMEM(x.shape, x.dtype) for x in args[5:]]
        + [
            pltpu.VMEM(message, BF16),
            pltpu.VMEM((plan.cells, depth), F32),
            pltpu.SemaphoreType.DMA((8,)),
            pltpu.SemaphoreType.DMA((chunks,)),
            pltpu.SemaphoreType.DMA((plan.devices,)),
        ],
        compiler_params=pltpu.CompilerParams(vmem_limit_bytes=24 * 2**20),
        name="project",
    )(*[in_hbm(x) for x in args])


def home_kernel(plan, v_ref, rows_ref, flat_ref, w_hbm, *refs):
    sources, refs = refs[:9], refs[9:]
    gain_hbm, out_ref, gate_hbm, gain_out, pair, w_ref, gate_ref = refs[:7]
    held, (sem, gain_sem, sems, gate_sems) = refs[7:16], refs[16:]
    states, cells, half = plan.states, plan.cells, plan.half
    reads = [pltpu.make_async_copy(a, b, sems.at[k]) for k, (a, b) in enumerate(zip(sources, held))]
    reads.append(pltpu.make_async_copy(gain_hbm, gain_out, gain_sem))
    copy = pltpu.make_async_copy(w_hbm.at[:, plan.width :], w_ref, sem)
    for each in reads + [copy]:
        each.start()
    rx_ref, ry_ref, skip_ref, t_ref, own1_ref, own2_ref, from1_ref, from2_ref, mask_ref = held
    b = rows_ref[0:states, :].astype(BF16)
    c = rows_ref[states : 2 * states, :].astype(BF16)
    pairs = tn_dot(c, b)
    pairs = jnp.concatenate([pairs[:half], pairs[LANES : LANES + cells - half]], axis=0)
    for each in reads:
        each.wait()
    pair[...] = pairs * mask_ref[...].astype(F32)
    lane = lax.broadcasted_iota(jnp.int32, (cells, LANES), 1)
    per = LANES // plan.head_width
    for block in range(plan.width // LANES):
        v = v_ref[:, block * LANES : (block + 1) * LANES]
        vc = jnp.concatenate([v[:half], v[LANES : LANES + cells - half]], axis=0).astype(F32)
        total = None
        for k in range(per):
            h = block * per + k
            dt = rows_ref[2 * states + h : 2 * states + h + 1, :]
            low = dt.astype(BF16)
            x = mm(own1_ref[...] * low, from1_ref[...])
            y = mm(own2_ref[...] * low, from2_ref[...])
            weight = jnp.exp(-(rx_ref[h] * x + ry_ref[h] * y)) * pair[...] * dt
            part = mm(weight.astype(BF16), v) + skip_ref[h] * vc
            total = part if total is None else jnp.where(lane < k * plan.head_width, total, part)
        out_ref[:, block * LANES : (block + 1) * LANES] = total.astype(BF16)
    keep = cell_mask_of(plan, t_ref)
    copy.wait()
    tile = plan.width // gate_sems.shape[0]
    sent = []
    for block in range(plan.width // tile):
        at = slice(block * tile, (block + 1) * tile)
        z = mm(flat_ref[...], w_ref[:, at]).astype(BF16).astype(F32)
        gate_ref[:, at] = (z * (1.0 / (1.0 + jnp.exp(-z))) * keep).astype(BF16)
        sent.append(pltpu.make_async_copy(gate_ref.at[:, at], gate_hbm.at[:, at], gate_sems.at[block]))
        sent[-1].start()
    for each in sent:
        each.wait()


def home(plan, consts, v, rows, flat, w_in, tissue, gain, rate_x, rate_y, d_skip):
    sources = [rate_x, rate_y, d_skip, tissue.T] + [consts[k] for k in ("own1", "own2", "from1", "from2", "ownmask")]
    fixed = [in_hbm(x) for x in [w_in] + sources + [gain]]
    outs = [((plan.cells, plan.width), BF16), ((plan.cells, plan.width), BF16), (gain.shape, F32)]
    return pl.pallas_call(
        functools.partial(home_kernel, plan),
        grid=(1,),
        in_specs=[full(x.shape) for x in (v, rows, flat)] + [HBM] * len(fixed),
        out_specs=[full(outs[0][0]), HBM, full(outs[2][0])],
        out_shape=[jax.ShapeDtypeStruct(s, d) for s, d in outs],
        scratch_shapes=[
            pltpu.VMEM((plan.cells, 2 * LANES), F32),
            pltpu.VMEM((w_in.shape[0], w_in.shape[1] - plan.width), BF16),
            pltpu.VMEM((plan.cells, plan.width), BF16),
        ]
        + [pltpu.SMEM(x.shape, F32) for x in sources[:3]]
        + [pltpu.VMEM(x.shape, x.dtype) for x in sources[3:]]
        + [
            pltpu.SemaphoreType.DMA,
            pltpu.SemaphoreType.DMA,
            pltpu.SemaphoreType.DMA((len(sources),)),
            pltpu.SemaphoreType.DMA((4,)),
        ],
        compiler_params=pltpu.CompilerParams(vmem_limit_bytes=24 * 2**20),
        name="home",
    )(v, rows, flat, *fixed)


def ones(mask):
    return jnp.where(mask, 1.0, 0.0).astype(BF16)


def places(plan, shape, axis):
    at = lax.broadcasted_iota(jnp.int32, shape, axis)
    late = at >= LANES
    cell = jnp.where(late, at - (LANES - plan.half), at)
    i, j = split_cell(plan, cell)
    return i, j, cell < jnp.where(late, plan.count, plan.half)


def wide_rows(pay_ref, t, at, count, gap):
    return jnp.concatenate([pay_ref[t, at : at + count, :], pay_ref[t, at + gap : at + gap + count, :]], axis=1)


def turn_all(plan, pay_ref, turned):
    for t in range(plan.devices):
        sides = []
        for lo, hi in ((0, plan.half), (plan.half, plan.cells)):
            v = pay_ref[t, lo:hi, :].astype(F32)
            if hi - lo < LANES:
                v = jnp.concatenate([v, jnp.zeros((LANES - hi + lo, LANES), F32)], axis=0)
            sides.append(v.T)
        v = jnp.concatenate(sides, axis=1).astype(BF16)
        for s in range(plan.slots):
            turned[s * plan.devices + t] = v[s * HALF : (s + 1) * HALF]


def load_steps(plan, pay_ref, dts):
    for t in range(plan.devices):
        rows = pay_ref[t, plan.at_dt : plan.message, :].astype(F32)
        for s in range(plan.slots):
            w = s * plan.devices + t
            dts[w : w + 1, :LANES] = rows[2 * s : 2 * s + 1]
            dts[w : w + 1, LANES:] = rows[2 * s + 1 : 2 * s + 2]


def rates_of(plan, pay_ref, kind):
    row = pay_ref[0, plan.at_dt : plan.message, :].astype(F32)[plan.at_rate - plan.at_dt : plan.at_rate - plan.at_dt + 1]
    at = lax.broadcasted_iota(jnp.int32, (1, LANES), 1)
    first = [8 * s + 3 * kind for s in range(plan.slots)]
    return [jnp.sum(jnp.where((at >= f) & (at < f + 3), row, 0.0), axis=1, keepdims=True) for f in first]


def slot_rates(plan, pay_ref, kind):
    return jnp.concatenate(
        [jnp.broadcast_to(r, (plan.devices, 1)) for r in rates_of(plan, pay_ref, kind)], axis=0
    )


def pack_edges(plan, out_ref, held):
    for s in range(plan.slots):
        for k in range(plan.solid):
            out_ref[s * plan.solid + k] = held[s][:, k * LANES : (k + 1) * LANES].astype(BF16)
    if plan.tail:
        first = plan.slots * plan.solid
        for k in range(plan.packed - first):
            parts = [x[:, plan.solid * LANES :] for x in held[k * plan.share : (k + 1) * plan.share]]
            spare = LANES - plan.tail * len(parts)
            parts += [jnp.zeros((HALF, spare), F32)] if spare else []
            out_ref[first + k] = jnp.concatenate(parts, axis=1).astype(BF16)


def unpack_edges(plan, ref, s):
    parts = [ref[s * plan.solid + k].astype(F32) for k in range(plan.solid)]
    if plan.tail:
        last = ref[plan.slots * plan.solid + s // plan.share].astype(F32)
        at = s % plan.share * plan.tail
        parts.append(last[:, at : at + plan.tail])
    return jnp.concatenate(parts, axis=1)


def scan_edges(plan, pay_ref, turned, dts, inner, kept, seen):
    states, tiles, wide = plan.states, plan.devices, 2 * LANES
    i, j, real = places(plan, (wide, wide), 0)
    ti, tj, treal = places(plan, (wide, wide), 1)
    from1 = ones((i == ti) & (j > tj) & real & treal)
    edge_row = lax.div(lax.broadcasted_iota(jnp.int32, (wide, plan.edge), 1), states)
    i, _, real = places(plan, (wide, plan.edge), 0)
    keep = ones((i == edge_row) & real)
    ti, _, treal = places(plan, (plan.rows, wide), 1)
    rowsel = ones((ti == lax.broadcasted_iota(jnp.int32, (plan.rows, wide), 0)) & treal)
    dt = dts[...]
    low = dt.astype(BF16)
    rate = slot_rates(plan, pay_ref, 0)
    inner[...] = jnp.exp(-rate * mm(low, from1)) * dt
    kept[...] = jnp.exp(-rate * mm(low, keep))
    ends = []
    for s in range(plan.slots):
        held = jnp.zeros((HALF, plan.edge), F32)
        product = jnp.ones((1, plan.edge), F32)
        for t in range(tiles):
            w = s * tiles + t
            seen(w, held, product)
            b = wide_rows(pay_ref, t, plan.at_bc, states, plan.bc).astype(F32)
            bd = (b * inner[w : w + 1, :]).astype(BF16)
            left = jnp.concatenate([bd * rowsel[i : i + 1] for i in range(plan.rows)], axis=0)
            now = kept[w : w + 1, :]
            held = held * now + nt_dot(turned[w], left)
            product = product * now
        ends.append(held)
    return ends


def last_kernel(plan, axis, pay_ref, last_ref, turned, dts, inner):
    @pl.when(lax.axis_index(axis) < (plan.parts - 1) * plan.devices)
    def _():
        states, tiles, wide = plan.states, plan.devices, 2 * LANES
        turn_all(plan, pay_ref, turned)
        load_steps(plan, pay_ref, dts)
        i, j, real = places(plan, (wide, wide), 0)
        ti, tj, treal = places(plan, (wide, wide), 1)
        same = (i == ti) & real & treal
        ti, _, treal = places(plan, (plan.rows, wide), 1)
        rowsel = ones((ti == lax.broadcasted_iota(jnp.int32, (plan.rows, wide), 0)) & treal)
        low = dts[...].astype(BF16)
        rest, whole = mm(low, ones(same & (j > tj))), mm(low, ones(same))
        left = []
        for s in range(plan.slots):
            after = jnp.zeros((1, wide), F32)
            rows = []
            for t in reversed(range(tiles)):
                rows.append(after)
                after = after + whole[s * tiles + t : s * tiles + t + 1]
            left += rows[::-1]
        inner[...] = jnp.exp(-slot_rates(plan, pay_ref, 0) * (rest + jnp.concatenate(left, axis=0))) * dts[...]
        ends = []
        for s in range(plan.slots):
            held = None
            for t in range(tiles):
                w = s * tiles + t
                b = wide_rows(pay_ref, t, plan.at_bc, states, plan.bc).astype(F32)
                bd = (b * inner[w : w + 1, :]).astype(BF16)
                left = jnp.concatenate([bd * rowsel[i : i + 1] for i in range(plan.rows)], axis=0)
                part = nt_dot(turned[w], left)
                held = part if held is None else held + part
            ends.append(held)
        pack_edges(plan, last_ref, ends)


def maps_kernel(
    plan, pay_ref, to1_ref, to2_ref, from1_ref, from2_ref, side1_ref, side2_ref,
    sidemask_ref, down1_ref, down2_ref, downmask_ref, pick_ref,
    side_ref, above_ref, passed_ref, top_ref, edge_ref, upto_ref, turned, dts, inner, kept, s1, s2, d1, d2,
):
    states, tiles, cp, work = plan.states, plan.devices, plan.col_pad, plan.work
    rp = side1_ref.shape[0]
    turn_all(plan, pay_ref, turned)
    load_steps(plan, pay_ref, dts)

    def seen(w, held, product):
        edge_ref[w] = held.astype(BF16)
        upto_ref[w : w + 1, :] = product

    scan_edges(plan, pay_ref, turned, dts, inner, kept, seen)
    low = dts[...].astype(BF16)
    above_ref[...] = jnp.exp(-slot_rates(plan, pay_ref, 1) * mm(low, to2_ref[...]))
    rates_x, rates_y = rates_of(plan, pay_ref, 0), rates_of(plan, pay_ref, 1)
    for w in range(work):
        rf = dts[w : w + 1, :]
        s1[w * rp : (w + 1) * rp, :] = side1_ref[...].astype(F32) * rf
        s2[w * rp : (w + 1) * rp, :] = side2_ref[...].astype(F32) * rf
        d1[w * cp : (w + 1) * cp, :] = down1_ref[...].astype(F32) * rf
        d2[w * cp : (w + 1) * cp, :] = down2_ref[...].astype(F32) * rf
    mask = sidemask_ref[...].astype(F32)
    x, y = mm(s1[...].astype(BF16), to1_ref[...]), mm(s2[...].astype(BF16), to2_ref[...])
    shape = (states, plan.top)
    n = lax.broadcasted_iota(jnp.int32, shape, 0)
    diag = ones(n == lax.div(lax.broadcasted_iota(jnp.int32, shape, 1), cp))
    for w in range(work):
        s = w // tiles
        at = slice(w * rp, (w + 1) * rp)
        side = (jnp.exp(-(rates_x[s] * x[at] + rates_y[s] * y[at])) * mask).astype(BF16)
        side_ref[w] = side
        bottom = mm(side, pick_ref[...]).astype(BF16)
        passed_ref[w] = jnp.concatenate([diag * bottom[i : i + 1] for i in range(plan.rows)], axis=0)
    x, y = mm(d1[...].astype(BF16), from1_ref[...]), mm(d2[...].astype(BF16), from2_ref[...])
    mask = downmask_ref[...].astype(F32)
    for w in range(work):
        s, t = w // tiles, w % tiles
        at = slice(w * cp, (w + 1) * cp)
        fall = jnp.exp(-(rates_x[s] * x[at] + rates_y[s] * y[at])) * mask * dts[w : w + 1, :]
        b = wide_rows(pay_ref, t, plan.at_bc, states, plan.bc).astype(F32)
        falls = jnp.concatenate([fall * b[n : n + 1] for n in range(states)], axis=0).astype(BF16)
        top_ref[w] = nt_dot(turned[w], falls) + mm(edge_ref[w], passed_ref[w])


def join_kernel(plan, upto_ref, entry_ref, passed_ref, top_ref, out_ref):
    for s in range(plan.slots):
        entry = unpack_edges(plan, entry_ref, s)
        for t in range(plan.devices):
            w = s * plan.devices + t
            late = (entry * upto_ref[w : w + 1, :]).astype(BF16)
            out_ref[w] = (top_ref[w] + mm(late, passed_ref[w])).astype(BF16)


def sides_kernel(plan, pay_ref, edge_ref, upto_ref, entry_ref, side_ref, above_ref, y_ref, down_ref):
    states, tiles = plan.states, plan.devices
    shape = (plan.col_pad, 2 * LANES)
    _, tj, treal = places(plan, shape, 1)
    colsel = jnp.where((tj == lax.broadcasted_iota(jnp.int32, shape, 0)) & treal, 1.0, 0.0)
    for s in range(plan.slots):
        entry = unpack_edges(plan, entry_ref, s)
        for t in range(tiles):
            w = s * tiles + t
            c = wide_rows(pay_ref, t, plan.at_bc + states, states, plan.bc)
            side = side_ref[w]
            left = jnp.concatenate([c * side[i : i + 1] for i in range(plan.rows)], axis=0)
            whole = (edge_ref[w].astype(F32) + entry * upto_ref[w : w + 1, :]).astype(BF16)
            y_ref[w] = mm(whole, left)
            ca = c.astype(F32) * above_ref[w : w + 1, :]
            down_ref[w] = jnp.concatenate([colsel * ca[n : n + 1] for n in range(states)], axis=0).astype(BF16)


def cells_kernel(plan, y_ref, down_ref, top_ref, out_ref):
    tiles = plan.devices
    for t in range(tiles):
        ys = [y_ref[w] + mm(top_ref[w], down_ref[w]) for w in range(t, plan.work, tiles)]
        if plan.slots == 1:
            ys.append(jnp.zeros_like(ys[0]))
        y = jnp.concatenate(ys, axis=0)
        for k, (lo, hi) in enumerate(((0, plan.half), (plan.half, plan.cells))):
            out_ref[t, lo:hi, :] = y[:, k * LANES : (k + 1) * LANES].T[: hi - lo].astype(BF16)


def call(kernel, name, args, outs, scratch=(), out_specs=None):
    return pl.pallas_call(
        kernel,
        grid=(1,),
        in_specs=[full(x.shape) for x in args],
        out_specs=out_specs or [full(s) for s, _ in outs],
        out_shape=[jax.ShapeDtypeStruct(s, d) for s, d in outs],
        scratch_shapes=[x if not isinstance(x, tuple) else pltpu.VMEM(*x) for x in scratch],
        compiler_params=pltpu.CompilerParams(vmem_limit_bytes=24 * 2**20),
        name=name,
    )(*args)


def scan_calls(plan, consts, row_axis, col_axis, pay):
    work, cp, wide = plan.work, plan.col_pad, 2 * LANES
    rp = consts["side1"].shape[0]
    steps = [((work, HALF, wide), BF16), ((work, wide), F32), ((work, wide), F32), ((work, plan.edge), F32)]
    shape = (plan.packed, HALF, LANES)
    if plan.parts > 1:
        last = call(functools.partial(last_kernel, plan, col_axis), "last", [pay], [(shape, BF16)], steps[:3])[0]
        entry = lax.ppermute(last, col_axis, [(k, k + plan.devices) for k in range(plan.devices)])
    else:
        entry = jnp.zeros(shape, BF16)
    names = ("to1", "to2", "from1", "from2", "side1", "side2", "sidemask", "down1", "down2", "downmask", "pick")
    side, above, passed, tops, edges, upto = call(
        functools.partial(maps_kernel, plan),
        "maps",
        [pay] + [consts[k] for k in names],
        [
            ((work, rp, wide), BF16),
            ((work, wide), F32),
            ((work, plan.edge, plan.top), BF16),
            ((work, HALF, plan.top), F32),
            ((work, HALF, plan.edge), BF16),
            ((work, plan.edge), F32),
        ],
        steps + [((work * rp, wide), F32)] * 2 + [((work * cp, wide), F32)] * 2,
    )
    edge_entry = entry
    tops = call(
        functools.partial(join_kernel, plan),
        "join",
        [upto, entry, passed, tops],
        [((work, HALF, plan.top), BF16)],
    )[0]
    count = lax.axis_size(row_axis)
    chain = [(r, r + 1) for r in range(count - 1)]
    entry = lax.ppermute(tops, row_axis, chain)
    if count > 2:
        keep = jnp.dot(above.astype(BF16), consts["pick"], preferred_element_type=F32)[:, None, :]
        for _ in range(count - 2):
            entry = lax.ppermute(
                (tops.astype(F32) + keep * entry.astype(F32)).astype(BF16), row_axis, chain
            )
    y, down = call(
        functools.partial(sides_kernel, plan),
        "sides",
        [pay, edges, upto, edge_entry, side, above],
        [((work, HALF, wide), F32), ((work, plan.top, wide), BF16)],
    )
    return call(
        functools.partial(cells_kernel, plan),
        "cells",
        [y, down, entry],
        [((plan.devices, plan.cells, LANES), BF16)],
    )[0]


def finish_kernel(plan, y_ref, own_ref, gate_ref, gain_ref, w_ref, out_hbm, full_ref, out_ref, sems):
    group = plan.group
    per = LANES // group
    lane = lax.broadcasted_iota(jnp.int32, (plan.cells, LANES), 1)
    for block in range(plan.width // LANES):
        joined = None
        for d in range(per):
            part = y_ref[block * per + d].astype(F32)
            if d:
                part = pltpu.roll(part, d * group, 1)
            joined = part if joined is None else jnp.where(lane < d * group, joined, part)
        at = slice(block * LANES, (block + 1) * LANES)
        y = joined + own_ref[:, at].astype(F32)
        full_ref[:, at] = y.astype(BF16).astype(F32) * gate_ref[:, at].astype(F32)
    gated = full_ref[...]
    scale = lax.rsqrt(jnp.mean(gated * gated, axis=-1, keepdims=True) + norm_eps)
    normed = (gated * scale * gain_ref[...]).astype(BF16)
    copies = []
    chunks = sems.shape[0]
    tile = w_ref.shape[1] // chunks
    for k in range(chunks):
        at = slice(k * tile, (k + 1) * tile)
        out = mm(normed, w_ref[:, at])
        for i in range(plan.rows):
            out_ref[i, :, at] = out[i * plan.cols : (i + 1) * plan.cols].astype(BF16)
        copies.append(pltpu.make_async_copy(out_ref.at[:, :, at], out_hbm.at[:, :, at], sems.at[k]))
        copies[-1].start()
    for copy in copies:
        copy.wait()


def finish(plan, y, own, gate, gain, w_out):
    args = (y, own, gate, gain, w_out)
    shape = (plan.rows, plan.cols, w_out.shape[1])
    assert w_out.shape[1] == plan.width
    return call(
        functools.partial(finish_kernel, plan),
        "finish",
        args,
        [(shape, BF16)],
        [((plan.cells, plan.width), F32), (shape, BF16), pltpu.SemaphoreType.DMA((4,))],
        [HBM],
    )[0]


def per_device(slide, tissue, w_in, w_bcd, dt_bias, rate_x, rate_y, d_skip, norm_gain, w_out):
    rows, cols, model_width = slide.shape
    width = w_out.shape[0]
    heads = dt_bias.shape[0]
    states = (w_bcd.shape[1] - heads) // 2
    plan = Plan(rows, cols, states, heads, width, lax.axis_size("col"))
    consts = plan.constants()
    v, pay, table, x = project(plan, consts, slide, w_in, w_bcd, tissue, dt_bias, rate_x, rate_y)
    groups = plan.segments()
    pay = lax.all_to_all(pay, "col", 0, 0, tiled=True, axis_index_groups=groups)
    gain = norm_gain.reshape(1, width)
    own, gate, gain = home(plan, consts, v, table, x, w_in, tissue, gain, rate_x, rate_y, d_skip)
    pay, own, gate, gain = lax.optimization_barrier((pay, own, gate, gain))
    y = scan_calls(plan, consts, "row", "col", pay)
    y = lax.all_to_all(y, "col", 0, 0, tiled=True, axis_index_groups=groups)
    return finish(plan, y, own, gate, gain, w_out)


def solution(mesh):
    placed = (
        P(("slides", "row"), "col", None),
        P(("slides", "row"), "col"),
        P(),
        P(),
        P(),
        P(),
        P(),
        P(),
        P(),
        P(),
    )
    return jax.shard_map(
        per_device,
        mesh=mesh,
        in_specs=placed,
        out_specs=P(("slides", "row"), "col", None),
        check_vma=False,
    )
```

```python
import functools

import jax
import jax.numpy as jnp
import numpy as np
from jax import lax
from jax.experimental import pallas as pl
from jax.experimental.pallas import tpu as pltpu
from jax.sharding import PartitionSpec as P

norm_eps = 1e-05
LANES = 128
HALF = LANES // 2
F32 = jnp.float32
BF16 = jnp.bfloat16


def round_up(value, step):
    return -(-value // step) * step


def in_hbm(x):
    return pltpu.with_memory_space_constraint(x, pltpu.HBM)


def mm(a, b):
    return jnp.dot(a, b, preferred_element_type=F32)


def nt_dot(a, b):
    return lax.dot_general(a, b, (((1,), (1,)), ((), ())), preferred_element_type=F32)


def tn_dot(a, b):
    return lax.dot_general(a, b, (((0,), (0,)), ((), ())), preferred_element_type=F32)


class Plan:
    def __init__(self, rows, cols, states, heads, width, devices):
        self.rows, self.cols, self.states, self.heads = rows, cols, states, heads
        self.width = width
        self.parts = 2 if devices % 2 == 0 and devices > 2 else 1
        self.devices = devices // self.parts
        self.group = width // self.devices
        self.slot = min(self.group, HALF)
        self.slots = self.group // self.slot
        self.work = self.slots * self.devices
        self.head_width = width // heads
        self.col_pad = round_up(cols, 8)
        self.count = rows * cols
        self.half = self.count // 2 // 8 * 8
        self.cells = round_up(self.count, 8)
        self.edge = rows * states
        self.top = states * self.col_pad
        self.bc = 2 * states
        self.spare = LANES - self.half
        self.tail_cells = self.count - self.half - HALF - self.spare
        self.at_bc = self.cells
        self.at_dt = self.at_bc + self.bc + states
        assert HALF <= self.half and 0 < self.tail_cells <= self.cells - self.count and self.bc <= HALF
        self.at_rate = self.at_dt + 2 * self.slots
        self.message = round_up(self.at_rate + 1, 8)
        self.tail = self.edge % LANES
        self.solid = self.edge // LANES
        self.share = LANES // self.tail if self.tail else 1
        self.packed = self.slots * self.solid + (-(-self.slots // self.share) if self.tail else 0)
        assert self.head_width % self.slot == 0 and self.group % self.slot == 0
        assert LANES % self.head_width == 0 and LANES % self.group == 0
        assert self.cells - self.half <= LANES
        assert states % 16 == 0 and heads % 8 == 0

    def segments(self):
        return [list(range(p * self.devices, (p + 1) * self.devices)) for p in range(self.parts)]

    def lanes(self):
        at = np.arange(2 * LANES)
        cell = np.where(at < LANES, at, at - LANES + self.half)
        live = np.where(at < LANES, at < self.half, cell < self.count)
        return cell // self.cols, cell % self.cols, live

    def constants(self):
        i, j, real = self.lanes()
        both = real[:, None] & real[None]
        cell = np.arange(self.cells)
        ci, cj = cell // self.cols, cell % self.cols
        creal = cell < self.count
        le = np.arange(round_up(self.rows, 8))
        lj = np.arange(self.col_pad)
        out = {}
        out["to1"] = (j[:, None] <= j[None]) & both
        out["to2"] = (j[:, None] == j[None]) & (i[:, None] <= i[None]) & both
        out["from1"] = (i[:, None] == i[None]) & (j[:, None] > j[None]) & both
        out["from2"] = (i[:, None] > i[None]) & both
        out["side1"] = (i[None] == le[:, None]) & real[None]
        out["side2"] = (i[None] > le[:, None]) & real[None]
        out["sidemask"] = (i[None] >= le[:, None]) & (le < self.rows)[:, None] & real[None]
        out["down1"] = (j[None] <= lj[:, None]) & real[None]
        out["down2"] = (j[None] == lj[:, None]) & real[None]
        out["downmask"] = (j[None] <= lj[:, None]) & (lj < self.cols)[:, None] & real[None]
        out["pick"] = (
            (i == self.rows - 1)[:, None] & real[:, None] & (j[:, None] == np.tile(lj, self.states)[None])
        )
        cboth = creal[:, None] & real[None]
        out["own1"] = (j[None] <= cj[:, None]) & cboth
        out["own2"] = (j[None] == cj[:, None]) & (i[None] <= ci[:, None]) & cboth
        out["ownmask"] = (i[None] <= ci[:, None]) & (j[None] <= cj[:, None]) & cboth
        out["lanei"] = (np.arange(self.rows)[:, None] == i[None]) & real[None]
        out["lanej"] = (np.arange(self.cols)[:, None] == j[None]) & real[None]
        return {k: in_hbm(jnp.asarray(x.astype(np.float32), BF16)) for k, x in out.items()}


def full(shape):
    return pl.BlockSpec(shape, lambda *_: (0,) * len(shape))


HBM = pl.BlockSpec(memory_space=pltpu.HBM)
SMEM = pl.BlockSpec(memory_space=pltpu.SMEM)


def split_cell(plan, cell):
    i = lax.shift_right_logical(cell * (-(-65536 // plan.cols)), 16)
    return i, cell - i * plan.cols


def cell_mask_of(plan, t_ref):
    t = t_ref[...].astype(F32).astype(BF16)
    shape = (plan.cells, plan.cols)
    _, j = split_cell(plan, lax.broadcasted_iota(jnp.int32, shape, 0))
    pick = ones(j == lax.broadcasted_iota(jnp.int32, shape, 1))
    shape = (plan.cells, plan.rows)
    i, _ = split_cell(plan, lax.broadcasted_iota(jnp.int32, shape, 0))
    here = i == lax.broadcasted_iota(jnp.int32, shape, 1)
    return jnp.sum(jnp.where(here, mm(pick, t), 0.0), axis=1, keepdims=True)


def rate_row(heads_of, rx_ref, ry_ref):
    at = lax.broadcasted_iota(jnp.int32, (1, LANES), 1)
    rate = jnp.zeros((1, LANES), F32)
    part = jnp.zeros((1, LANES), jnp.int32)
    for s, head in enumerate(heads_of):
        for k, ref in enumerate((rx_ref, ry_ref)):
            first = 8 * s + 3 * k
            here = (at >= first) & (at < first + 3)
            rate = jnp.where(here, ref[head], rate)
            part = jnp.where(here, at - first, part)
    high = rate.astype(BF16).astype(F32)
    middle = (rate - high).astype(BF16).astype(F32)
    low = rate - high - middle
    return jnp.where(part == 0, high, jnp.where(part == 1, middle, low))


def project_kernel(
    plan, chunks, bias_hbm, rx_hbm, ry_hbm, x_hbm, w_hbm, wt_hbm, t_hbm, lanei_hbm, lanej_hbm,
    v_ref, pay_hbm, rows_ref, flat_ref,
    bias_ref, rx_ref, ry_ref, x_ref, w_ref, wt_ref, t_ref, lanei_ref, lanej_ref, pay_ref, wide, sems, w_sems, out_sems,
):
    group, states, cells, heads = plan.group, plan.states, plan.cells, plan.heads
    half, rest = plan.half, plan.cells - plan.half
    tile = plan.width // chunks
    pairs = (
        (x_hbm, x_ref), (t_hbm, t_ref), (wt_hbm, wt_ref), (lanei_hbm, lanei_ref), (lanej_hbm, lanej_ref),
        (bias_hbm, bias_ref), (rx_hbm, rx_ref), (ry_hbm, ry_ref),
    )
    loads = [pltpu.make_async_copy(a, b, sems.at[k]) for k, (a, b) in enumerate(pairs)]
    copies = [
        pltpu.make_async_copy(w_hbm.at[:, k * tile : (k + 1) * tile], w_ref.at[k], w_sems.at[k])
        for k in range(chunks)
    ]
    for copy in loads + copies:
        copy.start()
    wide[...] = jnp.zeros_like(wide)
    v_ref[half:LANES, :] = jnp.zeros((LANES - half, plan.width), BF16)
    v_ref[LANES + rest :, :] = jnp.zeros((LANES - rest, plan.width), BF16)

    loads[0].wait()
    for i in range(plan.rows):
        wide[i * plan.cols : (i + 1) * plan.cols, :] = x_ref[i].astype(F32)
    x = wide[...].astype(BF16)
    flat_ref[...] = x
    for copy in loads[1:]:
        copy.wait()
    keep = cell_mask_of(plan, t_ref)
    t = t_ref[...].astype(F32).astype(BF16)
    m = jnp.sum(mm(t, lanei_ref[...]) * lanej_ref[...].astype(F32), axis=0, keepdims=True)
    table = nt_dot(wt_ref[...], x)
    ext = jnp.concatenate([table, jnp.zeros((table.shape[0], 2 * LANES - cells), F32)], axis=1)
    lane = lax.broadcasted_iota(jnp.int32, (table.shape[0], LANES), 1)
    lo, hi = ext[:, :LANES], ext[:, LANES:]
    shift = half % LANES
    if shift:
        moved = jnp.where(
            lane < LANES - shift, pltpu.roll(lo, LANES - shift, 1), pltpu.roll(hi, LANES - shift, 1)
        )
    else:
        moved = hi
    table = jnp.concatenate([jnp.where(lane < half, lo, 0.0), jnp.where(lane < plan.count - half, moved, 0.0)], axis=1)
    z = table[2 * states :]
    at = lax.broadcasted_iota(jnp.int32, z.shape, 0)
    for h in range(heads):
        z = jnp.where(at == h, z + bias_ref[h], z)
    soft = m * (jnp.maximum(z, 0.0) + jnp.log1p(jnp.exp(-jnp.abs(z))))
    table = jnp.concatenate([table[: 2 * states], soft], axis=0).astype(BF16)
    rows_ref[...] = table.astype(F32)
    bc = rows_ref[: 2 * states, :]
    lane = lax.broadcasted_iota(jnp.int32, (2 * states, LANES), 1)
    early = jnp.where(lane < half, bc[:, :LANES], pltpu.roll(bc[:, LANES:], half - HALF, 1)).astype(BF16)
    lane = lax.broadcasted_iota(jnp.int32, (states, LANES), 1)
    late = jnp.where(lane < HALF, bc[:states, LANES:], pltpu.roll(bc[states:, LANES:], HALF, 1)).astype(BF16)
    ends = nt_dot(x[cells - 8 :], wt_ref[0 : 2 * states, :])
    ends = jnp.concatenate([ends, jnp.zeros((8, LANES - 2 * states), F32)], axis=1)
    ends = pltpu.roll(ends, plan.tail_cells, 0)
    pad_row = lax.broadcasted_iota(jnp.int32, (8, LANES), 0) >= plan.count - (cells - 8)
    steps = rows_ref[2 * states :, :]

    lane = lax.broadcasted_iota(jnp.int32, (cells, LANES), 1)
    sent = []
    for chunk in range(chunks):
        copies[chunk].wait()
        v = mm(flat_ref[...], w_ref[chunk]).astype(BF16).astype(F32) * keep
        low = v.astype(BF16)
        v_ref[0:half, chunk * tile : (chunk + 1) * tile] = low[:half]
        v_ref[LANES : LANES + rest, chunk * tile : (chunk + 1) * tile] = low[half:]
        per = tile // group
        for k in range(per):
            dest = chunk * per + k
            base, at = k * group // LANES * LANES, k * group % LANES
            mine = v[:, base : base + LANES]
            if at:
                mine = pltpu.roll(mine, LANES - at, 1)
            if group < LANES:
                mine = jnp.where(lane < group, mine, 0.0)
            pay_ref[dest, 0 : cells - 8, :] = mine[: cells - 8].astype(BF16)
            pay_ref[dest, cells - 8 : cells, :] = jnp.where(pad_row, ends, mine[cells - 8 :]).astype(BF16)
            dts, heads_of = [], []
            for s in range(plan.slots):
                head = (chunk * tile + k * group + s * plan.slot) // plan.head_width
                heads_of.append(head)
                dts += [steps[head : head + 1, :LANES], steps[head : head + 1, LANES:]]
            dts.append(rate_row(heads_of, rx_ref, ry_ref))
            pay_ref[dest, plan.at_bc : plan.at_bc + plan.bc, :] = early
            pay_ref[dest, plan.at_bc + plan.bc : plan.at_dt, :] = late
            spare = plan.message - plan.at_dt - len(dts)
            dts += [jnp.zeros((spare, LANES), F32)] if spare else []
            pay_ref[dest, plan.at_dt : plan.message, :] = jnp.concatenate(dts, axis=0).astype(BF16)
            sent.append(pltpu.make_async_copy(pay_ref.at[dest], pay_hbm.at[dest], out_sems.at[dest]))
            sent[-1].start()
    for copy in sent:
        copy.wait()


def project(plan, consts, slide, w_in, w_bcd, tissue, dt_bias, rate_x, rate_y):
    chunks = 2
    tile = plan.width // chunks
    depth = slide.shape[2]
    args = [dt_bias, rate_x, rate_y, slide, w_in, w_bcd.T, tissue.T, consts["lanei"], consts["lanej"]]
    count = 2 * plan.states + plan.heads
    assert plan.width % chunks == 0 and tile % plan.group == 0 and tile % LANES == 0
    message = (plan.devices, plan.message, LANES)
    outs = [((2 * LANES, plan.width), BF16), (message, BF16), ((count, 2 * LANES), F32), ((plan.cells, depth), BF16)]
    specs = [full(s) for s, _ in outs]
    specs[1] = HBM
    return pl.pallas_call(
        functools.partial(project_kernel, plan, chunks),
        grid=(1,),
        in_specs=[HBM] * len(args),
        out_specs=specs,
        out_shape=[jax.ShapeDtypeStruct(s, d) for s, d in outs],
        scratch_shapes=[
            pltpu.SMEM(dt_bias.shape, F32),
            pltpu.SMEM(rate_x.shape, F32),
            pltpu.SMEM(rate_y.shape, F32),
            pltpu.VMEM(slide.shape, BF16),
            pltpu.VMEM((chunks, depth, tile), BF16),
        ]
        + [pltpu.VMEM(x.shape, x.dtype) for x in args[5:]]
        + [
            pltpu.VMEM(message, BF16),
            pltpu.VMEM((plan.cells, depth), F32),
            pltpu.SemaphoreType.DMA((8,)),
            pltpu.SemaphoreType.DMA((chunks,)),
            pltpu.SemaphoreType.DMA((plan.devices,)),
        ],
        compiler_params=pltpu.CompilerParams(vmem_limit_bytes=24 * 2**20),
        name="project",
    )(*[in_hbm(x) for x in args])


def home_kernel(plan, v_ref, rows_ref, flat_ref, w_hbm, *refs):
    sources, refs = refs[:9], refs[9:]
    gain_hbm, out_ref, gate_hbm, gain_out, pair, w_ref, gate_ref = refs[:7]
    held, (sem, gain_sem, sems, gate_sems) = refs[7:16], refs[16:]
    states, cells, half = plan.states, plan.cells, plan.half
    reads = [pltpu.make_async_copy(a, b, sems.at[k]) for k, (a, b) in enumerate(zip(sources, held))]
    reads.append(pltpu.make_async_copy(gain_hbm, gain_out, gain_sem))
    copy = pltpu.make_async_copy(w_hbm.at[:, plan.width :], w_ref, sem)
    for each in reads + [copy]:
        each.start()
    rx_ref, ry_ref, skip_ref, t_ref, own1_ref, own2_ref, from1_ref, from2_ref, mask_ref = held
    b = rows_ref[0:states, :].astype(BF16)
    c = rows_ref[states : 2 * states, :].astype(BF16)
    pairs = tn_dot(c, b)
    pairs = jnp.concatenate([pairs[:half], pairs[LANES : LANES + cells - half]], axis=0)
    for each in reads:
        each.wait()
    pair[...] = pairs * mask_ref[...].astype(F32)
    lane = lax.broadcasted_iota(jnp.int32, (cells, LANES), 1)
    per = LANES // plan.head_width
    for block in range(plan.width // LANES):
        v = v_ref[:, block * LANES : (block + 1) * LANES]
        vc = jnp.concatenate([v[:half], v[LANES : LANES + cells - half]], axis=0).astype(F32)
        total = None
        for k in range(per):
            h = block * per + k
            dt = rows_ref[2 * states + h : 2 * states + h + 1, :]
            low = dt.astype(BF16)
            x = mm(own1_ref[...] * low, from1_ref[...])
            y = mm(own2_ref[...] * low, from2_ref[...])
            weight = jnp.exp(-(rx_ref[h] * x + ry_ref[h] * y)) * pair[...] * dt
            part = mm(weight.astype(BF16), v) + skip_ref[h] * vc
            total = part if total is None else jnp.where(lane < k * plan.head_width, total, part)
        out_ref[:, block * LANES : (block + 1) * LANES] = total.astype(BF16)
    keep = cell_mask_of(plan, t_ref)
    copy.wait()
    tile = plan.width // gate_sems.shape[0]
    sent = []
    for block in range(plan.width // tile):
        at = slice(block * tile, (block + 1) * tile)
        z = mm(flat_ref[...], w_ref[:, at]).astype(BF16).astype(F32)
        gate_ref[:, at] = (z * (1.0 / (1.0 + jnp.exp(-z))) * keep).astype(BF16)
        sent.append(pltpu.make_async_copy(gate_ref.at[:, at], gate_hbm.at[:, at], gate_sems.at[block]))
        sent[-1].start()
    for each in sent:
        each.wait()


def home(plan, consts, v, rows, flat, w_in, tissue, gain, rate_x, rate_y, d_skip):
    sources = [rate_x, rate_y, d_skip, tissue.T] + [consts[k] for k in ("own1", "own2", "from1", "from2", "ownmask")]
    fixed = [in_hbm(x) for x in [w_in] + sources + [gain]]
    outs = [((plan.cells, plan.width), BF16), ((plan.cells, plan.width), BF16), (gain.shape, F32)]
    return pl.pallas_call(
        functools.partial(home_kernel, plan),
        grid=(1,),
        in_specs=[full(x.shape) for x in (v, rows, flat)] + [HBM] * len(fixed),
        out_specs=[full(outs[0][0]), HBM, full(outs[2][0])],
        out_shape=[jax.ShapeDtypeStruct(s, d) for s, d in outs],
        scratch_shapes=[
            pltpu.VMEM((plan.cells, 2 * LANES), F32),
            pltpu.VMEM((w_in.shape[0], w_in.shape[1] - plan.width), BF16),
            pltpu.VMEM((plan.cells, plan.width), BF16),
        ]
        + [pltpu.SMEM(x.shape, F32) for x in sources[:3]]
        + [pltpu.VMEM(x.shape, x.dtype) for x in sources[3:]]
        + [
            pltpu.SemaphoreType.DMA,
            pltpu.SemaphoreType.DMA,
            pltpu.SemaphoreType.DMA((len(sources),)),
            pltpu.SemaphoreType.DMA((4,)),
        ],
        compiler_params=pltpu.CompilerParams(vmem_limit_bytes=24 * 2**20),
        name="home",
    )(v, rows, flat, *fixed)


def ones(mask):
    return jnp.where(mask, 1.0, 0.0).astype(BF16)


def places(plan, shape, axis):
    at = lax.broadcasted_iota(jnp.int32, shape, axis)
    late = at >= LANES
    cell = jnp.where(late, at - (LANES - plan.half), at)
    i, j = split_cell(plan, cell)
    return i, j, cell < jnp.where(late, plan.count, plan.half)


def map_rows(plan, pay_ref, turned, t, k):
    n = plan.states
    first = pay_ref[t, plan.at_bc + k * n : plan.at_bc + (k + 1) * n, :].astype(F32)
    second = pay_ref[t, plan.at_bc + plan.bc : plan.at_dt, :].astype(F32)
    if k:
        second = pltpu.roll(second, HALF, 1)
    ends = turned[t][k * n : (k + 1) * n, LANES:].astype(F32)
    lane = lax.broadcasted_iota(jnp.int32, (n, LANES), 1)
    moved = pltpu.roll(first, LANES + HALF - plan.half, 1)
    ends = pltpu.roll(ends, LANES - plan.tail_cells, 1)
    second = jnp.where(lane < HALF, second, jnp.where(lane < HALF + plan.spare, moved, ends))
    return jnp.concatenate([first, second], axis=1)


def turn_all(plan, pay_ref, turned):
    for t in range(plan.devices):
        sides = []
        for lo, hi in ((0, plan.half), (plan.half, plan.cells)):
            v = pay_ref[t, lo:hi, :].astype(F32)
            if hi - lo < LANES:
                v = jnp.concatenate([v, jnp.zeros((LANES - hi + lo, LANES), F32)], axis=0)
            sides.append(v.T)
        v = jnp.concatenate(sides, axis=1).astype(BF16)
        for s in range(plan.slots):
            turned[s * plan.devices + t] = v[s * HALF : (s + 1) * HALF]


def load_steps(plan, pay_ref, dts):
    for t in range(plan.devices):
        rows = pay_ref[t, plan.at_dt : plan.message, :].astype(F32)
        for s in range(plan.slots):
            w = s * plan.devices + t
            dts[w : w + 1, :LANES] = rows[2 * s : 2 * s + 1]
            dts[w : w + 1, LANES:] = rows[2 * s + 1 : 2 * s + 2]


def rates_of(plan, pay_ref, kind):
    row = pay_ref[0, plan.at_dt : plan.message, :].astype(F32)[plan.at_rate - plan.at_dt : plan.at_rate - plan.at_dt + 1]
    at = lax.broadcasted_iota(jnp.int32, (1, LANES), 1)
    first = [8 * s + 3 * kind for s in range(plan.slots)]
    return [jnp.sum(jnp.where((at >= f) & (at < f + 3), row, 0.0), axis=1, keepdims=True) for f in first]


def slot_rates(plan, pay_ref, kind):
    return jnp.concatenate(
        [jnp.broadcast_to(r, (plan.devices, 1)) for r in rates_of(plan, pay_ref, kind)], axis=0
    )


def pack_edges(plan, out_ref, held):
    for s in range(plan.slots):
        for k in range(plan.solid):
            out_ref[s * plan.solid + k] = held[s][:, k * LANES : (k + 1) * LANES].astype(BF16)
    if plan.tail:
        first = plan.slots * plan.solid
        for k in range(plan.packed - first):
            parts = [x[:, plan.solid * LANES :] for x in held[k * plan.share : (k + 1) * plan.share]]
            spare = LANES - plan.tail * len(parts)
            parts += [jnp.zeros((HALF, spare), F32)] if spare else []
            out_ref[first + k] = jnp.concatenate(parts, axis=1).astype(BF16)


def unpack_edges(plan, ref, s):
    parts = [ref[s * plan.solid + k].astype(F32) for k in range(plan.solid)]
    if plan.tail:
        last = ref[plan.slots * plan.solid + s // plan.share].astype(F32)
        at = s % plan.share * plan.tail
        parts.append(last[:, at : at + plan.tail])
    return jnp.concatenate(parts, axis=1)


def scan_edges(plan, pay_ref, turned, dts, inner, kept, seen):
    states, tiles, wide = plan.states, plan.devices, 2 * LANES
    i, j, real = places(plan, (wide, wide), 0)
    ti, tj, treal = places(plan, (wide, wide), 1)
    from1 = ones((i == ti) & (j > tj) & real & treal)
    edge_row = lax.div(lax.broadcasted_iota(jnp.int32, (wide, plan.edge), 1), states)
    i, _, real = places(plan, (wide, plan.edge), 0)
    keep = ones((i == edge_row) & real)
    ti, _, treal = places(plan, (plan.rows, wide), 1)
    rowsel = ones((ti == lax.broadcasted_iota(jnp.int32, (plan.rows, wide), 0)) & treal)
    dt = dts[...]
    low = dt.astype(BF16)
    rate = slot_rates(plan, pay_ref, 0)
    inner[...] = jnp.exp(-rate * mm(low, from1)) * dt
    kept[...] = jnp.exp(-rate * mm(low, keep))
    ends = []
    for s in range(plan.slots):
        held = jnp.zeros((HALF, plan.edge), F32)
        product = jnp.ones((1, plan.edge), F32)
        for t in range(tiles):
            w = s * tiles + t
            seen(w, held, product)
            b = map_rows(plan, pay_ref, turned, t, 0)
            bd = (b * inner[w : w + 1, :]).astype(BF16)
            left = jnp.concatenate([bd * rowsel[i : i + 1] for i in range(plan.rows)], axis=0)
            now = kept[w : w + 1, :]
            held = held * now + nt_dot(turned[w], left)
            product = product * now
        ends.append(held)
    return ends


def last_kernel(plan, axis, pay_ref, last_ref, turned, dts, inner):
    @pl.when(lax.axis_index(axis) < (plan.parts - 1) * plan.devices)
    def _():
        states, tiles, wide = plan.states, plan.devices, 2 * LANES
        turn_all(plan, pay_ref, turned)
        load_steps(plan, pay_ref, dts)
        i, j, real = places(plan, (wide, wide), 0)
        ti, tj, treal = places(plan, (wide, wide), 1)
        same = (i == ti) & real & treal
        ti, _, treal = places(plan, (plan.rows, wide), 1)
        rowsel = ones((ti == lax.broadcasted_iota(jnp.int32, (plan.rows, wide), 0)) & treal)
        low = dts[...].astype(BF16)
        rest, whole = mm(low, ones(same & (j > tj))), mm(low, ones(same))
        left = []
        for s in range(plan.slots):
            after = jnp.zeros((1, wide), F32)
            rows = []
            for t in reversed(range(tiles)):
                rows.append(after)
                after = after + whole[s * tiles + t : s * tiles + t + 1]
            left += rows[::-1]
        inner[...] = jnp.exp(-slot_rates(plan, pay_ref, 0) * (rest + jnp.concatenate(left, axis=0))) * dts[...]
        ends = []
        for s in range(plan.slots):
            held = None
            for t in range(tiles):
                w = s * tiles + t
                b = map_rows(plan, pay_ref, turned, t, 0)
                bd = (b * inner[w : w + 1, :]).astype(BF16)
                left = jnp.concatenate([bd * rowsel[i : i + 1] for i in range(plan.rows)], axis=0)
                part = nt_dot(turned[w], left)
                held = part if held is None else held + part
            ends.append(held)
        pack_edges(plan, last_ref, ends)


def maps_kernel(
    plan, pay_ref, to1_ref, to2_ref, from1_ref, from2_ref, side1_ref, side2_ref,
    sidemask_ref, down1_ref, down2_ref, downmask_ref, pick_ref,
    side_ref, above_ref, passed_ref, top_ref, edge_ref, upto_ref, c_ref, turned, dts, inner, kept, s1, s2, d1, d2,
):
    states, tiles, cp, work = plan.states, plan.devices, plan.col_pad, plan.work
    rp = side1_ref.shape[0]
    turn_all(plan, pay_ref, turned)
    load_steps(plan, pay_ref, dts)
    for t in range(tiles):
        c_ref[t] = map_rows(plan, pay_ref, turned, t, 1).astype(BF16)

    def seen(w, held, product):
        edge_ref[w] = held.astype(BF16)
        upto_ref[w : w + 1, :] = product

    scan_edges(plan, pay_ref, turned, dts, inner, kept, seen)
    low = dts[...].astype(BF16)
    above_ref[...] = jnp.exp(-slot_rates(plan, pay_ref, 1) * mm(low, to2_ref[...]))
    rates_x, rates_y = rates_of(plan, pay_ref, 0), rates_of(plan, pay_ref, 1)
    for w in range(work):
        rf = dts[w : w + 1, :]
        s1[w * rp : (w + 1) * rp, :] = side1_ref[...].astype(F32) * rf
        s2[w * rp : (w + 1) * rp, :] = side2_ref[...].astype(F32) * rf
        d1[w * cp : (w + 1) * cp, :] = down1_ref[...].astype(F32) * rf
        d2[w * cp : (w + 1) * cp, :] = down2_ref[...].astype(F32) * rf
    mask = sidemask_ref[...].astype(F32)
    x, y = mm(s1[...].astype(BF16), to1_ref[...]), mm(s2[...].astype(BF16), to2_ref[...])
    shape = (states, plan.top)
    n = lax.broadcasted_iota(jnp.int32, shape, 0)
    diag = ones(n == lax.div(lax.broadcasted_iota(jnp.int32, shape, 1), cp))
    for w in range(work):
        s = w // tiles
        at = slice(w * rp, (w + 1) * rp)
        side = (jnp.exp(-(rates_x[s] * x[at] + rates_y[s] * y[at])) * mask).astype(BF16)
        side_ref[w] = side
        bottom = mm(side, pick_ref[...]).astype(BF16)
        passed_ref[w] = jnp.concatenate([diag * bottom[i : i + 1] for i in range(plan.rows)], axis=0)
    x, y = mm(d1[...].astype(BF16), from1_ref[...]), mm(d2[...].astype(BF16), from2_ref[...])
    mask = downmask_ref[...].astype(F32)
    for w in range(work):
        s, t = w // tiles, w % tiles
        at = slice(w * cp, (w + 1) * cp)
        fall = jnp.exp(-(rates_x[s] * x[at] + rates_y[s] * y[at])) * mask * dts[w : w + 1, :]
        b = map_rows(plan, pay_ref, turned, t, 0)
        falls = jnp.concatenate([fall * b[n : n + 1] for n in range(states)], axis=0).astype(BF16)
        top_ref[w] = nt_dot(turned[w], falls) + mm(edge_ref[w], passed_ref[w])


def join_kernel(plan, upto_ref, entry_ref, passed_ref, top_ref, out_ref):
    for s in range(plan.slots):
        entry = unpack_edges(plan, entry_ref, s)
        for t in range(plan.devices):
            w = s * plan.devices + t
            late = (entry * upto_ref[w : w + 1, :]).astype(BF16)
            out_ref[w] = (top_ref[w] + mm(late, passed_ref[w])).astype(BF16)


def sides_kernel(plan, c_ref, edge_ref, upto_ref, entry_ref, side_ref, above_ref, y_ref, down_ref):
    states, tiles = plan.states, plan.devices
    shape = (plan.col_pad, 2 * LANES)
    _, tj, treal = places(plan, shape, 1)
    colsel = jnp.where((tj == lax.broadcasted_iota(jnp.int32, shape, 0)) & treal, 1.0, 0.0)
    for s in range(plan.slots):
        entry = unpack_edges(plan, entry_ref, s)
        for t in range(tiles):
            w = s * tiles + t
            c = c_ref[t]
            side = side_ref[w]
            left = jnp.concatenate([c * side[i : i + 1] for i in range(plan.rows)], axis=0)
            whole = (edge_ref[w].astype(F32) + entry * upto_ref[w : w + 1, :]).astype(BF16)
            y_ref[w] = mm(whole, left)
            ca = c.astype(F32) * above_ref[w : w + 1, :]
            down_ref[w] = jnp.concatenate([colsel * ca[n : n + 1] for n in range(states)], axis=0).astype(BF16)


def cells_kernel(plan, y_ref, down_ref, top_ref, out_ref):
    tiles = plan.devices
    for t in range(tiles):
        ys = [y_ref[w] + mm(top_ref[w], down_ref[w]) for w in range(t, plan.work, tiles)]
        if plan.slots == 1:
            ys.append(jnp.zeros_like(ys[0]))
        y = jnp.concatenate(ys, axis=0)
        for k, (lo, hi) in enumerate(((0, plan.half), (plan.half, plan.cells))):
            out_ref[t, lo:hi, :] = y[:, k * LANES : (k + 1) * LANES].T[: hi - lo].astype(BF16)


def call(kernel, name, args, outs, scratch=(), out_specs=None):
    return pl.pallas_call(
        kernel,
        grid=(1,),
        in_specs=[full(x.shape) for x in args],
        out_specs=out_specs or [full(s) for s, _ in outs],
        out_shape=[jax.ShapeDtypeStruct(s, d) for s, d in outs],
        scratch_shapes=[x if not isinstance(x, tuple) else pltpu.VMEM(*x) for x in scratch],
        compiler_params=pltpu.CompilerParams(vmem_limit_bytes=24 * 2**20),
        name=name,
    )(*args)


def scan_calls(plan, consts, row_axis, col_axis, pay):
    work, cp, wide = plan.work, plan.col_pad, 2 * LANES
    rp = consts["side1"].shape[0]
    steps = [((work, HALF, wide), BF16), ((work, wide), F32), ((work, wide), F32), ((work, plan.edge), F32)]
    shape = (plan.packed, HALF, LANES)
    if plan.parts > 1:
        last = call(functools.partial(last_kernel, plan, col_axis), "last", [pay], [(shape, BF16)], steps[:3])[0]
        entry = lax.ppermute(last, col_axis, [(k, k + plan.devices) for k in range(plan.devices)])
    else:
        entry = jnp.zeros(shape, BF16)
    names = ("to1", "to2", "from1", "from2", "side1", "side2", "sidemask", "down1", "down2", "downmask", "pick")
    side, above, passed, tops, edges, upto, c = call(
        functools.partial(maps_kernel, plan),
        "maps",
        [pay] + [consts[k] for k in names],
        [
            ((work, rp, wide), BF16),
            ((work, wide), F32),
            ((work, plan.edge, plan.top), BF16),
            ((work, HALF, plan.top), F32),
            ((work, HALF, plan.edge), BF16),
            ((work, plan.edge), F32),
            ((plan.devices, plan.states, wide), BF16),
        ],
        steps + [((work * rp, wide), F32)] * 2 + [((work * cp, wide), F32)] * 2,
    )
    edge_entry = entry
    tops = call(
        functools.partial(join_kernel, plan),
        "join",
        [upto, entry, passed, tops],
        [((work, HALF, plan.top), BF16)],
    )[0]
    count = lax.axis_size(row_axis)
    chain = [(r, r + 1) for r in range(count - 1)]
    entry = lax.ppermute(tops, row_axis, chain)
    if count > 2:
        keep = jnp.dot(above.astype(BF16), consts["pick"], preferred_element_type=F32)[:, None, :]
        for _ in range(count - 2):
            entry = lax.ppermute(
                (tops.astype(F32) + keep * entry.astype(F32)).astype(BF16), row_axis, chain
            )
    y, down = call(
        functools.partial(sides_kernel, plan),
        "sides",
        [c, edges, upto, edge_entry, side, above],
        [((work, HALF, wide), F32), ((work, plan.top, wide), BF16)],
    )
    return call(
        functools.partial(cells_kernel, plan),
        "cells",
        [y, down, entry],
        [((plan.devices, plan.cells, LANES), BF16)],
    )[0]


def finish_kernel(plan, y_ref, own_ref, gate_ref, gain_ref, w_ref, out_hbm, full_ref, out_ref, sems):
    group = plan.group
    per = LANES // group
    lane = lax.broadcasted_iota(jnp.int32, (plan.cells, LANES), 1)
    for block in range(plan.width // LANES):
        joined = None
        for d in range(per):
            part = y_ref[block * per + d].astype(F32)
            if d:
                part = pltpu.roll(part, d * group, 1)
            joined = part if joined is None else jnp.where(lane < d * group, joined, part)
        at = slice(block * LANES, (block + 1) * LANES)
        y = joined + own_ref[:, at].astype(F32)
        full_ref[:, at] = y.astype(BF16).astype(F32) * gate_ref[:, at].astype(F32)
    gated = full_ref[...]
    scale = lax.rsqrt(jnp.mean(gated * gated, axis=-1, keepdims=True) + norm_eps)
    normed = (gated * scale * gain_ref[...]).astype(BF16)
    copies = []
    chunks = sems.shape[0]
    tile = w_ref.shape[1] // chunks
    for k in range(chunks):
        at = slice(k * tile, (k + 1) * tile)
        out = mm(normed, w_ref[:, at])
        for i in range(plan.rows):
            out_ref[i, :, at] = out[i * plan.cols : (i + 1) * plan.cols].astype(BF16)
        copies.append(pltpu.make_async_copy(out_ref.at[:, :, at], out_hbm.at[:, :, at], sems.at[k]))
        copies[-1].start()
    for copy in copies:
        copy.wait()


def finish(plan, y, own, gate, gain, w_out):
    args = (y, own, gate, gain, w_out)
    shape = (plan.rows, plan.cols, w_out.shape[1])
    assert w_out.shape[1] == plan.width
    return call(
        functools.partial(finish_kernel, plan),
        "finish",
        args,
        [(shape, BF16)],
        [((plan.cells, plan.width), F32), (shape, BF16), pltpu.SemaphoreType.DMA((4,))],
        [HBM],
    )[0]


def per_device(slide, tissue, w_in, w_bcd, dt_bias, rate_x, rate_y, d_skip, norm_gain, w_out):
    rows, cols, model_width = slide.shape
    width = w_out.shape[0]
    heads = dt_bias.shape[0]
    states = (w_bcd.shape[1] - heads) // 2
    plan = Plan(rows, cols, states, heads, width, lax.axis_size("col"))
    consts = plan.constants()
    v, pay, table, x = project(plan, consts, slide, w_in, w_bcd, tissue, dt_bias, rate_x, rate_y)
    groups = plan.segments()
    pay = lax.all_to_all(pay, "col", 0, 0, tiled=True, axis_index_groups=groups)
    gain = norm_gain.reshape(1, width)
    own, gate, gain = home(plan, consts, v, table, x, w_in, tissue, gain, rate_x, rate_y, d_skip)
    pay, own, gate, gain = lax.optimization_barrier((pay, own, gate, gain))
    y = scan_calls(plan, consts, "row", "col", pay)
    y = lax.all_to_all(y, "col", 0, 0, tiled=True, axis_index_groups=groups)
    return finish(plan, y, own, gate, gain, w_out)


def solution(mesh):
    placed = (
        P(("slides", "row"), "col", None),
        P(("slides", "row"), "col"),
        P(),
        P(),
        P(),
        P(),
        P(),
        P(),
        P(),
        P(),
    )
    return jax.shard_map(
        per_device,
        mesh=mesh,
        in_specs=placed,
        out_specs=P(("slides", "row"), "col", None),
        check_vma=False,
    )
```

```python
import functools

import jax
import jax.numpy as jnp
import numpy as np
from jax import lax
from jax.experimental import pallas as pl
from jax.experimental.pallas import tpu as pltpu
from jax.sharding import PartitionSpec as P

norm_eps = 1e-05
LANES = 128
HALF = LANES // 2
F32 = jnp.float32
BF16 = jnp.bfloat16


def round_up(value, step):
    return -(-value // step) * step


def in_hbm(x):
    return pltpu.with_memory_space_constraint(x, pltpu.HBM)


def mm(a, b):
    return jnp.dot(a, b, preferred_element_type=F32)


def nt_dot(a, b):
    return lax.dot_general(a, b, (((1,), (1,)), ((), ())), preferred_element_type=F32)


def tn_dot(a, b):
    return lax.dot_general(a, b, (((0,), (0,)), ((), ())), preferred_element_type=F32)


class Plan:
    def __init__(self, rows, cols, states, heads, width, devices):
        self.rows, self.cols, self.states, self.heads = rows, cols, states, heads
        self.width = width
        self.parts = 2 if devices % 2 == 0 and devices > 2 else 1
        self.devices = devices // self.parts
        self.group = width // self.devices
        self.slot = min(self.group, HALF)
        self.slots = self.group // self.slot
        self.work = self.slots * self.devices
        self.head_width = width // heads
        self.col_pad = round_up(cols, 8)
        self.count = rows * cols
        self.half = self.count // 2 // 8 * 8
        self.cells = round_up(self.count, 8)
        self.edge = rows * states
        self.top = states * self.col_pad
        self.bc = 2 * states
        self.spare = LANES - self.half
        self.tail_cells = self.count - self.half - HALF - self.spare
        self.at_bc = self.cells
        self.at_dt = self.at_bc + self.bc + states
        assert HALF <= self.half and 0 < self.tail_cells <= self.cells - self.count and self.bc <= HALF
        self.at_rate = self.at_dt + 2 * self.slots
        self.message = round_up(self.at_rate + 1, 8)
        self.tail = self.edge % LANES
        self.solid = self.edge // LANES
        self.share = LANES // self.tail if self.tail else 1
        self.packed = self.slots * self.solid + (-(-self.slots // self.share) if self.tail else 0)
        assert self.head_width % self.slot == 0 and self.group % self.slot == 0
        assert LANES % self.head_width == 0 and LANES % self.group == 0
        assert self.cells - self.half <= LANES
        assert states % 16 == 0 and heads % 8 == 0

    def segments(self):
        return [list(range(p * self.devices, (p + 1) * self.devices)) for p in range(self.parts)]

    def lanes(self):
        at = np.arange(2 * LANES)
        cell = np.where(at < LANES, at, at - LANES + self.half)
        live = np.where(at < LANES, at < self.half, cell < self.count)
        return cell // self.cols, cell % self.cols, live

    def constants(self):
        i, j, real = self.lanes()
        both = real[:, None] & real[None]
        cell = np.arange(self.cells)
        ci, cj = cell // self.cols, cell % self.cols
        creal = cell < self.count
        le = np.arange(round_up(self.rows, 8))
        lj = np.arange(self.col_pad)
        out = {}
        out["to1"] = (j[:, None] <= j[None]) & both
        out["to2"] = (j[:, None] == j[None]) & (i[:, None] <= i[None]) & both
        out["from1"] = (i[:, None] == i[None]) & (j[:, None] > j[None]) & both
        out["from2"] = (i[:, None] > i[None]) & both
        out["side1"] = (i[None] == le[:, None]) & real[None]
        out["side2"] = (i[None] > le[:, None]) & real[None]
        out["sidemask"] = (i[None] >= le[:, None]) & (le < self.rows)[:, None] & real[None]
        out["down1"] = (j[None] <= lj[:, None]) & real[None]
        out["down2"] = (j[None] == lj[:, None]) & real[None]
        out["downmask"] = (j[None] <= lj[:, None]) & (lj < self.cols)[:, None] & real[None]
        out["pick"] = (
            (i == self.rows - 1)[:, None] & real[:, None] & (j[:, None] == np.tile(lj, self.states)[None])
        )
        cboth = creal[:, None] & real[None]
        out["own1"] = (j[None] <= cj[:, None]) & cboth
        out["own2"] = (j[None] == cj[:, None]) & (i[None] <= ci[:, None]) & cboth
        out["ownmask"] = (i[None] <= ci[:, None]) & (j[None] <= cj[:, None]) & cboth
        out["lanei"] = (np.arange(self.rows)[:, None] == i[None]) & real[None]
        out["lanej"] = (np.arange(self.cols)[:, None] == j[None]) & real[None]
        return {k: in_hbm(jnp.asarray(x.astype(np.float32), BF16)) for k, x in out.items()}


def full(shape):
    return pl.BlockSpec(shape, lambda *_: (0,) * len(shape))


HBM = pl.BlockSpec(memory_space=pltpu.HBM)
SMEM = pl.BlockSpec(memory_space=pltpu.SMEM)


def split_cell(plan, cell):
    i = lax.shift_right_logical(cell * (-(-65536 // plan.cols)), 16)
    return i, cell - i * plan.cols


def cell_mask_of(plan, t_ref):
    t = t_ref[...].astype(F32).astype(BF16)
    shape = (plan.cells, plan.cols)
    _, j = split_cell(plan, lax.broadcasted_iota(jnp.int32, shape, 0))
    pick = ones(j == lax.broadcasted_iota(jnp.int32, shape, 1))
    shape = (plan.cells, plan.rows)
    i, _ = split_cell(plan, lax.broadcasted_iota(jnp.int32, shape, 0))
    here = i == lax.broadcasted_iota(jnp.int32, shape, 1)
    return jnp.sum(jnp.where(here, mm(pick, t), 0.0), axis=1, keepdims=True)


def rate_row(heads_of, rx_ref, ry_ref):
    at = lax.broadcasted_iota(jnp.int32, (1, LANES), 1)
    rate = jnp.zeros((1, LANES), F32)
    part = jnp.zeros((1, LANES), jnp.int32)
    for s, head in enumerate(heads_of):
        for k, ref in enumerate((rx_ref, ry_ref)):
            first = 8 * s + 3 * k
            here = (at >= first) & (at < first + 3)
            rate = jnp.where(here, ref[head], rate)
            part = jnp.where(here, at - first, part)
    high = rate.astype(BF16).astype(F32)
    middle = (rate - high).astype(BF16).astype(F32)
    low = rate - high - middle
    return jnp.where(part == 0, high, jnp.where(part == 1, middle, low))


def project_kernel(
    plan, chunks, bias_hbm, rx_hbm, ry_hbm, x_hbm, w_hbm, wt_hbm, t_hbm, lanei_hbm, lanej_hbm,
    v_ref, pay_hbm, rows_ref, flat_ref,
    bias_ref, rx_ref, ry_ref, x_ref, w_ref, wt_ref, t_ref, lanei_ref, lanej_ref, pay_ref, wide, sems, w_sems, out_sems,
):
    group, states, cells, heads = plan.group, plan.states, plan.cells, plan.heads
    half, rest = plan.half, plan.cells - plan.half
    tile = plan.width // chunks
    pairs = (
        (x_hbm, x_ref), (t_hbm, t_ref), (wt_hbm, wt_ref), (lanei_hbm, lanei_ref), (lanej_hbm, lanej_ref),
        (bias_hbm, bias_ref), (rx_hbm, rx_ref), (ry_hbm, ry_ref),
    )
    loads = [pltpu.make_async_copy(a, b, sems.at[k]) for k, (a, b) in enumerate(pairs)]
    copies = [
        pltpu.make_async_copy(w_hbm.at[:, k * tile : (k + 1) * tile], w_ref.at[k], w_sems.at[k])
        for k in range(chunks)
    ]
    for copy in loads + copies:
        copy.start()
    wide[...] = jnp.zeros_like(wide)
    v_ref[half:LANES, :] = jnp.zeros((LANES - half, plan.width), BF16)
    v_ref[LANES + rest :, :] = jnp.zeros((LANES - rest, plan.width), BF16)

    loads[0].wait()
    for i in range(plan.rows):
        wide[i * plan.cols : (i + 1) * plan.cols, :] = x_ref[i].astype(F32)
    x = wide[...].astype(BF16)
    flat_ref[...] = x
    for copy in loads[1:]:
        copy.wait()
    keep = cell_mask_of(plan, t_ref)
    t = t_ref[...].astype(F32).astype(BF16)
    m = jnp.sum(mm(t, lanei_ref[...]) * lanej_ref[...].astype(F32), axis=0, keepdims=True)
    table = nt_dot(wt_ref[...], x)
    ext = jnp.concatenate([table, jnp.zeros((table.shape[0], 2 * LANES - cells), F32)], axis=1)
    lane = lax.broadcasted_iota(jnp.int32, (table.shape[0], LANES), 1)
    lo, hi = ext[:, :LANES], ext[:, LANES:]
    shift = half % LANES
    if shift:
        moved = jnp.where(
            lane < LANES - shift, pltpu.roll(lo, LANES - shift, 1), pltpu.roll(hi, LANES - shift, 1)
        )
    else:
        moved = hi
    table = jnp.concatenate([jnp.where(lane < half, lo, 0.0), jnp.where(lane < plan.count - half, moved, 0.0)], axis=1)
    z = table[2 * states :]
    at = lax.broadcasted_iota(jnp.int32, z.shape, 0)
    for h in range(heads):
        z = jnp.where(at == h, z + bias_ref[h], z)
    soft = m * (jnp.maximum(z, 0.0) + jnp.log1p(jnp.exp(-jnp.abs(z))))
    table = jnp.concatenate([table[: 2 * states], soft], axis=0).astype(BF16)
    rows_ref[...] = table.astype(F32)
    bc = rows_ref[: 2 * states, :]
    lane = lax.broadcasted_iota(jnp.int32, (2 * states, LANES), 1)
    early = jnp.where(lane < half, bc[:, :LANES], pltpu.roll(bc[:, LANES:], half - HALF, 1)).astype(BF16)
    lane = lax.broadcasted_iota(jnp.int32, (states, LANES), 1)
    late = jnp.where(lane < HALF, bc[:states, LANES:], pltpu.roll(bc[states:, LANES:], HALF, 1)).astype(BF16)
    first_end = HALF + plan.spare
    ends = bc[:, LANES:].T[first_end : first_end + 8]
    ends = jnp.concatenate([ends, jnp.zeros((8, LANES - 2 * states), F32)], axis=1)
    ends = pltpu.roll(ends, plan.tail_cells, 0)
    pad_row = lax.broadcasted_iota(jnp.int32, (8, LANES), 0) >= plan.count - (cells - 8)
    steps = rows_ref[2 * states :, :]

    lane = lax.broadcasted_iota(jnp.int32, (cells, LANES), 1)
    sent = []
    for chunk in range(chunks):
        copies[chunk].wait()
        v = mm(flat_ref[...], w_ref[chunk]).astype(BF16).astype(F32) * keep
        low = v.astype(BF16)
        v_ref[0:half, chunk * tile : (chunk + 1) * tile] = low[:half]
        v_ref[LANES : LANES + rest, chunk * tile : (chunk + 1) * tile] = low[half:]
        per = tile // group
        for k in range(per):
            dest = chunk * per + k
            base, at = k * group // LANES * LANES, k * group % LANES
            mine = v[:, base : base + LANES]
            if at:
                mine = pltpu.roll(mine, LANES - at, 1)
            if group < LANES:
                mine = jnp.where(lane < group, mine, 0.0)
            pay_ref[dest, 0 : cells - 8, :] = mine[: cells - 8].astype(BF16)
            pay_ref[dest, cells - 8 : cells, :] = jnp.where(pad_row, ends, mine[cells - 8 :]).astype(BF16)
            dts, heads_of = [], []
            for s in range(plan.slots):
                head = (chunk * tile + k * group + s * plan.slot) // plan.head_width
                heads_of.append(head)
                dts += [steps[head : head + 1, :LANES], steps[head : head + 1, LANES:]]
            dts.append(rate_row(heads_of, rx_ref, ry_ref))
            pay_ref[dest, plan.at_bc : plan.at_bc + plan.bc, :] = early
            pay_ref[dest, plan.at_bc + plan.bc : plan.at_dt, :] = late
            spare = plan.message - plan.at_dt - len(dts)
            dts += [jnp.zeros((spare, LANES), F32)] if spare else []
            pay_ref[dest, plan.at_dt : plan.message, :] = jnp.concatenate(dts, axis=0).astype(BF16)
            sent.append(pltpu.make_async_copy(pay_ref.at[dest], pay_hbm.at[dest], out_sems.at[dest]))
            sent[-1].start()
    for copy in sent:
        copy.wait()


def project(plan, consts, slide, w_in, w_bcd, tissue, dt_bias, rate_x, rate_y):
    chunks = 2
    tile = plan.width // chunks
    depth = slide.shape[2]
    args = [dt_bias, rate_x, rate_y, slide, w_in, w_bcd.T, tissue.T, consts["lanei"], consts["lanej"]]
    count = 2 * plan.states + plan.heads
    assert plan.width % chunks == 0 and tile % plan.group == 0 and tile % LANES == 0
    message = (plan.devices, plan.message, LANES)
    outs = [((2 * LANES, plan.width), BF16), (message, BF16), ((count, 2 * LANES), F32), ((plan.cells, depth), BF16)]
    specs = [full(s) for s, _ in outs]
    specs[1] = HBM
    return pl.pallas_call(
        functools.partial(project_kernel, plan, chunks),
        grid=(1,),
        in_specs=[HBM] * len(args),
        out_specs=specs,
        out_shape=[jax.ShapeDtypeStruct(s, d) for s, d in outs],
        scratch_shapes=[
            pltpu.SMEM(dt_bias.shape, F32),
            pltpu.SMEM(rate_x.shape, F32),
            pltpu.SMEM(rate_y.shape, F32),
            pltpu.VMEM(slide.shape, BF16),
            pltpu.VMEM((chunks, depth, tile), BF16),
        ]
        + [pltpu.VMEM(x.shape, x.dtype) for x in args[5:]]
        + [
            pltpu.VMEM(message, BF16),
            pltpu.VMEM((plan.cells, depth), F32),
            pltpu.SemaphoreType.DMA((8,)),
            pltpu.SemaphoreType.DMA((chunks,)),
            pltpu.SemaphoreType.DMA((plan.devices,)),
        ],
        compiler_params=pltpu.CompilerParams(vmem_limit_bytes=24 * 2**20),
        name="project",
    )(*[in_hbm(x) for x in args])


def home_kernel(plan, v_ref, rows_ref, flat_ref, w_hbm, *refs):
    sources, refs = refs[:9], refs[9:]
    gain_hbm, out_ref, gate_hbm, gain_out, pair, w_ref, gate_ref = refs[:7]
    held, (sem, gain_sem, sems, gate_sems) = refs[7:16], refs[16:]
    states, cells, half = plan.states, plan.cells, plan.half
    reads = [pltpu.make_async_copy(a, b, sems.at[k]) for k, (a, b) in enumerate(zip(sources, held))]
    reads.append(pltpu.make_async_copy(gain_hbm, gain_out, gain_sem))
    copy = pltpu.make_async_copy(w_hbm.at[:, plan.width :], w_ref, sem)
    for each in reads + [copy]:
        each.start()
    rx_ref, ry_ref, skip_ref, t_ref, own1_ref, own2_ref, from1_ref, from2_ref, mask_ref = held
    b = rows_ref[0:states, :].astype(BF16)
    c = rows_ref[states : 2 * states, :].astype(BF16)
    pairs = tn_dot(c, b)
    pairs = jnp.concatenate([pairs[:half], pairs[LANES : LANES + cells - half]], axis=0)
    for each in reads:
        each.wait()
    pair[...] = pairs * mask_ref[...].astype(F32)
    lane = lax.broadcasted_iota(jnp.int32, (cells, LANES), 1)
    per = LANES // plan.head_width
    for block in range(plan.width // LANES):
        v = v_ref[:, block * LANES : (block + 1) * LANES]
        vc = jnp.concatenate([v[:half], v[LANES : LANES + cells - half]], axis=0).astype(F32)
        total = None
        for k in range(per):
            h = block * per + k
            dt = rows_ref[2 * states + h : 2 * states + h + 1, :]
            low = dt.astype(BF16)
            x = mm(own1_ref[...] * low, from1_ref[...])
            y = mm(own2_ref[...] * low, from2_ref[...])
            weight = jnp.exp(-(rx_ref[h] * x + ry_ref[h] * y)) * pair[...] * dt
            part = mm(weight.astype(BF16), v) + skip_ref[h] * vc
            total = part if total is None else jnp.where(lane < k * plan.head_width, total, part)
        out_ref[:, block * LANES : (block + 1) * LANES] = total.astype(BF16)
    keep = cell_mask_of(plan, t_ref)
    copy.wait()
    tile = plan.width // gate_sems.shape[0]
    sent = []
    for block in range(plan.width // tile):
        at = slice(block * tile, (block + 1) * tile)
        z = mm(flat_ref[...], w_ref[:, at]).astype(BF16).astype(F32)
        gate_ref[:, at] = (z * (1.0 / (1.0 + jnp.exp(-z))) * keep).astype(BF16)
        sent.append(pltpu.make_async_copy(gate_ref.at[:, at], gate_hbm.at[:, at], gate_sems.at[block]))
        sent[-1].start()
    for each in sent:
        each.wait()


def home(plan, consts, v, rows, flat, w_in, tissue, gain, rate_x, rate_y, d_skip):
    sources = [rate_x, rate_y, d_skip, tissue.T] + [consts[k] for k in ("own1", "own2", "from1", "from2", "ownmask")]
    fixed = [in_hbm(x) for x in [w_in] + sources + [gain]]
    outs = [((plan.cells, plan.width), BF16), ((plan.cells, plan.width), BF16), (gain.shape, F32)]
    return pl.pallas_call(
        functools.partial(home_kernel, plan),
        grid=(1,),
        in_specs=[full(x.shape) for x in (v, rows, flat)] + [HBM] * len(fixed),
        out_specs=[full(outs[0][0]), HBM, full(outs[2][0])],
        out_shape=[jax.ShapeDtypeStruct(s, d) for s, d in outs],
        scratch_shapes=[
            pltpu.VMEM((plan.cells, 2 * LANES), F32),
            pltpu.VMEM((w_in.shape[0], w_in.shape[1] - plan.width), BF16),
            pltpu.VMEM((plan.cells, plan.width), BF16),
        ]
        + [pltpu.SMEM(x.shape, F32) for x in sources[:3]]
        + [pltpu.VMEM(x.shape, x.dtype) for x in sources[3:]]
        + [
            pltpu.SemaphoreType.DMA,
            pltpu.SemaphoreType.DMA,
            pltpu.SemaphoreType.DMA((len(sources),)),
            pltpu.SemaphoreType.DMA((4,)),
        ],
        compiler_params=pltpu.CompilerParams(vmem_limit_bytes=24 * 2**20),
        name="home",
    )(v, rows, flat, *fixed)


def ones(mask):
    return jnp.where(mask, 1.0, 0.0).astype(BF16)


def places(plan, shape, axis):
    at = lax.broadcasted_iota(jnp.int32, shape, axis)
    late = at >= LANES
    cell = jnp.where(late, at - (LANES - plan.half), at)
    i, j = split_cell(plan, cell)
    return i, j, cell < jnp.where(late, plan.count, plan.half)


def map_rows(plan, pay_ref, turned, t, k):
    n = plan.states
    first = pay_ref[t, plan.at_bc + k * n : plan.at_bc + (k + 1) * n, :].astype(F32)
    second = pay_ref[t, plan.at_bc + plan.bc : plan.at_dt, :].astype(F32)
    if k:
        second = pltpu.roll(second, HALF, 1)
    ends = turned[k * n : (k + 1) * n, LANES:].astype(F32)
    lane = lax.broadcasted_iota(jnp.int32, (n, LANES), 1)
    moved = pltpu.roll(first, LANES + HALF - plan.half, 1)
    ends = pltpu.roll(ends, LANES - plan.tail_cells, 1)
    second = jnp.where(lane < HALF, second, jnp.where(lane < HALF + plan.spare, moved, ends))
    return jnp.concatenate([first, second], axis=1)


def turn_all(plan, pay_ref, turned, b_ref):
    for t in range(plan.devices):
        sides = []
        for lo, hi in ((0, plan.half), (plan.half, plan.cells)):
            v = pay_ref[t, lo:hi, :].astype(F32)
            if hi - lo < LANES:
                v = jnp.concatenate([v, jnp.zeros((LANES - hi + lo, LANES), F32)], axis=0)
            sides.append(v.T)
        v = jnp.concatenate(sides, axis=1).astype(BF16)
        for s in range(plan.slots):
            turned[s * plan.devices + t] = v[s * HALF : (s + 1) * HALF]
        b_ref[t] = map_rows(plan, pay_ref, v, t, 0)


def load_steps(plan, pay_ref, dts):
    for t in range(plan.devices):
        rows = pay_ref[t, plan.at_dt : plan.message, :].astype(F32)
        for s in range(plan.slots):
            w = s * plan.devices + t
            dts[w : w + 1, :LANES] = rows[2 * s : 2 * s + 1]
            dts[w : w + 1, LANES:] = rows[2 * s + 1 : 2 * s + 2]


def rates_of(plan, pay_ref, kind):
    row = pay_ref[0, plan.at_dt : plan.message, :].astype(F32)[plan.at_rate - plan.at_dt : plan.at_rate - plan.at_dt + 1]
    at = lax.broadcasted_iota(jnp.int32, (1, LANES), 1)
    first = [8 * s + 3 * kind for s in range(plan.slots)]
    return [jnp.sum(jnp.where((at >= f) & (at < f + 3), row, 0.0), axis=1, keepdims=True) for f in first]


def slot_rates(plan, pay_ref, kind):
    return jnp.concatenate(
        [jnp.broadcast_to(r, (plan.devices, 1)) for r in rates_of(plan, pay_ref, kind)], axis=0
    )


def pack_edges(plan, out_ref, held):
    for s in range(plan.slots):
        for k in range(plan.solid):
            out_ref[s * plan.solid + k] = held[s][:, k * LANES : (k + 1) * LANES].astype(BF16)
    if plan.tail:
        first = plan.slots * plan.solid
        for k in range(plan.packed - first):
            parts = [x[:, plan.solid * LANES :] for x in held[k * plan.share : (k + 1) * plan.share]]
            spare = LANES - plan.tail * len(parts)
            parts += [jnp.zeros((HALF, spare), F32)] if spare else []
            out_ref[first + k] = jnp.concatenate(parts, axis=1).astype(BF16)


def unpack_edges(plan, ref, s):
    parts = [ref[s * plan.solid + k].astype(F32) for k in range(plan.solid)]
    if plan.tail:
        last = ref[plan.slots * plan.solid + s // plan.share].astype(F32)
        at = s % plan.share * plan.tail
        parts.append(last[:, at : at + plan.tail])
    return jnp.concatenate(parts, axis=1)


def scan_edges(plan, pay_ref, turned, b_ref, dts, inner, kept, seen):
    states, tiles, wide = plan.states, plan.devices, 2 * LANES
    i, j, real = places(plan, (wide, wide), 0)
    ti, tj, treal = places(plan, (wide, wide), 1)
    from1 = ones((i == ti) & (j > tj) & real & treal)
    edge_row = lax.div(lax.broadcasted_iota(jnp.int32, (wide, plan.edge), 1), states)
    i, _, real = places(plan, (wide, plan.edge), 0)
    keep = ones((i == edge_row) & real)
    ti, _, treal = places(plan, (plan.rows, wide), 1)
    rowsel = ones((ti == lax.broadcasted_iota(jnp.int32, (plan.rows, wide), 0)) & treal)
    dt = dts[...]
    low = dt.astype(BF16)
    rate = slot_rates(plan, pay_ref, 0)
    inner[...] = jnp.exp(-rate * mm(low, from1)) * dt
    kept[...] = jnp.exp(-rate * mm(low, keep))
    ends = []
    for s in range(plan.slots):
        held = jnp.zeros((HALF, plan.edge), F32)
        product = jnp.ones((1, plan.edge), F32)
        for t in range(tiles):
            w = s * tiles + t
            seen(w, held, product)
            b = b_ref[t]
            bd = (b * inner[w : w + 1, :]).astype(BF16)
            left = jnp.concatenate([bd * rowsel[i : i + 1] for i in range(plan.rows)], axis=0)
            now = kept[w : w + 1, :]
            held = held * now + nt_dot(turned[w], left)
            product = product * now
        ends.append(held)
    return ends


def last_kernel(plan, axis, pay_ref, last_ref, turned, b_ref, dts, inner):
    @pl.when(lax.axis_index(axis) < (plan.parts - 1) * plan.devices)
    def _():
        states, tiles, wide = plan.states, plan.devices, 2 * LANES
        turn_all(plan, pay_ref, turned, b_ref)
        load_steps(plan, pay_ref, dts)
        i, j, real = places(plan, (wide, wide), 0)
        ti, tj, treal = places(plan, (wide, wide), 1)
        same = (i == ti) & real & treal
        ti, _, treal = places(plan, (plan.rows, wide), 1)
        rowsel = ones((ti == lax.broadcasted_iota(jnp.int32, (plan.rows, wide), 0)) & treal)
        low = dts[...].astype(BF16)
        rest, whole = mm(low, ones(same & (j > tj))), mm(low, ones(same))
        left = []
        for s in range(plan.slots):
            after = jnp.zeros((1, wide), F32)
            rows = []
            for t in reversed(range(tiles)):
                rows.append(after)
                after = after + whole[s * tiles + t : s * tiles + t + 1]
            left += rows[::-1]
        inner[...] = jnp.exp(-slot_rates(plan, pay_ref, 0) * (rest + jnp.concatenate(left, axis=0))) * dts[...]
        ends = []
        for s in range(plan.slots):
            held = None
            for t in range(tiles):
                w = s * tiles + t
                b = b_ref[t]
                bd = (b * inner[w : w + 1, :]).astype(BF16)
                left = jnp.concatenate([bd * rowsel[i : i + 1] for i in range(plan.rows)], axis=0)
                part = nt_dot(turned[w], left)
                held = part if held is None else held + part
            ends.append(held)
        pack_edges(plan, last_ref, ends)


def maps_kernel(
    plan, pay_ref, to1_ref, to2_ref, from1_ref, from2_ref, side1_ref, side2_ref,
    sidemask_ref, down1_ref, down2_ref, downmask_ref, pick_ref,
    side_ref, above_ref, passed_ref, top_ref, edge_ref, upto_ref, c_ref, turned, b_ref, dts, inner, kept, s1, s2, d1, d2,
):
    states, tiles, cp, work = plan.states, plan.devices, plan.col_pad, plan.work
    rp = side1_ref.shape[0]
    turn_all(plan, pay_ref, turned, b_ref)
    load_steps(plan, pay_ref, dts)
    for t in range(tiles):
        c_ref[t] = map_rows(plan, pay_ref, turned[t], t, 1).astype(BF16)

    def seen(w, held, product):
        edge_ref[w] = held.astype(BF16)
        upto_ref[w : w + 1, :] = product

    scan_edges(plan, pay_ref, turned, b_ref, dts, inner, kept, seen)
    low = dts[...].astype(BF16)
    above_ref[...] = jnp.exp(-slot_rates(plan, pay_ref, 1) * mm(low, to2_ref[...]))
    rates_x, rates_y = rates_of(plan, pay_ref, 0), rates_of(plan, pay_ref, 1)
    for w in range(work):
        rf = dts[w : w + 1, :]
        s1[w * rp : (w + 1) * rp, :] = side1_ref[...].astype(F32) * rf
        s2[w * rp : (w + 1) * rp, :] = side2_ref[...].astype(F32) * rf
        d1[w * cp : (w + 1) * cp, :] = down1_ref[...].astype(F32) * rf
        d2[w * cp : (w + 1) * cp, :] = down2_ref[...].astype(F32) * rf
    mask = sidemask_ref[...].astype(F32)
    x, y = mm(s1[...].astype(BF16), to1_ref[...]), mm(s2[...].astype(BF16), to2_ref[...])
    shape = (states, plan.top)
    n = lax.broadcasted_iota(jnp.int32, shape, 0)
    diag = ones(n == lax.div(lax.broadcasted_iota(jnp.int32, shape, 1), cp))
    for w in range(work):
        s = w // tiles
        at = slice(w * rp, (w + 1) * rp)
        side = (jnp.exp(-(rates_x[s] * x[at] + rates_y[s] * y[at])) * mask).astype(BF16)
        side_ref[w] = side
        bottom = mm(side, pick_ref[...]).astype(BF16)
        passed_ref[w] = jnp.concatenate([diag * bottom[i : i + 1] for i in range(plan.rows)], axis=0)
    x, y = mm(d1[...].astype(BF16), from1_ref[...]), mm(d2[...].astype(BF16), from2_ref[...])
    mask = downmask_ref[...].astype(F32)
    for w in range(work):
        s, t = w // tiles, w % tiles
        at = slice(w * cp, (w + 1) * cp)
        fall = jnp.exp(-(rates_x[s] * x[at] + rates_y[s] * y[at])) * mask * dts[w : w + 1, :]
        b = b_ref[t]
        falls = jnp.concatenate([fall * b[n : n + 1] for n in range(states)], axis=0).astype(BF16)
        top_ref[w] = nt_dot(turned[w], falls) + mm(edge_ref[w], passed_ref[w])


def join_kernel(plan, upto_ref, entry_ref, passed_ref, top_ref, out_ref):
    for s in range(plan.slots):
        entry = unpack_edges(plan, entry_ref, s)
        for t in range(plan.devices):
            w = s * plan.devices + t
            late = (entry * upto_ref[w : w + 1, :]).astype(BF16)
            out_ref[w] = (top_ref[w] + mm(late, passed_ref[w])).astype(BF16)


def sides_kernel(plan, c_ref, edge_ref, upto_ref, entry_ref, side_ref, above_ref, y_ref, down_ref):
    states, tiles = plan.states, plan.devices
    shape = (plan.col_pad, 2 * LANES)
    _, tj, treal = places(plan, shape, 1)
    colsel = jnp.where((tj == lax.broadcasted_iota(jnp.int32, shape, 0)) & treal, 1.0, 0.0)
    for s in range(plan.slots):
        entry = unpack_edges(plan, entry_ref, s)
        for t in range(tiles):
            w = s * tiles + t
            c = c_ref[t]
            side = side_ref[w]
            left = jnp.concatenate([c * side[i : i + 1] for i in range(plan.rows)], axis=0)
            whole = (edge_ref[w].astype(F32) + entry * upto_ref[w : w + 1, :]).astype(BF16)
            y_ref[w] = mm(whole, left)
            ca = c.astype(F32) * above_ref[w : w + 1, :]
            down_ref[w] = jnp.concatenate([colsel * ca[n : n + 1] for n in range(states)], axis=0).astype(BF16)


def cells_kernel(plan, y_ref, down_ref, top_ref, out_ref):
    tiles = plan.devices
    for t in range(tiles):
        ys = [y_ref[w] + mm(top_ref[w], down_ref[w]) for w in range(t, plan.work, tiles)]
        if plan.slots == 1:
            ys.append(jnp.zeros_like(ys[0]))
        y = jnp.concatenate(ys, axis=0)
        for k, (lo, hi) in enumerate(((0, plan.half), (plan.half, plan.cells))):
            out_ref[t, lo:hi, :] = y[:, k * LANES : (k + 1) * LANES].T[: hi - lo].astype(BF16)


def call(kernel, name, args, outs, scratch=(), out_specs=None):
    return pl.pallas_call(
        kernel,
        grid=(1,),
        in_specs=[full(x.shape) for x in args],
        out_specs=out_specs or [full(s) for s, _ in outs],
        out_shape=[jax.ShapeDtypeStruct(s, d) for s, d in outs],
        scratch_shapes=[x if not isinstance(x, tuple) else pltpu.VMEM(*x) for x in scratch],
        compiler_params=pltpu.CompilerParams(vmem_limit_bytes=24 * 2**20),
        name=name,
    )(*args)


def scan_calls(plan, consts, row_axis, col_axis, pay):
    work, cp, wide = plan.work, plan.col_pad, 2 * LANES
    rp = consts["side1"].shape[0]
    steps = [((work, HALF, wide), BF16), ((plan.devices, plan.states, wide), F32), ((work, wide), F32), ((work, wide), F32), ((work, plan.edge), F32)]
    shape = (plan.packed, HALF, LANES)
    if plan.parts > 1:
        last = call(functools.partial(last_kernel, plan, col_axis), "last", [pay], [(shape, BF16)], steps[:4])[0]
        entry = lax.ppermute(last, col_axis, [(k, k + plan.devices) for k in range(plan.devices)])
    else:
        entry = jnp.zeros(shape, BF16)
    names = ("to1", "to2", "from1", "from2", "side1", "side2", "sidemask", "down1", "down2", "downmask", "pick")
    side, above, passed, tops, edges, upto, c = call(
        functools.partial(maps_kernel, plan),
        "maps",
        [pay] + [consts[k] for k in names],
        [
            ((work, rp, wide), BF16),
            ((work, wide), F32),
            ((work, plan.edge, plan.top), BF16),
            ((work, HALF, plan.top), F32),
            ((work, HALF, plan.edge), BF16),
            ((work, plan.edge), F32),
            ((plan.devices, plan.states, wide), BF16),
        ],
        steps + [((work * rp, wide), F32)] * 2 + [((work * cp, wide), F32)] * 2,
    )
    edge_entry = entry
    tops = call(
        functools.partial(join_kernel, plan),
        "join",
        [upto, entry, passed, tops],
        [((work, HALF, plan.top), BF16)],
    )[0]
    count = lax.axis_size(row_axis)
    chain = [(r, r + 1) for r in range(count - 1)]
    entry = lax.ppermute(tops, row_axis, chain)
    if count > 2:
        keep = jnp.dot(above.astype(BF16), consts["pick"], preferred_element_type=F32)[:, None, :]
        for _ in range(count - 2):
            entry = lax.ppermute(
                (tops.astype(F32) + keep * entry.astype(F32)).astype(BF16), row_axis, chain
            )
    y, down = call(
        functools.partial(sides_kernel, plan),
        "sides",
        [c, edges, upto, edge_entry, side, above],
        [((work, HALF, wide), F32), ((work, plan.top, wide), BF16)],
    )
    return call(
        functools.partial(cells_kernel, plan),
        "cells",
        [y, down, entry],
        [((plan.devices, plan.cells, LANES), BF16)],
    )[0]


def finish_kernel(plan, y_ref, own_ref, gate_ref, gain_ref, w_ref, out_hbm, full_ref, out_ref, sems):
    group = plan.group
    per = LANES // group
    lane = lax.broadcasted_iota(jnp.int32, (plan.cells, LANES), 1)
    for block in range(plan.width // LANES):
        joined = None
        for d in range(per):
            part = y_ref[block * per + d].astype(F32)
            if d:
                part = pltpu.roll(part, d * group, 1)
            joined = part if joined is None else jnp.where(lane < d * group, joined, part)
        at = slice(block * LANES, (block + 1) * LANES)
        y = joined + own_ref[:, at].astype(F32)
        full_ref[:, at] = y.astype(BF16).astype(F32) * gate_ref[:, at].astype(F32)
    gated = full_ref[...]
    scale = lax.rsqrt(jnp.mean(gated * gated, axis=-1, keepdims=True) + norm_eps)
    normed = (gated * scale * gain_ref[...]).astype(BF16)
    copies = []
    chunks = sems.shape[0]
    tile = w_ref.shape[1] // chunks
    for k in range(chunks):
        at = slice(k * tile, (k + 1) * tile)
        out = mm(normed, w_ref[:, at])
        for i in range(plan.rows):
            out_ref[i, :, at] = out[i * plan.cols : (i + 1) * plan.cols].astype(BF16)
        copies.append(pltpu.make_async_copy(out_ref.at[:, :, at], out_hbm.at[:, :, at], sems.at[k]))
        copies[-1].start()
    for copy in copies:
        copy.wait()


def finish(plan, y, own, gate, gain, w_out):
    args = (y, own, gate, gain, w_out)
    shape = (plan.rows, plan.cols, w_out.shape[1])
    assert w_out.shape[1] == plan.width
    return call(
        functools.partial(finish_kernel, plan),
        "finish",
        args,
        [(shape, BF16)],
        [((plan.cells, plan.width), F32), (shape, BF16), pltpu.SemaphoreType.DMA((4,))],
        [HBM],
    )[0]


def per_device(slide, tissue, w_in, w_bcd, dt_bias, rate_x, rate_y, d_skip, norm_gain, w_out):
    rows, cols, model_width = slide.shape
    width = w_out.shape[0]
    heads = dt_bias.shape[0]
    states = (w_bcd.shape[1] - heads) // 2
    plan = Plan(rows, cols, states, heads, width, lax.axis_size("col"))
    consts = plan.constants()
    v, pay, table, x = project(plan, consts, slide, w_in, w_bcd, tissue, dt_bias, rate_x, rate_y)
    groups = plan.segments()
    pay = lax.all_to_all(pay, "col", 0, 0, tiled=True, axis_index_groups=groups)
    gain = norm_gain.reshape(1, width)
    own, gate, gain = home(plan, consts, v, table, x, w_in, tissue, gain, rate_x, rate_y, d_skip)
    pay, own, gate, gain = lax.optimization_barrier((pay, own, gate, gain))
    y = scan_calls(plan, consts, "row", "col", pay)
    y = lax.all_to_all(y, "col", 0, 0, tiled=True, axis_index_groups=groups)
    return finish(plan, y, own, gate, gain, w_out)


def solution(mesh):
    placed = (
        P(("slides", "row"), "col", None),
        P(("slides", "row"), "col"),
        P(),
        P(),
        P(),
        P(),
        P(),
        P(),
        P(),
        P(),
    )
    return jax.shard_map(
        per_device,
        mesh=mesh,
        in_specs=placed,
        out_specs=P(("slides", "row"), "col", None),
        check_vma=False,
    )
```

```python
import functools

import jax
import jax.numpy as jnp
import numpy as np
from jax import lax
from jax.experimental import pallas as pl
from jax.experimental.pallas import tpu as pltpu
from jax.sharding import PartitionSpec as P

norm_eps = 1e-05
LANES = 128
HALF = LANES // 2
F32 = jnp.float32
BF16 = jnp.bfloat16


def round_up(value, step):
    return -(-value // step) * step


def in_hbm(x):
    return pltpu.with_memory_space_constraint(x, pltpu.HBM)


def mm(a, b):
    return jnp.dot(a, b, preferred_element_type=F32)


def nt_dot(a, b):
    return lax.dot_general(a, b, (((1,), (1,)), ((), ())), preferred_element_type=F32)


def tn_dot(a, b):
    return lax.dot_general(a, b, (((0,), (0,)), ((), ())), preferred_element_type=F32)


class Plan:
    def __init__(self, rows, cols, states, heads, width, devices):
        self.rows, self.cols, self.states, self.heads = rows, cols, states, heads
        self.width = width
        self.parts = 2 if devices % 2 == 0 and devices > 2 else 1
        self.devices = devices // self.parts
        self.group = width // self.devices
        self.slot = min(self.group, HALF)
        self.slots = self.group // self.slot
        self.work = self.slots * self.devices
        self.head_width = width // heads
        self.col_pad = round_up(cols, 8)
        self.count = rows * cols
        self.half = self.count // 2 // 8 * 8
        self.cells = round_up(self.count, 8)
        self.edge = rows * states
        self.top = states * self.col_pad
        self.bc = 2 * states
        self.spare = LANES - self.half
        self.tail_cells = self.count - self.half - HALF - self.spare
        self.at_bc = self.cells
        self.at_dt = self.at_bc + self.bc + states
        assert HALF <= self.half and 0 < self.tail_cells <= self.cells - self.count and self.bc <= HALF
        self.at_rate = self.at_dt + 2 * self.slots
        self.message = round_up(self.at_rate + 1, 8)
        self.tail = self.edge % LANES
        self.solid = self.edge // LANES
        self.share = LANES // self.tail if self.tail else 1
        self.packed = self.slots * self.solid + (-(-self.slots // self.share) if self.tail else 0)
        assert self.head_width % self.slot == 0 and self.group % self.slot == 0
        assert LANES % self.head_width == 0 and LANES % self.group == 0
        assert self.cells - self.half <= LANES
        assert states % 16 == 0 and heads % 8 == 0

    def segments(self):
        return [list(range(p * self.devices, (p + 1) * self.devices)) for p in range(self.parts)]

    def lanes(self):
        at = np.arange(2 * LANES)
        cell = np.where(at < LANES, at, at - LANES + self.half)
        live = np.where(at < LANES, at < self.half, cell < self.count)
        return cell // self.cols, cell % self.cols, live

    def constants(self):
        i, j, real = self.lanes()
        both = real[:, None] & real[None]
        cell = np.arange(self.cells)
        ci, cj = cell // self.cols, cell % self.cols
        creal = cell < self.count
        le = np.arange(round_up(self.rows, 8))
        lj = np.arange(self.col_pad)
        out = {}
        out["to1"] = (j[:, None] <= j[None]) & both
        out["to2"] = (j[:, None] == j[None]) & (i[:, None] <= i[None]) & both
        out["from1"] = (i[:, None] == i[None]) & (j[:, None] > j[None]) & both
        out["from2"] = (i[:, None] > i[None]) & both
        out["side1"] = (i[None] == le[:, None]) & real[None]
        out["side2"] = (i[None] > le[:, None]) & real[None]
        out["sidemask"] = (i[None] >= le[:, None]) & (le < self.rows)[:, None] & real[None]
        out["down1"] = (j[None] <= lj[:, None]) & real[None]
        out["down2"] = (j[None] == lj[:, None]) & real[None]
        out["downmask"] = (j[None] <= lj[:, None]) & (lj < self.cols)[:, None] & real[None]
        out["pick"] = (
            (i == self.rows - 1)[:, None] & real[:, None] & (j[:, None] == np.tile(lj, self.states)[None])
        )
        cboth = creal[:, None] & real[None]
        out["own1"] = (j[None] <= cj[:, None]) & cboth
        out["own2"] = (j[None] == cj[:, None]) & (i[None] <= ci[:, None]) & cboth
        out["ownmask"] = (i[None] <= ci[:, None]) & (j[None] <= cj[:, None]) & cboth
        out["lanei"] = (np.arange(self.rows)[:, None] == i[None]) & real[None]
        out["lanej"] = (np.arange(self.cols)[:, None] == j[None]) & real[None]
        return {k: in_hbm(jnp.asarray(x.astype(np.float32), BF16)) for k, x in out.items()}


def full(shape):
    return pl.BlockSpec(shape, lambda *_: (0,) * len(shape))


HBM = pl.BlockSpec(memory_space=pltpu.HBM)
SMEM = pl.BlockSpec(memory_space=pltpu.SMEM)


def split_cell(plan, cell):
    i = lax.shift_right_logical(cell * (-(-65536 // plan.cols)), 16)
    return i, cell - i * plan.cols


def cell_mask_of(plan, t_ref):
    t = t_ref[...].astype(F32).astype(BF16)
    shape = (plan.cells, plan.cols)
    _, j = split_cell(plan, lax.broadcasted_iota(jnp.int32, shape, 0))
    pick = ones(j == lax.broadcasted_iota(jnp.int32, shape, 1))
    shape = (plan.cells, plan.rows)
    i, _ = split_cell(plan, lax.broadcasted_iota(jnp.int32, shape, 0))
    here = i == lax.broadcasted_iota(jnp.int32, shape, 1)
    return jnp.sum(jnp.where(here, mm(pick, t), 0.0), axis=1, keepdims=True)


def rate_row(heads_of, rx_ref, ry_ref):
    at = lax.broadcasted_iota(jnp.int32, (1, LANES), 1)
    rate = jnp.zeros((1, LANES), F32)
    part = jnp.zeros((1, LANES), jnp.int32)
    for s, head in enumerate(heads_of):
        for k, ref in enumerate((rx_ref, ry_ref)):
            first = 8 * s + 3 * k
            here = (at >= first) & (at < first + 3)
            rate = jnp.where(here, ref[head], rate)
            part = jnp.where(here, at - first, part)
    high = rate.astype(BF16).astype(F32)
    middle = (rate - high).astype(BF16).astype(F32)
    low = rate - high - middle
    return jnp.where(part == 0, high, jnp.where(part == 1, middle, low))


def project_kernel(
    plan, chunks, bias_hbm, rx_hbm, ry_hbm, x_hbm, w_hbm, wt_hbm, t_hbm, lanei_hbm, lanej_hbm,
    v_ref, pay_hbm, rows_ref, flat_ref,
    bias_ref, rx_ref, ry_ref, x_ref, w_ref, wt_ref, t_ref, lanei_ref, lanej_ref, pay_ref, wide, sems, w_sems, out_sems,
):
    group, states, cells, heads = plan.group, plan.states, plan.cells, plan.heads
    half, rest = plan.half, plan.cells - plan.half
    tile = plan.width // chunks
    pairs = (
        (x_hbm, x_ref), (t_hbm, t_ref), (wt_hbm, wt_ref), (lanei_hbm, lanei_ref), (lanej_hbm, lanej_ref),
        (bias_hbm, bias_ref), (rx_hbm, rx_ref), (ry_hbm, ry_ref),
    )
    loads = [pltpu.make_async_copy(a, b, sems.at[k]) for k, (a, b) in enumerate(pairs)]
    copies = [
        pltpu.make_async_copy(w_hbm.at[:, k * tile : (k + 1) * tile], w_ref.at[k], w_sems.at[k])
        for k in range(chunks)
    ]
    for copy in loads + copies:
        copy.start()
    wide[...] = jnp.zeros_like(wide)
    v_ref[half:LANES, :] = jnp.zeros((LANES - half, plan.width), BF16)
    v_ref[LANES + rest :, :] = jnp.zeros((LANES - rest, plan.width), BF16)

    loads[0].wait()
    for i in range(plan.rows):
        wide[i * plan.cols : (i + 1) * plan.cols, :] = x_ref[i].astype(F32)
    x = wide[...].astype(BF16)
    flat_ref[...] = x
    for copy in loads[1:]:
        copy.wait()
    keep = cell_mask_of(plan, t_ref)
    t = t_ref[...].astype(F32).astype(BF16)
    m = jnp.sum(mm(t, lanei_ref[...]) * lanej_ref[...].astype(F32), axis=0, keepdims=True)
    table = nt_dot(wt_ref[...], x)
    ext = jnp.concatenate([table, jnp.zeros((table.shape[0], 2 * LANES - cells), F32)], axis=1)
    lane = lax.broadcasted_iota(jnp.int32, (table.shape[0], LANES), 1)
    lo, hi = ext[:, :LANES], ext[:, LANES:]
    shift = half % LANES
    if shift:
        moved = jnp.where(
            lane < LANES - shift, pltpu.roll(lo, LANES - shift, 1), pltpu.roll(hi, LANES - shift, 1)
        )
    else:
        moved = hi
    table = jnp.concatenate([jnp.where(lane < half, lo, 0.0), jnp.where(lane < plan.count - half, moved, 0.0)], axis=1)
    z = table[2 * states :]
    at = lax.broadcasted_iota(jnp.int32, z.shape, 0)
    for h in range(heads):
        z = jnp.where(at == h, z + bias_ref[h], z)
    soft = m * (jnp.maximum(z, 0.0) + jnp.log1p(jnp.exp(-jnp.abs(z))))
    table = jnp.concatenate([table[: 2 * states], soft], axis=0).astype(BF16)
    rows_ref[...] = table.astype(F32)
    bc = rows_ref[: 2 * states, :]
    lane = lax.broadcasted_iota(jnp.int32, (2 * states, LANES), 1)
    early = jnp.where(lane < half, bc[:, :LANES], pltpu.roll(bc[:, LANES:], half - HALF, 1)).astype(BF16)
    lane = lax.broadcasted_iota(jnp.int32, (states, LANES), 1)
    late = jnp.where(lane < HALF, bc[:states, LANES:], pltpu.roll(bc[states:, LANES:], HALF, 1)).astype(BF16)
    first_end = HALF + plan.spare
    ends = bc[:, LANES:].T[first_end : first_end + 8]
    ends = jnp.concatenate([ends, jnp.zeros((8, LANES - 2 * states), F32)], axis=1)
    ends = pltpu.roll(ends, plan.tail_cells, 0)
    pad_row = lax.broadcasted_iota(jnp.int32, (8, LANES), 0) >= plan.count - (cells - 8)
    steps = rows_ref[2 * states :, :]

    lane = lax.broadcasted_iota(jnp.int32, (cells, LANES), 1)
    sent = []
    for chunk in range(chunks):
        copies[chunk].wait()
        v = mm(flat_ref[...], w_ref[chunk]).astype(BF16).astype(F32) * keep
        low = v.astype(BF16)
        v_ref[0:half, chunk * tile : (chunk + 1) * tile] = low[:half]
        v_ref[LANES : LANES + rest, chunk * tile : (chunk + 1) * tile] = low[half:]
        per = tile // group
        for k in range(per):
            dest = chunk * per + k
            base, at = k * group // LANES * LANES, k * group % LANES
            mine = v[:, base : base + LANES]
            if at:
                mine = pltpu.roll(mine, LANES - at, 1)
            if group < LANES:
                mine = jnp.where(lane < group, mine, 0.0)
            pay_ref[dest, 0 : cells - 8, :] = mine[: cells - 8].astype(BF16)
            pay_ref[dest, cells - 8 : cells, :] = jnp.where(pad_row, ends, mine[cells - 8 :]).astype(BF16)
            dts, heads_of = [], []
            for s in range(plan.slots):
                head = (chunk * tile + k * group + s * plan.slot) // plan.head_width
                heads_of.append(head)
                dts += [steps[head : head + 1, :LANES], steps[head : head + 1, LANES:]]
            dts.append(rate_row(heads_of, rx_ref, ry_ref))
            pay_ref[dest, plan.at_bc : plan.at_bc + plan.bc, :] = early
            pay_ref[dest, plan.at_bc + plan.bc : plan.at_dt, :] = late
            spare = plan.message - plan.at_dt - len(dts)
            dts += [jnp.zeros((spare, LANES), F32)] if spare else []
            pay_ref[dest, plan.at_dt : plan.message, :] = jnp.concatenate(dts, axis=0).astype(BF16)
            sent.append(pltpu.make_async_copy(pay_ref.at[dest], pay_hbm.at[dest], out_sems.at[dest]))
            sent[-1].start()
    for copy in sent:
        copy.wait()


def project(plan, consts, slide, w_in, w_bcd, tissue, dt_bias, rate_x, rate_y):
    chunks = 2
    tile = plan.width // chunks
    depth = slide.shape[2]
    args = [dt_bias, rate_x, rate_y, slide, w_in, w_bcd.T, tissue.T, consts["lanei"], consts["lanej"]]
    count = 2 * plan.states + plan.heads
    assert plan.width % chunks == 0 and tile % plan.group == 0 and tile % LANES == 0
    message = (plan.devices, plan.message, LANES)
    outs = [((2 * LANES, plan.width), BF16), (message, BF16), ((count, 2 * LANES), F32), ((plan.cells, depth), BF16)]
    specs = [full(s) for s, _ in outs]
    specs[1] = HBM
    return pl.pallas_call(
        functools.partial(project_kernel, plan, chunks),
        grid=(1,),
        in_specs=[HBM] * len(args),
        out_specs=specs,
        out_shape=[jax.ShapeDtypeStruct(s, d) for s, d in outs],
        scratch_shapes=[
            pltpu.SMEM(dt_bias.shape, F32),
            pltpu.SMEM(rate_x.shape, F32),
            pltpu.SMEM(rate_y.shape, F32),
            pltpu.VMEM(slide.shape, BF16),
            pltpu.VMEM((chunks, depth, tile), BF16),
        ]
        + [pltpu.VMEM(x.shape, x.dtype) for x in args[5:]]
        + [
            pltpu.VMEM(message, BF16),
            pltpu.VMEM((plan.cells, depth), F32),
            pltpu.SemaphoreType.DMA((8,)),
            pltpu.SemaphoreType.DMA((chunks,)),
            pltpu.SemaphoreType.DMA((plan.devices,)),
        ],
        compiler_params=pltpu.CompilerParams(vmem_limit_bytes=24 * 2**20),
        name="project",
    )(*[in_hbm(x) for x in args])


def home_kernel(plan, v_ref, rows_ref, flat_ref, w_hbm, *refs):
    sources, refs = refs[:9], refs[9:]
    gain_hbm, out_ref, gate_hbm, gain_out, pair, w_ref, gate_ref = refs[:7]
    held, (sem, gain_sem, sems, gate_sems) = refs[7:16], refs[16:]
    states, cells, half = plan.states, plan.cells, plan.half
    reads = [pltpu.make_async_copy(a, b, sems.at[k]) for k, (a, b) in enumerate(zip(sources, held))]
    reads.append(pltpu.make_async_copy(gain_hbm, gain_out, gain_sem))
    copy = pltpu.make_async_copy(w_hbm.at[:, plan.width :], w_ref, sem)
    for each in reads + [copy]:
        each.start()
    rx_ref, ry_ref, skip_ref, t_ref, own1_ref, own2_ref, from1_ref, from2_ref, mask_ref = held
    b = rows_ref[0:states, :].astype(BF16)
    c = rows_ref[states : 2 * states, :].astype(BF16)
    pairs = tn_dot(c, b)
    pairs = jnp.concatenate([pairs[:half], pairs[LANES : LANES + cells - half]], axis=0)
    for each in reads:
        each.wait()
    pair[...] = pairs * mask_ref[...].astype(F32)
    lane = lax.broadcasted_iota(jnp.int32, (cells, LANES), 1)
    per = LANES // plan.head_width
    for block in range(plan.width // LANES):
        v = v_ref[:, block * LANES : (block + 1) * LANES]
        vc = jnp.concatenate([v[:half], v[LANES : LANES + cells - half]], axis=0).astype(F32)
        total = None
        for k in range(per):
            h = block * per + k
            dt = rows_ref[2 * states + h : 2 * states + h + 1, :]
            low = dt.astype(BF16)
            x = mm(own1_ref[...] * low, from1_ref[...])
            y = mm(own2_ref[...] * low, from2_ref[...])
            weight = jnp.exp(-(rx_ref[h] * x + ry_ref[h] * y)) * pair[...] * dt
            part = mm(weight.astype(BF16), v) + skip_ref[h] * vc
            total = part if total is None else jnp.where(lane < k * plan.head_width, total, part)
        out_ref[:, block * LANES : (block + 1) * LANES] = total.astype(BF16)
    keep = cell_mask_of(plan, t_ref)
    copy.wait()
    tile = plan.width // gate_sems.shape[0]
    sent = []
    for block in range(plan.width // tile):
        at = slice(block * tile, (block + 1) * tile)
        z = mm(flat_ref[...], w_ref[:, at]).astype(BF16).astype(F32)
        gate_ref[:, at] = (z * (1.0 / (1.0 + jnp.exp(-z))) * keep).astype(BF16)
        sent.append(pltpu.make_async_copy(gate_ref.at[:, at], gate_hbm.at[:, at], gate_sems.at[block]))
        sent[-1].start()
    for each in sent:
        each.wait()


def home(plan, consts, v, rows, flat, w_in, tissue, gain, rate_x, rate_y, d_skip):
    sources = [rate_x, rate_y, d_skip, tissue.T] + [consts[k] for k in ("own1", "own2", "from1", "from2", "ownmask")]
    fixed = [in_hbm(x) for x in [w_in] + sources + [gain]]
    outs = [((plan.cells, plan.width), BF16), ((plan.cells, plan.width), BF16), (gain.shape, F32)]
    return pl.pallas_call(
        functools.partial(home_kernel, plan),
        grid=(1,),
        in_specs=[full(x.shape) for x in (v, rows, flat)] + [HBM] * len(fixed),
        out_specs=[full(outs[0][0]), HBM, full(outs[2][0])],
        out_shape=[jax.ShapeDtypeStruct(s, d) for s, d in outs],
        scratch_shapes=[
            pltpu.VMEM((plan.cells, 2 * LANES), F32),
            pltpu.VMEM((w_in.shape[0], w_in.shape[1] - plan.width), BF16),
            pltpu.VMEM((plan.cells, plan.width), BF16),
        ]
        + [pltpu.SMEM(x.shape, F32) for x in sources[:3]]
        + [pltpu.VMEM(x.shape, x.dtype) for x in sources[3:]]
        + [
            pltpu.SemaphoreType.DMA,
            pltpu.SemaphoreType.DMA,
            pltpu.SemaphoreType.DMA((len(sources),)),
            pltpu.SemaphoreType.DMA((4,)),
        ],
        compiler_params=pltpu.CompilerParams(vmem_limit_bytes=24 * 2**20),
        name="home",
    )(v, rows, flat, *fixed)


def ones(mask):
    return jnp.where(mask, 1.0, 0.0).astype(BF16)


def places(plan, shape, axis):
    at = lax.broadcasted_iota(jnp.int32, shape, axis)
    late = at >= LANES
    cell = jnp.where(late, at - (LANES - plan.half), at)
    i, j = split_cell(plan, cell)
    return i, j, cell < jnp.where(late, plan.count, plan.half)


def map_rows(plan, pay_ref, turned, t, k):
    n = plan.states
    first = pay_ref[t, plan.at_bc + k * n : plan.at_bc + (k + 1) * n, :].astype(F32)
    second = pay_ref[t, plan.at_bc + plan.bc : plan.at_dt, :].astype(F32)
    if k:
        second = pltpu.roll(second, HALF, 1)
    ends = turned[k * n : (k + 1) * n, LANES:].astype(F32)
    lane = lax.broadcasted_iota(jnp.int32, (n, LANES), 1)
    moved = pltpu.roll(first, LANES + HALF - plan.half, 1)
    ends = pltpu.roll(ends, LANES - plan.tail_cells, 1)
    second = jnp.where(lane < HALF, second, jnp.where(lane < HALF + plan.spare, moved, ends))
    return jnp.concatenate([first, second], axis=1)


def turn_all(plan, pay_ref, turned, b_ref):
    for t in range(plan.devices):
        sides = []
        for lo, hi in ((0, plan.half), (plan.half, plan.cells)):
            v = pay_ref[t, lo:hi, :].astype(F32)
            if hi - lo < LANES:
                v = jnp.concatenate([v, jnp.zeros((LANES - hi + lo, LANES), F32)], axis=0)
            sides.append(v.T)
        v = jnp.concatenate(sides, axis=1).astype(BF16)
        for s in range(plan.slots):
            turned[s * plan.devices + t] = v[s * HALF : (s + 1) * HALF]
        b_ref[t] = map_rows(plan, pay_ref, v, t, 0)


def load_steps(plan, pay_ref, dts):
    for t in range(plan.devices):
        rows = pay_ref[t, plan.at_dt : plan.message, :].astype(F32)
        for s in range(plan.slots):
            w = s * plan.devices + t
            dts[w : w + 1, :LANES] = rows[2 * s : 2 * s + 1]
            dts[w : w + 1, LANES:] = rows[2 * s + 1 : 2 * s + 2]


def rates_of(plan, pay_ref, kind):
    row = pay_ref[0, plan.at_dt : plan.message, :].astype(F32)[plan.at_rate - plan.at_dt : plan.at_rate - plan.at_dt + 1]
    at = lax.broadcasted_iota(jnp.int32, (1, LANES), 1)
    first = [8 * s + 3 * kind for s in range(plan.slots)]
    return [jnp.sum(jnp.where((at >= f) & (at < f + 3), row, 0.0), axis=1, keepdims=True) for f in first]


def slot_rates(plan, pay_ref, kind):
    return jnp.concatenate(
        [jnp.broadcast_to(r, (plan.devices, 1)) for r in rates_of(plan, pay_ref, kind)], axis=0
    )


def pack_edges(plan, out_ref, held):
    for s in range(plan.slots):
        for k in range(plan.solid):
            out_ref[s * plan.solid + k] = held[s][:, k * LANES : (k + 1) * LANES].astype(BF16)
    if plan.tail:
        first = plan.slots * plan.solid
        for k in range(plan.packed - first):
            parts = [x[:, plan.solid * LANES :] for x in held[k * plan.share : (k + 1) * plan.share]]
            spare = LANES - plan.tail * len(parts)
            parts += [jnp.zeros((HALF, spare), F32)] if spare else []
            out_ref[first + k] = jnp.concatenate(parts, axis=1).astype(BF16)


def unpack_edges(plan, ref, s):
    parts = [ref[s * plan.solid + k].astype(F32) for k in range(plan.solid)]
    if plan.tail:
        last = ref[plan.slots * plan.solid + s // plan.share].astype(F32)
        at = s % plan.share * plan.tail
        parts.append(last[:, at : at + plan.tail])
    return jnp.concatenate(parts, axis=1)


def scan_edges(plan, pay_ref, turned, b_ref, dts, inner, kept, seen):
    states, tiles, wide = plan.states, plan.devices, 2 * LANES
    i, j, real = places(plan, (wide, wide), 0)
    ti, tj, treal = places(plan, (wide, wide), 1)
    from1 = ones((i == ti) & (j > tj) & real & treal)
    edge_row = lax.div(lax.broadcasted_iota(jnp.int32, (wide, plan.edge), 1), states)
    i, _, real = places(plan, (wide, plan.edge), 0)
    keep = ones((i == edge_row) & real)
    ti, _, treal = places(plan, (plan.rows, wide), 1)
    rowsel = ones((ti == lax.broadcasted_iota(jnp.int32, (plan.rows, wide), 0)) & treal)
    dt = dts[...]
    low = dt.astype(BF16)
    rate = slot_rates(plan, pay_ref, 0)
    inner[...] = jnp.exp(-rate * mm(low, from1)) * dt
    kept[...] = jnp.exp(-rate * mm(low, keep))
    ends = []
    for s in range(plan.slots):
        held = jnp.zeros((HALF, plan.edge), F32)
        product = jnp.ones((1, plan.edge), F32)
        for t in range(tiles):
            w = s * tiles + t
            seen(w, held, product)
            b = b_ref[t]
            bd = (b * inner[w : w + 1, :]).astype(BF16)
            left = jnp.concatenate([bd * rowsel[i : i + 1] for i in range(plan.rows)], axis=0)
            now = kept[w : w + 1, :]
            held = held * now + nt_dot(turned[w], left)
            product = product * now
        ends.append(held)
    return ends


def last_kernel(plan, axis, pay_ref, last_ref, turned, b_ref, dts, inner):
    @pl.when(lax.axis_index(axis) < (plan.parts - 1) * plan.devices)
    def _():
        states, tiles, wide = plan.states, plan.devices, 2 * LANES
        turn_all(plan, pay_ref, turned, b_ref)
        load_steps(plan, pay_ref, dts)
        i, j, real = places(plan, (wide, wide), 0)
        ti, tj, treal = places(plan, (wide, wide), 1)
        same = (i == ti) & real & treal
        ti, _, treal = places(plan, (plan.rows, wide), 1)
        rowsel = ones((ti == lax.broadcasted_iota(jnp.int32, (plan.rows, wide), 0)) & treal)
        low = dts[...].astype(BF16)
        rest, whole = mm(low, ones(same & (j > tj))), mm(low, ones(same))
        left = []
        for s in range(plan.slots):
            after = jnp.zeros((1, wide), F32)
            rows = []
            for t in reversed(range(tiles)):
                rows.append(after)
                after = after + whole[s * tiles + t : s * tiles + t + 1]
            left += rows[::-1]
        inner[...] = jnp.exp(-slot_rates(plan, pay_ref, 0) * (rest + jnp.concatenate(left, axis=0))) * dts[...]
        ends = []
        for s in range(plan.slots):
            held = None
            for t in range(tiles):
                w = s * tiles + t
                b = b_ref[t]
                bd = (b * inner[w : w + 1, :]).astype(BF16)
                left = jnp.concatenate([bd * rowsel[i : i + 1] for i in range(plan.rows)], axis=0)
                part = nt_dot(turned[w], left)
                held = part if held is None else held + part
            ends.append(held)
        pack_edges(plan, last_ref, ends)


def maps_kernel(
    plan, pay_ref, to1_ref, to2_ref, from1_ref, from2_ref, side1_ref, side2_ref,
    sidemask_ref, down1_ref, down2_ref, downmask_ref, pick_ref,
    side_ref, above_ref, passed_ref, top_ref, edge_ref, upto_ref, c_ref, turned, b_ref, dts, inner, kept, s1, s2, d1, d2,
):
    states, tiles, cp, work = plan.states, plan.devices, plan.col_pad, plan.work
    rp = side1_ref.shape[0]
    turn_all(plan, pay_ref, turned, b_ref)
    load_steps(plan, pay_ref, dts)
    for t in range(tiles):
        c_ref[t] = map_rows(plan, pay_ref, turned[t], t, 1).astype(BF16)

    def seen(w, held, product):
        edge_ref[w] = held.astype(BF16)
        upto_ref[w : w + 1, :] = product

    scan_edges(plan, pay_ref, turned, b_ref, dts, inner, kept, seen)
    low = dts[...].astype(BF16)
    above_ref[...] = jnp.exp(-slot_rates(plan, pay_ref, 1) * mm(low, to2_ref[...]))
    rates_x, rates_y = rates_of(plan, pay_ref, 0), rates_of(plan, pay_ref, 1)
    for w in range(work):
        rf = dts[w : w + 1, :]
        s1[w * rp : (w + 1) * rp, :] = side1_ref[...].astype(F32) * rf
        s2[w * rp : (w + 1) * rp, :] = side2_ref[...].astype(F32) * rf
        d1[w * cp : (w + 1) * cp, :] = down1_ref[...].astype(F32) * rf
        d2[w * cp : (w + 1) * cp, :] = down2_ref[...].astype(F32) * rf
    mask = sidemask_ref[...].astype(F32)
    x, y = mm(s1[...].astype(BF16), to1_ref[...]), mm(s2[...].astype(BF16), to2_ref[...])
    shape = (states, plan.top)
    n = lax.broadcasted_iota(jnp.int32, shape, 0)
    diag = ones(n == lax.div(lax.broadcasted_iota(jnp.int32, shape, 1), cp))
    for w in range(work):
        s = w // tiles
        at = slice(w * rp, (w + 1) * rp)
        side = (jnp.exp(-(rates_x[s] * x[at] + rates_y[s] * y[at])) * mask).astype(BF16)
        side_ref[w] = side
        bottom = mm(side, pick_ref[...]).astype(BF16)
        passed_ref[w] = jnp.concatenate([diag * bottom[i : i + 1] for i in range(plan.rows)], axis=0)
    x, y = mm(d1[...].astype(BF16), from1_ref[...]), mm(d2[...].astype(BF16), from2_ref[...])
    mask = downmask_ref[...].astype(F32)
    for w in range(work):
        s, t = w // tiles, w % tiles
        at = slice(w * cp, (w + 1) * cp)
        fall = jnp.exp(-(rates_x[s] * x[at] + rates_y[s] * y[at])) * mask * dts[w : w + 1, :]
        b = b_ref[t]
        falls = jnp.concatenate([fall * b[n : n + 1] for n in range(states)], axis=0).astype(BF16)
        top_ref[w] = nt_dot(turned[w], falls) + mm(edge_ref[w], passed_ref[w])


def join_kernel(plan, axis, upto_ref, entry_ref, passed_ref, top_ref, out_ref):
    @pl.when(lax.axis_index(axis) < lax.axis_size(axis) - 1)
    def _():
        for s in range(plan.slots):
            entry = unpack_edges(plan, entry_ref, s)
            for t in range(plan.devices):
                w = s * plan.devices + t
                late = (entry * upto_ref[w : w + 1, :]).astype(BF16)
                out_ref[w] = (top_ref[w] + mm(late, passed_ref[w])).astype(BF16)


def sides_kernel(plan, c_ref, edge_ref, upto_ref, entry_ref, side_ref, above_ref, y_ref, down_ref):
    states, tiles = plan.states, plan.devices
    shape = (plan.col_pad, 2 * LANES)
    _, tj, treal = places(plan, shape, 1)
    colsel = jnp.where((tj == lax.broadcasted_iota(jnp.int32, shape, 0)) & treal, 1.0, 0.0)
    for s in range(plan.slots):
        entry = unpack_edges(plan, entry_ref, s)
        for t in range(tiles):
            w = s * tiles + t
            c = c_ref[t]
            side = side_ref[w]
            left = jnp.concatenate([c * side[i : i + 1] for i in range(plan.rows)], axis=0)
            whole = (edge_ref[w].astype(F32) + entry * upto_ref[w : w + 1, :]).astype(BF16)
            y_ref[w] = mm(whole, left)
            ca = c.astype(F32) * above_ref[w : w + 1, :]
            down_ref[w] = jnp.concatenate([colsel * ca[n : n + 1] for n in range(states)], axis=0).astype(BF16)


def cells_kernel(plan, y_ref, down_ref, top_ref, out_ref):
    tiles = plan.devices
    for t in range(tiles):
        ys = [y_ref[w] + mm(top_ref[w], down_ref[w]) for w in range(t, plan.work, tiles)]
        if plan.slots == 1:
            ys.append(jnp.zeros_like(ys[0]))
        y = jnp.concatenate(ys, axis=0)
        for k, (lo, hi) in enumerate(((0, plan.half), (plan.half, plan.cells))):
            out_ref[t, lo:hi, :] = y[:, k * LANES : (k + 1) * LANES].T[: hi - lo].astype(BF16)


def call(kernel, name, args, outs, scratch=(), out_specs=None):
    return pl.pallas_call(
        kernel,
        grid=(1,),
        in_specs=[full(x.shape) for x in args],
        out_specs=out_specs or [full(s) for s, _ in outs],
        out_shape=[jax.ShapeDtypeStruct(s, d) for s, d in outs],
        scratch_shapes=[x if not isinstance(x, tuple) else pltpu.VMEM(*x) for x in scratch],
        compiler_params=pltpu.CompilerParams(vmem_limit_bytes=24 * 2**20),
        name=name,
    )(*args)


def scan_calls(plan, consts, row_axis, col_axis, pay):
    work, cp, wide = plan.work, plan.col_pad, 2 * LANES
    rp = consts["side1"].shape[0]
    steps = [((work, HALF, wide), BF16), ((plan.devices, plan.states, wide), F32), ((work, wide), F32), ((work, wide), F32), ((work, plan.edge), F32)]
    shape = (plan.packed, HALF, LANES)
    if plan.parts > 1:
        last = call(functools.partial(last_kernel, plan, col_axis), "last", [pay], [(shape, BF16)], steps[:4])[0]
        entry = lax.ppermute(last, col_axis, [(k, k + plan.devices) for k in range(plan.devices)])
    else:
        entry = jnp.zeros(shape, BF16)
    names = ("to1", "to2", "from1", "from2", "side1", "side2", "sidemask", "down1", "down2", "downmask", "pick")
    side, above, passed, tops, edges, upto, c = call(
        functools.partial(maps_kernel, plan),
        "maps",
        [pay] + [consts[k] for k in names],
        [
            ((work, rp, wide), BF16),
            ((work, wide), F32),
            ((work, plan.edge, plan.top), BF16),
            ((work, HALF, plan.top), F32),
            ((work, HALF, plan.edge), BF16),
            ((work, plan.edge), F32),
            ((plan.devices, plan.states, wide), BF16),
        ],
        steps + [((work * rp, wide), F32)] * 2 + [((work * cp, wide), F32)] * 2,
    )
    edge_entry = entry
    tops = call(
        functools.partial(join_kernel, plan, row_axis),
        "join",
        [upto, entry, passed, tops],
        [((work, HALF, plan.top), BF16)],
    )[0]
    count = lax.axis_size(row_axis)
    chain = [(r, r + 1) for r in range(count - 1)]
    entry = lax.ppermute(tops, row_axis, chain)
    if count > 2:
        keep = jnp.dot(above.astype(BF16), consts["pick"], preferred_element_type=F32)[:, None, :]
        for _ in range(count - 2):
            entry = lax.ppermute(
                (tops.astype(F32) + keep * entry.astype(F32)).astype(BF16), row_axis, chain
            )
    y, down = call(
        functools.partial(sides_kernel, plan),
        "sides",
        [c, edges, upto, edge_entry, side, above],
        [((work, HALF, wide), F32), ((work, plan.top, wide), BF16)],
    )
    return call(
        functools.partial(cells_kernel, plan),
        "cells",
        [y, down, entry],
        [((plan.devices, plan.cells, LANES), BF16)],
    )[0]


def finish_kernel(plan, y_ref, own_ref, gate_ref, gain_ref, w_ref, out_hbm, full_ref, out_ref, sems):
    group = plan.group
    per = LANES // group
    lane = lax.broadcasted_iota(jnp.int32, (plan.cells, LANES), 1)
    for block in range(plan.width // LANES):
        joined = None
        for d in range(per):
            part = y_ref[block * per + d].astype(F32)
            if d:
                part = pltpu.roll(part, d * group, 1)
            joined = part if joined is None else jnp.where(lane < d * group, joined, part)
        at = slice(block * LANES, (block + 1) * LANES)
        y = joined + own_ref[:, at].astype(F32)
        full_ref[:, at] = y.astype(BF16).astype(F32) * gate_ref[:, at].astype(F32)
    gated = full_ref[...]
    scale = lax.rsqrt(jnp.mean(gated * gated, axis=-1, keepdims=True) + norm_eps)
    normed = (gated * scale * gain_ref[...]).astype(BF16)
    copies = []
    chunks = sems.shape[0]
    tile = w_ref.shape[1] // chunks
    for k in range(chunks):
        at = slice(k * tile, (k + 1) * tile)
        out = mm(normed, w_ref[:, at])
        for i in range(plan.rows):
            out_ref[i, :, at] = out[i * plan.cols : (i + 1) * plan.cols].astype(BF16)
        copies.append(pltpu.make_async_copy(out_ref.at[:, :, at], out_hbm.at[:, :, at], sems.at[k]))
        copies[-1].start()
    for copy in copies:
        copy.wait()


def finish(plan, y, own, gate, gain, w_out):
    args = (y, own, gate, gain, w_out)
    shape = (plan.rows, plan.cols, w_out.shape[1])
    assert w_out.shape[1] == plan.width
    return call(
        functools.partial(finish_kernel, plan),
        "finish",
        args,
        [(shape, BF16)],
        [((plan.cells, plan.width), F32), (shape, BF16), pltpu.SemaphoreType.DMA((4,))],
        [HBM],
    )[0]


def per_device(slide, tissue, w_in, w_bcd, dt_bias, rate_x, rate_y, d_skip, norm_gain, w_out):
    rows, cols, model_width = slide.shape
    width = w_out.shape[0]
    heads = dt_bias.shape[0]
    states = (w_bcd.shape[1] - heads) // 2
    plan = Plan(rows, cols, states, heads, width, lax.axis_size("col"))
    consts = plan.constants()
    v, pay, table, x = project(plan, consts, slide, w_in, w_bcd, tissue, dt_bias, rate_x, rate_y)
    groups = plan.segments()
    pay = lax.all_to_all(pay, "col", 0, 0, tiled=True, axis_index_groups=groups)
    gain = norm_gain.reshape(1, width)
    own, gate, gain = home(plan, consts, v, table, x, w_in, tissue, gain, rate_x, rate_y, d_skip)
    pay, own, gate, gain = lax.optimization_barrier((pay, own, gate, gain))
    y = scan_calls(plan, consts, "row", "col", pay)
    y = lax.all_to_all(y, "col", 0, 0, tiled=True, axis_index_groups=groups)
    return finish(plan, y, own, gate, gain, w_out)


def solution(mesh):
    placed = (
        P(("slides", "row"), "col", None),
        P(("slides", "row"), "col"),
        P(),
        P(),
        P(),
        P(),
        P(),
        P(),
        P(),
        P(),
    )
    return jax.shard_map(
        per_device,
        mesh=mesh,
        in_specs=placed,
        out_specs=P(("slides", "row"), "col", None),
        check_vma=False,
    )
```

```python
import functools

import jax
import jax.numpy as jnp
import numpy as np
from jax import lax
from jax.experimental import pallas as pl
from jax.experimental.pallas import tpu as pltpu
from jax.sharding import PartitionSpec as P

norm_eps = 1e-05
LANES = 128
HALF = LANES // 2
F32 = jnp.float32
BF16 = jnp.bfloat16


def round_up(value, step):
    return -(-value // step) * step


def in_hbm(x):
    return pltpu.with_memory_space_constraint(x, pltpu.HBM)


def mm(a, b):
    return jnp.dot(a, b, preferred_element_type=F32)


def nt_dot(a, b):
    return lax.dot_general(a, b, (((1,), (1,)), ((), ())), preferred_element_type=F32)


def tn_dot(a, b):
    return lax.dot_general(a, b, (((0,), (0,)), ((), ())), preferred_element_type=F32)


class Plan:
    def __init__(self, rows, cols, states, heads, width, devices):
        self.rows, self.cols, self.states, self.heads = rows, cols, states, heads
        self.width = width
        self.parts = 2 if devices % 2 == 0 and devices > 2 else 1
        self.devices = devices // self.parts
        self.group = width // self.devices
        self.slot = min(self.group, HALF)
        self.slots = self.group // self.slot
        self.work = self.slots * self.devices
        self.head_width = width // heads
        self.col_pad = round_up(cols, 8)
        self.count = rows * cols
        self.half = self.count // 2 // 8 * 8
        self.cells = round_up(self.count, 8)
        self.edge = rows * states
        self.top = states * self.col_pad
        self.bc = 2 * states
        self.spare = LANES - self.half
        self.tail_cells = self.count - self.half - HALF - self.spare
        self.at_bc = self.cells
        self.at_dt = self.at_bc + self.bc + states
        assert HALF <= self.half and 0 < self.tail_cells <= self.cells - self.count and self.bc <= HALF
        self.at_rate = self.at_dt + 2 * self.slots
        self.message = round_up(self.at_rate + 1, 8)
        self.tail = self.edge % LANES
        self.solid = self.edge // LANES
        self.share = LANES // self.tail if self.tail else 1
        self.packed = self.slots * self.solid + (-(-self.slots // self.share) if self.tail else 0)
        assert self.head_width % self.slot == 0 and self.group % self.slot == 0
        assert LANES % self.head_width == 0 and LANES % self.group == 0
        assert self.cells - self.half <= LANES
        assert states % 16 == 0 and heads % 8 == 0

    def segments(self):
        return [list(range(p * self.devices, (p + 1) * self.devices)) for p in range(self.parts)]

    def lanes(self):
        at = np.arange(2 * LANES)
        cell = np.where(at < LANES, at, at - LANES + self.half)
        live = np.where(at < LANES, at < self.half, cell < self.count)
        return cell // self.cols, cell % self.cols, live

    def constants(self):
        i, j, real = self.lanes()
        both = real[:, None] & real[None]
        cell = np.arange(self.cells)
        ci, cj = cell // self.cols, cell % self.cols
        creal = cell < self.count
        le = np.arange(round_up(self.rows, 8))
        lj = np.arange(self.col_pad)
        out = {}
        out["to1"] = (j[:, None] <= j[None]) & both
        out["to2"] = (j[:, None] == j[None]) & (i[:, None] <= i[None]) & both
        out["from1"] = (i[:, None] == i[None]) & (j[:, None] > j[None]) & both
        out["from2"] = (i[:, None] > i[None]) & both
        out["side1"] = (i[None] == le[:, None]) & real[None]
        out["side2"] = (i[None] > le[:, None]) & real[None]
        out["sidemask"] = (i[None] >= le[:, None]) & (le < self.rows)[:, None] & real[None]
        out["down1"] = (j[None] <= lj[:, None]) & real[None]
        out["down2"] = (j[None] == lj[:, None]) & real[None]
        out["downmask"] = (j[None] <= lj[:, None]) & (lj < self.cols)[:, None] & real[None]
        out["pick"] = (
            (i == self.rows - 1)[:, None] & real[:, None] & (j[:, None] == np.tile(lj, self.states)[None])
        )
        cboth = creal[:, None] & real[None]
        out["own1"] = (j[None] <= cj[:, None]) & cboth
        out["own2"] = (j[None] == cj[:, None]) & (i[None] <= ci[:, None]) & cboth
        out["ownmask"] = (i[None] <= ci[:, None]) & (j[None] <= cj[:, None]) & cboth
        out["lanei"] = (np.arange(self.rows)[:, None] == i[None]) & real[None]
        out["lanej"] = (np.arange(self.cols)[:, None] == j[None]) & real[None]
        return {k: in_hbm(jnp.asarray(x.astype(np.float32), BF16)) for k, x in out.items()}


def full(shape):
    return pl.BlockSpec(shape, lambda *_: (0,) * len(shape))


HBM = pl.BlockSpec(memory_space=pltpu.HBM)
SMEM = pl.BlockSpec(memory_space=pltpu.SMEM)


def split_cell(plan, cell):
    i = lax.shift_right_logical(cell * (-(-65536 // plan.cols)), 16)
    return i, cell - i * plan.cols


def cell_mask_of(plan, t_ref):
    t = t_ref[...].astype(F32).astype(BF16)
    shape = (plan.cells, plan.cols)
    _, j = split_cell(plan, lax.broadcasted_iota(jnp.int32, shape, 0))
    pick = ones(j == lax.broadcasted_iota(jnp.int32, shape, 1))
    shape = (plan.cells, plan.rows)
    i, _ = split_cell(plan, lax.broadcasted_iota(jnp.int32, shape, 0))
    here = i == lax.broadcasted_iota(jnp.int32, shape, 1)
    return jnp.sum(jnp.where(here, mm(pick, t), 0.0), axis=1, keepdims=True)


def rate_row(heads_of, rx_ref, ry_ref):
    at = lax.broadcasted_iota(jnp.int32, (1, LANES), 1)
    rate = jnp.zeros((1, LANES), F32)
    part = jnp.zeros((1, LANES), jnp.int32)
    for s, head in enumerate(heads_of):
        for k, ref in enumerate((rx_ref, ry_ref)):
            first = 8 * s + 3 * k
            here = (at >= first) & (at < first + 3)
            rate = jnp.where(here, ref[head], rate)
            part = jnp.where(here, at - first, part)
    high = rate.astype(BF16).astype(F32)
    middle = (rate - high).astype(BF16).astype(F32)
    low = rate - high - middle
    return jnp.where(part == 0, high, jnp.where(part == 1, middle, low))


def project_kernel(
    plan, chunks, bias_hbm, rx_hbm, ry_hbm, x_hbm, w_hbm, wt_hbm, t_hbm, lanei_hbm, lanej_hbm,
    v_ref, pay_hbm, rows_ref, flat_ref,
    bias_ref, rx_ref, ry_ref, x_ref, w_ref, wt_ref, t_ref, lanei_ref, lanej_ref, pay_ref, wide, sems, w_sems, out_sems,
):
    group, states, cells, heads = plan.group, plan.states, plan.cells, plan.heads
    half, rest = plan.half, plan.cells - plan.half
    tile = plan.width // chunks
    pairs = (
        (x_hbm, x_ref), (t_hbm, t_ref), (wt_hbm, wt_ref), (lanei_hbm, lanei_ref), (lanej_hbm, lanej_ref),
        (bias_hbm, bias_ref), (rx_hbm, rx_ref), (ry_hbm, ry_ref),
    )
    loads = [pltpu.make_async_copy(a, b, sems.at[k]) for k, (a, b) in enumerate(pairs)]
    copies = [
        pltpu.make_async_copy(w_hbm.at[:, k * tile : (k + 1) * tile], w_ref.at[k], w_sems.at[k])
        for k in range(chunks)
    ]
    for copy in loads + copies:
        copy.start()
    wide[...] = jnp.zeros_like(wide)
    v_ref[half:LANES, :] = jnp.zeros((LANES - half, plan.width), BF16)
    v_ref[LANES + rest :, :] = jnp.zeros((LANES - rest, plan.width), BF16)

    loads[0].wait()
    for i in range(plan.rows):
        wide[i * plan.cols : (i + 1) * plan.cols, :] = x_ref[i].astype(F32)
    x = wide[...].astype(BF16)
    flat_ref[...] = x
    for copy in loads[1:]:
        copy.wait()
    keep = cell_mask_of(plan, t_ref)
    t = t_ref[...].astype(F32).astype(BF16)
    m = jnp.sum(mm(t, lanei_ref[...]) * lanej_ref[...].astype(F32), axis=0, keepdims=True)
    table = nt_dot(wt_ref[...], x)
    ext = jnp.concatenate([table, jnp.zeros((table.shape[0], 2 * LANES - cells), F32)], axis=1)
    lane = lax.broadcasted_iota(jnp.int32, (table.shape[0], LANES), 1)
    lo, hi = ext[:, :LANES], ext[:, LANES:]
    shift = half % LANES
    if shift:
        moved = jnp.where(
            lane < LANES - shift, pltpu.roll(lo, LANES - shift, 1), pltpu.roll(hi, LANES - shift, 1)
        )
    else:
        moved = hi
    table = jnp.concatenate([jnp.where(lane < half, lo, 0.0), jnp.where(lane < plan.count - half, moved, 0.0)], axis=1)
    z = table[2 * states :]
    at = lax.broadcasted_iota(jnp.int32, z.shape, 0)
    for h in range(heads):
        z = jnp.where(at == h, z + bias_ref[h], z)
    soft = m * (jnp.maximum(z, 0.0) + jnp.log1p(jnp.exp(-jnp.abs(z))))
    table = jnp.concatenate([table[: 2 * states], soft], axis=0).astype(BF16)
    rows_ref[...] = table.astype(F32)
    bc = rows_ref[: 2 * states, :]
    lane = lax.broadcasted_iota(jnp.int32, (2 * states, LANES), 1)
    early = jnp.where(lane < half, bc[:, :LANES], pltpu.roll(bc[:, LANES:], half - HALF, 1)).astype(BF16)
    lane = lax.broadcasted_iota(jnp.int32, (states, LANES), 1)
    late = jnp.where(lane < HALF, bc[:states, LANES:], pltpu.roll(bc[states:, LANES:], HALF, 1)).astype(BF16)
    first_end = HALF + plan.spare
    ends = bc[:, LANES:].T[first_end : first_end + 8]
    ends = jnp.concatenate([ends, jnp.zeros((8, LANES - 2 * states), F32)], axis=1)
    ends = pltpu.roll(ends, plan.tail_cells, 0)
    pad_row = lax.broadcasted_iota(jnp.int32, (8, LANES), 0) >= plan.count - (cells - 8)
    steps = rows_ref[2 * states :, :]

    lane = lax.broadcasted_iota(jnp.int32, (cells, LANES), 1)
    sent = []
    for chunk in range(chunks):
        copies[chunk].wait()
        v = mm(flat_ref[...], w_ref[chunk]).astype(BF16).astype(F32) * keep
        low = v.astype(BF16)
        v_ref[0:half, chunk * tile : (chunk + 1) * tile] = low[:half]
        v_ref[LANES : LANES + rest, chunk * tile : (chunk + 1) * tile] = low[half:]
        per = tile // group
        for k in range(per):
            dest = chunk * per + k
            base, at = k * group // LANES * LANES, k * group % LANES
            mine = v[:, base : base + LANES]
            if at:
                mine = pltpu.roll(mine, LANES - at, 1)
            if group < LANES:
                mine = jnp.where(lane < group, mine, 0.0)
            pay_ref[dest, 0 : cells - 8, :] = mine[: cells - 8].astype(BF16)
            pay_ref[dest, cells - 8 : cells, :] = jnp.where(pad_row, ends, mine[cells - 8 :]).astype(BF16)
            dts, heads_of = [], []
            for s in range(plan.slots):
                head = (chunk * tile + k * group + s * plan.slot) // plan.head_width
                heads_of.append(head)
                dts += [steps[head : head + 1, :LANES], steps[head : head + 1, LANES:]]
            dts.append(rate_row(heads_of, rx_ref, ry_ref))
            pay_ref[dest, plan.at_bc : plan.at_bc + plan.bc, :] = early
            pay_ref[dest, plan.at_bc + plan.bc : plan.at_dt, :] = late
            spare = plan.message - plan.at_dt - len(dts)
            dts += [jnp.zeros((spare, LANES), F32)] if spare else []
            pay_ref[dest, plan.at_dt : plan.message, :] = jnp.concatenate(dts, axis=0).astype(BF16)
            sent.append(pltpu.make_async_copy(pay_ref.at[dest], pay_hbm.at[dest], out_sems.at[dest]))
            sent[-1].start()
    for copy in sent:
        copy.wait()


def project(plan, consts, slide, w_in, w_bcd, tissue, dt_bias, rate_x, rate_y):
    chunks = 2
    tile = plan.width // chunks
    depth = slide.shape[2]
    args = [dt_bias, rate_x, rate_y, slide, w_in, w_bcd.T, tissue.T, consts["lanei"], consts["lanej"]]
    count = 2 * plan.states + plan.heads
    assert plan.width % chunks == 0 and tile % plan.group == 0 and tile % LANES == 0
    message = (plan.devices, plan.message, LANES)
    outs = [((2 * LANES, plan.width), BF16), (message, BF16), ((count, 2 * LANES), F32), ((plan.cells, depth), BF16)]
    specs = [full(s) for s, _ in outs]
    specs[1] = HBM
    return pl.pallas_call(
        functools.partial(project_kernel, plan, chunks),
        grid=(1,),
        in_specs=[HBM] * len(args),
        out_specs=specs,
        out_shape=[jax.ShapeDtypeStruct(s, d) for s, d in outs],
        scratch_shapes=[
            pltpu.SMEM(dt_bias.shape, F32),
            pltpu.SMEM(rate_x.shape, F32),
            pltpu.SMEM(rate_y.shape, F32),
            pltpu.VMEM(slide.shape, BF16),
            pltpu.VMEM((chunks, depth, tile), BF16),
        ]
        + [pltpu.VMEM(x.shape, x.dtype) for x in args[5:]]
        + [
            pltpu.VMEM(message, BF16),
            pltpu.VMEM((plan.cells, depth), F32),
            pltpu.SemaphoreType.DMA((8,)),
            pltpu.SemaphoreType.DMA((chunks,)),
            pltpu.SemaphoreType.DMA((plan.devices,)),
        ],
        compiler_params=pltpu.CompilerParams(vmem_limit_bytes=24 * 2**20),
        name="project",
    )(*[in_hbm(x) for x in args])


def home_kernel(plan, v_ref, rows_ref, flat_ref, w_hbm, *refs):
    sources, refs = refs[:9], refs[9:]
    gain_hbm, out_ref, gate_hbm, gain_out, pair, w_ref, gate_ref = refs[:7]
    held, (sem, gain_sem, sems, gate_sems) = refs[7:16], refs[16:]
    states, cells, half = plan.states, plan.cells, plan.half
    reads = [pltpu.make_async_copy(a, b, sems.at[k]) for k, (a, b) in enumerate(zip(sources, held))]
    reads.append(pltpu.make_async_copy(gain_hbm, gain_out, gain_sem))
    copy = pltpu.make_async_copy(w_hbm.at[:, plan.width :], w_ref, sem)
    for each in reads + [copy]:
        each.start()
    rx_ref, ry_ref, skip_ref, t_ref, own1_ref, own2_ref, from1_ref, from2_ref, mask_ref = held
    b = rows_ref[0:states, :].astype(BF16)
    c = rows_ref[states : 2 * states, :].astype(BF16)
    pairs = tn_dot(c, b)
    pairs = jnp.concatenate([pairs[:half], pairs[LANES : LANES + cells - half]], axis=0)
    for each in reads:
        each.wait()
    pair[...] = pairs * mask_ref[...].astype(F32)
    lane = lax.broadcasted_iota(jnp.int32, (cells, LANES), 1)
    per = LANES // plan.head_width
    for block in range(plan.width // LANES):
        v = v_ref[:, block * LANES : (block + 1) * LANES]
        vc = jnp.concatenate([v[:half], v[LANES : LANES + cells - half]], axis=0).astype(F32)
        total = None
        for k in range(per):
            h = block * per + k
            dt = rows_ref[2 * states + h : 2 * states + h + 1, :]
            low = dt.astype(BF16)
            x = mm(own1_ref[...] * low, from1_ref[...])
            y = mm(own2_ref[...] * low, from2_ref[...])
            weight = jnp.exp(-(rx_ref[h] * x + ry_ref[h] * y)) * pair[...] * dt
            part = mm(weight.astype(BF16), v) + skip_ref[h] * vc
            total = part if total is None else jnp.where(lane < k * plan.head_width, total, part)
        out_ref[:, block * LANES : (block + 1) * LANES] = total.astype(BF16)
    keep = cell_mask_of(plan, t_ref)
    copy.wait()
    tile = plan.width // gate_sems.shape[0]
    sent = []
    for block in range(plan.width // tile):
        at = slice(block * tile, (block + 1) * tile)
        z = mm(flat_ref[...], w_ref[:, at]).astype(BF16).astype(F32)
        gate_ref[:, at] = (z * (1.0 / (1.0 + jnp.exp(-z))) * keep).astype(BF16)
        sent.append(pltpu.make_async_copy(gate_ref.at[:, at], gate_hbm.at[:, at], gate_sems.at[block]))
        sent[-1].start()
    for each in sent:
        each.wait()


def home(plan, consts, v, rows, flat, w_in, tissue, gain, rate_x, rate_y, d_skip):
    sources = [rate_x, rate_y, d_skip, tissue.T] + [consts[k] for k in ("own1", "own2", "from1", "from2", "ownmask")]
    fixed = [in_hbm(x) for x in [w_in] + sources + [gain]]
    outs = [((plan.cells, plan.width), BF16), ((plan.cells, plan.width), BF16), (gain.shape, F32)]
    return pl.pallas_call(
        functools.partial(home_kernel, plan),
        grid=(1,),
        in_specs=[full(x.shape) for x in (v, rows, flat)] + [HBM] * len(fixed),
        out_specs=[full(outs[0][0]), HBM, full(outs[2][0])],
        out_shape=[jax.ShapeDtypeStruct(s, d) for s, d in outs],
        scratch_shapes=[
            pltpu.VMEM((plan.cells, 2 * LANES), F32),
            pltpu.VMEM((w_in.shape[0], w_in.shape[1] - plan.width), BF16),
            pltpu.VMEM((plan.cells, plan.width), BF16),
        ]
        + [pltpu.SMEM(x.shape, F32) for x in sources[:3]]
        + [pltpu.VMEM(x.shape, x.dtype) for x in sources[3:]]
        + [
            pltpu.SemaphoreType.DMA,
            pltpu.SemaphoreType.DMA,
            pltpu.SemaphoreType.DMA((len(sources),)),
            pltpu.SemaphoreType.DMA((4,)),
        ],
        compiler_params=pltpu.CompilerParams(vmem_limit_bytes=24 * 2**20),
        name="home",
    )(v, rows, flat, *fixed)


def ones(mask):
    return jnp.where(mask, 1.0, 0.0).astype(BF16)


def places(plan, shape, axis):
    at = lax.broadcasted_iota(jnp.int32, shape, axis)
    late = at >= LANES
    cell = jnp.where(late, at - (LANES - plan.half), at)
    i, j = split_cell(plan, cell)
    return i, j, cell < jnp.where(late, plan.count, plan.half)


def map_rows(plan, pay_ref, turned, t, k):
    n = plan.states
    first = pay_ref[t, plan.at_bc + k * n : plan.at_bc + (k + 1) * n, :].astype(F32)
    second = pay_ref[t, plan.at_bc + plan.bc : plan.at_dt, :].astype(F32)
    if k:
        second = pltpu.roll(second, HALF, 1)
    ends = turned[k * n : (k + 1) * n, LANES:].astype(F32)
    lane = lax.broadcasted_iota(jnp.int32, (n, LANES), 1)
    moved = pltpu.roll(first, LANES + HALF - plan.half, 1)
    ends = pltpu.roll(ends, LANES - plan.tail_cells, 1)
    second = jnp.where(lane < HALF, second, jnp.where(lane < HALF + plan.spare, moved, ends))
    return jnp.concatenate([first, second], axis=1)


def turn_all(plan, pay_ref, turned, b_ref):
    for t in range(plan.devices):
        sides = []
        for lo, hi in ((0, plan.half), (plan.half, plan.cells)):
            v = pay_ref[t, lo:hi, :].astype(F32)
            if hi - lo < LANES:
                v = jnp.concatenate([v, jnp.zeros((LANES - hi + lo, LANES), F32)], axis=0)
            sides.append(v.T)
        v = jnp.concatenate(sides, axis=1).astype(BF16)
        for s in range(plan.slots):
            turned[s * plan.devices + t] = v[s * HALF : (s + 1) * HALF]
        b_ref[t] = map_rows(plan, pay_ref, v, t, 0)


def load_steps(plan, pay_ref, dts):
    for t in range(plan.devices):
        rows = pay_ref[t, plan.at_dt : plan.message, :].astype(F32)
        for s in range(plan.slots):
            w = s * plan.devices + t
            dts[w : w + 1, :LANES] = rows[2 * s : 2 * s + 1]
            dts[w : w + 1, LANES:] = rows[2 * s + 1 : 2 * s + 2]


def rates_of(plan, pay_ref, kind):
    row = pay_ref[0, plan.at_dt : plan.message, :].astype(F32)[plan.at_rate - plan.at_dt : plan.at_rate - plan.at_dt + 1]
    at = lax.broadcasted_iota(jnp.int32, (1, LANES), 1)
    first = [8 * s + 3 * kind for s in range(plan.slots)]
    return [jnp.sum(jnp.where((at >= f) & (at < f + 3), row, 0.0), axis=1, keepdims=True) for f in first]


def slot_rates(plan, pay_ref, kind):
    return jnp.concatenate(
        [jnp.broadcast_to(r, (plan.devices, 1)) for r in rates_of(plan, pay_ref, kind)], axis=0
    )


def pack_edges(plan, out_ref, held):
    for s in range(plan.slots):
        for k in range(plan.solid):
            out_ref[s * plan.solid + k] = held[s][:, k * LANES : (k + 1) * LANES].astype(BF16)
    if plan.tail:
        first = plan.slots * plan.solid
        for k in range(plan.packed - first):
            parts = [x[:, plan.solid * LANES :] for x in held[k * plan.share : (k + 1) * plan.share]]
            spare = LANES - plan.tail * len(parts)
            parts += [jnp.zeros((HALF, spare), F32)] if spare else []
            out_ref[first + k] = jnp.concatenate(parts, axis=1).astype(BF16)


def unpack_edges(plan, ref, s):
    parts = [ref[s * plan.solid + k].astype(F32) for k in range(plan.solid)]
    if plan.tail:
        last = ref[plan.slots * plan.solid + s // plan.share].astype(F32)
        at = s % plan.share * plan.tail
        parts.append(last[:, at : at + plan.tail])
    return jnp.concatenate(parts, axis=1)


def scan_edges(plan, pay_ref, turned, b_ref, dts, inner, kept, seen):
    states, tiles, wide = plan.states, plan.devices, 2 * LANES
    i, j, real = places(plan, (wide, wide), 0)
    ti, tj, treal = places(plan, (wide, wide), 1)
    from1 = ones((i == ti) & (j > tj) & real & treal)
    edge_row = lax.div(lax.broadcasted_iota(jnp.int32, (wide, plan.edge), 1), states)
    i, _, real = places(plan, (wide, plan.edge), 0)
    keep = ones((i == edge_row) & real)
    ti, _, treal = places(plan, (plan.rows, wide), 1)
    rowsel = ones((ti == lax.broadcasted_iota(jnp.int32, (plan.rows, wide), 0)) & treal)
    dt = dts[...]
    low = dt.astype(BF16)
    rate = slot_rates(plan, pay_ref, 0)
    inner[...] = jnp.exp(-rate * mm(low, from1)) * dt
    kept[...] = jnp.exp(-rate * mm(low, keep))
    ends = []
    for s in range(plan.slots):
        held = jnp.zeros((HALF, plan.edge), F32)
        product = jnp.ones((1, plan.edge), F32)
        for t in range(tiles):
            w = s * tiles + t
            seen(w, held, product)
            b = b_ref[t]
            bd = (b * inner[w : w + 1, :]).astype(BF16)
            left = jnp.concatenate([bd * rowsel[i : i + 1] for i in range(plan.rows)], axis=0)
            now = kept[w : w + 1, :]
            held = held * now + nt_dot(turned[w], left)
            product = product * now
        ends.append(held)
    return ends


def last_kernel(plan, axis, pay_ref, last_ref, turned, b_ref, dts, inner):
    @pl.when(lax.axis_index(axis) < (plan.parts - 1) * plan.devices)
    def _():
        states, tiles, wide = plan.states, plan.devices, 2 * LANES
        turn_all(plan, pay_ref, turned, b_ref)
        load_steps(plan, pay_ref, dts)
        i, j, real = places(plan, (wide, wide), 0)
        ti, tj, treal = places(plan, (wide, wide), 1)
        same = (i == ti) & real & treal
        ti, _, treal = places(plan, (plan.rows, wide), 1)
        rowsel = ones((ti == lax.broadcasted_iota(jnp.int32, (plan.rows, wide), 0)) & treal)
        low = dts[...].astype(BF16)
        rest, whole = mm(low, ones(same & (j > tj))), mm(low, ones(same))
        left = []
        for s in range(plan.slots):
            after = jnp.zeros((1, wide), F32)
            rows = []
            for t in reversed(range(tiles)):
                rows.append(after)
                after = after + whole[s * tiles + t : s * tiles + t + 1]
            left += rows[::-1]
        inner[...] = jnp.exp(-slot_rates(plan, pay_ref, 0) * (rest + jnp.concatenate(left, axis=0))) * dts[...]
        ends = []
        for s in range(plan.slots):
            held = None
            for t in range(tiles):
                w = s * tiles + t
                b = b_ref[t]
                bd = (b * inner[w : w + 1, :]).astype(BF16)
                left = jnp.concatenate([bd * rowsel[i : i + 1] for i in range(plan.rows)], axis=0)
                part = nt_dot(turned[w], left)
                held = part if held is None else held + part
            ends.append(held)
        pack_edges(plan, last_ref, ends)


def maps_kernel(
    plan, pay_ref, to1_ref, to2_ref, from1_ref, from2_ref, side1_ref, side2_ref,
    sidemask_ref, down1_ref, down2_ref, downmask_ref, pick_ref,
    side_ref, above_ref, passed_ref, top_ref, edge_ref, upto_ref, c_ref, turned, b_ref, dts, inner, kept, s1, s2, d1, d2,
):
    states, tiles, cp, work = plan.states, plan.devices, plan.col_pad, plan.work
    rp = side1_ref.shape[0]
    turn_all(plan, pay_ref, turned, b_ref)
    load_steps(plan, pay_ref, dts)
    for t in range(tiles):
        c_ref[t] = map_rows(plan, pay_ref, turned[t], t, 1).astype(BF16)

    def seen(w, held, product):
        edge_ref[w] = held.astype(BF16)
        upto_ref[w : w + 1, :] = product

    scan_edges(plan, pay_ref, turned, b_ref, dts, inner, kept, seen)
    low = dts[...].astype(BF16)
    above_ref[...] = jnp.exp(-slot_rates(plan, pay_ref, 1) * mm(low, to2_ref[...]))
    rates_x, rates_y = rates_of(plan, pay_ref, 0), rates_of(plan, pay_ref, 1)
    for w in range(work):
        rf = dts[w : w + 1, :]
        s1[w * rp : (w + 1) * rp, :] = side1_ref[...].astype(F32) * rf
        s2[w * rp : (w + 1) * rp, :] = side2_ref[...].astype(F32) * rf
        d1[w * cp : (w + 1) * cp, :] = down1_ref[...].astype(F32) * rf
        d2[w * cp : (w + 1) * cp, :] = down2_ref[...].astype(F32) * rf
    mask = sidemask_ref[...].astype(F32)
    x, y = mm(s1[...].astype(BF16), to1_ref[...]), mm(s2[...].astype(BF16), to2_ref[...])
    shape = (states, plan.top)
    n = lax.broadcasted_iota(jnp.int32, shape, 0)
    diag = ones(n == lax.div(lax.broadcasted_iota(jnp.int32, shape, 1), cp))
    for w in range(work):
        s = w // tiles
        at = slice(w * rp, (w + 1) * rp)
        side = (jnp.exp(-(rates_x[s] * x[at] + rates_y[s] * y[at])) * mask).astype(BF16)
        side_ref[w] = side
        bottom = mm(side, pick_ref[...]).astype(BF16)
        passed_ref[w] = jnp.concatenate([diag * bottom[i : i + 1] for i in range(plan.rows)], axis=0)
    x, y = mm(d1[...].astype(BF16), from1_ref[...]), mm(d2[...].astype(BF16), from2_ref[...])
    mask = downmask_ref[...].astype(F32)
    for w in range(work):
        s, t = w // tiles, w % tiles
        at = slice(w * cp, (w + 1) * cp)
        fall = jnp.exp(-(rates_x[s] * x[at] + rates_y[s] * y[at])) * mask * dts[w : w + 1, :]
        b = b_ref[t]
        falls = jnp.concatenate([fall * b[n : n + 1] for n in range(states)], axis=0).astype(BF16)
        top_ref[w] = nt_dot(turned[w], falls) + mm(edge_ref[w], passed_ref[w])


def join_kernel(plan, row_axis, col_axis, upto_ref, entry_ref, passed_ref, top_ref, out_ref):
    sends = lax.axis_index(row_axis) < lax.axis_size(row_axis) - 1
    first = lax.axis_index(col_axis) < plan.devices

    @pl.when(sends & first)
    def _():
        out_ref[...] = top_ref[...].astype(BF16)

    @pl.when(sends & jnp.logical_not(first))
    def _():
        for s in range(plan.slots):
            entry = unpack_edges(plan, entry_ref, s)
            for t in range(plan.devices):
                w = s * plan.devices + t
                late = (entry * upto_ref[w : w + 1, :]).astype(BF16)
                out_ref[w] = (top_ref[w] + mm(late, passed_ref[w])).astype(BF16)


def sides_kernel(plan, c_ref, edge_ref, upto_ref, entry_ref, side_ref, above_ref, y_ref, down_ref):
    states, tiles = plan.states, plan.devices
    shape = (plan.col_pad, 2 * LANES)
    _, tj, treal = places(plan, shape, 1)
    colsel = jnp.where((tj == lax.broadcasted_iota(jnp.int32, shape, 0)) & treal, 1.0, 0.0)
    for s in range(plan.slots):
        entry = unpack_edges(plan, entry_ref, s)
        for t in range(tiles):
            w = s * tiles + t
            c = c_ref[t]
            side = side_ref[w]
            left = jnp.concatenate([c * side[i : i + 1] for i in range(plan.rows)], axis=0)
            whole = (edge_ref[w].astype(F32) + entry * upto_ref[w : w + 1, :]).astype(BF16)
            y_ref[w] = mm(whole, left)
            ca = c.astype(F32) * above_ref[w : w + 1, :]
            down_ref[w] = jnp.concatenate([colsel * ca[n : n + 1] for n in range(states)], axis=0).astype(BF16)


def cells_kernel(plan, y_ref, down_ref, top_ref, out_ref):
    tiles = plan.devices
    for t in range(tiles):
        ys = [y_ref[w] + mm(top_ref[w], down_ref[w]) for w in range(t, plan.work, tiles)]
        if plan.slots == 1:
            ys.append(jnp.zeros_like(ys[0]))
        y = jnp.concatenate(ys, axis=0)
        for k, (lo, hi) in enumerate(((0, plan.half), (plan.half, plan.cells))):
            out_ref[t, lo:hi, :] = y[:, k * LANES : (k + 1) * LANES].T[: hi - lo].astype(BF16)


def call(kernel, name, args, outs, scratch=(), out_specs=None):
    return pl.pallas_call(
        kernel,
        grid=(1,),
        in_specs=[full(x.shape) for x in args],
        out_specs=out_specs or [full(s) for s, _ in outs],
        out_shape=[jax.ShapeDtypeStruct(s, d) for s, d in outs],
        scratch_shapes=[x if not isinstance(x, tuple) else pltpu.VMEM(*x) for x in scratch],
        compiler_params=pltpu.CompilerParams(vmem_limit_bytes=24 * 2**20),
        name=name,
    )(*args)


def scan_calls(plan, consts, row_axis, col_axis, pay):
    work, cp, wide = plan.work, plan.col_pad, 2 * LANES
    rp = consts["side1"].shape[0]
    steps = [((work, HALF, wide), BF16), ((plan.devices, plan.states, wide), F32), ((work, wide), F32), ((work, wide), F32), ((work, plan.edge), F32)]
    shape = (plan.packed, HALF, LANES)
    if plan.parts > 1:
        last = call(functools.partial(last_kernel, plan, col_axis), "last", [pay], [(shape, BF16)], steps[:4])[0]
        entry = lax.ppermute(last, col_axis, [(k, k + plan.devices) for k in range(plan.devices)])
    else:
        entry = jnp.zeros(shape, BF16)
    names = ("to1", "to2", "from1", "from2", "side1", "side2", "sidemask", "down1", "down2", "downmask", "pick")
    side, above, passed, tops, edges, upto, c = call(
        functools.partial(maps_kernel, plan),
        "maps",
        [pay] + [consts[k] for k in names],
        [
            ((work, rp, wide), BF16),
            ((work, wide), F32),
            ((work, plan.edge, plan.top), BF16),
            ((work, HALF, plan.top), F32),
            ((work, HALF, plan.edge), BF16),
            ((work, plan.edge), F32),
            ((plan.devices, plan.states, wide), BF16),
        ],
        steps + [((work * rp, wide), F32)] * 2 + [((work * cp, wide), F32)] * 2,
    )
    edge_entry = entry
    tops = call(
        functools.partial(join_kernel, plan, row_axis, col_axis),
        "join",
        [upto, entry, passed, tops],
        [((work, HALF, plan.top), BF16)],
    )[0]
    count = lax.axis_size(row_axis)
    chain = [(r, r + 1) for r in range(count - 1)]
    entry = lax.ppermute(tops, row_axis, chain)
    if count > 2:
        keep = jnp.dot(above.astype(BF16), consts["pick"], preferred_element_type=F32)[:, None, :]
        for _ in range(count - 2):
            entry = lax.ppermute(
                (tops.astype(F32) + keep * entry.astype(F32)).astype(BF16), row_axis, chain
            )
    y, down = call(
        functools.partial(sides_kernel, plan),
        "sides",
        [c, edges, upto, edge_entry, side, above],
        [((work, HALF, wide), F32), ((work, plan.top, wide), BF16)],
    )
    return call(
        functools.partial(cells_kernel, plan),
        "cells",
        [y, down, entry],
        [((plan.devices, plan.cells, LANES), BF16)],
    )[0]


def finish_kernel(plan, y_ref, own_ref, gate_ref, gain_ref, w_ref, out_hbm, full_ref, out_ref, sems):
    group = plan.group
    per = LANES // group
    lane = lax.broadcasted_iota(jnp.int32, (plan.cells, LANES), 1)
    for block in range(plan.width // LANES):
        joined = None
        for d in range(per):
            part = y_ref[block * per + d].astype(F32)
            if d:
                part = pltpu.roll(part, d * group, 1)
            joined = part if joined is None else jnp.where(lane < d * group, joined, part)
        at = slice(block * LANES, (block + 1) * LANES)
        y = joined + own_ref[:, at].astype(F32)
        full_ref[:, at] = y.astype(BF16).astype(F32) * gate_ref[:, at].astype(F32)
    gated = full_ref[...]
    scale = lax.rsqrt(jnp.mean(gated * gated, axis=-1, keepdims=True) + norm_eps)
    normed = (gated * scale * gain_ref[...]).astype(BF16)
    copies = []
    chunks = sems.shape[0]
    tile = w_ref.shape[1] // chunks
    for k in range(chunks):
        at = slice(k * tile, (k + 1) * tile)
        out = mm(normed, w_ref[:, at])
        for i in range(plan.rows):
            out_ref[i, :, at] = out[i * plan.cols : (i + 1) * plan.cols].astype(BF16)
        copies.append(pltpu.make_async_copy(out_ref.at[:, :, at], out_hbm.at[:, :, at], sems.at[k]))
        copies[-1].start()
    for copy in copies:
        copy.wait()


def finish(plan, y, own, gate, gain, w_out):
    args = (y, own, gate, gain, w_out)
    shape = (plan.rows, plan.cols, w_out.shape[1])
    assert w_out.shape[1] == plan.width
    return call(
        functools.partial(finish_kernel, plan),
        "finish",
        args,
        [(shape, BF16)],
        [((plan.cells, plan.width), F32), (shape, BF16), pltpu.SemaphoreType.DMA((4,))],
        [HBM],
    )[0]


def per_device(slide, tissue, w_in, w_bcd, dt_bias, rate_x, rate_y, d_skip, norm_gain, w_out):
    rows, cols, model_width = slide.shape
    width = w_out.shape[0]
    heads = dt_bias.shape[0]
    states = (w_bcd.shape[1] - heads) // 2
    plan = Plan(rows, cols, states, heads, width, lax.axis_size("col"))
    consts = plan.constants()
    v, pay, table, x = project(plan, consts, slide, w_in, w_bcd, tissue, dt_bias, rate_x, rate_y)
    groups = plan.segments()
    pay = lax.all_to_all(pay, "col", 0, 0, tiled=True, axis_index_groups=groups)
    gain = norm_gain.reshape(1, width)
    own, gate, gain = home(plan, consts, v, table, x, w_in, tissue, gain, rate_x, rate_y, d_skip)
    pay, own, gate, gain = lax.optimization_barrier((pay, own, gate, gain))
    y = scan_calls(plan, consts, "row", "col", pay)
    y = lax.all_to_all(y, "col", 0, 0, tiled=True, axis_index_groups=groups)
    return finish(plan, y, own, gate, gain, w_out)


def solution(mesh):
    placed = (
        P(("slides", "row"), "col", None),
        P(("slides", "row"), "col"),
        P(),
        P(),
        P(),
        P(),
        P(),
        P(),
        P(),
        P(),
    )
    return jax.shard_map(
        per_device,
        mesh=mesh,
        in_specs=placed,
        out_specs=P(("slides", "row"), "col", None),
        check_vma=False,
    )
```

```python
import functools

import jax
import jax.numpy as jnp
import numpy as np
from jax import lax
from jax.experimental import pallas as pl
from jax.experimental.pallas import tpu as pltpu
from jax.sharding import PartitionSpec as P

norm_eps = 1e-05
LANES = 128
HALF = LANES // 2
F32 = jnp.float32
BF16 = jnp.bfloat16


def round_up(value, step):
    return -(-value // step) * step


def in_hbm(x):
    return pltpu.with_memory_space_constraint(x, pltpu.HBM)


def mm(a, b):
    return jnp.dot(a, b, preferred_element_type=F32)


def nt_dot(a, b):
    return lax.dot_general(a, b, (((1,), (1,)), ((), ())), preferred_element_type=F32)


def tn_dot(a, b):
    return lax.dot_general(a, b, (((0,), (0,)), ((), ())), preferred_element_type=F32)


class Plan:
    def __init__(self, rows, cols, states, heads, width, devices):
        self.rows, self.cols, self.states, self.heads = rows, cols, states, heads
        self.width = width
        self.parts = 2 if devices % 2 == 0 and devices > 2 else 1
        self.devices = devices // self.parts
        self.group = width // self.devices
        self.slot = min(self.group, HALF)
        self.slots = self.group // self.slot
        self.work = self.slots * self.devices
        self.head_width = width // heads
        self.col_pad = round_up(cols, 8)
        self.count = rows * cols
        self.half = self.count // 2 // 8 * 8
        self.cells = round_up(self.count, 8)
        self.edge = rows * states
        self.top = states * self.col_pad
        self.bc = 2 * states
        self.spare = LANES - self.half
        self.tail_cells = self.count - self.half - HALF - self.spare
        self.at_bc = self.cells
        self.at_dt = self.at_bc + self.bc + states
        assert HALF <= self.half and 0 < self.tail_cells <= self.cells - self.count and self.bc <= HALF
        self.at_rate = self.at_dt + 2 * self.slots
        self.message = round_up(self.at_rate + 1, 8)
        self.tail = self.edge % LANES
        self.solid = self.edge // LANES
        self.share = LANES // self.tail if self.tail else 1
        self.packed = self.slots * self.solid + (-(-self.slots // self.share) if self.tail else 0)
        assert self.head_width % self.slot == 0 and self.group % self.slot == 0
        assert LANES % self.head_width == 0 and LANES % self.group == 0
        assert self.cells - self.half <= LANES
        assert states % 16 == 0 and heads % 8 == 0

    def segments(self):
        return [list(range(p * self.devices, (p + 1) * self.devices)) for p in range(self.parts)]

    def lanes(self):
        at = np.arange(2 * LANES)
        cell = np.where(at < LANES, at, at - LANES + self.half)
        live = np.where(at < LANES, at < self.half, cell < self.count)
        return cell // self.cols, cell % self.cols, live

    def constants(self):
        i, j, real = self.lanes()
        both = real[:, None] & real[None]
        cell = np.arange(self.cells)
        ci, cj = cell // self.cols, cell % self.cols
        creal = cell < self.count
        le = np.arange(round_up(self.rows, 8))
        lj = np.arange(self.col_pad)
        out = {}
        out["to1"] = (j[:, None] <= j[None]) & both
        out["to2"] = (j[:, None] == j[None]) & (i[:, None] <= i[None]) & both
        out["from1"] = (i[:, None] == i[None]) & (j[:, None] > j[None]) & both
        out["from2"] = (i[:, None] > i[None]) & both
        out["side1"] = (i[None] == le[:, None]) & real[None]
        out["side2"] = (i[None] > le[:, None]) & real[None]
        out["sidemask"] = (i[None] >= le[:, None]) & (le < self.rows)[:, None] & real[None]
        out["down1"] = (j[None] <= lj[:, None]) & real[None]
        out["down2"] = (j[None] == lj[:, None]) & real[None]
        out["downmask"] = (j[None] <= lj[:, None]) & (lj < self.cols)[:, None] & real[None]
        out["pick"] = (
            (i == self.rows - 1)[:, None] & real[:, None] & (j[:, None] == np.tile(lj, self.states)[None])
        )
        cboth = creal[:, None] & real[None]
        out["own1"] = (j[None] <= cj[:, None]) & cboth
        out["own2"] = (j[None] == cj[:, None]) & (i[None] <= ci[:, None]) & cboth
        out["ownmask"] = (i[None] <= ci[:, None]) & (j[None] <= cj[:, None]) & cboth
        out["lanei"] = (np.arange(self.rows)[:, None] == i[None]) & real[None]
        out["lanej"] = (np.arange(self.cols)[:, None] == j[None]) & real[None]
        return {k: in_hbm(jnp.asarray(x.astype(np.float32), BF16)) for k, x in out.items()}


def full(shape):
    return pl.BlockSpec(shape, lambda *_: (0,) * len(shape))


HBM = pl.BlockSpec(memory_space=pltpu.HBM)
SMEM = pl.BlockSpec(memory_space=pltpu.SMEM)


def split_cell(plan, cell):
    i = lax.shift_right_logical(cell * (-(-65536 // plan.cols)), 16)
    return i, cell - i * plan.cols


def cell_mask_of(plan, t_ref):
    t = t_ref[...].astype(F32).astype(BF16)
    shape = (plan.cells, plan.cols)
    _, j = split_cell(plan, lax.broadcasted_iota(jnp.int32, shape, 0))
    pick = ones(j == lax.broadcasted_iota(jnp.int32, shape, 1))
    shape = (plan.cells, plan.rows)
    i, _ = split_cell(plan, lax.broadcasted_iota(jnp.int32, shape, 0))
    here = i == lax.broadcasted_iota(jnp.int32, shape, 1)
    return jnp.sum(jnp.where(here, mm(pick, t), 0.0), axis=1, keepdims=True)


def rate_row(heads_of, rx_ref, ry_ref):
    at = lax.broadcasted_iota(jnp.int32, (1, LANES), 1)
    rate = jnp.zeros((1, LANES), F32)
    part = jnp.zeros((1, LANES), jnp.int32)
    for s, head in enumerate(heads_of):
        for k, ref in enumerate((rx_ref, ry_ref)):
            first = 8 * s + 3 * k
            here = (at >= first) & (at < first + 3)
            rate = jnp.where(here, ref[head], rate)
            part = jnp.where(here, at - first, part)
    high = rate.astype(BF16).astype(F32)
    middle = (rate - high).astype(BF16).astype(F32)
    low = rate - high - middle
    return jnp.where(part == 0, high, jnp.where(part == 1, middle, low))


def project_kernel(
    plan, chunks, bias_hbm, rx_hbm, ry_hbm, x_hbm, w_hbm, wt_hbm, t_hbm, lanei_hbm, lanej_hbm,
    v_ref, pay_hbm, rows_ref, flat_ref,
    bias_ref, rx_ref, ry_ref, x_ref, w_ref, wt_ref, t_ref, lanei_ref, lanej_ref, pay_ref, wide, sems, w_sems, out_sems,
):
    group, states, cells, heads = plan.group, plan.states, plan.cells, plan.heads
    half, rest = plan.half, plan.cells - plan.half
    tile = plan.width // chunks
    pairs = (
        (x_hbm, x_ref), (t_hbm, t_ref), (wt_hbm, wt_ref), (lanei_hbm, lanei_ref), (lanej_hbm, lanej_ref),
        (bias_hbm, bias_ref), (rx_hbm, rx_ref), (ry_hbm, ry_ref),
    )
    loads = [pltpu.make_async_copy(a, b, sems.at[k]) for k, (a, b) in enumerate(pairs)]
    copies = [
        pltpu.make_async_copy(w_hbm.at[:, k * tile : (k + 1) * tile], w_ref.at[k], w_sems.at[k])
        for k in range(chunks)
    ]
    for copy in loads + copies:
        copy.start()
    wide[...] = jnp.zeros_like(wide)
    v_ref[half:LANES, :] = jnp.zeros((LANES - half, plan.width), BF16)
    v_ref[LANES + rest :, :] = jnp.zeros((LANES - rest, plan.width), BF16)

    loads[0].wait()
    for i in range(plan.rows):
        wide[i * plan.cols : (i + 1) * plan.cols, :] = x_ref[i].astype(F32)
    x = wide[...].astype(BF16)
    flat_ref[...] = x
    for copy in loads[1:]:
        copy.wait()
    keep = cell_mask_of(plan, t_ref)
    t = t_ref[...].astype(F32).astype(BF16)
    m = jnp.sum(mm(t, lanei_ref[...]) * lanej_ref[...].astype(F32), axis=0, keepdims=True)
    table = nt_dot(wt_ref[...], x)
    ext = jnp.concatenate([table, jnp.zeros((table.shape[0], 2 * LANES - cells), F32)], axis=1)
    lane = lax.broadcasted_iota(jnp.int32, (table.shape[0], LANES), 1)
    lo, hi = ext[:, :LANES], ext[:, LANES:]
    shift = half % LANES
    if shift:
        moved = jnp.where(
            lane < LANES - shift, pltpu.roll(lo, LANES - shift, 1), pltpu.roll(hi, LANES - shift, 1)
        )
    else:
        moved = hi
    table = jnp.concatenate([jnp.where(lane < half, lo, 0.0), jnp.where(lane < plan.count - half, moved, 0.0)], axis=1)
    z = table[2 * states :]
    at = lax.broadcasted_iota(jnp.int32, z.shape, 0)
    for h in range(heads):
        z = jnp.where(at == h, z + bias_ref[h], z)
    soft = m * (jnp.maximum(z, 0.0) + jnp.log1p(jnp.exp(-jnp.abs(z))))
    table = jnp.concatenate([table[: 2 * states], soft], axis=0).astype(BF16)
    rows_ref[...] = table.astype(F32)
    bc = rows_ref[: 2 * states, :]
    lane = lax.broadcasted_iota(jnp.int32, (2 * states, LANES), 1)
    early = jnp.where(lane < half, bc[:, :LANES], pltpu.roll(bc[:, LANES:], half - HALF, 1)).astype(BF16)
    lane = lax.broadcasted_iota(jnp.int32, (states, LANES), 1)
    late = jnp.where(lane < HALF, bc[:states, LANES:], pltpu.roll(bc[states:, LANES:], HALF, 1)).astype(BF16)
    first_end = HALF + plan.spare
    ends = bc[:, LANES:].T[first_end : first_end + 8]
    ends = jnp.concatenate([ends, jnp.zeros((8, LANES - 2 * states), F32)], axis=1)
    ends = pltpu.roll(ends, plan.tail_cells, 0)
    pad_row = lax.broadcasted_iota(jnp.int32, (8, LANES), 0) >= plan.count - (cells - 8)
    steps = rows_ref[2 * states :, :]

    lane = lax.broadcasted_iota(jnp.int32, (cells, LANES), 1)
    sent = []
    for chunk in range(chunks):
        copies[chunk].wait()
        v = mm(flat_ref[...], w_ref[chunk]).astype(BF16).astype(F32) * keep
        low = v.astype(BF16)
        v_ref[0:half, chunk * tile : (chunk + 1) * tile] = low[:half]
        v_ref[LANES : LANES + rest, chunk * tile : (chunk + 1) * tile] = low[half:]
        per = tile // group
        for k in range(per):
            dest = chunk * per + k
            base, at = k * group // LANES * LANES, k * group % LANES
            mine = v[:, base : base + LANES]
            if at:
                mine = pltpu.roll(mine, LANES - at, 1)
            if group < LANES:
                mine = jnp.where(lane < group, mine, 0.0)
            pay_ref[dest, 0 : cells - 8, :] = mine[: cells - 8].astype(BF16)
            pay_ref[dest, cells - 8 : cells, :] = jnp.where(pad_row, ends, mine[cells - 8 :]).astype(BF16)
            dts, heads_of = [], []
            for s in range(plan.slots):
                head = (chunk * tile + k * group + s * plan.slot) // plan.head_width
                heads_of.append(head)
                dts += [steps[head : head + 1, :LANES], steps[head : head + 1, LANES:]]
            dts.append(rate_row(heads_of, rx_ref, ry_ref))
            pay_ref[dest, plan.at_bc : plan.at_bc + plan.bc, :] = early
            pay_ref[dest, plan.at_bc + plan.bc : plan.at_dt, :] = late
            spare = plan.message - plan.at_dt - len(dts)
            dts += [jnp.zeros((spare, LANES), F32)] if spare else []
            pay_ref[dest, plan.at_dt : plan.message, :] = jnp.concatenate(dts, axis=0).astype(BF16)
            sent.append(pltpu.make_async_copy(pay_ref.at[dest], pay_hbm.at[dest], out_sems.at[dest]))
            sent[-1].start()
    for copy in sent:
        copy.wait()


def project(plan, consts, slide, w_in, w_bcd, tissue, dt_bias, rate_x, rate_y):
    chunks = 2
    tile = plan.width // chunks
    depth = slide.shape[2]
    args = [dt_bias, rate_x, rate_y, slide, w_in, w_bcd.T, tissue.T, consts["lanei"], consts["lanej"]]
    count = 2 * plan.states + plan.heads
    assert plan.width % chunks == 0 and tile % plan.group == 0 and tile % LANES == 0
    message = (plan.devices, plan.message, LANES)
    outs = [((2 * LANES, plan.width), BF16), (message, BF16), ((count, 2 * LANES), F32), ((plan.cells, depth), BF16)]
    specs = [full(s) for s, _ in outs]
    specs[1] = HBM
    return pl.pallas_call(
        functools.partial(project_kernel, plan, chunks),
        grid=(1,),
        in_specs=[HBM] * len(args),
        out_specs=specs,
        out_shape=[jax.ShapeDtypeStruct(s, d) for s, d in outs],
        scratch_shapes=[
            pltpu.SMEM(dt_bias.shape, F32),
            pltpu.SMEM(rate_x.shape, F32),
            pltpu.SMEM(rate_y.shape, F32),
            pltpu.VMEM(slide.shape, BF16),
            pltpu.VMEM((chunks, depth, tile), BF16),
        ]
        + [pltpu.VMEM(x.shape, x.dtype) for x in args[5:]]
        + [
            pltpu.VMEM(message, BF16),
            pltpu.VMEM((plan.cells, depth), F32),
            pltpu.SemaphoreType.DMA((8,)),
            pltpu.SemaphoreType.DMA((chunks,)),
            pltpu.SemaphoreType.DMA((plan.devices,)),
        ],
        compiler_params=pltpu.CompilerParams(vmem_limit_bytes=24 * 2**20),
        name="project",
    )(*[in_hbm(x) for x in args])


def home_kernel(plan, v_ref, rows_ref, flat_ref, w_hbm, *refs):
    sources, refs = refs[:9], refs[9:]
    gain_hbm, out_ref, gate_hbm, gain_out, pair, w_ref, gate_ref = refs[:7]
    held, (sem, gain_sem, sems, gate_sems) = refs[7:16], refs[16:]
    states, cells, half = plan.states, plan.cells, plan.half
    reads = [pltpu.make_async_copy(a, b, sems.at[k]) for k, (a, b) in enumerate(zip(sources, held))]
    reads.append(pltpu.make_async_copy(gain_hbm, gain_out, gain_sem))
    copy = pltpu.make_async_copy(w_hbm.at[:, plan.width :], w_ref, sem)
    for each in reads + [copy]:
        each.start()
    rx_ref, ry_ref, skip_ref, t_ref, own1_ref, own2_ref, from1_ref, from2_ref, mask_ref = held
    b = rows_ref[0:states, :].astype(BF16)
    c = rows_ref[states : 2 * states, :].astype(BF16)
    pairs = tn_dot(c, b)
    pairs = jnp.concatenate([pairs[:half], pairs[LANES : LANES + cells - half]], axis=0)
    for each in reads:
        each.wait()
    pair[...] = pairs * mask_ref[...].astype(F32)
    lane = lax.broadcasted_iota(jnp.int32, (cells, LANES), 1)
    per = LANES // plan.head_width
    for block in range(plan.width // LANES):
        v = v_ref[:, block * LANES : (block + 1) * LANES]
        vc = jnp.concatenate([v[:half], v[LANES : LANES + cells - half]], axis=0).astype(F32)
        total = None
        for k in range(per):
            h = block * per + k
            dt = rows_ref[2 * states + h : 2 * states + h + 1, :]
            low = dt.astype(BF16)
            x = mm(own1_ref[...] * low, from1_ref[...])
            y = mm(own2_ref[...] * low, from2_ref[...])
            weight = jnp.exp(-(rx_ref[h] * x + ry_ref[h] * y)) * pair[...] * dt
            part = mm(weight.astype(BF16), v) + skip_ref[h] * vc
            total = part if total is None else jnp.where(lane < k * plan.head_width, total, part)
        out_ref[:, block * LANES : (block + 1) * LANES] = total.astype(BF16)
    keep = cell_mask_of(plan, t_ref)
    copy.wait()
    tile = plan.width // gate_sems.shape[0]
    sent = []
    for block in range(plan.width // tile):
        at = slice(block * tile, (block + 1) * tile)
        z = mm(flat_ref[...], w_ref[:, at]).astype(BF16).astype(F32)
        gate_ref[:, at] = (z * (1.0 / (1.0 + jnp.exp(-z))) * keep).astype(BF16)
        sent.append(pltpu.make_async_copy(gate_ref.at[:, at], gate_hbm.at[:, at], gate_sems.at[block]))
        sent[-1].start()
    for each in sent:
        each.wait()


def home(plan, consts, v, rows, flat, w_in, tissue, gain, rate_x, rate_y, d_skip):
    sources = [rate_x, rate_y, d_skip, tissue.T] + [consts[k] for k in ("own1", "own2", "from1", "from2", "ownmask")]
    fixed = [in_hbm(x) for x in [w_in] + sources + [gain]]
    outs = [((plan.cells, plan.width), BF16), ((plan.cells, plan.width), BF16), (gain.shape, F32)]
    return pl.pallas_call(
        functools.partial(home_kernel, plan),
        grid=(1,),
        in_specs=[full(x.shape) for x in (v, rows, flat)] + [HBM] * len(fixed),
        out_specs=[full(outs[0][0]), HBM, full(outs[2][0])],
        out_shape=[jax.ShapeDtypeStruct(s, d) for s, d in outs],
        scratch_shapes=[
            pltpu.VMEM((plan.cells, 2 * LANES), F32),
            pltpu.VMEM((w_in.shape[0], w_in.shape[1] - plan.width), BF16),
            pltpu.VMEM((plan.cells, plan.width), BF16),
        ]
        + [pltpu.SMEM(x.shape, F32) for x in sources[:3]]
        + [pltpu.VMEM(x.shape, x.dtype) for x in sources[3:]]
        + [
            pltpu.SemaphoreType.DMA,
            pltpu.SemaphoreType.DMA,
            pltpu.SemaphoreType.DMA((len(sources),)),
            pltpu.SemaphoreType.DMA((4,)),
        ],
        compiler_params=pltpu.CompilerParams(vmem_limit_bytes=24 * 2**20),
        name="home",
    )(v, rows, flat, *fixed)


def ones(mask):
    return jnp.where(mask, 1.0, 0.0).astype(BF16)


def places(plan, shape, axis):
    at = lax.broadcasted_iota(jnp.int32, shape, axis)
    late = at >= LANES
    cell = jnp.where(late, at - (LANES - plan.half), at)
    i, j = split_cell(plan, cell)
    return i, j, cell < jnp.where(late, plan.count, plan.half)


def map_rows(plan, pay_ref, turned, t, k):
    n = plan.states
    first = pay_ref[t, plan.at_bc + k * n : plan.at_bc + (k + 1) * n, :].astype(F32)
    second = pay_ref[t, plan.at_bc + plan.bc : plan.at_dt, :].astype(F32)
    if k:
        second = pltpu.roll(second, HALF, 1)
    ends = turned[k * n : (k + 1) * n, LANES:].astype(F32)
    lane = lax.broadcasted_iota(jnp.int32, (n, LANES), 1)
    moved = pltpu.roll(first, LANES + HALF - plan.half, 1)
    ends = pltpu.roll(ends, LANES - plan.tail_cells, 1)
    second = jnp.where(lane < HALF, second, jnp.where(lane < HALF + plan.spare, moved, ends))
    return jnp.concatenate([first, second], axis=1)


def turn_all(plan, pay_ref, turned, b_ref):
    for t in range(plan.devices):
        sides = []
        for lo, hi in ((0, plan.half), (plan.half, plan.cells)):
            v = pay_ref[t, lo:hi, :].astype(F32)
            if hi - lo < LANES:
                v = jnp.concatenate([v, jnp.zeros((LANES - hi + lo, LANES), F32)], axis=0)
            sides.append(v.T)
        v = jnp.concatenate(sides, axis=1).astype(BF16)
        for s in range(plan.slots):
            turned[s * plan.devices + t] = v[s * HALF : (s + 1) * HALF]
        b_ref[t] = map_rows(plan, pay_ref, v, t, 0)


def load_steps(plan, pay_ref, dts):
    for t in range(plan.devices):
        rows = pay_ref[t, plan.at_dt : plan.message, :].astype(F32)
        for s in range(plan.slots):
            w = s * plan.devices + t
            dts[w : w + 1, :LANES] = rows[2 * s : 2 * s + 1]
            dts[w : w + 1, LANES:] = rows[2 * s + 1 : 2 * s + 2]


def rates_of(plan, pay_ref, kind):
    row = pay_ref[0, plan.at_dt : plan.message, :].astype(F32)[plan.at_rate - plan.at_dt : plan.at_rate - plan.at_dt + 1]
    at = lax.broadcasted_iota(jnp.int32, (1, LANES), 1)
    first = [8 * s + 3 * kind for s in range(plan.slots)]
    return [jnp.sum(jnp.where((at >= f) & (at < f + 3), row, 0.0), axis=1, keepdims=True) for f in first]


def slot_rates(plan, pay_ref, kind):
    return jnp.concatenate(
        [jnp.broadcast_to(r, (plan.devices, 1)) for r in rates_of(plan, pay_ref, kind)], axis=0
    )


def pack_edges(plan, out_ref, held):
    for s in range(plan.slots):
        for k in range(plan.solid):
            out_ref[s * plan.solid + k] = held[s][:, k * LANES : (k + 1) * LANES].astype(BF16)
    if plan.tail:
        first = plan.slots * plan.solid
        for k in range(plan.packed - first):
            parts = [x[:, plan.solid * LANES :] for x in held[k * plan.share : (k + 1) * plan.share]]
            spare = LANES - plan.tail * len(parts)
            parts += [jnp.zeros((HALF, spare), F32)] if spare else []
            out_ref[first + k] = jnp.concatenate(parts, axis=1).astype(BF16)


def unpack_edges(plan, ref, s):
    parts = [ref[s * plan.solid + k].astype(F32) for k in range(plan.solid)]
    if plan.tail:
        last = ref[plan.slots * plan.solid + s // plan.share].astype(F32)
        at = s % plan.share * plan.tail
        parts.append(last[:, at : at + plan.tail])
    return jnp.concatenate(parts, axis=1)


def scan_edges(plan, pay_ref, turned, b_ref, dts, inner, kept, seen):
    states, tiles, wide = plan.states, plan.devices, 2 * LANES
    i, j, real = places(plan, (wide, wide), 0)
    ti, tj, treal = places(plan, (wide, wide), 1)
    from1 = ones((i == ti) & (j > tj) & real & treal)
    edge_row = lax.div(lax.broadcasted_iota(jnp.int32, (wide, plan.edge), 1), states)
    i, _, real = places(plan, (wide, plan.edge), 0)
    keep = ones((i == edge_row) & real)
    ti, _, treal = places(plan, (plan.rows, wide), 1)
    rowsel = ones((ti == lax.broadcasted_iota(jnp.int32, (plan.rows, wide), 0)) & treal)
    dt = dts[...]
    low = dt.astype(BF16)
    rate = slot_rates(plan, pay_ref, 0)
    inner[...] = jnp.exp(-rate * mm(low, from1)) * dt
    kept[...] = jnp.exp(-rate * mm(low, keep))
    ends = []
    for s in range(plan.slots):
        held = jnp.zeros((HALF, plan.edge), F32)
        product = jnp.ones((1, plan.edge), F32)
        for t in range(tiles):
            w = s * tiles + t
            seen(w, held, product)
            b = b_ref[t]
            bd = (b * inner[w : w + 1, :]).astype(BF16)
            left = jnp.concatenate([bd * rowsel[i : i + 1] for i in range(plan.rows)], axis=0)
            now = kept[w : w + 1, :]
            held = held * now + nt_dot(turned[w], left)
            product = product * now
        ends.append(held)
    return ends


def last_kernel(plan, axis, pay_ref, last_ref, turned, b_ref, dts, inner):
    @pl.when(lax.axis_index(axis) < (plan.parts - 1) * plan.devices)
    def _():
        states, tiles, wide = plan.states, plan.devices, 2 * LANES
        turn_all(plan, pay_ref, turned, b_ref)
        load_steps(plan, pay_ref, dts)
        i, j, real = places(plan, (wide, wide), 0)
        ti, tj, treal = places(plan, (wide, wide), 1)
        same = (i == ti) & real & treal
        ti, _, treal = places(plan, (plan.rows, wide), 1)
        rowsel = ones((ti == lax.broadcasted_iota(jnp.int32, (plan.rows, wide), 0)) & treal)
        low = dts[...].astype(BF16)
        rest, whole = mm(low, ones(same & (j > tj))), mm(low, ones(same))
        left = []
        for s in range(plan.slots):
            after = jnp.zeros((1, wide), F32)
            rows = []
            for t in reversed(range(tiles)):
                rows.append(after)
                after = after + whole[s * tiles + t : s * tiles + t + 1]
            left += rows[::-1]
        inner[...] = jnp.exp(-slot_rates(plan, pay_ref, 0) * (rest + jnp.concatenate(left, axis=0))) * dts[...]
        ends = []
        for s in range(plan.slots):
            held = None
            for t in range(tiles):
                w = s * tiles + t
                b = b_ref[t]
                bd = (b * inner[w : w + 1, :]).astype(BF16)
                left = jnp.concatenate([bd * rowsel[i : i + 1] for i in range(plan.rows)], axis=0)
                part = nt_dot(turned[w], left)
                held = part if held is None else held + part
            ends.append(held)
        pack_edges(plan, last_ref, ends)


def maps_kernel(
    plan, pay_ref, to1_ref, to2_ref, from1_ref, from2_ref, side1_ref, side2_ref,
    sidemask_ref, down1_ref, down2_ref, downmask_ref, pick_ref,
    side_ref, above_ref, passed_ref, top_ref, edge_ref, upto_ref, c_ref, turned, b_ref, dts, inner, kept, s1, s2, d1, d2,
):
    states, tiles, cp, work = plan.states, plan.devices, plan.col_pad, plan.work
    rp = side1_ref.shape[0]
    turn_all(plan, pay_ref, turned, b_ref)
    load_steps(plan, pay_ref, dts)
    for t in range(tiles):
        c_ref[t] = map_rows(plan, pay_ref, turned[t], t, 1).astype(BF16)

    def seen(w, held, product):
        edge_ref[w] = held.astype(BF16)
        upto_ref[w : w + 1, :] = product

    scan_edges(plan, pay_ref, turned, b_ref, dts, inner, kept, seen)
    low = dts[...].astype(BF16)
    above_ref[...] = jnp.exp(-slot_rates(plan, pay_ref, 1) * mm(low, to2_ref[...]))
    rates_x, rates_y = rates_of(plan, pay_ref, 0), rates_of(plan, pay_ref, 1)
    for w in range(work):
        rf = dts[w : w + 1, :]
        s1[w * rp : (w + 1) * rp, :] = side1_ref[...].astype(F32) * rf
        s2[w * rp : (w + 1) * rp, :] = side2_ref[...].astype(F32) * rf
        d1[w * cp : (w + 1) * cp, :] = down1_ref[...].astype(F32) * rf
        d2[w * cp : (w + 1) * cp, :] = down2_ref[...].astype(F32) * rf
    mask = sidemask_ref[...].astype(F32)
    x, y = mm(s1[...].astype(BF16), to1_ref[...]), mm(s2[...].astype(BF16), to2_ref[...])
    shape = (states, plan.top)
    n = lax.broadcasted_iota(jnp.int32, shape, 0)
    diag = ones(n == lax.div(lax.broadcasted_iota(jnp.int32, shape, 1), cp))
    for w in range(work):
        s = w // tiles
        at = slice(w * rp, (w + 1) * rp)
        side = (jnp.exp(-(rates_x[s] * x[at] + rates_y[s] * y[at])) * mask).astype(BF16)
        side_ref[w] = side
        bottom = mm(side, pick_ref[...]).astype(BF16)
        passed_ref[w] = jnp.concatenate([diag * bottom[i : i + 1] for i in range(plan.rows)], axis=0)
    x, y = mm(d1[...].astype(BF16), from1_ref[...]), mm(d2[...].astype(BF16), from2_ref[...])
    mask = downmask_ref[...].astype(F32)
    for w in range(work):
        s, t = w // tiles, w % tiles
        at = slice(w * cp, (w + 1) * cp)
        fall = jnp.exp(-(rates_x[s] * x[at] + rates_y[s] * y[at])) * mask * dts[w : w + 1, :]
        b = b_ref[t]
        falls = jnp.concatenate([fall * b[n : n + 1] for n in range(states)], axis=0).astype(BF16)
        top_ref[w] = nt_dot(turned[w], falls) + mm(edge_ref[w], passed_ref[w])


def join_kernel(plan, row_axis, col_axis, upto_ref, entry_ref, passed_ref, top_ref, out_ref):
    sends = lax.axis_index(row_axis) < lax.axis_size(row_axis) - 1
    first = lax.axis_index(col_axis) < plan.devices

    @pl.when(sends & first)
    def _():
        out_ref[...] = top_ref[...].astype(BF16)

    @pl.when(sends & jnp.logical_not(first))
    def _():
        for s in range(plan.slots):
            entry = unpack_edges(plan, entry_ref, s)
            for t in range(plan.devices):
                w = s * plan.devices + t
                late = (entry * upto_ref[w : w + 1, :]).astype(BF16)
                out_ref[w] = (top_ref[w] + mm(late, passed_ref[w])).astype(BF16)


def sides_kernel(plan, axis, c_ref, edge_ref, upto_ref, entry_ref, side_ref, above_ref, y_ref, down_ref):
    states, tiles = plan.states, plan.devices
    shape = (plan.col_pad, 2 * LANES)
    _, tj, treal = places(plan, shape, 1)
    colsel = jnp.where((tj == lax.broadcasted_iota(jnp.int32, shape, 0)) & treal, 1.0, 0.0)
    first = lax.axis_index(axis) < plan.devices

    @pl.when(first)
    def _():
        for s in range(plan.slots):
            for t in range(tiles):
                w = s * tiles + t
                c = c_ref[t]
                side = side_ref[w]
                left = jnp.concatenate([c * side[i : i + 1] for i in range(plan.rows)], axis=0)
                whole = edge_ref[w]
                y_ref[w] = mm(whole, left)
                ca = c.astype(F32) * above_ref[w : w + 1, :]
                down_ref[w] = jnp.concatenate([colsel * ca[n : n + 1] for n in range(states)], axis=0).astype(BF16)

    @pl.when(jnp.logical_not(first))
    def _():
        for s in range(plan.slots):
            entry = unpack_edges(plan, entry_ref, s)
            for t in range(tiles):
                w = s * tiles + t
                c = c_ref[t]
                side = side_ref[w]
                left = jnp.concatenate([c * side[i : i + 1] for i in range(plan.rows)], axis=0)
                whole = (edge_ref[w].astype(F32) + entry * upto_ref[w : w + 1, :]).astype(BF16)
                y_ref[w] = mm(whole, left)
                ca = c.astype(F32) * above_ref[w : w + 1, :]
                down_ref[w] = jnp.concatenate([colsel * ca[n : n + 1] for n in range(states)], axis=0).astype(BF16)


def cells_kernel(plan, y_ref, down_ref, top_ref, out_ref):
    tiles = plan.devices
    for t in range(tiles):
        ys = [y_ref[w] + mm(top_ref[w], down_ref[w]) for w in range(t, plan.work, tiles)]
        if plan.slots == 1:
            ys.append(jnp.zeros_like(ys[0]))
        y = jnp.concatenate(ys, axis=0)
        for k, (lo, hi) in enumerate(((0, plan.half), (plan.half, plan.cells))):
            out_ref[t, lo:hi, :] = y[:, k * LANES : (k + 1) * LANES].T[: hi - lo].astype(BF16)


def call(kernel, name, args, outs, scratch=(), out_specs=None):
    return pl.pallas_call(
        kernel,
        grid=(1,),
        in_specs=[full(x.shape) for x in args],
        out_specs=out_specs or [full(s) for s, _ in outs],
        out_shape=[jax.ShapeDtypeStruct(s, d) for s, d in outs],
        scratch_shapes=[x if not isinstance(x, tuple) else pltpu.VMEM(*x) for x in scratch],
        compiler_params=pltpu.CompilerParams(vmem_limit_bytes=24 * 2**20),
        name=name,
    )(*args)


def scan_calls(plan, consts, row_axis, col_axis, pay):
    work, cp, wide = plan.work, plan.col_pad, 2 * LANES
    rp = consts["side1"].shape[0]
    steps = [((work, HALF, wide), BF16), ((plan.devices, plan.states, wide), F32), ((work, wide), F32), ((work, wide), F32), ((work, plan.edge), F32)]
    shape = (plan.packed, HALF, LANES)
    if plan.parts > 1:
        last = call(functools.partial(last_kernel, plan, col_axis), "last", [pay], [(shape, BF16)], steps[:4])[0]
        entry = lax.ppermute(last, col_axis, [(k, k + plan.devices) for k in range(plan.devices)])
    else:
        entry = jnp.zeros(shape, BF16)
    names = ("to1", "to2", "from1", "from2", "side1", "side2", "sidemask", "down1", "down2", "downmask", "pick")
    side, above, passed, tops, edges, upto, c = call(
        functools.partial(maps_kernel, plan),
        "maps",
        [pay] + [consts[k] for k in names],
        [
            ((work, rp, wide), BF16),
            ((work, wide), F32),
            ((work, plan.edge, plan.top), BF16),
            ((work, HALF, plan.top), F32),
            ((work, HALF, plan.edge), BF16),
            ((work, plan.edge), F32),
            ((plan.devices, plan.states, wide), BF16),
        ],
        steps + [((work * rp, wide), F32)] * 2 + [((work * cp, wide), F32)] * 2,
    )
    edge_entry = entry
    tops = call(
        functools.partial(join_kernel, plan, row_axis, col_axis),
        "join",
        [upto, entry, passed, tops],
        [((work, HALF, plan.top), BF16)],
    )[0]
    count = lax.axis_size(row_axis)
    chain = [(r, r + 1) for r in range(count - 1)]
    entry = lax.ppermute(tops, row_axis, chain)
    if count > 2:
        keep = jnp.dot(above.astype(BF16), consts["pick"], preferred_element_type=F32)[:, None, :]
        for _ in range(count - 2):
            entry = lax.ppermute(
                (tops.astype(F32) + keep * entry.astype(F32)).astype(BF16), row_axis, chain
            )
    y, down = call(
        functools.partial(sides_kernel, plan, col_axis),
        "sides",
        [c, edges, upto, edge_entry, side, above],
        [((work, HALF, wide), F32), ((work, plan.top, wide), BF16)],
    )
    return call(
        functools.partial(cells_kernel, plan),
        "cells",
        [y, down, entry],
        [((plan.devices, plan.cells, LANES), BF16)],
    )[0]


def finish_kernel(plan, y_ref, own_ref, gate_ref, gain_ref, w_ref, out_hbm, full_ref, out_ref, sems):
    group = plan.group
    per = LANES // group
    lane = lax.broadcasted_iota(jnp.int32, (plan.cells, LANES), 1)
    for block in range(plan.width // LANES):
        joined = None
        for d in range(per):
            part = y_ref[block * per + d].astype(F32)
            if d:
                part = pltpu.roll(part, d * group, 1)
            joined = part if joined is None else jnp.where(lane < d * group, joined, part)
        at = slice(block * LANES, (block + 1) * LANES)
        y = joined + own_ref[:, at].astype(F32)
        full_ref[:, at] = y.astype(BF16).astype(F32) * gate_ref[:, at].astype(F32)
    gated = full_ref[...]
    scale = lax.rsqrt(jnp.mean(gated * gated, axis=-1, keepdims=True) + norm_eps)
    normed = (gated * scale * gain_ref[...]).astype(BF16)
    copies = []
    chunks = sems.shape[0]
    tile = w_ref.shape[1] // chunks
    for k in range(chunks):
        at = slice(k * tile, (k + 1) * tile)
        out = mm(normed, w_ref[:, at])
        for i in range(plan.rows):
            out_ref[i, :, at] = out[i * plan.cols : (i + 1) * plan.cols].astype(BF16)
        copies.append(pltpu.make_async_copy(out_ref.at[:, :, at], out_hbm.at[:, :, at], sems.at[k]))
        copies[-1].start()
    for copy in copies:
        copy.wait()


def finish(plan, y, own, gate, gain, w_out):
    args = (y, own, gate, gain, w_out)
    shape = (plan.rows, plan.cols, w_out.shape[1])
    assert w_out.shape[1] == plan.width
    return call(
        functools.partial(finish_kernel, plan),
        "finish",
        args,
        [(shape, BF16)],
        [((plan.cells, plan.width), F32), (shape, BF16), pltpu.SemaphoreType.DMA((4,))],
        [HBM],
    )[0]


def per_device(slide, tissue, w_in, w_bcd, dt_bias, rate_x, rate_y, d_skip, norm_gain, w_out):
    rows, cols, model_width = slide.shape
    width = w_out.shape[0]
    heads = dt_bias.shape[0]
    states = (w_bcd.shape[1] - heads) // 2
    plan = Plan(rows, cols, states, heads, width, lax.axis_size("col"))
    consts = plan.constants()
    v, pay, table, x = project(plan, consts, slide, w_in, w_bcd, tissue, dt_bias, rate_x, rate_y)
    groups = plan.segments()
    pay = lax.all_to_all(pay, "col", 0, 0, tiled=True, axis_index_groups=groups)
    gain = norm_gain.reshape(1, width)
    own, gate, gain = home(plan, consts, v, table, x, w_in, tissue, gain, rate_x, rate_y, d_skip)
    pay, own, gate, gain = lax.optimization_barrier((pay, own, gate, gain))
    y = scan_calls(plan, consts, "row", "col", pay)
    y = lax.all_to_all(y, "col", 0, 0, tiled=True, axis_index_groups=groups)
    return finish(plan, y, own, gate, gain, w_out)


def solution(mesh):
    placed = (
        P(("slides", "row"), "col", None),
        P(("slides", "row"), "col"),
        P(),
        P(),
        P(),
        P(),
        P(),
        P(),
        P(),
        P(),
    )
    return jax.shard_map(
        per_device,
        mesh=mesh,
        in_specs=placed,
        out_specs=P(("slides", "row"), "col", None),
        check_vma=False,
    )
```
